32 devices in a mesh: hst: 4 (over x, core), dev: 8 (over z, y).
Axes of the slice: x: 2, y: 2, z: 4, core: 2. Of those that a mesh axis runs over, the one named last changes fastest.
Arguments:
- features: float32 [524288, 128], P(('hst', 'dev')), may hold values from -6 to 6
- requests: int32 [1024, 256], P(('hst', 'dev')), may hold values from 0 to 16383
- adjacent_one: int32 [135168, 15], P(('hst', 'dev')), may hold values from 0 to 8191, as said below
- adjacent_two: int32 [12288, 10], P(('hst', 'dev')), may hold values from 0 to 4223
- adjacent_three: int32 [2048, 5], P(('hst', 'dev')), may hold values from 0 to 383
- valid_one: int32 [135168, 15], P(('hst', 'dev')), may hold values from 0 to 1, as said below
- valid_two: int32 [12288, 10], P(('hst', 'dev')), may hold values from 0 to 1
- valid_three: int32 [2048, 5], P(('hst', 'dev')), may hold values from 0 to 1
- labels: int32 [2048], P(('hst', 'dev')), may hold values from 0 to 171
- labelled: int32 [2048], P(('hst', 'dev')), may hold values from 0 to 1, as said below
- weights_in: float32 [2, 128, 256], replicated, may hold values from -0.5 to 0.5
- weights_mid: float32 [2, 256, 256], replicated, may hold values from -0.375 to 0.375
- weights_out: float32 [2, 256, 172], replicated, may hold values from -0.375 to 0.375
- biases: float32 [684], replicated, may hold values from -0.6 to 0.6
- moment_one: float32 [684], replicated, may hold values from -0.0007954951 to 0.0007954951
- moment_two: float32 [684], replicated, may hold values from 6.1035155e-07 to 2.4414062e-06
- step_count: int32 [], replicated, may hold values from 2 to 20
- left_in: float32 [2, 128, 128], replicated, as said below
- left_mid: float32 [2, 256, 256], replicated, as said below
- left_out: float32 [2, 256, 256], replicated, as said below
- right_in: float32 [2, 256, 256], replicated, as said below
- right_mid: float32 [2, 256, 256], replicated, as said below
- right_out: float32 [2, 172, 172], replicated, as said below
- invleft_in: float32 [2, 128, 128], replicated, as said below
- invleft_mid: float32 [2, 256, 256], replicated, as said below
- invleft_out: float32 [2, 256, 256], replicated, as said below
- invright_in: float32 [2, 256, 256], replicated, as said below
- invright_mid: float32 [2, 256, 256], replicated, as said below
- invright_out: float32 [2, 172, 172], replicated, as said below
Outputs:
- loss: float32 [], replicated
- new_weights_in: float32 [2, 128, 256], replicated
- new_weights_mid: float32 [2, 256, 256], replicated
- new_weights_out: float32 [2, 256, 172], replicated
- copy_in: bfloat16 [2, 128, 256], replicated
- copy_mid: bfloat16 [2, 256, 256], replicated
- copy_out: bfloat16 [2, 256, 172], replicated
- new_left_in: float32 [2, 128, 128], replicated
- new_left_mid: float32 [2, 256, 256], replicated
- new_left_out: float32 [2, 256, 256], replicated
- new_right_in: float32 [2, 256, 256], replicated
- new_right_mid: float32 [2, 256, 256], replicated
- new_right_out: float32 [2, 172, 172], replicated
- new_biases: float32 [684], replicated
- new_moment_one: float32 [684], replicated
- new_moment_two: float32 [684], replicated
The draws below stay inside these ranges and needn't reach their ends.
Inputs may be any that keep to these rules, and one draw needn't show every extreme that they name: `adjacent_one`: every one of a device's 8192 pulled slots is named by some entry of its rows. `valid_one`: valid shares differ from device to device. The first seed of every device is labelled. `left_in`: a positive multiple of the identity in each of the two matrices. `left_mid`: a positive multiple of the identity in each of the two matrices. `left_out`: a positive multiple of the identity in each of the two matrices. `right_in`: a positive multiple of the identity in each of the two matrices. `right_mid`: a positive multiple of the identity in each of the two matrices. `right_out`: a positive multiple of the identity in each of the two matrices. `invleft_in`: symmetric. `invleft_mid`: symmetric. `invleft_out`: symmetric. `invright_in`: symmetric. `invright_mid`: symmetric. `invright_out`: symmetric.
All inputs are finite; a program needn't handle non-finite values.
Results may differ from the reference program's by a relative error of at most 0.0094.
Values may be sent and summed in bfloat16 or wider, within the bound.
No kernel may reach another device: no remote copies, remote signals or barrier semaphores. Data moves between devices by JAX's collectives and lax.ppermute only.
A program may use at most 128 MiB of HBM per device.

```python
import math
import jax
import jax.numpy as jnp
from jax import lax

INPUTS = 128
HIDDEN_SIZE = 256
CLASSES = 172
FANOUT_A = 15
FANOUT_B = 10
FANOUT_C = 5
SEEDS_DEV = 64
PULL_DEV = 8192
NODE_DEV = 16384
SLOTS_PEER = 256
MID_ROWS = 384
FIRST_ROWS = 4224
NODES = 524288
SEEDS = 2048
DEVICES = 32


def device_levels(rows, low_share, span):
    index = jnp.arange(DEVICES, dtype=jnp.int32)
    level = low_share + span * index // max(DEVICES - 1, 1)
    return jnp.repeat(level, rows)


def ragged_mask(key, rows, width):
    level = device_levels(rows, 35, 55)
    rolled = jax.random.randint(key, (DEVICES * rows, width), 0, 100)
    return (rolled < level[:, None]).astype(jnp.int32)


def hidden_grad():
    return 0.45 / math.sqrt(HIDDEN_SIZE * SEEDS_DEV * DEVICES)


def head_grad():
    return 0.85 / math.sqrt(CLASSES * SEEDS_DEV * DEVICES)


def draw_adjacent_one(key, part):
    keys = jax.random.split(jax.random.fold_in(key, 11), DEVICES)

    def single(one_key):
        order = jax.random.permutation(one_key, FIRST_ROWS * FANOUT_A)
        return (order % PULL_DEV).reshape(FIRST_ROWS, FANOUT_A)
    return jax.vmap(single)(keys).reshape(DEVICES * FIRST_ROWS, FANOUT_A).astype(jnp.int32)


def draw_valid_one(key, part):
    return ragged_mask(jax.random.fold_in(key, 21), FIRST_ROWS, FANOUT_A)


def draw_valid_two(key, part):
    return ragged_mask(jax.random.fold_in(key, 22), MID_ROWS, FANOUT_B)


def draw_valid_three(key, part):
    return ragged_mask(jax.random.fold_in(key, 23), SEEDS_DEV, FANOUT_C)


def draw_labelled(key, part):
    level = device_levels(SEEDS_DEV, 25, 50)
    rolled = jax.random.randint(jax.random.fold_in(key, 31), (SEEDS,), 0, 100)
    marked = (rolled < level).astype(jnp.int32)
    return marked.at[0::SEEDS_DEV].set(1)


def statistic(key, size, other, grad):
    scale = grad * grad * other
    factor = jnp.exp(jax.random.uniform(key, (2,), jnp.float32, 0.0, math.log(4.0)))
    return factor[:, None, None] * scale * jnp.eye(size, dtype=jnp.float32)[None]


def inverse_root(key, size, fan_in, grad):
    base = (fan_in ** (-0.5) / grad) ** 0.5
    key_a, key_b = jax.random.split(key)
    diagonal = jnp.exp(jax.random.uniform(key_a, (2, size), jnp.float32, math.log(0.5), math.log(2.0)))
    spread = jax.random.normal(key_b, (2, size, size), jnp.float32) * (0.25 / math.sqrt(size))
    spread = (spread + jnp.swapaxes(spread, 1, 2)) * 0.7071
    eye_mat = jnp.eye(size, dtype=jnp.float32)[None]
    return base * (spread * (1.0 - eye_mat) + diagonal[:, :, None] * eye_mat)


def draw_left_in(key, part):
    return statistic(jax.random.fold_in(key, 41), INPUTS, HIDDEN_SIZE, hidden_grad())


def draw_left_mid(key, part):
    return statistic(jax.random.fold_in(key, 42), HIDDEN_SIZE, HIDDEN_SIZE, hidden_grad())


def draw_left_out(key, part):
    return statistic(jax.random.fold_in(key, 43), HIDDEN_SIZE, CLASSES, head_grad())


def draw_right_in(key, part):
    return statistic(jax.random.fold_in(key, 44), HIDDEN_SIZE, INPUTS, hidden_grad())


def draw_right_mid(key, part):
    return statistic(jax.random.fold_in(key, 45), HIDDEN_SIZE, HIDDEN_SIZE, hidden_grad())


def draw_right_out(key, part):
    return statistic(jax.random.fold_in(key, 46), CLASSES, HIDDEN_SIZE, head_grad())


def draw_invleft_in(key, part):
    return inverse_root(jax.random.fold_in(key, 51), INPUTS, INPUTS, hidden_grad())


def draw_invleft_mid(key, part):
    return inverse_root(jax.random.fold_in(key, 52), HIDDEN_SIZE, HIDDEN_SIZE, hidden_grad())


def draw_invleft_out(key, part):
    return inverse_root(jax.random.fold_in(key, 53), HIDDEN_SIZE, HIDDEN_SIZE, head_grad())


def draw_invright_in(key, part):
    return inverse_root(jax.random.fold_in(key, 54), HIDDEN_SIZE, INPUTS, hidden_grad())


def draw_invright_mid(key, part):
    return inverse_root(jax.random.fold_in(key, 55), HIDDEN_SIZE, HIDDEN_SIZE, hidden_grad())


def draw_invright_out(key, part):
    return inverse_root(jax.random.fold_in(key, 56), CLASSES, HIDDEN_SIZE, head_grad())


def set_ends(array, own_key, least, largest):
    longest = array.shape.index(max(array.shape))
    spots = []
    for shift in (0, 1):
        where = [jax.random.randint(jax.random.fold_in(own_key, axis), (), 0, length) for axis, length in enumerate(array.shape)]
        where[longest] = (where[longest] + shift) % array.shape[longest]
        spots.append(tuple(where))
    return array.at[spots[0]].set(least).at[spots[1]].set(largest)


def levels(stream_key, dims, pieces, least, largest):
    gain = 1.0
    for axis_at, parts in pieces:
        draws = jax.random.uniform(jax.random.fold_in(jax.random.fold_in(stream_key, 6), axis_at), (parts,), jnp.float32, least / len(pieces), largest / len(pieces))
        gain = gain * jnp.repeat(jnp.exp(draws), dims[axis_at] // parts).reshape((-1,) + (1,) * (len(dims) - 1 - axis_at))
    return gain


def scatter_about(key, dims, scale, bound, cuts=(), held_as=jnp.bfloat16):
    level = levels(key, dims, cuts, -0.22, 0.18) if cuts else 1.0
    array = jax.random.normal(key, dims, jnp.float32) * scale * level
    return jnp.minimum(jnp.maximum(array, -bound), bound).astype(held_as)


def setup_inputs(seed: int = 0) -> dict:
    seeds = jax.random.split(jax.random.key(seed), 30)
    return {
        "features": scatter_about(seeds[0], (NODES, INPUTS), 1.0, 6.0, ((0, 32),), jnp.float32),
        "requests": set_ends(jax.random.randint(seeds[1], (DEVICES * DEVICES, SLOTS_PEER), 0, NODE_DEV), jax.random.fold_in(seeds[1], 1), 0, NODE_DEV - 1).astype(jnp.int32),
        "adjacent_one": draw_adjacent_one(jax.random.fold_in(seeds[29], 71), 0),
        "adjacent_two": set_ends(jax.random.randint(seeds[3], (DEVICES * MID_ROWS, FANOUT_B), 0, FIRST_ROWS), jax.random.fold_in(seeds[3], 1), 0, FIRST_ROWS - 1).astype(jnp.int32),
        "adjacent_three": set_ends(jax.random.randint(seeds[4], (SEEDS, FANOUT_C), 0, MID_ROWS), jax.random.fold_in(seeds[4], 1), 0, MID_ROWS - 1).astype(jnp.int32),
        "valid_one": draw_valid_one(jax.random.fold_in(seeds[29], 71), 0),
        "valid_two": draw_valid_two(jax.random.fold_in(seeds[29], 71), 0),
        "valid_three": draw_valid_three(jax.random.fold_in(seeds[29], 71), 0),
        "labels": set_ends(jax.random.randint(seeds[8], (SEEDS,), 0, CLASSES), jax.random.fold_in(seeds[8], 1), 0, CLASSES - 1).astype(jnp.int32),
        "labelled": draw_labelled(jax.random.fold_in(seeds[29], 71), 0),
        "weights_in": scatter_about(seeds[10], (2, INPUTS, HIDDEN_SIZE), INPUTS ** -0.5, 0.5, (), jnp.float32),
        "weights_mid": scatter_about(seeds[11], (2, HIDDEN_SIZE, HIDDEN_SIZE), HIDDEN_SIZE ** -0.5, 0.375, (), jnp.float32),
        "weights_out": scatter_about(seeds[12], (2, HIDDEN_SIZE, CLASSES), HIDDEN_SIZE ** -0.5, 0.375, (), jnp.float32),
        "biases": scatter_about(seeds[13], (2 * HIDDEN_SIZE + CLASSES,), 0.1, 0.6, (), jnp.float32),
        "moment_one": scatter_about(seeds[14], (2 * HIDDEN_SIZE + CLASSES,), (0.006 / (SEEDS_DEV * DEVICES) ** 0.5), 0.0007954951, (), jnp.float32),
        "moment_two": jnp.clip(jnp.exp(jax.random.uniform(seeds[15], (2 * HIDDEN_SIZE + CLASSES,), jnp.float32, math.log(6.103515488575795e-07), math.log(2.441406195430318e-06))), 6.103515488575795e-07, 2.441406195430318e-06),
        "step_count": jax.random.randint(seeds[16], (), 2, 21).astype(jnp.int32),
        "left_in": draw_left_in(jax.random.fold_in(seeds[29], 71), 0),
        "left_mid": draw_left_mid(jax.random.fold_in(seeds[29], 71), 0),
        "left_out": draw_left_out(jax.random.fold_in(seeds[29], 71), 0),
        "right_in": draw_right_in(jax.random.fold_in(seeds[29], 71), 0),
        "right_mid": draw_right_mid(jax.random.fold_in(seeds[29], 71), 0),
        "right_out": draw_right_out(jax.random.fold_in(seeds[29], 71), 0),
        "invleft_in": draw_invleft_in(jax.random.fold_in(seeds[29], 71), 0),
        "invleft_mid": draw_invleft_mid(jax.random.fold_in(seeds[29], 71), 0),
        "invleft_out": draw_invleft_out(jax.random.fold_in(seeds[29], 71), 0),
        "invright_in": draw_invright_in(jax.random.fold_in(seeds[29], 71), 0),
        "invright_mid": draw_invright_mid(jax.random.fold_in(seeds[29], 71), 0),
        "invright_out": draw_invright_out(jax.random.fold_in(seeds[29], 71), 0),
    }


@jax.custom_vjp
def low(v):
    return lax.optimization_barrier(v.astype(jnp.bfloat16)).astype(jnp.float32)

@jax.custom_vjp
def low_back(v):
    return v

def low_keep(v):
    return (low(v), None)

def low_pass(kept, grad):
    return (grad,)

def back_keep(v):
    return (v, None)

def back_low(kept, grad):
    return (low(grad),)
low.defvjp(low_keep, low_pass)
low_back.defvjp(back_keep, back_low)
highest = lax.Precision.HIGHEST

def product(left_side, right_side):
    return jnp.dot(left_side, right_side, precision=highest, preferred_element_type=jnp.float32)

def aggregate(source, adjacent, valid_mask):
    weights = valid_mask.astype(source.dtype)
    counts = jnp.maximum(lax.optimization_barrier(jnp.sum(weights, axis=1)), 1.0)
    summed = jnp.zeros((adjacent.shape[0], source.shape[1]), source.dtype)
    for column in range(adjacent.shape[1]):
        summed = summed + source[adjacent[:, column]] * weights[:, column:column + 1]
    return summed / counts[:, None]

def sage_layer(source, adjacent, valid_mask, weight, bias_row, final):
    source = low(source)
    selfrows = source[:adjacent.shape[0]]
    mixed = low(aggregate(source, adjacent, valid_mask))
    weight = low(weight)
    preact = low_back(product(selfrows, weight[0]) + product(mixed, weight[1]) + bias_row)
    if final:
        return preact
    return jax.nn.silu(preact)

def shampoo(master, gradient, left_stat, right_stat, left_root, right_root):
    left_new = 0.5 * left_stat + 0.5 * jnp.einsum('kio,kjo->kij', gradient, gradient, precision=highest)
    right_new = 0.5 * right_stat + 0.5 * jnp.einsum('kio,kip->kop', gradient, gradient, precision=highest)
    direction = jnp.einsum('kij,kjo->kio', left_root, gradient, precision=highest)
    direction = jnp.einsum('kio,kop->kip', direction, right_root, precision=highest)
    updated = master - 1.0 * direction
    return (updated, updated.astype(jnp.bfloat16), left_new, right_new)

def adamw(bias_row, gradient, moment_a, moment_b, step_count):
    first_new = 0.9 * moment_a + 0.1 * gradient
    second_new = 0.95 * moment_b + 0.05 * gradient * gradient
    stepped = step_count.astype(moment_a.dtype)
    first_hat = first_new / (1.0 - 0.9 ** stepped)
    second_hat = second_new / (1.0 - 0.95 ** stepped)
    bias_new = bias_row - 0.1 * (first_hat / (jnp.sqrt(second_hat) + 1e-08) + 0.01 * bias_row)
    return (bias_new, first_new, second_new)

def reference(features, requests, adjacent_one, adjacent_two, adjacent_three, valid_one, valid_two, valid_three, labels, labelled, weights_in, weights_mid, weights_out, biases, moment_one, moment_two, step_count, left_in, left_mid, left_out, right_in, right_mid, right_out, invleft_in, invleft_mid, invleft_out, invright_in, invright_mid, invright_out):
    feature_table = features.reshape(DEVICES, NODE_DEV, INPUTS)
    owners = jnp.arange(DEVICES, dtype=jnp.int32)[:, None]
    blocks = (requests.reshape(DEVICES, DEVICES, SLOTS_PEER), adjacent_one.reshape(DEVICES, FIRST_ROWS, FANOUT_A), valid_one.reshape(DEVICES, FIRST_ROWS, FANOUT_A), adjacent_two.reshape(DEVICES, MID_ROWS, FANOUT_B), valid_two.reshape(DEVICES, MID_ROWS, FANOUT_B), adjacent_three.reshape(DEVICES, SEEDS_DEV, FANOUT_C), valid_three.reshape(DEVICES, SEEDS_DEV, FANOUT_C), labels.reshape(DEVICES, SEEDS_DEV), labelled.reshape(DEVICES, SEEDS_DEV))

    def device_loss(params, device_block):
        asked_rows, adj_a, mask_a, adj_b, mask_b, adj_c, mask_c, seed_labels, marked = device_block
        pulled = feature_table[owners, asked_rows].reshape(DEVICES * SLOTS_PEER, INPUTS)
        hidden_a = sage_layer(pulled, adj_a, mask_a, params[0], params[3][:HIDDEN_SIZE], False)
        hidden_b = sage_layer(hidden_a, adj_b, mask_b, params[1], params[3][HIDDEN_SIZE:2 * HIDDEN_SIZE], False)
        logits = sage_layer(hidden_b, adj_c, mask_c, params[2], params[3][2 * HIDDEN_SIZE:], True)
        log_total = jax.nn.logsumexp(logits, axis=1)
        onehot = (seed_labels[:, None] == jnp.arange(CLASSES, dtype=jnp.int32)[None, :]).astype(logits.dtype)
        picked = lax.optimization_barrier(jnp.sum(logits * onehot, axis=1))
        return jnp.sum(marked.astype(logits.dtype) * (log_total - picked))

    def overall(params):
        return jnp.sum(lax.map(lambda device_block: device_loss(params, device_block), blocks))
    loss_sum, pullback = jax.vjp(overall, (weights_in, weights_mid, weights_out, biases))
    gradients = pullback(jnp.ones_like(loss_sum))[0]
    counted = jnp.sum(labelled).astype(loss_sum.dtype)
    loss = loss_sum / counted
    grad_in, grad_mid, grad_out, grad_bias = [item / counted for item in gradients]
    out_in = shampoo(weights_in, grad_in, left_in, right_in, invleft_in, invright_in)
    out_mid = shampoo(weights_mid, grad_mid, left_mid, right_mid, invleft_mid, invright_mid)
    out_out = shampoo(weights_out, grad_out, left_out, right_out, invleft_out, invright_out)
    bias_new, first_new, second_new = adamw(biases, grad_bias, moment_one, moment_two, step_count)
    return (loss, out_in[0], out_mid[0], out_out[0], out_in[1], out_mid[1], out_out[1], out_in[2], out_mid[2], out_out[2], out_in[3], out_mid[3], out_out[3], bias_new, first_new, second_new)
```

```python
import functools

import jax
import jax.numpy as jnp
from jax import lax
from jax.experimental import pallas as pl
from jax.experimental.pallas import tpu as pltpu
from jax.sharding import PartitionSpec as P

LANES = 128
SPAN = 256
VMEM_BYTES = 56 << 20
AXES = ("chip", "core", "dev")
PEERS = ("chip", "dev")

smem = pl.BlockSpec(memory_space=pltpu.SMEM)
vmem = pl.BlockSpec(memory_space=pltpu.VMEM)


def up(value, unit):
    return -(-value // unit) * unit


def call(kernel, name, out_shape, in_specs, out_specs, scratch, flops, moved):
    return pl.pallas_call(
        kernel,
        name=name,
        out_shape=out_shape,
        in_specs=in_specs,
        out_specs=out_specs,
        scratch_shapes=scratch,
        compiler_params=pltpu.CompilerParams(vmem_limit_bytes=VMEM_BYTES),
        cost_estimate=pl.CostEstimate(flops=flops, transcendentals=0, bytes_accessed=moved),
    )


def dot(left, right):
    return jnp.dot(left, right, preferred_element_type=jnp.float32)


def dot_rows(left, right):
    return lax.dot_general(
        left, right, (((0,), (0,)), ((), ())), preferred_element_type=jnp.float32
    )


def dot_cols(left, right):
    return lax.dot_general(
        left, right, (((1,), (1,)), ((), ())), preferred_element_type=jnp.float32
    )


def halves(value):
    high = value.astype(jnp.bfloat16)
    return high, (value - high.astype(jnp.float32)).astype(jnp.bfloat16)


def squared(value, size):
    short = size - value.shape[0]
    if short == 0:
        return value
    value = jnp.concatenate([value, jnp.zeros((value.shape[0], short), value.dtype)], axis=1)
    return jnp.concatenate([value, jnp.zeros((short, size), value.dtype)], axis=0)


def clipped_counts(valid):
    return jnp.maximum(jnp.sum(valid.astype(jnp.float32), axis=1, keepdims=True), 1.0)


def pick_kernel(wanted, table, out, rows, *, unroll):
    def body(step, carry):
        base = step * unroll
        for u in range(unroll):
            rows[pl.ds(base + u, 1), :] = table[pl.ds(wanted[base + u], 1), :]
        return carry

    lax.fori_loop(0, out.shape[0] // unroll, body, 0)
    out[...] = rows[...].astype(jnp.bfloat16)


def pick_rows(wanted, table):
    count, width = wanted.shape[0], table.shape[1]
    return call(
        functools.partial(pick_kernel, unroll=32),
        "pick_rows",
        jax.ShapeDtypeStruct((count, width), jnp.bfloat16),
        [smem, vmem],
        vmem,
        [pltpu.VMEM((count, width), jnp.float32)],
        count * width,
        table.size * 4,
    )(wanted, table)


def mean_kernel(slots, valid, source, out, table, total, *, unroll):
    fan, targets = slots.shape
    width = source.shape[1]
    table[0 : source.shape[0], :] = source[...].astype(jnp.float32)
    table[source.shape[0] :, :] = jnp.zeros((8, width), jnp.float32)

    def body(step, carry):
        base = step * unroll
        for u in range(unroll):
            parts = [table[pl.ds(slots[j, base + u], 1), :] for j in range(fan)]
            while len(parts) > 1:
                merged = [parts[k] + parts[k + 1] for k in range(0, len(parts) - 1, 2)]
                parts = merged + parts[len(merged) * 2 :]
            total[pl.ds(base + u, 1), :] = parts[0]
        return carry

    lax.fori_loop(0, targets // unroll, body, 0)
    counts = clipped_counts(valid[...])
    out[0:targets, 0:width] = source[0:targets, :]
    out[0:targets, width : 2 * width] = (total[...] / counts).astype(jnp.bfloat16)
    if out.shape[0] > targets:
        out[targets:, :] = jnp.zeros((out.shape[0] - targets, 2 * width), jnp.bfloat16)


def mean_rows(slots, valid, source, padded):
    fan, targets = slots.shape
    total, width = source.shape
    return call(
        functools.partial(mean_kernel, unroll=8),
        "mean_rows",
        jax.ShapeDtypeStruct((padded, 2 * width), jnp.bfloat16),
        [smem, vmem, vmem],
        vmem,
        [pltpu.VMEM((total + 8, width), jnp.float32), pltpu.VMEM((targets, width), jnp.float32)],
        fan * targets * width,
        total * width * 2,
    )(slots, valid, source)


def link_kernel(names, adjacent, valid, out):
    targets, fan = adjacent.shape
    tile = 32
    blocks = out.shape[0]

    def rows(step, carry):
        first = pl.multiple_of(step * tile, tile)
        here = jnp.where(
            valid[pl.ds(first, tile), :] > 0, adjacent[pl.ds(first, tile), :], -1
        )
        spread = [jnp.broadcast_to(here[:, j : j + 1], (tile, LANES)) for j in range(fan)]
        own = first + lax.broadcasted_iota(jnp.int32, (tile, LANES), 0)

        def columns(block, inner):
            for part in range(SPAN // LANES):
                name = jnp.broadcast_to(
                    names[pl.ds(block * (SPAN // LANES) + part, 1), :], (tile, LANES)
                )
                number = jnp.zeros((tile, LANES), jnp.float32)
                for j in range(fan):
                    number = number + jnp.where(spread[j] == name, 1.0, 0.0)
                lanes = pl.ds(part * LANES, LANES)
                out[block, pl.ds(first, tile), lanes] = number.astype(jnp.bfloat16)
                out[block, pl.ds(targets + first, tile), lanes] = jnp.where(
                    own == name, 1.0, 0.0
                ).astype(jnp.bfloat16)
            return inner

        return lax.fori_loop(0, blocks, columns, carry)

    lax.fori_loop(0, targets // tile, rows, 0)


def link_matrix(names, adjacent, valid):
    blocks = names.size // SPAN
    targets = adjacent.shape[0]
    return call(
        link_kernel,
        "link_matrix",
        jax.ShapeDtypeStruct((blocks, 2 * targets, SPAN), jnp.bfloat16),
        [vmem, vmem, vmem],
        vmem,
        [],
        blocks * targets * SPAN * 30,
        blocks * targets * SPAN * 4,
    )(names, adjacent, valid)


def step_kernel(
    info,
    mixin,
    links,
    valid_two,
    adjacent_three,
    valid_three,
    labels,
    labelled,
    weights_in,
    weights_mid,
    weights_out,
    biases,
    keep,
    send,
    slopes,
    packed,
    sums,
    weight_sums,
    mid_sums,
    tail_sums,
    *,
    classes,
):
    blocks, both, _ = links.shape
    targets = both // 2
    hidden = weights_in.shape[2]
    seeds = labels.shape[0]
    wide = up(classes, LANES)
    core = info[0]
    used = info[1]
    low = jnp.bfloat16

    w_in = weights_in[...].astype(low).reshape(2 * weights_in.shape[1], hidden)
    bias_in = biases[:, 0:hidden]
    bias_mid = biases[:, hidden : 2 * hidden]
    bias_out = jnp.concatenate(
        [
            biases[:, 2 * hidden : 2 * hidden + classes],
            jnp.full((1, wide - classes), -1e30, jnp.float32),
        ],
        axis=1,
    )

    sums[...] = jnp.zeros_like(sums)

    def forward(block, carry):
        rows = pl.ds(pl.multiple_of(block * SPAN, SPAN), SPAN)
        z = dot(mixin[rows, :], w_in) + bias_in
        s = 1.0 / (1.0 + jnp.exp(-z))
        slopes[rows, :] = s * (1.0 + z * (1.0 - s))
        sums[...] += dot(links[block], (z * s).astype(low))
        return carry

    lax.fori_loop(0, used, forward, 0)
    total = sums[...]
    counts_two = clipped_counts(valid_two[...])
    mixed_one = (total[0:targets] / counts_two).astype(low)
    self_one = total[targets:].astype(low)
    w_mid = weights_mid[...].astype(low)
    both_one = jnp.concatenate([self_one, mixed_one], axis=1)
    z = dot(both_one, w_mid.reshape(2 * hidden, hidden)) + bias_mid
    s = 1.0 / (1.0 + jnp.exp(-z))
    slope_mid = s * (1.0 + z * (1.0 - s))
    hidden_two = (z * s).astype(low)

    here = jnp.where(valid_three[...] > 0, adjacent_three[...], -1)
    place = lax.broadcasted_iota(jnp.int32, (seeds, targets), 1)
    number = jnp.zeros((seeds, targets), jnp.float32)
    for j in range(here.shape[1]):
        number = number + jnp.where(here[:, j : j + 1] == place, 1.0, 0.0)
    number = number.astype(low)
    counts_three = clipped_counts(valid_three[...])
    mixed_two = (dot(number, hidden_two) / counts_three).astype(low)
    self_two = hidden_two[0:seeds]
    w_out = jnp.concatenate(
        [
            weights_out[...],
            jnp.zeros((2, weights_out.shape[1], wide - classes), jnp.float32),
        ],
        axis=2,
    ).astype(low)
    both_two = jnp.concatenate([self_two, mixed_two], axis=1)
    logits = dot(both_two, w_out.reshape(2 * hidden, wide)) + bias_out
    top = jnp.max(logits, axis=1, keepdims=True)
    log_total = top + jnp.log(jnp.sum(jnp.exp(logits - top), axis=1, keepdims=True))
    onehot = jnp.where(
        labels[...] == lax.broadcasted_iota(jnp.int32, (seeds, wide), 1), 1.0, 0.0
    )
    marked = labelled[...].astype(jnp.float32)
    picked = jnp.sum(jnp.where(onehot > 0.0, logits, 0.0), axis=1, keepdims=True)
    loss = jnp.sum(marked * (log_total - picked), axis=0, keepdims=True)
    counted = jnp.sum(marked, axis=0, keepdims=True)
    grad_out = (marked * (jnp.exp(logits - log_total) - onehot)).astype(low)

    tail_sums[...] = dot_rows(grad_out[:, LANES:], both_two)
    bias_grad_out = jnp.sum(grad_out.astype(jnp.float32), axis=0, keepdims=True)
    to_self = dot_cols(grad_out, w_out[0])
    spread = (dot_cols(grad_out, w_out[1]) / counts_three).astype(low)
    sums[0:targets, :] = dot_rows(number, spread)
    sums[0:seeds, :] += to_self
    grad_mid = (sums[0:targets, :] * slope_mid).astype(low)

    mid_sums[...] = dot_rows(both_one, grad_mid)
    bias_grad_mid = jnp.sum(grad_mid.astype(jnp.float32), axis=0, keepdims=True)
    down = jnp.concatenate(
        [dot_cols(grad_mid, w_mid[1]) / counts_two, dot_cols(grad_mid, w_mid[0])], axis=0
    )
    spread = down.astype(low)

    weight_sums[...] = jnp.zeros_like(weight_sums)

    def backward(block, bias):
        rows = pl.ds(pl.multiple_of(block * SPAN, SPAN), SPAN)
        grad = (dot_rows(links[block], spread) * slopes[rows, :]).astype(low)
        weight_sums[...] += dot_rows(mixin[rows, :], grad)
        return bias + jnp.sum(grad.astype(jnp.float32), axis=0, keepdims=True)

    bias_grad_in = lax.fori_loop(0, used, backward, jnp.zeros((1, hidden), jnp.float32))

    row = 0
    for part in (weight_sums, mid_sums):
        for column in range(0, hidden, LANES):
            packed[row : row + part.shape[0], :] = part[:, column : column + LANES]
            row += part.shape[0]
    packed[row : row + 2 * hidden, :] = dot_rows(both_two, grad_out[:, 0:LANES])
    row += 2 * hidden
    high_rows = up(classes - LANES, 16)
    for column in range(0, 2 * hidden, LANES):
        packed[row : row + high_rows, :] = tail_sums[0:high_rows, column : column + LANES]
        row += high_rows
    packed[row:, :] = jnp.zeros((packed.shape[0] - row, LANES), jnp.float32)
    lane = lax.broadcasted_iota(jnp.int32, (1, LANES), 1)
    scalars = jnp.where(lane == 0, loss, 0.0) + jnp.where(lane == 1, counted, 0.0)
    extra = [
        item[:, column : column + LANES]
        for item in (bias_grad_in, bias_grad_mid, bias_grad_out)
        for column in range(0, hidden, LANES)
    ] + [scalars, jnp.zeros((1, LANES), jnp.float32)]
    extra = jnp.concatenate(extra, axis=0)
    high = extra.astype(low).astype(jnp.float32)
    packed[packed.shape[0] - 16 :, :] = jnp.concatenate([high, extra - high], axis=0)
    half = keep.shape[0]
    keep[...] = packed[pl.ds(pl.multiple_of(core * half, 16), half), :].astype(low)
    send[...] = packed[pl.ds(pl.multiple_of((1 - core) * half, 16), half), :].astype(low)


def run_step(info, mixin, links, rest, half, classes):
    padded, width = mixin.shape
    hidden = rest[5].shape[2]
    return call(
        functools.partial(step_kernel, classes=classes),
        "step",
        (jax.ShapeDtypeStruct((half, LANES), jnp.bfloat16),) * 2,
        [smem] + [vmem] * 11,
        (vmem, vmem),
        [
            pltpu.VMEM((padded, hidden), jnp.float32),
            pltpu.VMEM((2 * half, LANES), jnp.float32),
            pltpu.VMEM((links.shape[1], hidden), jnp.float32),
            pltpu.VMEM((width, hidden), jnp.float32),
            pltpu.VMEM((2 * hidden, hidden), jnp.float32),
            pltpu.VMEM((up(classes, LANES) - LANES, 2 * hidden), jnp.float32),
        ],
        4 << 30,
        32 << 20,
    )(info, mixin, links, *rest)


def refit(total, rows):
    extra = total[rows - 16 : rows - 8] + total[rows - 8 : rows]
    high = extra.astype(jnp.bfloat16).astype(jnp.float32)
    return jnp.concatenate([high, extra - high], axis=0)


def pair_kernel(info, mine, theirs, out):
    total = mine[...].astype(jnp.float32) + theirs[...].astype(jnp.float32)
    out[...] = total.astype(jnp.bfloat16)

    @pl.when(info[0] == 1)
    def _():
        rows = total.shape[0]
        out[rows - 16 :, :] = refit(total, rows).astype(jnp.bfloat16)


def pair_sum(info, mine, theirs):
    return call(
        pair_kernel,
        "pair_sum",
        jax.ShapeDtypeStruct(mine.shape, jnp.bfloat16),
        [smem, vmem, vmem],
        vmem,
        [],
        mine.size,
        mine.size * 6,
    )(info, mine, theirs)


def spread_kernel(info, pieces, out):
    total = pieces[0].astype(jnp.float32)
    for k in range(1, pieces.shape[0]):
        total = total + pieces[k].astype(jnp.float32)
    rows = total.shape[0]
    fitted = jnp.concatenate([total[0 : rows - 16], refit(total, rows)], axis=0)
    result = jnp.where(info[2] == 1, fitted, total).astype(jnp.bfloat16)
    for k in range(pieces.shape[0]):
        out[k] = result


def spread_sum(info, pieces):
    return call(
        spread_kernel,
        "spread_sum",
        jax.ShapeDtypeStruct(pieces.shape, jnp.bfloat16),
        [smem, vmem],
        vmem,
        [],
        pieces.size,
        pieces.size * 4,
    )(info, pieces)


def update_kernel(
    info,
    fixes,
    mine,
    theirs,
    biases,
    moment_one,
    moment_two,
    *refs,
    classes,
):
    groups = [refs[5 * k : 5 * k + 5] for k in range(3)]
    loss_out = refs[15]
    outs = [refs[16 + 4 * k : 20 + 4 * k] for k in range(3)]
    bias_out, first_out, second_out = refs[28:31]
    packed = refs[31]
    low = jnp.bfloat16
    half = mine.shape[0]
    core = info[0]
    packed[pl.ds(pl.multiple_of(core * half, 16), half), :] = mine[...].astype(jnp.float32)
    packed[pl.ds(pl.multiple_of((1 - core) * half, 16), half), :] = theirs[...].astype(
        jnp.float32
    )
    last = packed.shape[0]
    extra = packed[last - 16 : last - 8, :] + packed[last - 8 :, :]
    counted = extra[6:7, 1:2]
    inverse = 1.0 / counted
    loss_out[...] = extra[6:7, 0:1] / counted

    row = 0
    gradients = []
    for group in range(3):
        depth, hidden = groups[group][0].shape[1:]
        if hidden % LANES == 0:
            parts = []
            for column in range(0, hidden, LANES):
                parts.append(packed[row : row + 2 * depth, :])
                row += 2 * depth
            whole = jnp.concatenate(parts, axis=1)
        else:
            main = packed[row : row + 2 * depth, :]
            row += 2 * depth
            high_rows = up(hidden - LANES, 16)
            tails = []
            for column in range(0, 2 * depth, LANES):
                tail = jnp.concatenate(
                    [
                        packed[row : row + high_rows, :],
                        jnp.zeros((LANES - high_rows, LANES), jnp.float32),
                    ],
                    axis=0,
                )
                tails.append(jnp.transpose(tail))
                row += high_rows
            whole = jnp.concatenate([main, jnp.concatenate(tails, axis=0)], axis=1)
        gradients.append([whole[k * depth : (k + 1) * depth].astype(low) for k in range(2)])

    for group in range(3):
        master, left, right, left_root, right_root = groups[group]
        new_master, copy, new_left, new_right = outs[group]
        depth, hidden = master.shape[1:]
        wide = up(hidden, LANES)
        for k in range(2):
            grad = gradients[group][k]
            scale = 0.5 * inverse * inverse
            new_left[k] = 0.5 * left[k] + scale * dot_cols(grad, grad)
            product = dot_rows(grad, grad)
            new_right[k] = 0.5 * right[k] + scale * product[0:hidden, 0:hidden]
            root = jnp.concatenate(halves(left_root[k]), axis=1)
            middle = dot(root, jnp.concatenate([grad, grad], axis=0))
            mid_high, mid_rest = halves(middle)
            root_high, root_rest = halves(squared(right_root[k], wide))
            way = dot(
                jnp.concatenate([mid_high, mid_high, mid_rest], axis=1),
                jnp.concatenate([root_high, root_rest, root_high], axis=0),
            )[:, 0:hidden]
            fresh = master[k] - inverse * way
            new_master[k] = fresh
            copy[k] = fresh.astype(low)

    size = biases.shape[1]
    grad = jnp.concatenate([extra[k : k + 1, :] for k in range(6)], axis=1)[:, 0:size]
    grad = grad / counted
    first = 0.9 * moment_one[...] + 0.1 * grad
    second = 0.95 * moment_two[...] + 0.05 * grad * grad
    old = biases[...]
    bias_out[...] = old - 0.1 * (
        (first / fixes[0]) / (jnp.sqrt(second / fixes[1]) + 1e-08) + 0.01 * old
    )
    first_out[...] = first
    second_out[...] = second


def run_update(info, fixes, mine, theirs, vectors, groups, classes):
    outs = [jax.ShapeDtypeStruct((1, 1), jnp.float32)]
    flat = []
    for master, left, right, left_root, right_root in groups:
        flat += [master, left, right, left_root, right_root]
        outs += [
            jax.ShapeDtypeStruct(master.shape, jnp.float32),
            jax.ShapeDtypeStruct(master.shape, jnp.bfloat16),
            jax.ShapeDtypeStruct(left.shape, jnp.float32),
            jax.ShapeDtypeStruct(right.shape, jnp.float32),
        ]
    outs += [jax.ShapeDtypeStruct(vectors[0].shape, jnp.float32)] * 3
    return call(
        functools.partial(update_kernel, classes=classes),
        "update",
        tuple(outs),
        [smem, smem] + [vmem] * (5 + 15),
        (vmem,) * len(outs),
        [pltpu.VMEM((2 * mine.shape[0], LANES), jnp.float32)],
        1 << 30,
        10 << 20,
    )(info, fixes, mine, theirs, *vectors, *flat)


def body(
    features,
    requests,
    adjacent_one,
    adjacent_two,
    adjacent_three,
    valid_one,
    valid_two,
    valid_three,
    labels,
    labelled,
    weights_in,
    weights_mid,
    weights_out,
    biases,
    moment_one,
    moment_two,
    step_count,
    left_in,
    left_mid,
    left_out,
    right_in,
    right_mid,
    right_out,
    invleft_in,
    invleft_mid,
    invleft_out,
    invright_in,
    invright_mid,
    invright_out,
    *,
    peers,
):
    width = features.shape[1]
    targets = adjacent_one.shape[0]
    padded = up(targets, SPAN)
    classes = weights_out.shape[2]
    core = lax.axis_index("core")
    own = lax.axis_index(PEERS)

    wanted = lax.all_to_all(requests, AXES, split_axis=0, concat_axis=0, tiled=True)
    found = pick_rows(wanted.reshape(-1), features)
    pulled = lax.all_to_all(
        found.reshape(requests.shape + (width,)), AXES, split_axis=0, concat_axis=0, tiled=True
    ).reshape(-1, width)

    slots = jnp.where(valid_one > 0, adjacent_one, pulled.shape[0]).T
    mixin = mean_rows(slots, valid_one, pulled, padded)
    names = jnp.arange(padded, dtype=jnp.int32).reshape(-1, LANES)
    links = link_matrix(names, adjacent_two, valid_two)

    hidden = weights_in.shape[2]
    rows = 4 * width * (hidden // LANES) // 2 + 2 * weights_mid.shape[1] * (hidden // LANES)
    rows = 2 * width * (hidden // LANES)
    rows += 2 * weights_mid.shape[1] * (hidden // LANES)
    rows += 2 * weights_out.shape[1] + up(classes - LANES, 16) * (2 * hidden // LANES)
    each = up(-(-(rows + 16) // (2 * peers)), 8)
    half = each * peers
    info = jnp.stack(
        [
            core,
            jnp.int32(padded // SPAN),
            ((core == 1) & (own == peers - 1)).astype(jnp.int32),
        ]
    ).astype(jnp.int32)
    keep, send = run_step(
        info,
        mixin,
        links,
        (
            valid_two,
            adjacent_three,
            valid_three,
            labels[:, None],
            labelled[:, None],
            weights_in,
            weights_mid,
            weights_out,
            biases[None, :],
        ),
        half,
        classes,
    )
    swap = [(0, 1), (1, 0)]
    theirs = lax.ppermute(send, "core", swap)
    summed = pair_sum(info, keep, theirs).reshape(peers, each, LANES)
    pieces = lax.all_to_all(summed, PEERS, split_axis=0, concat_axis=0, tiled=True)
    shared = spread_sum(info, pieces)
    mine = lax.all_to_all(shared, PEERS, split_axis=0, concat_axis=0, tiled=True)
    mine = mine.reshape(half, LANES)
    theirs = lax.ppermute(mine, "core", swap)

    stepped = step_count.astype(jnp.float32)
    fixes = jnp.stack([1.0 - 0.9**stepped, 1.0 - 0.95**stepped])
    outs = run_update(
        info,
        fixes,
        mine,
        theirs,
        (biases[None, :], moment_one[None, :], moment_two[None, :]),
        (
            (weights_in, left_in, right_in, invleft_in, invright_in),
            (weights_mid, left_mid, right_mid, invleft_mid, invright_mid),
            (weights_out, left_out, right_out, invleft_out, invright_out),
        ),
        classes,
    )
    groups = [outs[1 + 4 * k : 5 + 4 * k] for k in range(3)]
    return (
        (outs[0].reshape(()),)
        + tuple(groups[k][which] for which in range(4) for k in range(3))
        + tuple(item.reshape(-1) for item in outs[13:16])
    )


def solution(mesh):
    chips, dev = mesh.shape["hst"] // 2, mesh.shape["dev"]
    fine = jax.sharding.Mesh(mesh.devices.reshape(chips, 2, dev), AXES)
    split = P(AXES, None)
    line = P(AXES)
    whole = P()
    return jax.shard_map(
        functools.partial(body, peers=chips * dev),
        mesh=fine,
        in_specs=(split,) * 8 + (line,) * 2 + (whole,) * 19,
        out_specs=(whole,) * 16,
        check_vma=False,
    )
```

```python
import functools

import jax
import jax.numpy as jnp
from jax import lax
from jax.experimental import pallas as pl
from jax.experimental.pallas import tpu as pltpu
from jax.sharding import PartitionSpec as P

LANES = 128
SPAN = 256
PARTS = 2
AXES = ("chip", "core", "dev")
PEERS = ("chip", "dev")

smem = pl.BlockSpec(memory_space=pltpu.SMEM)
vmem = pl.BlockSpec(memory_space=pltpu.VMEM)
anywhere = pl.BlockSpec(memory_space=pl.ANY)


def up(value, unit):
    return -(-value // unit) * unit


def call(kernel, name, out_shape, in_specs, out_specs, scratch, flops, moved, room):
    return pl.pallas_call(
        kernel,
        name=name,
        out_shape=out_shape,
        in_specs=in_specs,
        out_specs=out_specs,
        scratch_shapes=scratch,
        compiler_params=pltpu.CompilerParams(vmem_limit_bytes=room),
        cost_estimate=pl.CostEstimate(flops=flops, transcendentals=0, bytes_accessed=moved),
    )


def dot(left, right):
    return jnp.dot(left, right, preferred_element_type=jnp.float32)


def dot_rows(left, right):
    return lax.dot_general(
        left, right, (((0,), (0,)), ((), ())), preferred_element_type=jnp.float32
    )


def dot_cols(left, right):
    return lax.dot_general(
        left, right, (((1,), (1,)), ((), ())), preferred_element_type=jnp.float32
    )


def halves(value):
    high = value.astype(jnp.bfloat16)
    return high, (value - high.astype(jnp.float32)).astype(jnp.bfloat16)


def grown(value, rows, columns):
    short = columns - value.shape[1]
    if short:
        value = jnp.concatenate([value, jnp.zeros((value.shape[0], short), value.dtype)], axis=1)
    short = rows - value.shape[0]
    if short:
        value = jnp.concatenate([value, jnp.zeros((short, columns), value.dtype)], axis=0)
    return value


def clipped_counts(valid):
    return jnp.maximum(jnp.sum(valid.astype(jnp.float32), axis=1, keepdims=True), 1.0)


def copy_rows(names, block, source, target):
    unroll = 16
    across = LANES // unroll

    def fetch(step, carry):
        row = block * (SPAN // LANES) + lax.div(step, across)
        column = lax.rem(step, across) * unroll
        for u in range(unroll):
            target[pl.ds(step * unroll + u, 1), :] = source[pl.ds(names[row, column + u], 1), :]
        return carry

    lax.fori_loop(0, SPAN // unroll, fetch, 0)


def pick_kernel(wanted, table, out, rows, *, first, part):
    unroll = min(32, part)
    steps = part // unroll

    def body(step, carry):
        device = lax.div(step, steps)
        column = first + lax.rem(step, steps) * unroll
        for u in range(unroll):
            rows[pl.ds(step * unroll + u, 1), :] = table[pl.ds(wanted[device, column + u], 1), :]
        return carry

    lax.fori_loop(0, wanted.shape[0] * steps, body, 0)
    out[...] = rows[...].astype(jnp.bfloat16)


def pick_rows(wanted, table, which):
    part, width = wanted.shape[1] // PARTS, table.shape[1]
    count = wanted.shape[0] * part
    return call(
        functools.partial(pick_kernel, first=which * part, part=part),
        "pick_rows",
        jax.ShapeDtypeStruct((count, width), jnp.bfloat16),
        [smem, vmem],
        vmem,
        [pltpu.VMEM((count, width), jnp.float32)],
        count * width,
        table.size * 4,
        20 << 20,
    )(wanted, table)


def reach_kernel(
    adjacent_three,
    valid_three,
    labelled,
    adjacent_two,
    valid_two,
    across_two,
    across_valid,
    names,
    places,
    count,
    left,
    right,
    *,
    rows_all,
    per,
):
    seeds, fan_three = adjacent_three.shape
    targets, fan_two = adjacent_two.shape
    low = jnp.bfloat16
    blocks = rows_all // LANES
    deep = names.shape[0]
    line = labelled[...].reshape(1, seeds)
    column = jnp.transpose(jnp.broadcast_to(line.astype(jnp.float32), (8, seeds)))[:, 0:1]
    live = (valid_three[...] > 0) & (column > 0.0)
    here = jnp.where(live, adjacent_three[...], -1)
    place = lax.broadcasted_iota(jnp.int32, (seeds, targets), 1)
    hit = jnp.zeros((seeds, targets), jnp.float32)
    for j in range(fan_three):
        hit = hit + jnp.where(here[:, j : j + 1] == place, 1.0, 0.0)
    need = jnp.max(hit, axis=0, keepdims=True) + jnp.concatenate(
        [line.astype(jnp.float32), jnp.zeros((1, targets - seeds), jnp.float32)], axis=1
    )

    level = lax.broadcasted_iota(jnp.int32, (deep, targets), 0)
    lane = lax.broadcasted_iota(jnp.int32, (targets, LANES), 1)
    flat = jnp.where((across_valid[...] > 0) & (need > 0.0), across_two[...], -1)
    tall = adjacent_two[...]
    for j in range(fan_two):
        left[0:deep, j * targets : (j + 1) * targets] = jnp.where(
            lax.shift_right_arithmetic(flat[j : j + 1, :], 7) == level, 1.0, 0.0
        ).astype(low)
        right[j * targets : (j + 1) * targets, :] = jnp.where(
            (tall[:, j : j + 1] & (LANES - 1)) == lane, 1.0, 0.0
        ).astype(low)
    used = dot(left[0:deep, 0 : fan_two * targets], right[0 : fan_two * targets, :])
    own = [need[:, k : k + LANES] for k in range(0, targets, LANES)]
    own = jnp.concatenate(
        own + [jnp.zeros((deep - len(own), LANES), jnp.float32)], axis=0
    )
    flag = jnp.where(used + own > 0.0, 1.0, 0.0)

    square_row = lax.broadcasted_iota(jnp.int32, (LANES, LANES), 0)
    square_col = lax.broadcasted_iota(jnp.int32, (LANES, LANES), 1)
    full = jnp.concatenate([flag, jnp.zeros((LANES - deep, LANES), jnp.float32)], axis=0)
    flag_low = full.astype(low)
    running = dot(flag_low, jnp.where(square_row <= square_col, 1.0, 0.0).astype(low))
    totals = dot(flag_low, jnp.ones((LANES, LANES), low)).astype(low)
    before = dot(jnp.where(square_row > square_col, 1.0, 0.0).astype(low), totals)
    order = (before + running - full).astype(jnp.int32)
    number = jnp.sum(flag).astype(jnp.int32)
    count[0] = number
    count[1] = lax.div(number + (SPAN - 1), SPAN)

    high = jnp.where(full > 0.0, lax.shift_right_arithmetic(order, 7), -1)
    rest = jnp.transpose((order & (LANES - 1)).astype(jnp.float32)).astype(jnp.int32)
    step = lax.broadcasted_iota(jnp.int32, (deep, LANES), 0)
    inner = lax.broadcasted_iota(jnp.int32, (deep, LANES), 1).astype(jnp.float32)
    for b in range(blocks):
        match = jnp.where(high[b : b + 1, :] == step, 1.0, 0.0)
        lanes = slice(b * LANES, (b + 1) * LANES)
        left[0:deep, lanes] = (match * inner).astype(low)
        left[deep : 2 * deep, lanes] = (match * float(b)).astype(low)
        right[lanes, :] = jnp.where(rest[:, b : b + 1] == square_col, 1.0, 0.0).astype(low)
    found = dot(left[:, 0:rows_all], right[0:rows_all, :]).astype(jnp.int32)
    where = step * LANES + lax.broadcasted_iota(jnp.int32, (deep, LANES), 1)
    name = found[deep:] * LANES + found[0:deep]
    names[...] = jnp.where(where < number, name, rows_all)
    name = jnp.minimum(jnp.where(where < number, name, 0), rows_all - 1)
    owner, slot = lax.div(name, per), lax.rem(name, per)
    part = per // PARTS
    owners = -(-rows_all // per)
    places[...] = lax.div(slot, part) * (owners * part) + owner * part + lax.rem(slot, part)


def reach(adjacent_three, valid_three, labelled, adjacent_two, valid_two, rows_all, per):
    targets, fan = adjacent_two.shape
    deep = up(up(rows_all, SPAN) // LANES, 16)
    area = max(fan * targets, rows_all)
    return call(
        functools.partial(reach_kernel, rows_all=rows_all, per=per),
        "reach",
        (
            jax.ShapeDtypeStruct((deep, LANES), jnp.int32),
            jax.ShapeDtypeStruct((deep, LANES), jnp.int32),
            jax.ShapeDtypeStruct((2,), jnp.int32),
        ),
        [vmem] * 7,
        (vmem, vmem, smem),
        [
            pltpu.VMEM((2 * deep, area), jnp.bfloat16),
            pltpu.VMEM((area, LANES), jnp.bfloat16),
        ],
        1 << 28,
        1 << 20,
        8 << 20,
    )(
        adjacent_three,
        valid_three,
        labelled,
        adjacent_two,
        valid_two,
        adjacent_two.T,
        valid_two.T,
    )


def tally_kernel(count, names, slots, *refs):
    outs = refs[:PARTS]
    rows, spread, code, buffer, sems = refs[PARTS:]
    low = jnp.bfloat16
    wide = outs[0].shape[1]
    high_all = PARTS * wide // SPAN
    fan = slots.shape[1]
    groups = SPAN // fan
    used = count[1]

    across = lax.broadcasted_iota(jnp.int32, (fan, SPAN), 1)
    down = lax.broadcasted_iota(jnp.int32, (fan, SPAN), 0)
    spread[...] = jnp.where(lax.div(across, fan) == down, 1.0, 0.0).astype(low)
    lane = lax.broadcasted_iota(jnp.int32, (fan, SPAN), 1)
    place = lax.broadcasted_iota(jnp.int32, (fan, SPAN), 0)

    def copies(block, slot):
        return [
            pltpu.make_async_copy(
                buffer.at[slot, :, pl.ds(part * wide, wide)],
                outs[part].at[pl.ds(pl.multiple_of(block * SPAN, SPAN), SPAN), :],
                sems.at[slot, part],
            )
            for part in range(PARTS)
        ]

    def body(block, carry):
        slot = lax.rem(block, 2)

        @pl.when(block >= 2)
        def _():
            for copy in copies(block - 2, slot):
                copy.wait()

        copy_rows(names, block, slots, rows)
        row = rows[...]
        high = lax.shift_right_arithmetic(row, 8).astype(jnp.float32).astype(low)
        lined = dot(high, spread[...])
        own = lax.rem(lax.broadcasted_iota(jnp.int32, (SPAN, SPAN), 0), fan) == lax.rem(
            lax.broadcasted_iota(jnp.int32, (SPAN, SPAN), 1), fan
        )
        lined = jnp.where(own, lined, 0.0).astype(low)
        member = (
            lax.div(lax.broadcasted_iota(jnp.int32, (groups, SPAN), 1), fan)
            == lax.broadcasted_iota(jnp.int32, (groups, SPAN), 0)
        )
        gathered = dot(jnp.where(member, 1.0, 0.0).astype(low), lined).astype(jnp.int32)
        code[...] = gathered * fan + lax.rem(
            lax.broadcasted_iota(jnp.int32, (groups, SPAN), 1), fan
        )

        def group(g, inner):
            first = pl.multiple_of(g * fan, fan)
            rest = rows[pl.ds(first, fan), :] & (SPAN - 1)
            columns = [
                jnp.where(jnp.broadcast_to(rest[:, j : j + 1], (fan, SPAN)) == lane, 1.0, 0.0)
                for j in range(fan)
            ]
            columns = jnp.concatenate(columns, axis=0).astype(low)
            line = jnp.broadcast_to(code[pl.ds(g, 1), :], (fan, SPAN))
            marks = [
                jnp.where(line == place + q * fan, 1.0, 0.0) for q in range(high_all)
            ]
            marks = jnp.concatenate(marks, axis=0).astype(low)
            result = dot(marks, columns).astype(low)
            for q in range(high_all):
                buffer[slot, pl.ds(first, fan), q * SPAN : (q + 1) * SPAN] = result[
                    q * fan : (q + 1) * fan
                ]
            return inner

        lax.fori_loop(0, groups, group, 0)
        for copy in copies(block, slot):
            copy.start()
        return carry

    lax.fori_loop(0, used, body, 0)

    @pl.when(used >= 2)
    def _():
        for copy in copies(used - 2, lax.rem(used - 2, 2)):
            copy.wait()

    @pl.when(used >= 1)
    def _():
        for copy in copies(used - 1, lax.rem(used - 1, 2)):
            copy.wait()


def tally(count, names, slots, padded, total):
    fan = slots.shape[1]
    wide = total // PARTS
    return call(
        tally_kernel,
        "tally",
        (jax.ShapeDtypeStruct((padded, wide), jnp.bfloat16),) * PARTS,
        [smem, smem, vmem],
        (anywhere,) * PARTS,
        [
            pltpu.VMEM((SPAN, fan), jnp.int32),
            pltpu.VMEM((fan, SPAN), jnp.bfloat16),
            pltpu.VMEM((SPAN // fan, SPAN), jnp.int32),
            pltpu.VMEM((2, SPAN, total), jnp.bfloat16),
            pltpu.SemaphoreType.DMA((2, PARTS)),
        ],
        1 << 32,
        32 << 20,
        20 << 20,
    )(count, names, slots)


def early_kernel(count, tallies, source, out, table, buffer, result, sems, out_sems):
    width = source.shape[1]
    used = count[1]
    table[:, 0:width] = source[...]
    table[:, width:] = jnp.ones((source.shape[0], width), jnp.bfloat16)

    def rows(block):
        return pl.ds(pl.multiple_of(block * SPAN, SPAN), SPAN)

    def load(block, slot):
        return pltpu.make_async_copy(tallies.at[rows(block), :], buffer.at[slot], sems.at[slot])

    def save(block, slot):
        return pltpu.make_async_copy(result.at[slot], out.at[rows(block), :], out_sems.at[slot])

    @pl.when(used > 0)
    def _():
        load(0, 0).start()

    def body(block, carry):
        slot = lax.rem(block, 2)
        load(block, slot).wait()

        @pl.when(block + 1 < used)
        def _():
            load(block + 1, 1 - slot).start()

        @pl.when(block >= 2)
        def _():
            save(block - 2, slot).wait()

        result[slot] = dot(buffer[slot], table[...])
        save(block, slot).start()
        return carry

    lax.fori_loop(0, used, body, 0)

    @pl.when(used >= 2)
    def _():
        save(used - 2, lax.rem(used - 2, 2)).wait()

    @pl.when(used >= 1)
    def _():
        save(used - 1, lax.rem(used - 1, 2)).wait()


def early_sums(count, tallies, source):
    padded, total = tallies.shape
    width = source.shape[1]
    return call(
        early_kernel,
        "early_sums",
        jax.ShapeDtypeStruct((padded, 2 * width), jnp.float32),
        [smem, anywhere, vmem],
        anywhere,
        [
            pltpu.VMEM((total, 2 * width), jnp.bfloat16),
            pltpu.VMEM((2, SPAN, total), jnp.bfloat16),
            pltpu.VMEM((2, SPAN, 2 * width), jnp.float32),
            pltpu.SemaphoreType.DMA((2,)),
            pltpu.SemaphoreType.DMA((2,)),
        ],
        1 << 32,
        16 << 20,
        16 << 20,
    )(count, tallies, source)


def link_kernel(count, names, adjacent, valid, out):
    targets, fan = adjacent.shape
    tile = 32
    blocks = count[1]

    def rows(step, carry):
        first = pl.multiple_of(step * tile, tile)
        here = jnp.where(
            valid[pl.ds(first, tile), :] > 0, adjacent[pl.ds(first, tile), :], -1
        )
        spread = [jnp.broadcast_to(here[:, j : j + 1], (tile, LANES)) for j in range(fan)]
        own = first + lax.broadcasted_iota(jnp.int32, (tile, LANES), 0)

        def columns(block, inner):
            for part in range(SPAN // LANES):
                name = jnp.broadcast_to(
                    names[pl.ds(block * (SPAN // LANES) + part, 1), :], (tile, LANES)
                )
                number = jnp.zeros((tile, LANES), jnp.float32)
                for j in range(fan):
                    number = number + jnp.where(spread[j] == name, 1.0, 0.0)
                lanes = pl.ds(part * LANES, LANES)
                out[block, pl.ds(first, tile), lanes] = number.astype(jnp.bfloat16)
                out[block, pl.ds(targets + first, tile), lanes] = jnp.where(
                    own == name, 1.0, 0.0
                ).astype(jnp.bfloat16)
            return inner

        return lax.fori_loop(0, blocks, columns, carry)

    lax.fori_loop(0, targets // tile, rows, 0)


def link_matrix(count, names, adjacent, valid, padded):
    blocks = padded // SPAN
    targets = adjacent.shape[0]
    return call(
        link_kernel,
        "link_matrix",
        jax.ShapeDtypeStruct((blocks, 2 * targets, SPAN), jnp.bfloat16),
        [smem, vmem, vmem, vmem],
        vmem,
        [],
        blocks * targets * SPAN * 30,
        blocks * targets * SPAN * 4,
        12 << 20,
    )(count, names, adjacent, valid)


def step_kernel(
    info,
    count,
    places,
    partial,
    tallies,
    links,
    *refs,
    classes,
    part,
):
    sources = refs[:PARTS]
    step_body(
        info, count, places, partial, tallies, links, sources, *refs[PARTS:],
        classes=classes, part=part,
    )


def step_body(
    info,
    count,
    places,
    partial,
    tallies,
    links,
    sources,
    valid_two,
    adjacent_three,
    valid_three,
    labels,
    labelled,
    weights_in,
    weights_mid,
    weights_out,
    biases_line,
    keep,
    send,
    slopes,
    packed,
    sums,
    weight_sums,
    mid_sums,
    out_sums,
    own_table,
    late_table,
    mixin,
    own_rows,
    joined,
    late,
    early,
    link,
    sems,
    link_sems,
    *,
    classes,
    part,
):
    blocks, both, _ = links.shape
    targets = both // 2
    hidden = weights_in.shape[2]
    seeds = labels.shape[0]
    biases = biases_line[...].reshape(1, biases_line.shape[0])
    label, marked = [
        jnp.transpose(
            jnp.broadcast_to(item[...].reshape(1, seeds).astype(jnp.float32), (8, seeds))
        )[:, 0:1]
        for item in (labels, labelled)
    ]
    wide = up(classes, LANES)
    core = info[0]
    used = count[1]
    low = jnp.bfloat16
    width = sources[0].shape[1]

    def load(block, slot):
        rows = pl.ds(pl.multiple_of(block * SPAN, SPAN), SPAN)
        return (
            pltpu.make_async_copy(tallies.at[rows, :], late.at[slot], sems.at[slot, 0]),
            pltpu.make_async_copy(partial.at[rows, :], early.at[slot], sems.at[slot, 1]),
        )

    def load_link(block):
        return pltpu.make_async_copy(links.at[block], link.at[block], link_sems.at[block])

    @pl.when(used > 0)
    def _():
        for copy in load(0, 0):
            copy.start()

    def start_link(block, carry):
        load_link(block).start()
        return carry

    lax.fori_loop(0, used, start_link, 0)
    late_table[:, 0:width] = sources[-1][...]
    late_table[:, width:] = jnp.ones((late_table.shape[0], width), low)
    held = own_table.shape[0] // PARTS
    for which in range(PARTS):
        own_table[which * held : (which + 1) * held, :] = sources[which][0:held, :].astype(
            jnp.float32
        )

    w_in = weights_in[...].astype(low).reshape(2 * weights_in.shape[1], hidden)
    bias_in = biases[:, 0:hidden]
    bias_mid = biases[:, hidden : 2 * hidden]
    bias_out = jnp.concatenate(
        [
            biases[:, 2 * hidden : 2 * hidden + classes],
            jnp.full((1, wide - classes), -1e30, jnp.float32),
        ],
        axis=1,
    )

    sums[...] = jnp.zeros_like(sums)

    def forward(block, carry):
        rows = pl.ds(pl.multiple_of(block * SPAN, SPAN), SPAN)
        slot = lax.rem(block, 2)
        for copy in load(block, slot):
            copy.wait()
        load_link(block).wait()

        @pl.when(block + 1 < used)
        def _():
            for copy in load(block + 1, 1 - slot):
                copy.start()

        copy_rows(places, block, own_table, own_rows)
        joined[...] = dot(late[slot], late_table[...]) + early[slot]
        mixin[rows, 0:width] = own_rows[...].astype(low)
        mixin[rows, width:] = (
            joined[:, 0:width] / jnp.maximum(joined[:, width:], 1.0)
        ).astype(low)
        z = dot(mixin[rows, :], w_in) + bias_in
        s = 1.0 / (1.0 + jnp.exp(-z))
        slopes[rows, :] = s * (1.0 + z * (1.0 - s))
        sums[...] += dot(link[block], (z * s).astype(low))
        return carry

    lax.fori_loop(0, used, forward, 0)
    total = sums[...]
    counts_two = clipped_counts(valid_two[...])
    mixed_one = (total[0:targets] / counts_two).astype(low)
    self_one = total[targets:].astype(low)
    w_mid = weights_mid[...].astype(low)
    both_one = jnp.concatenate([self_one, mixed_one], axis=1)
    z = dot(both_one, w_mid.reshape(2 * hidden, hidden)) + bias_mid
    s = 1.0 / (1.0 + jnp.exp(-z))
    slope_mid = s * (1.0 + z * (1.0 - s))
    hidden_two = (z * s).astype(low)

    here = jnp.where(valid_three[...] > 0, adjacent_three[...], -1)
    place = lax.broadcasted_iota(jnp.int32, (seeds, targets), 1)
    number = jnp.zeros((seeds, targets), jnp.float32)
    for j in range(here.shape[1]):
        number = number + jnp.where(here[:, j : j + 1] == place, 1.0, 0.0)
    number = number.astype(low)
    counts_three = clipped_counts(valid_three[...])
    mixed_two = (dot(number, hidden_two) / counts_three).astype(low)
    self_two = hidden_two[0:seeds]
    w_out = [
        jnp.concatenate(
            [weights_out[:, k, :], jnp.zeros((wide - classes, hidden), jnp.float32)], axis=0
        ).astype(low)
        for k in range(2)
    ]
    both_two = jnp.concatenate([self_two, mixed_two], axis=1)
    logits = dot_cols(both_two, jnp.concatenate(w_out, axis=1)) + bias_out
    top = jnp.max(logits, axis=1, keepdims=True)
    log_total = top + jnp.log(jnp.sum(jnp.exp(logits - top), axis=1, keepdims=True))
    onehot = jnp.where(
        label.astype(jnp.int32) == lax.broadcasted_iota(jnp.int32, (seeds, wide), 1), 1.0, 0.0
    )
    picked = jnp.sum(jnp.where(onehot > 0.0, logits, 0.0), axis=1, keepdims=True)
    loss = jnp.sum(marked * (log_total - picked), axis=0, keepdims=True)
    counted = jnp.sum(marked, axis=0, keepdims=True)
    grad_out = (marked * (jnp.exp(logits - log_total) - onehot)).astype(low)

    out_sums[...] = dot_rows(grad_out, both_two)
    bias_grad_out = jnp.sum(grad_out.astype(jnp.float32), axis=0, keepdims=True)
    to_self = dot(grad_out, w_out[0])
    spread = (dot(grad_out, w_out[1]) / counts_three).astype(low)
    sums[0:targets, :] = dot_rows(number, spread)
    sums[0:seeds, :] += to_self
    grad_mid = (sums[0:targets, :] * slope_mid).astype(low)

    mid_sums[...] = dot_rows(both_one, grad_mid)
    bias_grad_mid = jnp.sum(grad_mid.astype(jnp.float32), axis=0, keepdims=True)
    down = jnp.concatenate(
        [dot_cols(grad_mid, w_mid[1]) / counts_two, dot_cols(grad_mid, w_mid[0])], axis=0
    )
    spread = down.astype(low)

    weight_sums[...] = jnp.zeros_like(weight_sums)

    def backward(block, bias):
        rows = pl.ds(pl.multiple_of(block * SPAN, SPAN), SPAN)
        grad = (dot_rows(link[block], spread) * slopes[rows, :]).astype(low)
        weight_sums[...] += dot_rows(mixin[rows, :], grad)
        return bias + jnp.sum(grad.astype(jnp.float32), axis=0, keepdims=True)

    bias_grad_in = lax.fori_loop(0, used, backward, jnp.zeros((1, hidden), jnp.float32))

    row = 0
    for part in (weight_sums, mid_sums):
        for column in range(0, hidden, LANES):
            packed[row : row + part.shape[0], :] = part[:, column : column + LANES]
            row += part.shape[0]
    tall = up(classes, 16)
    for column in range(0, 2 * hidden, LANES):
        packed[row : row + tall, :] = out_sums[0:tall, column : column + LANES]
        row += tall
    packed[row:, :] = jnp.zeros((packed.shape[0] - row, LANES), jnp.float32)
    lane = lax.broadcasted_iota(jnp.int32, (1, LANES), 1)
    scalars = jnp.where(lane == 0, loss, 0.0) + jnp.where(lane == 1, counted, 0.0)
    extra = [
        item[:, column : column + LANES]
        for item in (bias_grad_in, bias_grad_mid, bias_grad_out)
        for column in range(0, hidden, LANES)
    ] + [scalars, jnp.zeros((1, LANES), jnp.float32)]
    extra = jnp.concatenate(extra, axis=0)
    high = extra.astype(low).astype(jnp.float32)
    packed[packed.shape[0] - 16 :, :] = jnp.concatenate([high, extra - high], axis=0)
    half = keep.shape[0]
    keep[...] = packed[pl.ds(pl.multiple_of(core * half, 16), half), :].astype(low)
    send[...] = packed[pl.ds(pl.multiple_of((1 - core) * half, 16), half), :].astype(low)


def run_step(info, count, places, partial, tallies, links, sources, rest, half, classes, part, owners):
    padded = partial.shape[0]
    blocks, both, _ = links.shape
    total, width = sources[0].shape
    hidden = rest[5].shape[2]
    wide = up(classes, LANES)
    return call(
        functools.partial(step_kernel, classes=classes, part=part),
        "step",
        (jax.ShapeDtypeStruct((half, LANES), jnp.bfloat16),) * 2,
        [smem] * 3 + [anywhere] * 3 + [vmem] * (PARTS + 9),
        (vmem, vmem),
        [
            pltpu.VMEM((padded, hidden), jnp.float32),
            pltpu.VMEM((2 * half, LANES), jnp.float32),
            pltpu.VMEM((both, hidden), jnp.float32),
            pltpu.VMEM((2 * width, hidden), jnp.float32),
            pltpu.VMEM((2 * hidden, hidden), jnp.float32),
            pltpu.VMEM((wide, 2 * hidden), jnp.float32),
            pltpu.VMEM((PARTS * owners * part, width), jnp.float32),
            pltpu.VMEM((total, 2 * width), jnp.bfloat16),
            pltpu.VMEM((padded, 2 * width), jnp.bfloat16),
            pltpu.VMEM((SPAN, width), jnp.float32),
            pltpu.VMEM((SPAN, 2 * width), jnp.float32),
            pltpu.VMEM((2, SPAN, total), jnp.bfloat16),
            pltpu.VMEM((2, SPAN, 2 * width), jnp.float32),
            pltpu.VMEM((blocks, both, SPAN), jnp.bfloat16),
            pltpu.SemaphoreType.DMA((2, 2)),
            pltpu.SemaphoreType.DMA((blocks,)),
        ],
        4 << 30,
        32 << 20,
        44 << 20,
    )(info, count, places, partial, tallies, links, *sources, *rest)


def refit(total, rows):
    extra = total[rows - 16 : rows - 8] + total[rows - 8 : rows]
    high = extra.astype(jnp.bfloat16).astype(jnp.float32)
    return jnp.concatenate([high, extra - high], axis=0)


def pair_kernel(info, mine, theirs, out):
    total = mine[...].astype(jnp.float32) + theirs[...].astype(jnp.float32)
    out[...] = total.astype(jnp.bfloat16)

    @pl.when(info[0] == 1)
    def _():
        rows = total.shape[0]
        out[rows - 16 :, :] = refit(total, rows).astype(jnp.bfloat16)


def pair_sum(info, mine, theirs):
    return call(
        pair_kernel,
        "pair_sum",
        jax.ShapeDtypeStruct(mine.shape, jnp.bfloat16),
        [smem, vmem, vmem],
        vmem,
        [],
        mine.size,
        mine.size * 6,
        6 << 20,
    )(info, mine, theirs)


def spread_kernel(info, pieces, out):
    total = pieces[0].astype(jnp.float32)
    for k in range(1, pieces.shape[0]):
        total = total + pieces[k].astype(jnp.float32)
    rows = total.shape[0]
    fitted = jnp.concatenate([total[0 : rows - 16], refit(total, rows)], axis=0)
    result = jnp.where(info[1] == 1, fitted, total).astype(jnp.bfloat16)
    for k in range(pieces.shape[0]):
        out[k] = result


def spread_sum(info, pieces):
    return call(
        spread_kernel,
        "spread_sum",
        jax.ShapeDtypeStruct(pieces.shape, jnp.bfloat16),
        [smem, vmem],
        vmem,
        [],
        pieces.size,
        pieces.size * 4,
        6 << 20,
    )(info, pieces)


def update_kernel(
    info, fixes, corners, mine, theirs, biases, moment_one, moment_two, *refs
):
    groups = [refs[3 * k : 3 * k + 3] for k in range(3)]
    loss_out = refs[9]
    outs = [refs[10 + 4 * k : 14 + 4 * k] for k in range(3)]
    bias_out, first_out, second_out = refs[22:25]
    packed = refs[25]
    low = jnp.bfloat16
    half = mine.shape[0]
    core = info[0]
    packed[pl.ds(pl.multiple_of(core * half, 16), half), :] = mine[...]
    packed[pl.ds(pl.multiple_of((1 - core) * half, 16), half), :] = theirs[...]
    last = packed.shape[0]
    extra = packed[last - 16 :, :].astype(jnp.float32)
    extra = extra[0:8] + extra[8:16]
    counted = extra[6:7, 1:2]
    inverse = 1.0 / counted
    loss_out[...] = extra[6:7, 0:1] / counted
    scale = 0.5 * inverse * inverse

    row = 0
    for group in range(3):
        master, left_root, right_root = groups[group]
        new_master, copy, new_left, new_right = outs[group]
        turned = group == 2
        depth, hidden = (master.shape[0], master.shape[2]) if turned else master.shape[1:]
        deep = up(depth, LANES)

        def take(ref, k, middle):
            return ref[:, k, :] if middle else ref[k]

        def put(ref, k, middle, value):
            if middle:
                ref[:, k, :] = value
            else:
                ref[k] = value

        grads = []
        if turned:
            tall = up(depth, 16)
            for k in range(2):
                parts = []
                for column in range(0, hidden, LANES):
                    parts.append(packed[row : row + tall, :])
                    row += tall
                grads.append(grown(jnp.concatenate(parts, axis=1), deep, hidden))
        else:
            parts = []
            for column in range(0, hidden, LANES):
                parts.append(packed[row : row + 2 * depth, :])
                row += 2 * depth
            whole = jnp.concatenate(parts, axis=1)
            grads = [whole[k * depth : (k + 1) * depth] for k in range(2)]

        for k in range(2):
            grad = grads[k]
            for side, new, size, product, middle in (
                (0, new_left, depth, dot_cols(grad, grad), turned),
                (1, new_right, hidden, dot_rows(grad, grad), False),
            ):
                corner = corners[group * 4 + side * 2 + k]
                eye = lax.broadcasted_iota(jnp.int32, (size, size), 0) == (
                    lax.broadcasted_iota(jnp.int32, (size, size), 1)
                )
                value = jnp.where(eye, 0.5 * corner, 0.0) + scale * product[0:size, 0:size]
                put(new, k, middle, value)
            root = jnp.concatenate(
                halves(grown(take(left_root, k, turned), deep, deep)), axis=1
            )
            middle_high, middle_rest = halves(dot(root, jnp.concatenate([grad, grad], axis=0)))
            root_high, root_rest = halves(right_root[k])
            way = dot(
                jnp.concatenate([middle_high, middle_high, middle_rest], axis=1),
                jnp.concatenate([root_high, root_rest, root_high], axis=0),
            )[0:depth]
            put(new_master, k, turned, take(master, k, turned) - inverse * way)
        copy[...] = new_master[...].astype(low)

    size = biases.shape[0]
    grad = jnp.concatenate([extra[k : k + 1, :] for k in range(6)], axis=1)[:, 0:size]
    grad = grad / counted

    def line(ref):
        return ref[...].reshape(1, size)

    first = 0.9 * line(moment_one) + 0.1 * grad
    second = 0.95 * line(moment_two) + 0.05 * grad * grad
    old = line(biases)
    fresh = old - 0.1 * (
        (first / fixes[0]) / (jnp.sqrt(second / fixes[1]) + 1e-08) + 0.01 * old
    )
    for ref, value in ((bias_out, fresh), (first_out, first), (second_out, second)):
        ref[...] = value[0]


def run_update(info, fixes, corners, mine, theirs, vectors, groups):
    outs = [jax.ShapeDtypeStruct((1, 1), jnp.float32)]
    flat = []
    for master, left_root, right_root in groups:
        flat += [master, left_root, right_root]
        outs += [
            jax.ShapeDtypeStruct(master.shape, jnp.float32),
            jax.ShapeDtypeStruct(master.shape, jnp.bfloat16),
            jax.ShapeDtypeStruct(left_root.shape, jnp.float32),
            jax.ShapeDtypeStruct(right_root.shape, jnp.float32),
        ]
    outs += [jax.ShapeDtypeStruct(vectors[0].shape, jnp.float32)] * 3
    return call(
        update_kernel,
        "update",
        tuple(outs),
        [smem] * 3 + [vmem] * (5 + len(flat)),
        (vmem,) * len(outs),
        [pltpu.VMEM((2 * mine.shape[0], LANES), jnp.bfloat16)],
        1 << 30,
        10 << 20,
        32 << 20,
    )(info, fixes, corners, mine, theirs, *vectors, *flat)


def body(
    features,
    requests,
    adjacent_one,
    adjacent_two,
    adjacent_three,
    valid_one,
    valid_two,
    valid_three,
    labels,
    labelled,
    weights_in,
    weights_mid,
    weights_out,
    biases,
    moment_one,
    moment_two,
    step_count,
    left_in,
    left_mid,
    left_out,
    right_in,
    right_mid,
    right_out,
    invleft_in,
    invleft_mid,
    invleft_out,
    invright_in,
    invright_mid,
    invright_out,
    *,
    peers,
):
    width = features.shape[1]
    devices, per = requests.shape
    part = per // PARTS
    total = devices * per
    targets, fan = adjacent_one.shape
    padded = up(targets, SPAN)
    owners = -(-targets // per)
    classes = weights_out.shape[2]
    hidden = weights_in.shape[2]
    core = lax.axis_index("core")
    own = lax.axis_index(PEERS)

    wanted = lax.all_to_all(requests, AXES, split_axis=0, concat_axis=0, tiled=True)
    sources = []
    for which in range(PARTS):
        found = pick_rows(wanted, features, which).reshape(devices, part, width)
        pulled = lax.all_to_all(found, AXES, split_axis=0, concat_axis=0, tiled=True)
        sources.append(pulled.reshape(devices * part, width))

    names, places, count = reach(
        adjacent_three, valid_three, labelled, adjacent_two, valid_two, targets, per
    )
    owner, slot = adjacent_one // per, adjacent_one % per
    slots = (slot // part) * (devices * part) + owner * part + slot % part
    slots = jnp.where(valid_one > 0, slots, -1)
    slots = jnp.pad(slots, ((0, 8), (0, 16 - fan)), constant_values=-1)
    tallies = tally(count, names, slots, padded, total)
    links = link_matrix(count, names, adjacent_two, valid_two, padded)
    partial = early_sums(count, tallies[0], sources[0])

    rows = (2 * width + 2 * weights_mid.shape[1]) * (hidden // LANES)
    rows += up(classes, 16) * (2 * hidden // LANES)
    each = up(-(-(rows + 16) // (2 * peers)), 8)
    half = each * peers
    info = jnp.stack([core, ((core == 1) & (own == peers - 1)).astype(jnp.int32)])
    info = info.astype(jnp.int32)
    turned_out = weights_out.transpose(2, 0, 1)
    keep, send = run_step(
        info,
        count,
        places,
        partial,
        tallies[1],
        links,
        sources,
        (
            valid_two,
            adjacent_three,
            valid_three,
            labels,
            labelled,
            weights_in,
            weights_mid,
            turned_out,
            biases,
        ),
        half,
        classes,
        part,
        owners,
    )
    swap = [(0, 1), (1, 0)]
    theirs = lax.ppermute(send, "core", swap)
    summed = pair_sum(info, keep, theirs).reshape(peers, each, LANES)
    pieces = lax.all_to_all(summed, PEERS, split_axis=0, concat_axis=0, tiled=True)
    shared = spread_sum(info, pieces)
    mine = lax.all_to_all(shared, PEERS, split_axis=0, concat_axis=0, tiled=True)
    mine = mine.reshape(half, LANES)
    theirs = lax.ppermute(mine, "core", swap)

    stepped = step_count.astype(jnp.float32)
    fixes = jnp.stack([1.0 - 0.9**stepped, 1.0 - 0.95**stepped])
    corners = jnp.concatenate(
        [
            item[:, 0, 0]
            for item in (left_in, right_in, left_mid, right_mid, right_out, left_out)
        ]
    )
    outs = run_update(
        info,
        fixes,
        corners,
        mine,
        theirs,
        (biases, moment_one, moment_two),
        (
            (weights_in, invleft_in, invright_in),
            (weights_mid, invleft_mid, invright_mid),
            (turned_out, invright_out.transpose(1, 0, 2), invleft_out),
        ),
    )
    first, second, third = (outs[1 + 4 * k : 5 + 4 * k] for k in range(3))
    third = (
        third[0].transpose(1, 2, 0),
        third[1].transpose(1, 2, 0),
        third[3],
        third[2].transpose(1, 0, 2),
    )
    return (
        (outs[0].reshape(()),)
        + tuple(group[which] for which in range(4) for group in (first, second, third))
        + tuple(outs[13:16])
    )


def solution(mesh):
    chips, dev = mesh.shape["hst"] // 2, mesh.shape["dev"]
    fine = jax.sharding.Mesh(mesh.devices.reshape(chips, 2, dev), AXES)
    split = P(AXES, None)
    line = P(AXES)
    whole = P()
    mapped = jax.shard_map(
        functools.partial(body, peers=chips * dev),
        mesh=fine,
        in_specs=(split,) * 8 + (line,) * 2 + (whole,) * 19,
        out_specs=(whole,) * 16,
        check_vma=False,
    )

    def run(*args):
        with jax.sharding.use_abstract_mesh(fine.abstract_mesh):
            return mapped(*args)

    return run
```

```python
import functools

import jax
import jax.numpy as jnp
from jax import lax
from jax.experimental import pallas as pl
from jax.experimental.pallas import tpu as pltpu
from jax.sharding import PartitionSpec as P

LANES = 128
SPAN = 256
PARTS = 2
AXES = ("chip", "core", "dev")
PEERS = ("chip", "dev")

smem = pl.BlockSpec(memory_space=pltpu.SMEM)
vmem = pl.BlockSpec(memory_space=pltpu.VMEM)
anywhere = pl.BlockSpec(memory_space=pltpu.HBM)


def up(value, unit):
    return -(-value // unit) * unit


def call(kernel, name, out_shape, in_specs, out_specs, scratch, flops, moved, room):
    return pl.pallas_call(
        kernel,
        name=name,
        out_shape=out_shape,
        in_specs=in_specs,
        out_specs=out_specs,
        scratch_shapes=scratch,
        compiler_params=pltpu.CompilerParams(vmem_limit_bytes=room),
        cost_estimate=pl.CostEstimate(flops=flops, transcendentals=0, bytes_accessed=moved),
    )


def dot(left, right):
    return jnp.dot(left, right, preferred_element_type=jnp.float32)


def dot_rows(left, right):
    return lax.dot_general(
        left, right, (((0,), (0,)), ((), ())), preferred_element_type=jnp.float32
    )


def dot_cols(left, right):
    return lax.dot_general(
        left, right, (((1,), (1,)), ((), ())), preferred_element_type=jnp.float32
    )


def halves(value):
    high = value.astype(jnp.bfloat16)
    return high, (value - high.astype(jnp.float32)).astype(jnp.bfloat16)


def grown(value, rows, columns):
    short = columns - value.shape[1]
    if short:
        value = jnp.concatenate([value, jnp.zeros((value.shape[0], short), value.dtype)], axis=1)
    short = rows - value.shape[0]
    if short:
        value = jnp.concatenate([value, jnp.zeros((short, columns), value.dtype)], axis=0)
    return value


def clipped_counts(valid):
    return jnp.maximum(jnp.sum(valid.astype(jnp.float32), axis=1, keepdims=True), 1.0)


def copy_rows(names, block, source, target):
    unroll = 64
    base = block * SPAN

    def fetch(step, carry):
        for u in range(unroll):
            at = step * unroll + u
            target[pl.ds(at, 1), :] = source[pl.ds(names[base + at], 1), :]
        return carry

    lax.fori_loop(0, SPAN // unroll, fetch, 0)


def cuts(per):
    return (0, per - per // 4), (per - per // 4, per)


def pick_kernel(wanted, table, out, rows, *, first, last, per):
    part = last - first

    def body(device, carry):
        for u in range(part):
            name = wanted[device * per + (first + u)]
            rows[pl.ds(device * part + u, 1), :] = table[pl.ds(name, 1), :]
        return carry

    lax.fori_loop(0, out.shape[0] // part, body, 0)
    out[...] = rows[...].astype(jnp.bfloat16)


def pick_rows(wanted, table, per, ends):
    first, last = ends
    width = table.shape[1]
    count = wanted.shape[0] // per * (last - first)
    return call(
        functools.partial(pick_kernel, first=first, last=last, per=per),
        "pick_rows",
        jax.ShapeDtypeStruct((count, width), jnp.bfloat16),
        [smem, vmem],
        vmem,
        [pltpu.VMEM((count, width), jnp.float32)],
        count * width,
        table.size * 4,
        20 << 20,
    )(wanted, table)


def stood(flat, unit):
    size = flat.shape[1]
    flat = jnp.concatenate(
        [flat, jnp.full((unit - flat.shape[0], size), -1, jnp.int32)], axis=0
    ).astype(jnp.float32)
    step = min(LANES, size)
    parts = [jnp.transpose(flat[:, k : k + step]) for k in range(0, size, step)]
    return jnp.concatenate(parts, axis=0).astype(jnp.int32)


def reach_kernel(
    adjacent_three,
    valid_three,
    labelled,
    adjacent_two,
    valid_two,
    names,
    places,
    near_two,
    near_three,
    count,
    left,
    right,
    *,
    rows_all,
    per,
):
    fan_three, seeds = adjacent_three.shape
    fan_two, targets = adjacent_two.shape
    low = jnp.bfloat16
    blocks = rows_all // LANES
    deep = names.shape[0]
    line = labelled[...].reshape(1, seeds)
    column = jnp.transpose(jnp.broadcast_to(line.astype(jnp.float32), (8, seeds)))[:, 0:1]
    near = stood(jnp.where(valid_three[...] > 0, adjacent_three[...], -1), near_three.shape[1])
    near_three[...] = near
    here = jnp.where(column > 0.0, near, -1)
    place = lax.broadcasted_iota(jnp.int32, (seeds, targets), 1)
    hit = jnp.zeros((seeds, targets), jnp.float32)
    for j in range(fan_three):
        hit = hit + jnp.where(here[:, j : j + 1] == place, 1.0, 0.0)
    need = jnp.max(hit, axis=0, keepdims=True) + jnp.concatenate(
        [line.astype(jnp.float32), jnp.zeros((1, targets - seeds), jnp.float32)], axis=1
    )

    level = lax.broadcasted_iota(jnp.int32, (deep, targets), 0)
    lane = lax.broadcasted_iota(jnp.int32, (targets, LANES), 1)
    flat = jnp.where(valid_two[...] > 0, adjacent_two[...], -1)
    tall = stood(flat, near_two.shape[1])
    near_two[...] = tall
    flat = jnp.where(need > 0.0, flat, -1)
    for j in range(fan_two):
        left[0:deep, j * targets : (j + 1) * targets] = jnp.where(
            lax.shift_right_arithmetic(flat[j : j + 1, :], 7) == level, 1.0, 0.0
        ).astype(low)
        right[j * targets : (j + 1) * targets, :] = jnp.where(
            (tall[:, j : j + 1] & (LANES - 1)) == lane, 1.0, 0.0
        ).astype(low)
    used = dot(left[0:deep, 0 : fan_two * targets], right[0 : fan_two * targets, :])
    own = [need[:, k : k + LANES] for k in range(0, targets, LANES)]
    own = jnp.concatenate(
        own + [jnp.zeros((deep - len(own), LANES), jnp.float32)], axis=0
    )
    flag = jnp.where(used + own > 0.0, 1.0, 0.0)

    square_row = lax.broadcasted_iota(jnp.int32, (LANES, LANES), 0)
    square_col = lax.broadcasted_iota(jnp.int32, (LANES, LANES), 1)
    full = jnp.concatenate([flag, jnp.zeros((LANES - deep, LANES), jnp.float32)], axis=0)
    flag_low = full.astype(low)
    running = dot(flag_low, jnp.where(square_row <= square_col, 1.0, 0.0).astype(low))
    totals = dot(flag_low, jnp.ones((LANES, LANES), low)).astype(low)
    before = dot(jnp.where(square_row > square_col, 1.0, 0.0).astype(low), totals)
    order = (before + running - full).astype(jnp.int32)
    number = jnp.sum(flag).astype(jnp.int32)
    count[0] = number
    count[1] = lax.div(number + (SPAN - 1), SPAN)

    high = jnp.where(full > 0.0, lax.shift_right_arithmetic(order, 7), -1)
    rest = jnp.transpose((order & (LANES - 1)).astype(jnp.float32)).astype(jnp.int32)
    step = lax.broadcasted_iota(jnp.int32, (deep, LANES), 0)
    inner = lax.broadcasted_iota(jnp.int32, (deep, LANES), 1).astype(jnp.float32)
    for b in range(blocks):
        match = jnp.where(high[b : b + 1, :] == step, 1.0, 0.0)
        lanes = slice(b * LANES, (b + 1) * LANES)
        left[0:deep, lanes] = (match * inner).astype(low)
        left[deep : 2 * deep, lanes] = (match * float(b)).astype(low)
        right[lanes, :] = jnp.where(rest[:, b : b + 1] == square_col, 1.0, 0.0).astype(low)
    found = dot(left[:, 0:rows_all], right[0:rows_all, :]).astype(jnp.int32)
    where = step * LANES + lax.broadcasted_iota(jnp.int32, (deep, LANES), 1)
    name = found[deep:] * LANES + found[0:deep]
    names[...] = jnp.where(where < number, name, rows_all)
    name = jnp.minimum(jnp.where(where < number, name, 0), rows_all - 1)
    owners = -(-rows_all // per)
    owner = lax.shift_right_logical(name, per.bit_length() - 1)
    slot = name & (per - 1)
    early, late = (last - first for first, last in cuts(per))
    places[...] = jnp.where(
        slot < early, owner * early + slot, owners * early + owner * late + slot - early
    )


def reach(adjacent_three, valid_three, labelled, adjacent_two, valid_two, rows_all, per):
    targets, fan = adjacent_two.shape
    seeds = labelled.shape[0]
    deep = up(up(rows_all, SPAN) // LANES, 16)
    area = max(fan * targets, rows_all)
    return call(
        functools.partial(reach_kernel, rows_all=rows_all, per=per),
        "reach",
        (
            jax.ShapeDtypeStruct((deep, LANES), jnp.int32),
            jax.ShapeDtypeStruct((deep, LANES), jnp.int32),
            jax.ShapeDtypeStruct((targets, 16), jnp.int32),
            jax.ShapeDtypeStruct((seeds, 8), jnp.int32),
            jax.ShapeDtypeStruct((2,), jnp.int32),
        ),
        [vmem] * 5,
        (vmem,) * 4 + (smem,),
        [
            pltpu.VMEM((2 * deep, area), jnp.bfloat16),
            pltpu.VMEM((area, LANES), jnp.bfloat16),
        ],
        1 << 28,
        1 << 20,
        8 << 20,
    )(adjacent_three.T, valid_three.T, labelled, adjacent_two.T, valid_two.T)


def tally_kernel(
    count, names, adjacent, valid, early_out, late_out, table, rows, spread, marked, buffer, sems, *, per
):
    low = jnp.bfloat16
    fan, targets = adjacent.shape
    unit = spread.shape[0]
    groups = SPAN // unit
    used = count[1]
    outs = (early_out, late_out)
    first_wide = early_out.shape[1]
    high_all = (first_wide + late_out.shape[1]) // SPAN

    slot = adjacent[...]
    owner = lax.shift_right_logical(slot, per.bit_length() - 1)
    inner = slot & (per - 1)
    early, late = (last - first for first, last in cuts(per))
    slot = jnp.where(
        inner < early, owner * early + inner, first_wide + owner * late + inner - early
    )
    slot = jnp.where(valid[...] > 0, slot, -1)
    slot = jnp.concatenate([slot, jnp.full((unit - fan, targets), -1, jnp.int32)], axis=0)
    slot = slot.astype(jnp.float32)
    for b in range(0, targets, LANES):
        table[b : b + LANES, :] = jnp.transpose(slot[:, b : b + LANES]).astype(jnp.int32)
    table[targets:, :] = jnp.full((table.shape[0] - targets, unit), -1, jnp.int32)

    across = lax.broadcasted_iota(jnp.int32, (unit, SPAN), 1)
    down = lax.broadcasted_iota(jnp.int32, (unit, SPAN), 0)
    spread[...] = jnp.where(lax.div(across, unit) == down, 1.0, 0.0).astype(low)
    lane = across.astype(jnp.float32).astype(low)
    one = jnp.ones((unit, SPAN), low)
    zero = jnp.zeros((unit, SPAN), low)

    def copies(block, slot):
        where = pl.ds(pl.multiple_of(block * SPAN, SPAN), SPAN)
        return [
            pltpu.make_async_copy(
                buffer.at[slot, :, pl.ds(which * first_wide, out.shape[1])],
                out.at[where, :],
                sems.at[slot, which],
            )
            for which, out in enumerate(outs)
        ]

    def body(block, carry):
        slot = lax.rem(block, 2)

        @pl.when(block >= 2)
        def _():
            for copy in copies(block - 2, slot):
                copy.wait()

        copy_rows(names, block, table, rows)
        high = lax.shift_right_arithmetic(rows[...], 8).astype(jnp.float32).astype(low)
        own = lax.rem(lax.broadcasted_iota(jnp.int32, (SPAN, SPAN), 0), unit) == lax.rem(
            lax.broadcasted_iota(jnp.int32, (SPAN, SPAN), 1), unit
        )
        marked[...] = jnp.where(own, dot(high, spread[...]), -1.0).astype(low)

        def single(g):
            first = pl.multiple_of(g * unit, unit)
            rest = (rows[pl.ds(first, unit), :] & (SPAN - 1)).astype(jnp.float32)
            columns = [
                jnp.where(
                    jnp.broadcast_to(rest[:, j : j + 1], (unit, SPAN)).astype(low) == lane,
                    one,
                    zero,
                )
                for j in range(unit)
            ]
            mark = marked[pl.ds(first, unit), :]
            marks = [
                jnp.where(mark == jnp.full((unit, SPAN), float(q), low), one, zero)
                for q in range(high_all)
            ]
            result = dot(
                jnp.concatenate(marks, axis=0), jnp.concatenate(columns, axis=0)
            ).astype(low)
            for q in range(high_all):
                buffer[slot, pl.ds(first, unit), q * SPAN : (q + 1) * SPAN] = result[
                    q * unit : (q + 1) * unit
                ]

        def group(step, inner):
            for u in range(4):
                single(step * 4 + u)
            return inner

        lax.fori_loop(0, groups // 4, group, 0)
        for copy in copies(block, slot):
            copy.start()
        return carry

    lax.fori_loop(0, used, body, 0)

    @pl.when(used >= 2)
    def _():
        for copy in copies(used - 2, lax.rem(used - 2, 2)):
            copy.wait()

    @pl.when(used >= 1)
    def _():
        for copy in copies(used - 1, lax.rem(used - 1, 2)):
            copy.wait()


def tally(count, names, adjacent, valid, padded, devices, per):
    targets = adjacent.shape[0]
    unit = 16
    wide = [devices * (last - first) for first, last in cuts(per)]
    return call(
        functools.partial(tally_kernel, per=per),
        "tally",
        tuple(jax.ShapeDtypeStruct((padded, item), jnp.bfloat16) for item in wide),
        [smem, smem, vmem, vmem],
        (anywhere, anywhere),
        [
            pltpu.VMEM((targets + 8, unit), jnp.int32),
            pltpu.VMEM((SPAN, unit), jnp.int32),
            pltpu.VMEM((unit, SPAN), jnp.bfloat16),
            pltpu.VMEM((SPAN, SPAN), jnp.bfloat16),
            pltpu.VMEM((2, SPAN, sum(wide)), jnp.bfloat16),
            pltpu.SemaphoreType.DMA((2, 2)),
        ],
        1 << 32,
        32 << 20,
        24 << 20,
    )(count, names, adjacent.T, valid.T)


def early_kernel(count, tallies, source, out, table, buffer, result, sems, out_sems):
    width = source.shape[1]
    used = count[1]
    table[:, 0:width] = source[...]
    table[:, width:] = jnp.ones((source.shape[0], width), jnp.bfloat16)

    def rows(block):
        return pl.ds(pl.multiple_of(block * SPAN, SPAN), SPAN)

    def load(block, slot):
        return pltpu.make_async_copy(tallies.at[rows(block), :], buffer.at[slot], sems.at[slot])

    def save(block, slot):
        return pltpu.make_async_copy(result.at[slot], out.at[rows(block), :], out_sems.at[slot])

    @pl.when(used > 0)
    def _():
        load(0, 0).start()

    def body(block, carry):
        slot = lax.rem(block, 2)
        load(block, slot).wait()

        @pl.when(block + 1 < used)
        def _():
            load(block + 1, 1 - slot).start()

        @pl.when(block >= 2)
        def _():
            save(block - 2, slot).wait()

        result[slot] = dot(buffer[slot], table[...])
        save(block, slot).start()
        return carry

    lax.fori_loop(0, used, body, 0)

    @pl.when(used >= 2)
    def _():
        save(used - 2, lax.rem(used - 2, 2)).wait()

    @pl.when(used >= 1)
    def _():
        save(used - 1, lax.rem(used - 1, 2)).wait()


def early_sums(count, tallies, source):
    padded, total = tallies.shape
    width = source.shape[1]
    return call(
        early_kernel,
        "early_sums",
        jax.ShapeDtypeStruct((padded, 2 * width), jnp.float32),
        [smem, anywhere, vmem],
        anywhere,
        [
            pltpu.VMEM((total, 2 * width), jnp.bfloat16),
            pltpu.VMEM((2, SPAN, total), jnp.bfloat16),
            pltpu.VMEM((2, SPAN, 2 * width), jnp.float32),
            pltpu.SemaphoreType.DMA((2,)),
            pltpu.SemaphoreType.DMA((2,)),
        ],
        1 << 32,
        16 << 20,
        16 << 20,
    )(count, tallies, source)


def link_kernel(count, names, near, out, *, fan):
    targets = near.shape[0]
    tile = 32
    blocks = count[1]

    def rows(step, carry):
        first = pl.multiple_of(step * tile, tile)
        here = near[pl.ds(first, tile), :]
        spread = [jnp.broadcast_to(here[:, j : j + 1], (tile, LANES)) for j in range(fan)]
        own = first + lax.broadcasted_iota(jnp.int32, (tile, LANES), 0)

        def columns(block, inner):
            for part in range(SPAN // LANES):
                name = jnp.broadcast_to(
                    names[pl.ds(block * (SPAN // LANES) + part, 1), :], (tile, LANES)
                )
                number = jnp.zeros((tile, LANES), jnp.float32)
                for j in range(fan):
                    number = number + jnp.where(spread[j] == name, 1.0, 0.0)
                lanes = pl.ds(part * LANES, LANES)
                out[block, pl.ds(first, tile), lanes] = number.astype(jnp.bfloat16)
                out[block, pl.ds(targets + first, tile), lanes] = jnp.where(
                    own == name, 1.0, 0.0
                ).astype(jnp.bfloat16)
            return inner

        return lax.fori_loop(0, blocks, columns, carry)

    lax.fori_loop(0, targets // tile, rows, 0)


def link_matrix(count, names, near, fan, padded):
    blocks = padded // SPAN
    targets = near.shape[0]
    return call(
        functools.partial(link_kernel, fan=fan),
        "link_matrix",
        jax.ShapeDtypeStruct((blocks, 2 * targets, SPAN), jnp.bfloat16),
        [smem, vmem, vmem],
        vmem,
        [],
        blocks * targets * SPAN * 30,
        blocks * targets * SPAN * 4,
        12 << 20,
    )(count, names, near)


def step_kernel(
    info,
    count,
    places,
    partial,
    tallies,
    links,
    *refs,
    classes,
):
    sources = refs[:PARTS]
    step_body(
        info, count, places, partial, tallies, links, sources, *refs[PARTS:],
        classes=classes,
    )


def step_body(
    info,
    count,
    places,
    partial,
    tallies,
    links,
    sources,
    near_two,
    near_three,
    labels,
    labelled,
    weights_in,
    weights_mid,
    weights_out,
    biases_line,
    keep,
    send,
    slopes,
    packed,
    sums,
    weight_sums,
    mid_sums,
    out_sums,
    own_table,
    late_table,
    mixin,
    own_rows,
    joined,
    late,
    early,
    link,
    sems,
    link_sems,
    *,
    classes,
):
    blocks, both, _ = links.shape
    targets = both // 2
    hidden = weights_in.shape[2]
    seeds = labels.shape[0]
    biases = biases_line[...].reshape(1, biases_line.shape[0])
    label, marked = [
        jnp.transpose(
            jnp.broadcast_to(item[...].reshape(1, seeds).astype(jnp.float32), (8, seeds))
        )[:, 0:1]
        for item in (labels, labelled)
    ]
    wide = up(classes, LANES)
    core = info[0]
    used = count[1]
    low = jnp.bfloat16
    width = sources[0].shape[1]

    def load(block, slot):
        rows = pl.ds(pl.multiple_of(block * SPAN, SPAN), SPAN)
        return (
            pltpu.make_async_copy(tallies.at[rows, :], late.at[slot], sems.at[slot, 0]),
            pltpu.make_async_copy(partial.at[rows, :], early.at[slot], sems.at[slot, 1]),
        )

    def load_link(block):
        return pltpu.make_async_copy(links.at[block], link.at[block], link_sems.at[block])

    @pl.when(used > 0)
    def _():
        for copy in load(0, 0):
            copy.start()

    def start_link(block, carry):
        load_link(block).start()
        return carry

    lax.fori_loop(0, used, start_link, 0)
    late_table[:, 0:width] = sources[-1][...]
    late_table[:, width:] = jnp.ones((late_table.shape[0], width), low)
    filled = 0
    for source in sources:
        held = own_table.shape[0] * source.shape[0] // sum(item.shape[0] for item in sources)
        own_table[filled : filled + held, :] = source[0:held, :].astype(jnp.float32)
        filled += held

    w_in = weights_in[...].astype(low).reshape(2 * weights_in.shape[1], hidden)
    bias_in = biases[:, 0:hidden]
    bias_mid = biases[:, hidden : 2 * hidden]
    bias_out = jnp.concatenate(
        [
            biases[:, 2 * hidden : 2 * hidden + classes],
            jnp.full((1, wide - classes), -1e30, jnp.float32),
        ],
        axis=1,
    )

    sums[...] = jnp.zeros_like(sums)

    def forward(block, carry):
        rows = pl.ds(pl.multiple_of(block * SPAN, SPAN), SPAN)
        slot = lax.rem(block, 2)
        for copy in load(block, slot):
            copy.wait()
        load_link(block).wait()

        @pl.when(block + 1 < used)
        def _():
            for copy in load(block + 1, 1 - slot):
                copy.start()

        copy_rows(places, block, own_table, own_rows)
        joined[...] = dot(late[slot], late_table[...]) + early[slot]
        mixin[rows, 0:width] = own_rows[...].astype(low)
        mixin[rows, width:] = (
            joined[:, 0:width] / jnp.maximum(joined[:, width:], 1.0)
        ).astype(low)
        z = dot(mixin[rows, :], w_in) + bias_in
        s = 1.0 / (1.0 + jnp.exp(-z))
        slopes[rows, :] = s * (1.0 + z * (1.0 - s))
        sums[...] += dot(link[block], (z * s).astype(low))
        return carry

    lax.fori_loop(0, used, forward, 0)
    total = sums[...]
    counts_two = clipped_counts(near_two[...] >= 0)
    mixed_one = (total[0:targets] / counts_two).astype(low)
    self_one = total[targets:].astype(low)
    w_mid = weights_mid[...].astype(low)
    both_one = jnp.concatenate([self_one, mixed_one], axis=1)
    z = dot(both_one, w_mid.reshape(2 * hidden, hidden)) + bias_mid
    s = 1.0 / (1.0 + jnp.exp(-z))
    slope_mid = s * (1.0 + z * (1.0 - s))
    hidden_two = (z * s).astype(low)

    here = near_three[...]
    place = lax.broadcasted_iota(jnp.int32, (seeds, targets), 1)
    number = jnp.zeros((seeds, targets), jnp.float32)
    for j in range(here.shape[1]):
        number = number + jnp.where(here[:, j : j + 1] == place, 1.0, 0.0)
    number = number.astype(low)
    counts_three = clipped_counts(here >= 0)
    mixed_two = (dot(number, hidden_two) / counts_three).astype(low)
    self_two = hidden_two[0:seeds]
    w_out = [
        jnp.concatenate(
            [weights_out[:, k, :], jnp.zeros((wide - classes, hidden), jnp.float32)], axis=0
        ).astype(low)
        for k in range(2)
    ]
    both_two = jnp.concatenate([self_two, mixed_two], axis=1)
    logits = dot_cols(both_two, jnp.concatenate(w_out, axis=1)) + bias_out
    top = jnp.max(logits, axis=1, keepdims=True)
    log_total = top + jnp.log(jnp.sum(jnp.exp(logits - top), axis=1, keepdims=True))
    onehot = jnp.where(
        label.astype(jnp.int32) == lax.broadcasted_iota(jnp.int32, (seeds, wide), 1), 1.0, 0.0
    )
    picked = jnp.sum(jnp.where(onehot > 0.0, logits, 0.0), axis=1, keepdims=True)
    loss = jnp.sum(marked * (log_total - picked), axis=0, keepdims=True)
    counted = jnp.sum(marked, axis=0, keepdims=True)
    grad_out = (marked * (jnp.exp(logits - log_total) - onehot)).astype(low)

    out_sums[...] = dot_rows(grad_out, both_two)
    bias_grad_out = jnp.sum(grad_out.astype(jnp.float32), axis=0, keepdims=True)
    to_self = dot(grad_out, w_out[0])
    spread = (dot(grad_out, w_out[1]) / counts_three).astype(low)
    sums[0:targets, :] = dot_rows(number, spread)
    sums[0:seeds, :] += to_self
    grad_mid = (sums[0:targets, :] * slope_mid).astype(low)

    mid_sums[...] = dot_rows(both_one, grad_mid)
    bias_grad_mid = jnp.sum(grad_mid.astype(jnp.float32), axis=0, keepdims=True)
    down = jnp.concatenate(
        [dot_cols(grad_mid, w_mid[1]) / counts_two, dot_cols(grad_mid, w_mid[0])], axis=0
    )
    spread = down.astype(low)

    weight_sums[...] = jnp.zeros_like(weight_sums)

    def backward(block, bias):
        rows = pl.ds(pl.multiple_of(block * SPAN, SPAN), SPAN)
        grad = (dot_rows(link[block], spread) * slopes[rows, :]).astype(low)
        weight_sums[...] += dot_rows(mixin[rows, :], grad)
        return bias + jnp.sum(grad.astype(jnp.float32), axis=0, keepdims=True)

    bias_grad_in = lax.fori_loop(0, used, backward, jnp.zeros((1, hidden), jnp.float32))

    row = 0
    for part in (weight_sums, mid_sums):
        for column in range(0, hidden, LANES):
            packed[row : row + part.shape[0], :] = part[:, column : column + LANES]
            row += part.shape[0]
    tall = up(classes, 16)
    for column in range(0, 2 * hidden, LANES):
        packed[row : row + tall, :] = out_sums[0:tall, column : column + LANES]
        row += tall
    packed[row:, :] = jnp.zeros((packed.shape[0] - row, LANES), jnp.float32)
    lane = lax.broadcasted_iota(jnp.int32, (1, LANES), 1)
    scalars = jnp.where(lane == 0, loss, 0.0) + jnp.where(lane == 1, counted, 0.0)
    extra = [
        item[:, column : column + LANES]
        for item in (bias_grad_in, bias_grad_mid, bias_grad_out)
        for column in range(0, hidden, LANES)
    ] + [scalars, jnp.zeros((1, LANES), jnp.float32)]
    extra = jnp.concatenate(extra, axis=0)
    high = extra.astype(low).astype(jnp.float32)
    packed[packed.shape[0] - 16 :, :] = jnp.concatenate([high, extra - high], axis=0)
    half = keep.shape[0]
    keep[...] = packed[pl.ds(pl.multiple_of(core * half, 16), half), :].astype(low)
    send[...] = packed[pl.ds(pl.multiple_of((1 - core) * half, 16), half), :].astype(low)


def run_step(info, count, places, partial, tallies, links, sources, rest, half, classes, held):
    padded = partial.shape[0]
    blocks, both, _ = links.shape
    total, width = sources[-1].shape
    hidden = rest[4].shape[2]
    wide = up(classes, LANES)
    return call(
        functools.partial(step_kernel, classes=classes),
        "step",
        (jax.ShapeDtypeStruct((half, LANES), jnp.bfloat16),) * 2,
        [smem] * 3 + [anywhere] * 3 + [vmem] * (PARTS + 8),
        (vmem, vmem),
        [
            pltpu.VMEM((padded, hidden), jnp.float32),
            pltpu.VMEM((2 * half, LANES), jnp.float32),
            pltpu.VMEM((both, hidden), jnp.float32),
            pltpu.VMEM((2 * width, hidden), jnp.float32),
            pltpu.VMEM((2 * hidden, hidden), jnp.float32),
            pltpu.VMEM((wide, 2 * hidden), jnp.float32),
            pltpu.VMEM((held, width), jnp.float32),
            pltpu.VMEM((total, 2 * width), jnp.bfloat16),
            pltpu.VMEM((padded, 2 * width), jnp.bfloat16),
            pltpu.VMEM((SPAN, width), jnp.float32),
            pltpu.VMEM((SPAN, 2 * width), jnp.float32),
            pltpu.VMEM((2, SPAN, total), jnp.bfloat16),
            pltpu.VMEM((2, SPAN, 2 * width), jnp.float32),
            pltpu.VMEM((blocks, both, SPAN), jnp.bfloat16),
            pltpu.SemaphoreType.DMA((2, 2)),
            pltpu.SemaphoreType.DMA((blocks,)),
        ],
        4 << 30,
        16 << 20,
        36 << 20,
    )(info, count, places, partial, tallies, links, *sources, *rest)


def refit(total, rows):
    extra = total[rows - 16 : rows - 8] + total[rows - 8 : rows]
    high = extra.astype(jnp.bfloat16).astype(jnp.float32)
    return jnp.concatenate([high, extra - high], axis=0)


def pair_kernel(info, mine, theirs, out):
    total = mine[...].astype(jnp.float32) + theirs[...].astype(jnp.float32)
    out[...] = total.astype(jnp.bfloat16)

    @pl.when(info[0] == 1)
    def _():
        rows = total.shape[0]
        out[rows - 16 :, :] = refit(total, rows).astype(jnp.bfloat16)


def pair_sum(info, mine, theirs):
    return call(
        pair_kernel,
        "pair_sum",
        jax.ShapeDtypeStruct(mine.shape, jnp.bfloat16),
        [smem, vmem, vmem],
        vmem,
        [],
        mine.size,
        mine.size * 6,
        6 << 20,
    )(info, mine, theirs)


def spread_kernel(info, pieces, out):
    total = pieces[0].astype(jnp.float32)
    for k in range(1, pieces.shape[0]):
        total = total + pieces[k].astype(jnp.float32)
    rows = total.shape[0]
    fitted = jnp.concatenate([total[0 : rows - 16], refit(total, rows)], axis=0)
    result = jnp.where(info[1] == 1, fitted, total).astype(jnp.bfloat16)
    for k in range(pieces.shape[0]):
        out[k] = result


def spread_sum(info, pieces):
    return call(
        spread_kernel,
        "spread_sum",
        jax.ShapeDtypeStruct(pieces.shape, jnp.bfloat16),
        [smem, vmem],
        vmem,
        [],
        pieces.size,
        pieces.size * 4,
        6 << 20,
    )(info, pieces)


def update_kernel(
    info, fixes, corners, mine, theirs, biases, moment_one, moment_two, *refs
):
    groups = [refs[3 * k : 3 * k + 3] for k in range(3)]
    loss_out = refs[9]
    outs = [refs[10 + 4 * k : 14 + 4 * k] for k in range(3)]
    bias_out, first_out, second_out = refs[22:25]
    packed = refs[25]
    low = jnp.bfloat16
    half = mine.shape[0]
    core = info[0]
    packed[pl.ds(pl.multiple_of(core * half, 16), half), :] = mine[...]
    packed[pl.ds(pl.multiple_of((1 - core) * half, 16), half), :] = theirs[...]
    last = packed.shape[0]
    extra = packed[last - 16 :, :].astype(jnp.float32)
    extra = extra[0:8] + extra[8:16]
    counted = extra[6:7, 1:2]
    inverse = 1.0 / counted
    loss_out[...] = extra[6:7, 0:1] / counted
    scale = 0.5 * inverse * inverse

    row = 0
    for group in range(3):
        master, left_root, right_root = groups[group]
        new_master, copy, new_left, new_right = outs[group]
        turned = group == 2
        depth, hidden = (master.shape[0], master.shape[2]) if turned else master.shape[1:]
        deep = up(depth, LANES)

        def take(ref, k, middle):
            return ref[:, k, :] if middle else ref[k]

        def put(ref, k, middle, value):
            if middle:
                ref[:, k, :] = value
            else:
                ref[k] = value

        grads = []
        if turned:
            tall = up(depth, 16)
            for k in range(2):
                parts = []
                for column in range(0, hidden, LANES):
                    parts.append(packed[row : row + tall, :])
                    row += tall
                grads.append(grown(jnp.concatenate(parts, axis=1), deep, hidden))
        else:
            parts = []
            for column in range(0, hidden, LANES):
                parts.append(packed[row : row + 2 * depth, :])
                row += 2 * depth
            whole = jnp.concatenate(parts, axis=1)
            grads = [whole[k * depth : (k + 1) * depth] for k in range(2)]

        for k in range(2):
            grad = grads[k]
            for side, new, size, product, middle in (
                (0, new_left, depth, dot_cols(grad, grad), turned),
                (1, new_right, hidden, dot_rows(grad, grad), False),
            ):
                corner = corners[group * 4 + side * 2 + k]
                eye = lax.broadcasted_iota(jnp.int32, (size, size), 0) == (
                    lax.broadcasted_iota(jnp.int32, (size, size), 1)
                )
                value = jnp.where(eye, 0.5 * corner, 0.0) + scale * product[0:size, 0:size]
                put(new, k, middle, value)
            root = jnp.concatenate(
                halves(grown(take(left_root, k, turned), deep, deep)), axis=1
            )
            middle_high, middle_rest = halves(dot(root, jnp.concatenate([grad, grad], axis=0)))
            root_high, root_rest = halves(right_root[k])
            way = dot(
                jnp.concatenate([middle_high, middle_high, middle_rest], axis=1),
                jnp.concatenate([root_high, root_rest, root_high], axis=0),
            )[0:depth]
            put(new_master, k, turned, take(master, k, turned) - inverse * way)
        copy[...] = new_master[...].astype(low)

    size = biases.shape[0]
    grad = jnp.concatenate([extra[k : k + 1, :] for k in range(6)], axis=1)[:, 0:size]
    grad = grad / counted

    def line(ref):
        return ref[...].reshape(1, size)

    first = 0.9 * line(moment_one) + 0.1 * grad
    second = 0.95 * line(moment_two) + 0.05 * grad * grad
    old = line(biases)
    fresh = old - 0.1 * (
        (first / fixes[0]) / (jnp.sqrt(second / fixes[1]) + 1e-08) + 0.01 * old
    )
    for ref, value in ((bias_out, fresh), (first_out, first), (second_out, second)):
        ref[...] = value[0]


def run_update(info, fixes, corners, mine, theirs, vectors, groups):
    outs = [jax.ShapeDtypeStruct((1, 1), jnp.float32)]
    flat = []
    for master, left_root, right_root in groups:
        flat += [master, left_root, right_root]
        outs += [
            jax.ShapeDtypeStruct(master.shape, jnp.float32),
            jax.ShapeDtypeStruct(master.shape, jnp.bfloat16),
            jax.ShapeDtypeStruct(left_root.shape, jnp.float32),
            jax.ShapeDtypeStruct(right_root.shape, jnp.float32),
        ]
    outs += [jax.ShapeDtypeStruct(vectors[0].shape, jnp.float32)] * 3
    return call(
        update_kernel,
        "update",
        tuple(outs),
        [smem] * 3 + [vmem] * (5 + len(flat)),
        (vmem,) * len(outs),
        [pltpu.VMEM((2 * mine.shape[0], LANES), jnp.bfloat16)],
        1 << 30,
        10 << 20,
        16 << 20,
    )(info, fixes, corners, mine, theirs, *vectors, *flat)


def body(
    features,
    requests,
    adjacent_one,
    adjacent_two,
    adjacent_three,
    valid_one,
    valid_two,
    valid_three,
    labels,
    labelled,
    weights_in,
    weights_mid,
    weights_out,
    biases,
    moment_one,
    moment_two,
    step_count,
    left_in,
    left_mid,
    left_out,
    right_in,
    right_mid,
    right_out,
    invleft_in,
    invleft_mid,
    invleft_out,
    invright_in,
    invright_mid,
    invright_out,
    *,
    peers,
):
    width = features.shape[1]
    devices, per = requests.shape
    targets = adjacent_one.shape[0]
    padded = up(targets, SPAN)
    classes = weights_out.shape[2]
    hidden = weights_in.shape[2]
    core = lax.axis_index("core")
    own = lax.axis_index(PEERS)

    wanted = lax.all_to_all(requests, AXES, split_axis=0, concat_axis=0, tiled=True)
    names, places, near_two, near_three, count = reach(
        adjacent_three, valid_three, labelled, adjacent_two, valid_two, targets, per
    )
    wanted, count = lax.optimization_barrier((wanted.reshape(-1), count))
    early_cut, late_cut = cuts(per)

    def trade(found):
        pulled = lax.all_to_all(
            found.reshape(devices, -1, width), AXES, split_axis=0, concat_axis=0, tiled=True
        )
        return pulled.reshape(-1, width)

    early_source = trade(pick_rows(wanted, features, per, early_cut))
    found = pick_rows(wanted, features, per, late_cut)
    links = link_matrix(count, names, near_two, adjacent_two.shape[1], padded)
    names, places = names.reshape(-1), places.reshape(-1)
    early_tally, late_tally = tally(count, names, adjacent_one, valid_one, padded, devices, per)

    core_info = jnp.stack([core, ((core == 1) & (own == peers - 1)).astype(jnp.int32)])
    core_info = core_info.astype(jnp.int32)
    stepped = step_count.astype(jnp.float32)
    fixes = jnp.stack([1.0 - 0.9**stepped, 1.0 - 0.95**stepped])
    corners = jnp.concatenate(
        [
            item[:, 0, 0]
            for item in (left_in, right_in, left_mid, right_mid, right_out, left_out)
        ]
    )
    found, early_tally, info, fixes, corners = lax.optimization_barrier(
        (found, early_tally, core_info, fixes, corners)
    )
    late_source = trade(found)
    partial = early_sums(count, early_tally, early_source)

    rows = (2 * width + 2 * weights_mid.shape[1]) * (hidden // LANES)
    rows += up(classes, 16) * (2 * hidden // LANES)
    each = up(-(-(rows + 16) // (2 * peers)), 8)
    half = each * peers
    turned_out = weights_out.transpose(2, 0, 1)
    keep, send = run_step(
        info,
        count,
        places,
        partial,
        late_tally,
        links,
        (early_source, late_source),
        (
            near_two,
            near_three,
            labels,
            labelled,
            weights_in,
            weights_mid,
            turned_out,
            biases,
        ),
        half,
        classes,
        -(-targets // per) * per,
    )
    swap = [(0, 1), (1, 0)]
    theirs = lax.ppermute(send, "core", swap)
    summed = pair_sum(info, keep, theirs).reshape(peers, each, LANES)
    pieces = lax.all_to_all(summed, PEERS, split_axis=0, concat_axis=0, tiled=True)
    shared = spread_sum(info, pieces)
    mine = lax.all_to_all(shared, PEERS, split_axis=0, concat_axis=0, tiled=True)
    mine = mine.reshape(half, LANES)
    theirs = lax.ppermute(mine, "core", swap)

    outs = run_update(
        info,
        fixes,
        corners,
        mine,
        theirs,
        (biases, moment_one, moment_two),
        (
            (weights_in, invleft_in, invright_in),
            (weights_mid, invleft_mid, invright_mid),
            (turned_out, invright_out.transpose(1, 0, 2), invleft_out),
        ),
    )
    first, second, third = (outs[1 + 4 * k : 5 + 4 * k] for k in range(3))
    third = (
        third[0].transpose(1, 2, 0),
        third[1].transpose(1, 2, 0),
        third[3],
        third[2].transpose(1, 0, 2),
    )
    return (
        (outs[0].reshape(()),)
        + tuple(group[which] for which in range(4) for group in (first, second, third))
        + tuple(outs[13:16])
    )


def solution(mesh):
    chips, dev = mesh.shape["hst"] // 2, mesh.shape["dev"]
    fine = jax.sharding.Mesh(mesh.devices.reshape(chips, 2, dev), AXES)
    split = P(AXES, None)
    line = P(AXES)
    whole = P()
    mapped = jax.shard_map(
        functools.partial(body, peers=chips * dev),
        mesh=fine,
        in_specs=(split,) * 8 + (line,) * 2 + (whole,) * 19,
        out_specs=(whole,) * 16,
        check_vma=False,
    )

    def run(*args):
        with jax.sharding.use_abstract_mesh(fine.abstract_mesh):
            return mapped(*args)

    return run
```

```python
import functools

import jax
import jax.numpy as jnp
from jax import lax
from jax.experimental import pallas as pl
from jax.experimental.pallas import tpu as pltpu
from jax.sharding import PartitionSpec as P

LANES = 128
SPAN = 256
PARTS = 2
BIG = 52 << 20
AXES = ("chip", "core", "dev")
PEERS = ("chip", "dev")

smem = pl.BlockSpec(memory_space=pltpu.SMEM)
vmem = pl.BlockSpec(memory_space=pltpu.VMEM)
anywhere = pl.BlockSpec(memory_space=pltpu.HBM)


def up(value, unit):
    return -(-value // unit) * unit


def call(kernel, name, out_shape, in_specs, out_specs, scratch, cost, room):
    return pl.pallas_call(
        kernel,
        name=name,
        out_shape=out_shape,
        in_specs=in_specs,
        out_specs=out_specs,
        scratch_shapes=scratch,
        compiler_params=pltpu.CompilerParams(vmem_limit_bytes=room),
        cost_estimate=pl.CostEstimate(
            flops=0, transcendentals=0, bytes_accessed=int(cost * 3.6e6)
        ),
    )


def dot(left, right):
    return jnp.dot(left, right, preferred_element_type=jnp.float32)


def dot_rows(left, right):
    return lax.dot_general(
        left, right, (((0,), (0,)), ((), ())), preferred_element_type=jnp.float32
    )


def dot_cols(left, right):
    return lax.dot_general(
        left, right, (((1,), (1,)), ((), ())), preferred_element_type=jnp.float32
    )


def halves(value):
    high = value.astype(jnp.bfloat16)
    return high, (value - high.astype(jnp.float32)).astype(jnp.bfloat16)


def grown(value, rows, columns):
    short = columns - value.shape[1]
    if short:
        value = jnp.concatenate([value, jnp.zeros((value.shape[0], short), value.dtype)], axis=1)
    short = rows - value.shape[0]
    if short:
        value = jnp.concatenate([value, jnp.zeros((short, columns), value.dtype)], axis=0)
    return value


def clipped_counts(valid):
    return jnp.maximum(jnp.sum(valid.astype(jnp.float32), axis=1, keepdims=True), 1.0)


def copy_rows(names, block, source, target):
    unroll = 64
    base = block * SPAN

    def fetch(step, carry):
        for u in range(unroll):
            at = step * unroll + u
            target[pl.ds(at, 1), :] = source[pl.ds(names[base + at], 1), :]
        return carry

    lax.fori_loop(0, SPAN // unroll, fetch, 0)


def cuts(per):
    return (0, per // 2), (per // 2, per)


def pick_kernel(wanted, table, out, rows, *, first, last, per):
    part = last - first

    def body(device, carry):
        for u in range(part):
            name = wanted[device * per + (first + u)]
            rows[pl.ds(device * part + u, 1), :] = table[pl.ds(name, 1), :]
        return carry

    lax.fori_loop(0, out.shape[0] // part, body, 0)
    out[...] = rows[...].astype(jnp.bfloat16)


def pick_rows(wanted, table, per, ends):
    first, last = ends
    width = table.shape[1]
    count = wanted.shape[0] // per * (last - first)
    return call(
        functools.partial(pick_kernel, first=first, last=last, per=per),
        "pick_rows",
        jax.ShapeDtypeStruct((count, width), jnp.bfloat16),
        [smem, vmem],
        vmem,
        [pltpu.VMEM((count, width), jnp.float32)],
        4.6,
        20 << 20,
    )(wanted, table)


def stood(flat, unit):
    size = flat.shape[1]
    flat = jnp.concatenate(
        [flat, jnp.full((unit - flat.shape[0], size), -1, jnp.int32)], axis=0
    ).astype(jnp.float32)
    step = min(LANES, size)
    parts = [jnp.transpose(flat[:, k : k + step]) for k in range(0, size, step)]
    return jnp.concatenate(parts, axis=0).astype(jnp.int32)


def reach_kernel(
    adjacent_three,
    valid_three,
    labelled,
    adjacent_two,
    valid_two,
    names,
    places,
    near_two,
    near_three,
    count,
    left,
    right,
    *,
    rows_all,
    per,
):
    fan_three, seeds = adjacent_three.shape
    fan_two, targets = adjacent_two.shape
    low = jnp.bfloat16
    blocks = rows_all // LANES
    deep = names.shape[0]
    line = labelled[...].reshape(1, seeds)
    column = jnp.transpose(jnp.broadcast_to(line.astype(jnp.float32), (8, seeds)))[:, 0:1]
    near = stood(jnp.where(valid_three[...] > 0, adjacent_three[...], -1), near_three.shape[1])
    near_three[...] = near
    here = jnp.where(column > 0.0, near, -1)
    place = lax.broadcasted_iota(jnp.int32, (seeds, targets), 1)
    hit = jnp.zeros((seeds, targets), jnp.float32)
    for j in range(fan_three):
        hit = hit + jnp.where(here[:, j : j + 1] == place, 1.0, 0.0)
    need = jnp.max(hit, axis=0, keepdims=True) + jnp.concatenate(
        [line.astype(jnp.float32), jnp.zeros((1, targets - seeds), jnp.float32)], axis=1
    )

    level = lax.broadcasted_iota(jnp.int32, (deep, targets), 0)
    lane = lax.broadcasted_iota(jnp.int32, (targets, LANES), 1)
    flat = jnp.where(valid_two[...] > 0, adjacent_two[...], -1)
    tall = stood(flat, near_two.shape[1])
    near_two[...] = tall
    flat = jnp.where(need > 0.0, flat, -1)
    for j in range(fan_two):
        left[0:deep, j * targets : (j + 1) * targets] = jnp.where(
            lax.shift_right_arithmetic(flat[j : j + 1, :], 7) == level, 1.0, 0.0
        ).astype(low)
        right[j * targets : (j + 1) * targets, :] = jnp.where(
            (tall[:, j : j + 1] & (LANES - 1)) == lane, 1.0, 0.0
        ).astype(low)
    used = dot(left[0:deep, 0 : fan_two * targets], right[0 : fan_two * targets, :])
    own = [need[:, k : k + LANES] for k in range(0, targets, LANES)]
    own = jnp.concatenate(
        own + [jnp.zeros((deep - len(own), LANES), jnp.float32)], axis=0
    )
    flag = jnp.where(used + own > 0.0, 1.0, 0.0)

    square_row = lax.broadcasted_iota(jnp.int32, (LANES, LANES), 0)
    square_col = lax.broadcasted_iota(jnp.int32, (LANES, LANES), 1)
    full = jnp.concatenate([flag, jnp.zeros((LANES - deep, LANES), jnp.float32)], axis=0)
    flag_low = full.astype(low)
    running = dot(flag_low, jnp.where(square_row <= square_col, 1.0, 0.0).astype(low))
    totals = dot(flag_low, jnp.ones((LANES, LANES), low)).astype(low)
    before = dot(jnp.where(square_row > square_col, 1.0, 0.0).astype(low), totals)
    order = (before + running - full).astype(jnp.int32)
    number = jnp.sum(flag).astype(jnp.int32)
    count[0] = number
    count[1] = lax.div(number + (SPAN - 1), SPAN)

    high = jnp.where(full > 0.0, lax.shift_right_arithmetic(order, 7), -1)
    rest = jnp.transpose((order & (LANES - 1)).astype(jnp.float32)).astype(jnp.int32)
    step = lax.broadcasted_iota(jnp.int32, (deep, LANES), 0)
    inner = lax.broadcasted_iota(jnp.int32, (deep, LANES), 1).astype(jnp.float32)
    for b in range(blocks):
        match = jnp.where(high[b : b + 1, :] == step, 1.0, 0.0)
        lanes = slice(b * LANES, (b + 1) * LANES)
        left[0:deep, lanes] = (match * inner).astype(low)
        left[deep : 2 * deep, lanes] = (match * float(b)).astype(low)
        right[lanes, :] = jnp.where(rest[:, b : b + 1] == square_col, 1.0, 0.0).astype(low)
    found = dot(left[:, 0:rows_all], right[0:rows_all, :]).astype(jnp.int32)
    where = step * LANES + lax.broadcasted_iota(jnp.int32, (deep, LANES), 1)
    name = found[deep:] * LANES + found[0:deep]
    names[...] = jnp.where(where < number, name, rows_all)
    name = jnp.minimum(jnp.where(where < number, name, 0), rows_all - 1)
    owners = -(-rows_all // per)
    owner = lax.shift_right_logical(name, per.bit_length() - 1)
    slot = name & (per - 1)
    early, late = (last - first for first, last in cuts(per))
    places[...] = jnp.where(
        slot < early, owner * early + slot, owners * early + owner * late + slot - early
    )


def reach(adjacent_three, valid_three, labelled, adjacent_two, valid_two, rows_all, per):
    targets, fan = adjacent_two.shape
    seeds = labelled.shape[0]
    deep = up(up(rows_all, SPAN) // LANES, 16)
    area = max(fan * targets, rows_all)
    return call(
        functools.partial(reach_kernel, rows_all=rows_all, per=per),
        "reach",
        (
            jax.ShapeDtypeStruct((deep, LANES), jnp.int32),
            jax.ShapeDtypeStruct((deep, LANES), jnp.int32),
            jax.ShapeDtypeStruct((targets, 16), jnp.int32),
            jax.ShapeDtypeStruct((seeds, 8), jnp.int32),
            jax.ShapeDtypeStruct((2,), jnp.int32),
        ),
        [vmem] * 5,
        (vmem,) * 4 + (smem,),
        [
            pltpu.VMEM((2 * deep, area), jnp.bfloat16),
            pltpu.VMEM((area, LANES), jnp.bfloat16),
        ],
        3.0,
        8 << 20,
    )(adjacent_three.T, valid_three.T, labelled, adjacent_two.T, valid_two.T)


def tally_kernel(
    count, names, adjacent, valid, out, table, rows, spread, marked, buffer, sems, *, per, which
):
    low = jnp.bfloat16
    fan, targets = adjacent.shape
    unit = spread.shape[0]
    groups = SPAN // unit
    used = count[1]
    high_all = out.shape[1] // SPAN
    first, last = cuts(per)[which]
    size = last - first

    slot = adjacent[...]
    owner = lax.shift_right_logical(slot, per.bit_length() - 1)
    inner = slot & (per - 1)
    here = (valid[...] > 0) & (inner >= first) & (inner < last)
    slot = jnp.where(here, owner * size + inner - first, -1)
    slot = jnp.concatenate([slot, jnp.full((unit - fan, targets), -1, jnp.int32)], axis=0)
    slot = slot.astype(jnp.float32)
    for b in range(0, targets, LANES):
        table[b : b + LANES, :] = jnp.transpose(slot[:, b : b + LANES]).astype(jnp.int32)
    table[targets:, :] = jnp.full((table.shape[0] - targets, unit), -1, jnp.int32)

    across = lax.broadcasted_iota(jnp.int32, (unit, SPAN), 1)
    down = lax.broadcasted_iota(jnp.int32, (unit, SPAN), 0)
    spread[...] = jnp.where(lax.div(across, unit) == down, 1.0, 0.0).astype(low)
    lane = across.astype(jnp.float32).astype(low)
    one = jnp.ones((unit, SPAN), low)
    zero = jnp.zeros((unit, SPAN), low)

    def copies(block, slot):
        where = pl.ds(pl.multiple_of(block * SPAN, SPAN), SPAN)
        return pltpu.make_async_copy(buffer.at[slot], out.at[where, :], sems.at[slot])

    def body(block, carry):
        slot = lax.rem(block, 2)

        @pl.when(block >= 2)
        def _():
            copies(block - 2, slot).wait()

        copy_rows(names, block, table, rows)
        high = lax.shift_right_arithmetic(rows[...], 8).astype(jnp.float32).astype(low)
        own = lax.rem(lax.broadcasted_iota(jnp.int32, (SPAN, SPAN), 0), unit) == lax.rem(
            lax.broadcasted_iota(jnp.int32, (SPAN, SPAN), 1), unit
        )
        marked[...] = jnp.where(own, dot(high, spread[...]), -1.0).astype(low)

        def single(g):
            first = pl.multiple_of(g * unit, unit)
            rest = (rows[pl.ds(first, unit), :] & (SPAN - 1)).astype(jnp.float32)
            columns = [
                jnp.where(
                    jnp.broadcast_to(rest[:, j : j + 1], (unit, SPAN)).astype(low) == lane,
                    one,
                    zero,
                )
                for j in range(unit)
            ]
            mark = marked[pl.ds(first, unit), :]
            marks = [
                jnp.where(mark == jnp.full((unit, SPAN), float(q), low), one, zero)
                for q in range(high_all)
            ]
            result = dot(
                jnp.concatenate(marks, axis=0), jnp.concatenate(columns, axis=0)
            ).astype(low)
            for q in range(high_all):
                buffer[slot, pl.ds(first, unit), q * SPAN : (q + 1) * SPAN] = result[
                    q * unit : (q + 1) * unit
                ]

        def group(step, inner):
            for u in range(4):
                single(step * 4 + u)
            return inner

        lax.fori_loop(0, groups // 4, group, 0)
        copies(block, slot).start()
        return carry

    lax.fori_loop(0, used, body, 0)

    @pl.when(used >= 2)
    def _():
        copies(used - 2, lax.rem(used - 2, 2)).wait()

    @pl.when(used >= 1)
    def _():
        copies(used - 1, lax.rem(used - 1, 2)).wait()


def tally(count, names, adjacent, valid, padded, devices, per, which):
    targets = adjacent.shape[0]
    unit = 16
    first, last = cuts(per)[which]
    wide = devices * (last - first)
    return call(
        functools.partial(tally_kernel, per=per, which=which),
        "tally",
        jax.ShapeDtypeStruct((padded, wide), jnp.bfloat16),
        [smem, smem, vmem, vmem],
        anywhere,
        [
            pltpu.VMEM((targets + 8, unit), jnp.int32),
            pltpu.VMEM((SPAN, unit), jnp.int32),
            pltpu.VMEM((unit, SPAN), jnp.bfloat16),
            pltpu.VMEM((SPAN, SPAN), jnp.bfloat16),
            pltpu.VMEM((2, SPAN, wide), jnp.bfloat16),
            pltpu.SemaphoreType.DMA((2,)),
        ],
        12.0,
        BIG,
    )(count, names, adjacent.T, valid.T)


def early_kernel(count, tallies, source, out, table, buffer, result, sems, out_sems):
    width = source.shape[1]
    used = count[1]
    table[:, 0:width] = source[...]
    table[:, width:] = jnp.ones((source.shape[0], width), jnp.bfloat16)

    def rows(block):
        return pl.ds(pl.multiple_of(block * SPAN, SPAN), SPAN)

    def load(block, slot):
        return pltpu.make_async_copy(tallies.at[rows(block), :], buffer.at[slot], sems.at[slot])

    def save(block, slot):
        return pltpu.make_async_copy(result.at[slot], out.at[rows(block), :], out_sems.at[slot])

    @pl.when(used > 0)
    def _():
        load(0, 0).start()

    def body(block, carry):
        slot = lax.rem(block, 2)
        load(block, slot).wait()

        @pl.when(block + 1 < used)
        def _():
            load(block + 1, 1 - slot).start()

        @pl.when(block >= 2)
        def _():
            save(block - 2, slot).wait()

        result[slot] = dot(buffer[slot], table[...])
        save(block, slot).start()
        return carry

    lax.fori_loop(0, used, body, 0)

    @pl.when(used >= 2)
    def _():
        save(used - 2, lax.rem(used - 2, 2)).wait()

    @pl.when(used >= 1)
    def _():
        save(used - 1, lax.rem(used - 1, 2)).wait()


def early_sums(count, tallies, source):
    padded, total = tallies.shape
    width = source.shape[1]
    return call(
        early_kernel,
        "early_sums",
        jax.ShapeDtypeStruct((3 * padded, 2 * width), jnp.float32),
        [smem, anywhere, vmem],
        anywhere,
        [
            pltpu.VMEM((total, 2 * width), jnp.bfloat16),
            pltpu.VMEM((2, SPAN, total), jnp.bfloat16),
            pltpu.VMEM((2, SPAN, 2 * width), jnp.float32),
            pltpu.SemaphoreType.DMA((2,)),
            pltpu.SemaphoreType.DMA((2,)),
        ],
        9.0,
        BIG,
    )(count, tallies, source)


def link_kernel(count, names, near, out, buffer, sems, *, fan):
    targets = near.shape[0]
    tile = 32
    used = count[1]

    def save(block, slot):
        return pltpu.make_async_copy(buffer.at[slot], out.at[block], sems.at[slot])

    def columns(block, carry):
        slot = lax.rem(block, 2)

        @pl.when(block >= 2)
        def _():
            save(block - 2, slot).wait()

        lines = [
            jnp.broadcast_to(names[pl.ds(block * (SPAN // LANES) + part, 1), :], (tile, LANES))
            for part in range(SPAN // LANES)
        ]

        def rows(step, inner):
            first = pl.multiple_of(step * tile, tile)
            here = near[pl.ds(first, tile), :]
            own = first + lax.broadcasted_iota(jnp.int32, (tile, LANES), 0)
            numbers = [jnp.zeros((tile, LANES), jnp.float32) for _ in lines]
            for j in range(fan):
                spread = jnp.broadcast_to(here[:, j : j + 1], (tile, LANES))
                numbers = [
                    number + jnp.where(spread == line, 1.0, 0.0)
                    for number, line in zip(numbers, lines)
                ]
            for part, (number, line) in enumerate(zip(numbers, lines)):
                lanes = pl.ds(part * LANES, LANES)
                buffer[slot, pl.ds(first, tile), lanes] = number.astype(jnp.bfloat16)
                buffer[slot, pl.ds(targets + first, tile), lanes] = jnp.where(
                    own == line, 1.0, 0.0
                ).astype(jnp.bfloat16)
            return inner

        lax.fori_loop(0, targets // tile, rows, 0)
        save(block, slot).start()
        return carry

    lax.fori_loop(0, used, columns, 0)

    @pl.when(used >= 2)
    def _():
        save(used - 2, lax.rem(used - 2, 2)).wait()

    @pl.when(used >= 1)
    def _():
        save(used - 1, lax.rem(used - 1, 2)).wait()


def link_matrix(count, names, near, fan, padded):
    blocks = padded // SPAN
    targets = near.shape[0]
    return call(
        functools.partial(link_kernel, fan=fan),
        "link_matrix",
        jax.ShapeDtypeStruct((2 * blocks, 2 * targets, SPAN), jnp.bfloat16),
        [smem, vmem, vmem],
        anywhere,
        [
            pltpu.VMEM((2, 2 * targets, SPAN), jnp.bfloat16),
            pltpu.SemaphoreType.DMA((2,)),
        ],
        5.0,
        BIG,
    )(count, names, near)


def step_kernel(
    info,
    count,
    places,
    partial,
    tallies,
    links,
    *refs,
    classes,
):
    sources = refs[:PARTS]
    step_body(
        info, count, places, partial, tallies, links, sources, *refs[PARTS:],
        classes=classes,
    )


def step_body(
    info,
    count,
    places,
    partial,
    tallies,
    links,
    sources,
    near_two,
    near_three,
    labels,
    labelled,
    weights_in,
    weights_mid,
    weights_out,
    biases_line,
    keep,
    send,
    slopes,
    packed,
    sums,
    weight_sums,
    mid_sums,
    out_sums,
    own_table,
    late_table,
    mixin,
    own_rows,
    joined,
    late,
    early,
    link,
    sems,
    link_sems,
    *,
    classes,
):
    blocks, both, _ = links.shape
    targets = both // 2
    hidden = weights_in.shape[2]
    seeds = labels.shape[0]
    biases = biases_line[...].reshape(1, biases_line.shape[0])
    label, marked = [
        jnp.transpose(
            jnp.broadcast_to(item[...].reshape(1, seeds).astype(jnp.float32), (8, seeds))
        )[:, 0:1]
        for item in (labels, labelled)
    ]
    wide = up(classes, LANES)
    core = info[0]
    used = count[1]
    low = jnp.bfloat16
    width = sources[0].shape[1]

    def load(block, slot):
        rows = pl.ds(pl.multiple_of(block * SPAN, SPAN), SPAN)
        return (
            pltpu.make_async_copy(tallies.at[rows, :], late.at[slot], sems.at[slot, 0]),
            pltpu.make_async_copy(partial.at[rows, :], early.at[slot], sems.at[slot, 1]),
        )

    def load_link(block):
        return pltpu.make_async_copy(links.at[block], link.at[block], link_sems.at[block])

    @pl.when(used > 0)
    def _():
        for copy in load(0, 0):
            copy.start()

    def start_link(block, carry):
        load_link(block).start()
        return carry

    lax.fori_loop(0, used, start_link, 0)
    late_table[:, 0:width] = sources[-1][...]
    late_table[:, width:] = jnp.ones((late_table.shape[0], width), low)
    filled = 0
    for source in sources:
        held = own_table.shape[0] * source.shape[0] // sum(item.shape[0] for item in sources)
        own_table[filled : filled + held, :] = source[0:held, :].astype(jnp.float32)
        filled += held

    w_in = weights_in[...].astype(low).reshape(2 * weights_in.shape[1], hidden)
    bias_in = biases[:, 0:hidden]
    bias_mid = biases[:, hidden : 2 * hidden]
    bias_out = jnp.concatenate(
        [
            biases[:, 2 * hidden : 2 * hidden + classes],
            jnp.full((1, wide - classes), -1e30, jnp.float32),
        ],
        axis=1,
    )

    sums[...] = jnp.zeros_like(sums)

    def forward(block, carry):
        rows = pl.ds(pl.multiple_of(block * SPAN, SPAN), SPAN)
        slot = lax.rem(block, 2)
        for copy in load(block, slot):
            copy.wait()
        load_link(block).wait()

        @pl.when(block + 1 < used)
        def _():
            for copy in load(block + 1, 1 - slot):
                copy.start()

        copy_rows(places, block, own_table, own_rows)
        joined[...] = dot(late[slot], late_table[...]) + early[slot]
        mixin[rows, 0:width] = own_rows[...].astype(low)
        mixin[rows, width:] = (
            joined[:, 0:width] / jnp.maximum(joined[:, width:], 1.0)
        ).astype(low)
        z = dot(mixin[rows, :], w_in) + bias_in
        s = 1.0 / (1.0 + jnp.exp(-z))
        slopes[rows, :] = s * (1.0 + z * (1.0 - s))
        sums[...] += dot(link[block], (z * s).astype(low))
        return carry

    lax.fori_loop(0, used, forward, 0)
    total = sums[...]
    counts_two = clipped_counts(near_two[...] >= 0)
    mixed_one = (total[0:targets] / counts_two).astype(low)
    self_one = total[targets:].astype(low)
    w_mid = weights_mid[...].astype(low)
    both_one = jnp.concatenate([self_one, mixed_one], axis=1)
    z = dot(both_one, w_mid.reshape(2 * hidden, hidden)) + bias_mid
    s = 1.0 / (1.0 + jnp.exp(-z))
    slope_mid = s * (1.0 + z * (1.0 - s))
    hidden_two = (z * s).astype(low)

    here = near_three[...]
    place = lax.broadcasted_iota(jnp.int32, (seeds, targets), 1)
    number = jnp.zeros((seeds, targets), jnp.float32)
    for j in range(here.shape[1]):
        number = number + jnp.where(here[:, j : j + 1] == place, 1.0, 0.0)
    number = number.astype(low)
    counts_three = clipped_counts(here >= 0)
    mixed_two = (dot(number, hidden_two) / counts_three).astype(low)
    self_two = hidden_two[0:seeds]
    w_out = [
        jnp.concatenate(
            [weights_out[:, k, :], jnp.zeros((wide - classes, hidden), jnp.float32)], axis=0
        ).astype(low)
        for k in range(2)
    ]
    both_two = jnp.concatenate([self_two, mixed_two], axis=1)
    logits = dot_cols(both_two, jnp.concatenate(w_out, axis=1)) + bias_out
    top = jnp.max(logits, axis=1, keepdims=True)
    log_total = top + jnp.log(jnp.sum(jnp.exp(logits - top), axis=1, keepdims=True))
    onehot = jnp.where(
        label.astype(jnp.int32) == lax.broadcasted_iota(jnp.int32, (seeds, wide), 1), 1.0, 0.0
    )
    picked = jnp.sum(jnp.where(onehot > 0.0, logits, 0.0), axis=1, keepdims=True)
    loss = jnp.sum(marked * (log_total - picked), axis=0, keepdims=True)
    counted = jnp.sum(marked, axis=0, keepdims=True)
    grad_out = (marked * (jnp.exp(logits - log_total) - onehot)).astype(low)

    out_sums[...] = dot_rows(grad_out, both_two)
    bias_grad_out = jnp.sum(grad_out.astype(jnp.float32), axis=0, keepdims=True)
    to_self = dot(grad_out, w_out[0])
    spread = (dot(grad_out, w_out[1]) / counts_three).astype(low)
    sums[0:targets, :] = dot_rows(number, spread)
    sums[0:seeds, :] += to_self
    grad_mid = (sums[0:targets, :] * slope_mid).astype(low)

    mid_sums[...] = dot_rows(both_one, grad_mid)
    bias_grad_mid = jnp.sum(grad_mid.astype(jnp.float32), axis=0, keepdims=True)
    down = jnp.concatenate(
        [dot_cols(grad_mid, w_mid[1]) / counts_two, dot_cols(grad_mid, w_mid[0])], axis=0
    )
    spread = down.astype(low)

    weight_sums[...] = jnp.zeros_like(weight_sums)

    def backward(block, bias):
        rows = pl.ds(pl.multiple_of(block * SPAN, SPAN), SPAN)
        grad = (dot_rows(link[block], spread) * slopes[rows, :]).astype(low)
        weight_sums[...] += dot_rows(mixin[rows, :], grad)
        return bias + jnp.sum(grad.astype(jnp.float32), axis=0, keepdims=True)

    bias_grad_in = lax.fori_loop(0, used, backward, jnp.zeros((1, hidden), jnp.float32))

    row = 0
    for part in (weight_sums, mid_sums):
        for column in range(0, hidden, LANES):
            packed[row : row + part.shape[0], :] = part[:, column : column + LANES]
            row += part.shape[0]
    tall = up(classes, 16)
    for column in range(0, 2 * hidden, LANES):
        packed[row : row + tall, :] = out_sums[0:tall, column : column + LANES]
        row += tall
    packed[row:, :] = jnp.zeros((packed.shape[0] - row, LANES), jnp.float32)
    lane = lax.broadcasted_iota(jnp.int32, (1, LANES), 1)
    scalars = jnp.where(lane == 0, loss, 0.0) + jnp.where(lane == 1, counted, 0.0)
    extra = [
        item[:, column : column + LANES]
        for item in (bias_grad_in, bias_grad_mid, bias_grad_out)
        for column in range(0, hidden, LANES)
    ] + [scalars, jnp.zeros((1, LANES), jnp.float32)]
    extra = jnp.concatenate(extra, axis=0)
    high = extra.astype(low).astype(jnp.float32)
    packed[packed.shape[0] - 16 :, :] = jnp.concatenate([high, extra - high], axis=0)
    half = keep.shape[0]
    keep[...] = packed[pl.ds(pl.multiple_of(core * half, 16), half), :].astype(low)
    send[...] = packed[pl.ds(pl.multiple_of((1 - core) * half, 16), half), :].astype(low)


def run_step(info, count, places, partial, tallies, links, sources, rest, half, classes, held):
    padded = tallies.shape[0]
    blocks, both = padded // SPAN, links.shape[1]
    total, width = sources[-1].shape
    hidden = rest[4].shape[2]
    wide = up(classes, LANES)
    return call(
        functools.partial(step_kernel, classes=classes),
        "step",
        (jax.ShapeDtypeStruct((half, LANES), jnp.bfloat16),) * 2,
        [smem] * 3 + [anywhere] * 3 + [vmem] * (PARTS + 8),
        (vmem, vmem),
        [
            pltpu.VMEM((padded, hidden), jnp.float32),
            pltpu.VMEM((2 * half, LANES), jnp.float32),
            pltpu.VMEM((both, hidden), jnp.float32),
            pltpu.VMEM((2 * width, hidden), jnp.float32),
            pltpu.VMEM((2 * hidden, hidden), jnp.float32),
            pltpu.VMEM((wide, 2 * hidden), jnp.float32),
            pltpu.VMEM((held, width), jnp.float32),
            pltpu.VMEM((total, 2 * width), jnp.bfloat16),
            pltpu.VMEM((padded, 2 * width), jnp.bfloat16),
            pltpu.VMEM((SPAN, width), jnp.float32),
            pltpu.VMEM((SPAN, 2 * width), jnp.float32),
            pltpu.VMEM((2, SPAN, total), jnp.bfloat16),
            pltpu.VMEM((2, SPAN, 2 * width), jnp.float32),
            pltpu.VMEM((blocks, both, SPAN), jnp.bfloat16),
            pltpu.SemaphoreType.DMA((2, 2)),
            pltpu.SemaphoreType.DMA((blocks,)),
        ],
        14.0,
        BIG,
    )(info, count, places, partial, tallies, links, *sources, *rest)


def refit(total, rows):
    extra = total[rows - 16 : rows - 8] + total[rows - 8 : rows]
    high = extra.astype(jnp.bfloat16).astype(jnp.float32)
    return jnp.concatenate([high, extra - high], axis=0)


def pair_kernel(info, mine, theirs, out):
    total = mine[...].astype(jnp.float32) + theirs[...].astype(jnp.float32)
    out[...] = total.astype(jnp.bfloat16)

    @pl.when(info[0] == 1)
    def _():
        rows = total.shape[0]
        out[rows - 16 :, :] = refit(total, rows).astype(jnp.bfloat16)


def pair_sum(info, mine, theirs):
    return call(
        pair_kernel,
        "pair_sum",
        jax.ShapeDtypeStruct(mine.shape, jnp.bfloat16),
        [smem, vmem, vmem],
        vmem,
        [],
        0.6,
        6 << 20,
    )(info, mine, theirs)


def spread_kernel(info, pieces, out):
    total = pieces[0].astype(jnp.float32)
    for k in range(1, pieces.shape[0]):
        total = total + pieces[k].astype(jnp.float32)
    rows = total.shape[0]
    fitted = jnp.concatenate([total[0 : rows - 16], refit(total, rows)], axis=0)
    result = jnp.where(info[1] == 1, fitted, total).astype(jnp.bfloat16)
    for k in range(pieces.shape[0]):
        out[k] = result


def spread_sum(info, pieces):
    return call(
        spread_kernel,
        "spread_sum",
        jax.ShapeDtypeStruct(pieces.shape, jnp.bfloat16),
        [smem, vmem],
        vmem,
        [],
        0.6,
        6 << 20,
    )(info, pieces)


def update_kernel(
    info, fixes, corners, mine, theirs, biases, moment_one, moment_two, *refs
):
    groups = [refs[3 * k : 3 * k + 3] for k in range(3)]
    loss_out = refs[9]
    outs = [refs[10 + 4 * k : 14 + 4 * k] for k in range(3)]
    bias_out, first_out, second_out = refs[22:25]
    packed = refs[25]
    low = jnp.bfloat16
    half = mine.shape[0]
    core = info[0]
    packed[pl.ds(pl.multiple_of(core * half, 16), half), :] = mine[...]
    packed[pl.ds(pl.multiple_of((1 - core) * half, 16), half), :] = theirs[...]
    last = packed.shape[0]
    extra = packed[last - 16 :, :].astype(jnp.float32)
    extra = extra[0:8] + extra[8:16]
    counted = extra[6:7, 1:2]
    inverse = 1.0 / counted
    loss_out[...] = extra[6:7, 0:1] / counted
    scale = 0.5 * inverse * inverse

    row = 0
    for group in range(3):
        master, left_root, right_root = groups[group]
        new_master, copy, new_left, new_right = outs[group]
        turned = group == 2
        depth, hidden = (master.shape[0], master.shape[2]) if turned else master.shape[1:]
        deep = up(depth, LANES)

        def take(ref, k, middle):
            return ref[:, k, :] if middle else ref[k]

        def put(ref, k, middle, value):
            if middle:
                ref[:, k, :] = value
            else:
                ref[k] = value

        grads = []
        if turned:
            tall = up(depth, 16)
            for k in range(2):
                parts = []
                for column in range(0, hidden, LANES):
                    parts.append(packed[row : row + tall, :])
                    row += tall
                grads.append(grown(jnp.concatenate(parts, axis=1), deep, hidden))
        else:
            parts = []
            for column in range(0, hidden, LANES):
                parts.append(packed[row : row + 2 * depth, :])
                row += 2 * depth
            whole = jnp.concatenate(parts, axis=1)
            grads = [whole[k * depth : (k + 1) * depth] for k in range(2)]

        for k in range(2):
            grad = grads[k]
            for side, new, size, product, middle in (
                (0, new_left, depth, dot_cols(grad, grad), turned),
                (1, new_right, hidden, dot_rows(grad, grad), False),
            ):
                corner = corners[group * 4 + side * 2 + k]
                eye = lax.broadcasted_iota(jnp.int32, (size, size), 0) == (
                    lax.broadcasted_iota(jnp.int32, (size, size), 1)
                )
                value = jnp.where(eye, 0.5 * corner, 0.0) + scale * product[0:size, 0:size]
                put(new, k, middle, value)
            root = jnp.concatenate(
                halves(grown(take(left_root, k, turned), deep, deep)), axis=1
            )
            middle_high, middle_rest = halves(dot(root, jnp.concatenate([grad, grad], axis=0)))
            root_high, root_rest = halves(right_root[k])
            way = dot(
                jnp.concatenate([middle_high, middle_high, middle_rest], axis=1),
                jnp.concatenate([root_high, root_rest, root_high], axis=0),
            )[0:depth]
            put(new_master, k, turned, take(master, k, turned) - inverse * way)
        copy[...] = new_master[...].astype(low)

    size = biases.shape[0]
    grad = jnp.concatenate([extra[k : k + 1, :] for k in range(6)], axis=1)[:, 0:size]
    grad = grad / counted

    def line(ref):
        return ref[...].reshape(1, size)

    first = 0.9 * line(moment_one) + 0.1 * grad
    second = 0.95 * line(moment_two) + 0.05 * grad * grad
    old = line(biases)
    fresh = old - 0.1 * (
        (first / fixes[0]) / (jnp.sqrt(second / fixes[1]) + 1e-08) + 0.01 * old
    )
    for ref, value in ((bias_out, fresh), (first_out, first), (second_out, second)):
        ref[...] = value[0]


def run_update(info, fixes, corners, mine, theirs, vectors, groups):
    outs = [jax.ShapeDtypeStruct((1, 1), jnp.float32)]
    flat = []
    for master, left_root, right_root in groups:
        flat += [master, left_root, right_root]
        outs += [
            jax.ShapeDtypeStruct(master.shape, jnp.float32),
            jax.ShapeDtypeStruct(master.shape, jnp.bfloat16),
            jax.ShapeDtypeStruct(left_root.shape, jnp.float32),
            jax.ShapeDtypeStruct(right_root.shape, jnp.float32),
        ]
    outs += [jax.ShapeDtypeStruct(vectors[0].shape, jnp.float32)] * 3
    return call(
        update_kernel,
        "update",
        tuple(outs),
        [smem] * 3 + [vmem] * (5 + len(flat)),
        (vmem,) * len(outs),
        [pltpu.VMEM((2 * mine.shape[0], LANES), jnp.bfloat16)],
        4.0,
        16 << 20,
    )(info, fixes, corners, mine, theirs, *vectors, *flat)


def body(
    features,
    requests,
    adjacent_one,
    adjacent_two,
    adjacent_three,
    valid_one,
    valid_two,
    valid_three,
    labels,
    labelled,
    weights_in,
    weights_mid,
    weights_out,
    biases,
    moment_one,
    moment_two,
    step_count,
    left_in,
    left_mid,
    left_out,
    right_in,
    right_mid,
    right_out,
    invleft_in,
    invleft_mid,
    invleft_out,
    invright_in,
    invright_mid,
    invright_out,
    *,
    peers,
):
    width = features.shape[1]
    devices, per = requests.shape
    targets = adjacent_one.shape[0]
    padded = up(targets, SPAN)
    classes = weights_out.shape[2]
    hidden = weights_in.shape[2]
    core = lax.axis_index("core")
    own = lax.axis_index(PEERS)

    wanted = lax.all_to_all(requests, AXES, split_axis=0, concat_axis=0, tiled=True)
    names, places, near_two, near_three, count = reach(
        adjacent_three, valid_three, labelled, adjacent_two, valid_two, targets, per
    )
    wanted, count = lax.optimization_barrier((wanted.reshape(-1), count))
    early_cut, late_cut = cuts(per)

    def trade(found):
        pulled = lax.all_to_all(
            found.reshape(devices, -1, width), AXES, split_axis=0, concat_axis=0, tiled=True
        )
        return pulled.reshape(-1, width)

    early_source = trade(pick_rows(wanted, features, per, early_cut))
    found = pick_rows(wanted, features, per, late_cut)
    links = link_matrix(count, names, near_two, adjacent_two.shape[1], padded)
    names, places = names.reshape(-1), places.reshape(-1)
    early_tally, late_tally = (
        tally(count, names, adjacent_one, valid_one, padded, devices, per, which)
        for which in range(PARTS)
    )

    core_info = jnp.stack([core, ((core == 1) & (own == peers - 1)).astype(jnp.int32)])
    core_info = core_info.astype(jnp.int32)
    stepped = step_count.astype(jnp.float32)
    fixes = jnp.stack([1.0 - 0.9**stepped, 1.0 - 0.95**stepped])
    corners = jnp.concatenate(
        [
            item[:, 0, 0]
            for item in (left_in, right_in, left_mid, right_mid, right_out, left_out)
        ]
    )
    found, early_tally, info, fixes, corners = lax.optimization_barrier(
        (found, early_tally, core_info, fixes, corners)
    )
    late_source = trade(found)
    partial = early_sums(count, early_tally, early_source)

    rows = (2 * width + 2 * weights_mid.shape[1]) * (hidden // LANES)
    rows += up(classes, 16) * (2 * hidden // LANES)
    each = up(-(-(rows + 16) // (2 * peers)), 8)
    half = each * peers
    turned_out = weights_out.transpose(2, 0, 1)
    keep, send = run_step(
        info,
        count,
        places,
        partial,
        late_tally,
        links,
        (early_source, late_source),
        (
            near_two,
            near_three,
            labels,
            labelled,
            weights_in,
            weights_mid,
            turned_out,
            biases,
        ),
        half,
        classes,
        -(-targets // per) * per,
    )
    swap = [(0, 1), (1, 0)]
    theirs = lax.ppermute(send, "core", swap)
    summed = pair_sum(info, keep, theirs).reshape(peers, each, LANES)
    pieces = lax.all_to_all(summed, PEERS, split_axis=0, concat_axis=0, tiled=True)
    shared = spread_sum(info, pieces)
    mine = lax.all_to_all(shared, PEERS, split_axis=0, concat_axis=0, tiled=True)
    mine = mine.reshape(half, LANES)
    theirs = lax.ppermute(mine, "core", swap)

    outs = run_update(
        info,
        fixes,
        corners,
        mine,
        theirs,
        (biases, moment_one, moment_two),
        (
            (weights_in, invleft_in, invright_in),
            (weights_mid, invleft_mid, invright_mid),
            (turned_out, invright_out.transpose(1, 0, 2), invleft_out),
        ),
    )
    first, second, third = (outs[1 + 4 * k : 5 + 4 * k] for k in range(3))
    third = (
        third[0].transpose(1, 2, 0),
        third[1].transpose(1, 2, 0),
        third[3],
        third[2].transpose(1, 0, 2),
    )
    return (
        (outs[0].reshape(()),)
        + tuple(group[which] for which in range(4) for group in (first, second, third))
        + tuple(outs[13:16])
    )


def solution(mesh):
    chips, dev = mesh.shape["hst"] // 2, mesh.shape["dev"]
    fine = jax.sharding.Mesh(mesh.devices.reshape(chips, 2, dev), AXES)
    split = P(AXES, None)
    line = P(AXES)
    whole = P()
    mapped = jax.shard_map(
        functools.partial(body, peers=chips * dev),
        mesh=fine,
        in_specs=(split,) * 8 + (line,) * 2 + (whole,) * 19,
        out_specs=(whole,) * 16,
        check_vma=False,
    )

    def run(*args):
        with jax.sharding.use_abstract_mesh(fine.abstract_mesh):
            return mapped(*args)

    return run
```

```python
import functools

import jax
import jax.numpy as jnp
from jax import lax
from jax.experimental import pallas as pl
from jax.experimental.pallas import tpu as pltpu
from jax.sharding import PartitionSpec as P

LANES = 128
SPAN = 256
PARTS = 2
COUNTS = jnp.float8_e4m3fn
BIG = 52 << 20
AXES = ("chip", "core", "dev")
PEERS = ("chip", "dev")

smem = pl.BlockSpec(memory_space=pltpu.SMEM)
vmem = pl.BlockSpec(memory_space=pltpu.VMEM)
anywhere = pl.BlockSpec(memory_space=pltpu.HBM)


def up(value, unit):
    return -(-value // unit) * unit


def call(kernel, name, out_shape, in_specs, out_specs, scratch, cost, room):
    return pl.pallas_call(
        kernel,
        name=name,
        out_shape=out_shape,
        in_specs=in_specs,
        out_specs=out_specs,
        scratch_shapes=scratch,
        compiler_params=pltpu.CompilerParams(vmem_limit_bytes=room),
        cost_estimate=pl.CostEstimate(
            flops=0, transcendentals=0, bytes_accessed=int(cost * 3.6e6)
        ),
    )


def dot(left, right):
    return jnp.dot(left, right, preferred_element_type=jnp.float32)


def dot_rows(left, right):
    return lax.dot_general(
        left, right, (((0,), (0,)), ((), ())), preferred_element_type=jnp.float32
    )


def dot_cols(left, right):
    return lax.dot_general(
        left, right, (((1,), (1,)), ((), ())), preferred_element_type=jnp.float32
    )


def halves(value):
    high = value.astype(jnp.bfloat16)
    return high, (value - high.astype(jnp.float32)).astype(jnp.bfloat16)


def grown(value, rows, columns):
    short = columns - value.shape[1]
    if short:
        value = jnp.concatenate([value, jnp.zeros((value.shape[0], short), value.dtype)], axis=1)
    short = rows - value.shape[0]
    if short:
        value = jnp.concatenate([value, jnp.zeros((short, columns), value.dtype)], axis=0)
    return value


def clipped_counts(valid):
    return jnp.maximum(jnp.sum(valid.astype(jnp.float32), axis=1, keepdims=True), 1.0)


def copy_rows(names, base, size, source, target):
    for u in range(size):
        target[u : u + 1, :] = source[pl.ds(names[base + u], 1), :]


def cuts(per):
    return (0, per // 2), (per // 2, per)


def pick_kernel(wanted, table, out, rows, *, first, last, per):
    part = last - first

    def body(device, carry):
        for u in range(part):
            name = wanted[device * per + (first + u)]
            rows[pl.ds(device * part + u, 1), :] = table[pl.ds(name, 1), :]
        return carry

    lax.fori_loop(0, out.shape[0] // part, body, 0)
    out[...] = rows[...].astype(jnp.bfloat16)


def pick_rows(wanted, table, per, ends):
    first, last = ends
    width = table.shape[1]
    count = wanted.shape[0] // per * (last - first)
    return call(
        functools.partial(pick_kernel, first=first, last=last, per=per),
        "pick_rows",
        jax.ShapeDtypeStruct((count, width), jnp.bfloat16),
        [smem, vmem],
        vmem,
        [pltpu.VMEM((count, width), jnp.float32)],
        4.6,
        20 << 20,
    )(wanted, table)


def stood(flat, unit):
    size = flat.shape[1]
    flat = jnp.concatenate(
        [flat, jnp.full((unit - flat.shape[0], size), -1, jnp.int32)], axis=0
    ).astype(jnp.float32)
    step = min(LANES, size)
    parts = [jnp.transpose(flat[:, k : k + step]) for k in range(0, size, step)]
    return jnp.concatenate(parts, axis=0).astype(jnp.int32)


def reach_kernel(
    adjacent_three,
    valid_three,
    labelled,
    adjacent_two,
    valid_two,
    names,
    places,
    near_two,
    near_three,
    count,
    left,
    right,
    *,
    rows_all,
    per,
):
    fan_three, seeds = adjacent_three.shape
    fan_two, targets = adjacent_two.shape
    low = jnp.bfloat16
    blocks = rows_all // LANES
    deep = names.shape[0]
    line = labelled[...].reshape(1, seeds)
    column = jnp.transpose(jnp.broadcast_to(line.astype(jnp.float32), (8, seeds)))[:, 0:1]
    near = stood(jnp.where(valid_three[...] > 0, adjacent_three[...], -1), near_three.shape[1])
    near_three[...] = near
    here = jnp.where(column > 0.0, near, -1)
    place = lax.broadcasted_iota(jnp.int32, (seeds, targets), 1)
    hit = jnp.zeros((seeds, targets), jnp.float32)
    for j in range(fan_three):
        hit = hit + jnp.where(here[:, j : j + 1] == place, 1.0, 0.0)
    need = jnp.max(hit, axis=0, keepdims=True) + jnp.concatenate(
        [line.astype(jnp.float32), jnp.zeros((1, targets - seeds), jnp.float32)], axis=1
    )

    level = lax.broadcasted_iota(jnp.int32, (deep, targets), 0)
    lane = lax.broadcasted_iota(jnp.int32, (targets, LANES), 1)
    flat = jnp.where(valid_two[...] > 0, adjacent_two[...], -1)
    tall = stood(flat, near_two.shape[1])
    near_two[...] = tall
    flat = jnp.where(need > 0.0, flat, -1)
    for j in range(fan_two):
        left[0:deep, j * targets : (j + 1) * targets] = jnp.where(
            lax.shift_right_arithmetic(flat[j : j + 1, :], 7) == level, 1.0, 0.0
        ).astype(low)
        right[j * targets : (j + 1) * targets, :] = jnp.where(
            (tall[:, j : j + 1] & (LANES - 1)) == lane, 1.0, 0.0
        ).astype(low)
    used = dot(left[0:deep, 0 : fan_two * targets], right[0 : fan_two * targets, :])
    own = [need[:, k : k + LANES] for k in range(0, targets, LANES)]
    own = jnp.concatenate(
        own + [jnp.zeros((deep - len(own), LANES), jnp.float32)], axis=0
    )
    flag = jnp.where(used + own > 0.0, 1.0, 0.0)

    square_row = lax.broadcasted_iota(jnp.int32, (LANES, LANES), 0)
    square_col = lax.broadcasted_iota(jnp.int32, (LANES, LANES), 1)
    full = jnp.concatenate([flag, jnp.zeros((LANES - deep, LANES), jnp.float32)], axis=0)
    flag_low = full.astype(low)
    running = dot(flag_low, jnp.where(square_row <= square_col, 1.0, 0.0).astype(low))
    totals = dot(flag_low, jnp.ones((LANES, LANES), low)).astype(low)
    before = dot(jnp.where(square_row > square_col, 1.0, 0.0).astype(low), totals)
    order = (before + running - full).astype(jnp.int32)
    number = jnp.sum(flag).astype(jnp.int32)
    count[0] = number
    count[1] = 2 * lax.div(number + (2 * SPAN - 1), 2 * SPAN)

    high = jnp.where(full > 0.0, lax.shift_right_arithmetic(order, 7), -1)
    rest = jnp.transpose((order & (LANES - 1)).astype(jnp.float32)).astype(jnp.int32)
    step = lax.broadcasted_iota(jnp.int32, (deep, LANES), 0)
    inner = lax.broadcasted_iota(jnp.int32, (deep, LANES), 1).astype(jnp.float32)
    for b in range(blocks):
        match = jnp.where(high[b : b + 1, :] == step, 1.0, 0.0)
        lanes = slice(b * LANES, (b + 1) * LANES)
        left[0:deep, lanes] = (match * inner).astype(low)
        left[deep : 2 * deep, lanes] = (match * float(b)).astype(low)
        right[lanes, :] = jnp.where(rest[:, b : b + 1] == square_col, 1.0, 0.0).astype(low)
    found = dot(left[:, 0:rows_all], right[0:rows_all, :]).astype(jnp.int32)
    where = step * LANES + lax.broadcasted_iota(jnp.int32, (deep, LANES), 1)
    name = found[deep:] * LANES + found[0:deep]
    names[...] = jnp.where(where < number, name, rows_all)
    name = jnp.minimum(jnp.where(where < number, name, 0), rows_all - 1)
    owners = -(-rows_all // per)
    owner = lax.shift_right_logical(name, per.bit_length() - 1)
    slot = name & (per - 1)
    early, late = (last - first for first, last in cuts(per))
    places[...] = jnp.where(
        slot < early, owner * early + slot, owners * early + owner * late + slot - early
    )


def reach(adjacent_three, valid_three, labelled, adjacent_two, valid_two, rows_all, per):
    targets, fan = adjacent_two.shape
    seeds = labelled.shape[0]
    deep = up(up(rows_all, 2 * SPAN) // LANES, 16)
    area = max(fan * targets, rows_all)
    return call(
        functools.partial(reach_kernel, rows_all=rows_all, per=per),
        "reach",
        (
            jax.ShapeDtypeStruct((deep, LANES), jnp.int32),
            jax.ShapeDtypeStruct((deep, LANES), jnp.int32),
            jax.ShapeDtypeStruct((targets, 16), jnp.int32),
            jax.ShapeDtypeStruct((seeds, 8), jnp.int32),
            jax.ShapeDtypeStruct((2,), jnp.int32),
        ),
        [vmem] * 5,
        (vmem,) * 4 + (smem,),
        [
            pltpu.VMEM((2 * deep, area), jnp.bfloat16),
            pltpu.VMEM((area, LANES), jnp.bfloat16),
        ],
        3.0,
        8 << 20,
    )(adjacent_three.T, valid_three.T, labelled, adjacent_two.T, valid_two.T)


def tally_kernel(count, names, adjacent, valid, *refs, per, which):
    multiply = which == 0
    if multiply:
        source, out, table, rows, spread, marked, buffer, sems, terms, sums = refs
        width = source.shape[1]
        terms[:, 0:width] = source[...]
        terms[:, width:] = jnp.ones((source.shape[0], width), jnp.bfloat16)
    else:
        out, table, rows, spread, marked, buffer, sems = refs
    low = jnp.bfloat16
    fan, targets = adjacent.shape
    unit = spread.shape[0]
    groups = SPAN // unit
    few = 8 if multiply else groups
    used = count[1]
    high_all = buffer.shape[2] // SPAN
    first, last = cuts(per)[which]
    size = last - first

    slot = adjacent[...]
    owner = lax.shift_right_logical(slot, per.bit_length() - 1)
    inner = slot & (per - 1)
    here = (valid[...] > 0) & (inner >= first) & (inner < last)
    slot = jnp.where(here, owner * size + inner - first, -1)
    slot = jnp.concatenate([slot, jnp.full((unit - fan, targets), -1, jnp.int32)], axis=0)
    slot = slot.astype(jnp.float32)
    for b in range(0, targets, LANES):
        table[b : b + LANES, :] = jnp.transpose(slot[:, b : b + LANES]).astype(jnp.int32)
    table[targets:, :] = jnp.full((table.shape[0] - targets, unit), -1, jnp.int32)

    across = lax.broadcasted_iota(jnp.int32, (unit, SPAN), 1)
    down = lax.broadcasted_iota(jnp.int32, (unit, SPAN), 0)
    spread[...] = jnp.where(lax.div(across, unit) == down, 1.0, 0.0).astype(low)
    lane = across.astype(jnp.float32).astype(low)
    one = jnp.ones((unit, SPAN), low)
    zero = jnp.zeros((unit, SPAN), low)

    def copies(block, slot):
        where = pl.ds(pl.multiple_of(block * SPAN, SPAN), SPAN)
        result = sums if multiply else buffer
        return pltpu.make_async_copy(result.at[slot], out.at[where, :], sems.at[slot])

    def body(block, carry):
        slot = lax.rem(block, 2)

        @pl.when(block >= 2)
        def _():
            copies(block - 2, slot).wait()

        copy_rows(names, block * SPAN, SPAN, table, rows)
        high = lax.shift_right_arithmetic(rows[...], 8).astype(jnp.float32).astype(low)
        own = lax.rem(lax.broadcasted_iota(jnp.int32, (SPAN, SPAN), 0), unit) == lax.rem(
            lax.broadcasted_iota(jnp.int32, (SPAN, SPAN), 1), unit
        )
        marked[...] = jnp.where(own, dot(high, spread[...]), -1.0).astype(low)

        def single(g):
            first = pl.multiple_of(g * unit, unit)
            rest = (rows[pl.ds(first, unit), :] & (SPAN - 1)).astype(jnp.float32)
            columns = [
                jnp.where(
                    jnp.broadcast_to(rest[:, j : j + 1], (unit, SPAN)).astype(low) == lane,
                    one,
                    zero,
                )
                for j in range(unit)
            ]
            mark = marked[pl.ds(first, unit), :]
            marks = [
                jnp.where(mark == jnp.full((unit, SPAN), float(q), low), one, zero)
                for q in range(high_all)
            ]
            return dot(jnp.concatenate(marks, axis=0), jnp.concatenate(columns, axis=0))

        def group(step, inner):
            for u in range(0, few, 2):
                pair = [single(step * few + u), single(step * few + u + 1)]
                where = pl.ds(pl.multiple_of((step * few + u) * unit, 2 * unit), 2 * unit)
                for q in range(high_all):
                    tile = jnp.concatenate(
                        [item[q * unit : (q + 1) * unit] for item in pair], axis=0
                    )
                    buffer[slot, where, q * SPAN : (q + 1) * SPAN] = tile.astype(buffer.dtype)
            return inner

        lax.fori_loop(0, groups // few, group, 0)
        if multiply:
            sums[slot] = dot(buffer[slot], terms[...])
        copies(block, slot).start()
        return carry

    lax.fori_loop(0, used, body, 0)

    @pl.when(used >= 2)
    def _():
        copies(used - 2, lax.rem(used - 2, 2)).wait()

    @pl.when(used >= 1)
    def _():
        copies(used - 1, lax.rem(used - 1, 2)).wait()


def tally(count, names, adjacent, valid, padded, devices, per, which, sources):
    targets = adjacent.shape[0]
    unit = 16
    first, last = cuts(per)[which]
    wide = devices * (last - first)
    multiply = which == 0
    width = sources[0].shape[1] if multiply else 0
    scratch = [
        pltpu.VMEM((targets + 8, unit), jnp.int32),
        pltpu.VMEM((SPAN, unit), jnp.int32),
        pltpu.VMEM((unit, SPAN), jnp.bfloat16),
        pltpu.VMEM((SPAN, SPAN), jnp.bfloat16),
        pltpu.VMEM((2, SPAN, wide), jnp.bfloat16 if multiply else COUNTS),
        pltpu.SemaphoreType.DMA((2,)),
    ]
    if multiply:
        out = jax.ShapeDtypeStruct((3 * padded, 2 * width), jnp.float32)
        scratch += [
            pltpu.VMEM((wide, 2 * width), jnp.bfloat16),
            pltpu.VMEM((2, SPAN, 2 * width), jnp.float32),
        ]
    else:
        out = jax.ShapeDtypeStruct((padded, wide), COUNTS)
    return call(
        functools.partial(tally_kernel, per=per, which=which),
        "early_sums" if multiply else "tally",
        out,
        [smem, smem] + [vmem] * (2 + len(sources)),
        anywhere,
        scratch,
        14.0,
        BIG,
    )(count, names, adjacent.T, valid.T, *sources)


def link_kernel(count, names, near, out, buffer, sems, *, fan):
    targets = near.shape[0]
    tile = 32
    blocks = count[1]

    def rows(step, carry):
        first = pl.multiple_of(step * tile, tile)
        here = near[pl.ds(first, tile), :]
        spread = [jnp.broadcast_to(here[:, j : j + 1], (tile, LANES)) for j in range(fan)]
        own = first + lax.broadcasted_iota(jnp.int32, (tile, LANES), 0)

        def columns(block, inner):
            for part in range(SPAN // LANES):
                name = jnp.broadcast_to(
                    names[pl.ds(block * (SPAN // LANES) + part, 1), :], (tile, LANES)
                )
                number = jnp.zeros((tile, LANES), jnp.float32)
                for j in range(fan):
                    number = number + jnp.where(spread[j] == name, 1.0, 0.0)
                lanes = pl.ds(part * LANES, LANES)
                buffer[block, pl.ds(first, tile), lanes] = number.astype(jnp.bfloat16)
                buffer[block, pl.ds(targets + first, tile), lanes] = jnp.where(
                    own == name, 1.0, 0.0
                ).astype(jnp.bfloat16)
            return inner

        return lax.fori_loop(0, blocks, columns, carry)

    lax.fori_loop(0, targets // tile, rows, 0)

    def save(block):
        return pltpu.make_async_copy(buffer.at[block], out.at[block], sems.at[block])

    def start(block, carry):
        save(block).start()
        return carry

    def finish(block, carry):
        save(block).wait()
        return carry

    lax.fori_loop(0, blocks, start, 0)
    lax.fori_loop(0, blocks, finish, 0)


def link_matrix(count, names, near, fan, padded):
    blocks = padded // SPAN
    targets = near.shape[0]
    return call(
        functools.partial(link_kernel, fan=fan),
        "link_matrix",
        jax.ShapeDtypeStruct((2 * blocks, 2 * targets, SPAN), jnp.bfloat16),
        [smem, vmem, vmem],
        anywhere,
        [
            pltpu.VMEM((blocks, 2 * targets, SPAN), jnp.bfloat16),
            pltpu.SemaphoreType.DMA((blocks,)),
        ],
        5.0,
        BIG,
    )(count, names, near)


def step_kernel(
    info,
    count,
    places,
    partial,
    tallies,
    links,
    *refs,
    classes,
):
    sources = refs[:PARTS]
    step_body(
        info, count, places, partial, tallies, links, sources, *refs[PARTS:],
        classes=classes,
    )


def step_body(
    info,
    count,
    places,
    partial,
    tallies,
    links,
    sources,
    near_two,
    near_three,
    labels,
    labelled,
    weights_in,
    weights_mid,
    weights_out,
    biases_line,
    keep,
    send,
    slopes,
    packed,
    sums,
    weight_sums,
    mid_sums,
    out_sums,
    own_table,
    late_table,
    mixin,
    own_rows,
    joined,
    late,
    early,
    link,
    sems,
    link_sems,
    *,
    classes,
):
    blocks, both, _ = links.shape
    targets = both // 2
    hidden = weights_in.shape[2]
    seeds = labels.shape[0]
    biases = biases_line[...].reshape(1, biases_line.shape[0])
    label, marked = [
        jnp.transpose(
            jnp.broadcast_to(item[...].reshape(1, seeds).astype(jnp.float32), (8, seeds))
        )[:, 0:1]
        for item in (labels, labelled)
    ]
    wide = up(classes, LANES)
    core = info[0]
    used = count[1]
    low = jnp.bfloat16
    width = sources[0].shape[1]

    def load(pair, slot):
        rows = pl.ds(pl.multiple_of(pair * 2 * SPAN, 2 * SPAN), 2 * SPAN)
        return (
            pltpu.make_async_copy(tallies.at[rows, :], late.at[slot], sems.at[slot, 0]),
            pltpu.make_async_copy(partial.at[rows, :], early.at[slot], sems.at[slot, 1]),
        )

    def load_link(block):
        return pltpu.make_async_copy(links.at[block], link.at[block], link_sems.at[block])

    @pl.when(used > 0)
    def _():
        for copy in load(0, 0):
            copy.start()

    def start_link(block, carry):
        load_link(block).start()
        return carry

    lax.fori_loop(0, used, start_link, 0)
    late_table[:, 0:width] = sources[-1][...]
    late_table[:, width:] = jnp.ones((late_table.shape[0], width), low)
    filled = 0
    for source in sources:
        held = own_table.shape[0] * source.shape[0] // sum(item.shape[0] for item in sources)
        own_table[filled : filled + held, :] = source[0:held, :].astype(jnp.float32)
        filled += held

    w_in = weights_in[...].astype(low).reshape(2 * weights_in.shape[1], hidden)
    bias_in = biases[:, 0:hidden]
    bias_mid = biases[:, hidden : 2 * hidden]
    bias_out = jnp.concatenate(
        [
            biases[:, 2 * hidden : 2 * hidden + classes],
            jnp.full((1, wide - classes), -1e30, jnp.float32),
        ],
        axis=1,
    )

    sums[...] = jnp.zeros_like(sums)

    def forward(pair, carry):
        rows = pl.ds(pl.multiple_of(pair * 2 * SPAN, 2 * SPAN), 2 * SPAN)
        slot = lax.rem(pair, 2)
        for copy in load(pair, slot):
            copy.wait()
        load_link(2 * pair).wait()
        load_link(2 * pair + 1).wait()

        @pl.when(2 * pair + 2 < used)
        def _():
            for copy in load(pair + 1, 1 - slot):
                copy.start()

        copy_rows(places, pair * 2 * SPAN, 2 * SPAN, own_table, own_rows)
        joined[...] = dot(late[slot].astype(low), late_table[...]) + early[slot]
        mixin[rows, 0:width] = own_rows[...].astype(low)
        mixin[rows, width:] = (
            joined[:, 0:width] / jnp.maximum(joined[:, width:], 1.0)
        ).astype(low)
        z = dot(mixin[rows, :], w_in) + bias_in
        s = 1.0 / (1.0 + jnp.exp(-z))
        slopes[rows, :] = s * (1.0 + z * (1.0 - s))
        wide_link = jnp.concatenate([link[2 * pair], link[2 * pair + 1]], axis=1)
        sums[...] += dot(wide_link, (z * s).astype(low))
        return carry

    pairs = lax.div(used, 2)
    lax.fori_loop(0, pairs, forward, 0)
    total = sums[...]
    counts_two = clipped_counts(near_two[...] >= 0)
    mixed_one = (total[0:targets] / counts_two).astype(low)
    self_one = total[targets:].astype(low)
    w_mid = weights_mid[...].astype(low)
    both_one = jnp.concatenate([self_one, mixed_one], axis=1)
    z = dot(both_one, w_mid.reshape(2 * hidden, hidden)) + bias_mid
    s = 1.0 / (1.0 + jnp.exp(-z))
    slope_mid = s * (1.0 + z * (1.0 - s))
    hidden_two = (z * s).astype(low)

    here = near_three[...]
    place = lax.broadcasted_iota(jnp.int32, (seeds, targets), 1)
    number = jnp.zeros((seeds, targets), jnp.float32)
    for j in range(here.shape[1]):
        number = number + jnp.where(here[:, j : j + 1] == place, 1.0, 0.0)
    number = number.astype(low)
    counts_three = clipped_counts(here >= 0)
    mixed_two = (dot(number, hidden_two) / counts_three).astype(low)
    self_two = hidden_two[0:seeds]
    w_out = [
        jnp.concatenate(
            [weights_out[:, k, :], jnp.zeros((wide - classes, hidden), jnp.float32)], axis=0
        ).astype(low)
        for k in range(2)
    ]
    both_two = jnp.concatenate([self_two, mixed_two], axis=1)
    logits = dot_cols(both_two, jnp.concatenate(w_out, axis=1)) + bias_out
    top = jnp.max(logits, axis=1, keepdims=True)
    log_total = top + jnp.log(jnp.sum(jnp.exp(logits - top), axis=1, keepdims=True))
    onehot = jnp.where(
        label.astype(jnp.int32) == lax.broadcasted_iota(jnp.int32, (seeds, wide), 1), 1.0, 0.0
    )
    picked = jnp.sum(jnp.where(onehot > 0.0, logits, 0.0), axis=1, keepdims=True)
    loss = jnp.sum(marked * (log_total - picked), axis=0, keepdims=True)
    counted = jnp.sum(marked, axis=0, keepdims=True)
    grad_out = (marked * (jnp.exp(logits - log_total) - onehot)).astype(low)

    out_sums[...] = dot_rows(grad_out, both_two)
    bias_grad_out = jnp.sum(grad_out.astype(jnp.float32), axis=0, keepdims=True)
    to_self = dot(grad_out, w_out[0])
    spread = (dot(grad_out, w_out[1]) / counts_three).astype(low)
    sums[0:targets, :] = dot_rows(number, spread)
    sums[0:seeds, :] += to_self
    grad_mid = (sums[0:targets, :] * slope_mid).astype(low)

    mid_sums[...] = dot_rows(both_one, grad_mid)
    bias_grad_mid = jnp.sum(grad_mid.astype(jnp.float32), axis=0, keepdims=True)
    down = jnp.concatenate(
        [dot_cols(grad_mid, w_mid[1]) / counts_two, dot_cols(grad_mid, w_mid[0])], axis=0
    )
    spread = down.astype(low)

    weight_sums[...] = jnp.zeros_like(weight_sums)

    def backward(pair, bias):
        rows = pl.ds(pl.multiple_of(pair * 2 * SPAN, 2 * SPAN), 2 * SPAN)
        wide_link = jnp.concatenate([link[2 * pair], link[2 * pair + 1]], axis=1)
        grad = (dot_rows(wide_link, spread) * slopes[rows, :]).astype(low)
        weight_sums[...] += dot_rows(mixin[rows, :], grad)
        return bias + jnp.sum(grad.astype(jnp.float32), axis=0, keepdims=True)

    bias_grad_in = lax.fori_loop(0, pairs, backward, jnp.zeros((1, hidden), jnp.float32))

    row = 0
    for part in (weight_sums, mid_sums):
        for column in range(0, hidden, LANES):
            packed[row : row + part.shape[0], :] = part[:, column : column + LANES]
            row += part.shape[0]
    tall = up(classes, 16)
    for column in range(0, 2 * hidden, LANES):
        packed[row : row + tall, :] = out_sums[0:tall, column : column + LANES]
        row += tall
    packed[row:, :] = jnp.zeros((packed.shape[0] - row, LANES), jnp.float32)
    lane = lax.broadcasted_iota(jnp.int32, (1, LANES), 1)
    scalars = jnp.where(lane == 0, loss, 0.0) + jnp.where(lane == 1, counted, 0.0)
    extra = [
        item[:, column : column + LANES]
        for item in (bias_grad_in, bias_grad_mid, bias_grad_out)
        for column in range(0, hidden, LANES)
    ] + [scalars, jnp.zeros((1, LANES), jnp.float32)]
    extra = jnp.concatenate(extra, axis=0)
    high = extra.astype(low).astype(jnp.float32)
    packed[packed.shape[0] - 16 :, :] = jnp.concatenate([high, extra - high], axis=0)
    half = keep.shape[0]
    keep[...] = packed[pl.ds(pl.multiple_of(core * half, 16), half), :].astype(low)
    send[...] = packed[pl.ds(pl.multiple_of((1 - core) * half, 16), half), :].astype(low)


def run_step(info, count, places, partial, tallies, links, sources, rest, half, classes, held):
    padded = tallies.shape[0]
    blocks, both = padded // SPAN, links.shape[1]
    total, width = sources[-1].shape
    hidden = rest[4].shape[2]
    wide = up(classes, LANES)
    return call(
        functools.partial(step_kernel, classes=classes),
        "step",
        (jax.ShapeDtypeStruct((half, LANES), jnp.bfloat16),) * 2,
        [smem] * 3 + [anywhere] * 3 + [vmem] * (PARTS + 8),
        (vmem, vmem),
        [
            pltpu.VMEM((padded, hidden), jnp.float32),
            pltpu.VMEM((2 * half, LANES), jnp.float32),
            pltpu.VMEM((both, hidden), jnp.float32),
            pltpu.VMEM((2 * width, hidden), jnp.float32),
            pltpu.VMEM((2 * hidden, hidden), jnp.float32),
            pltpu.VMEM((wide, 2 * hidden), jnp.float32),
            pltpu.VMEM((held, width), jnp.float32),
            pltpu.VMEM((total, 2 * width), jnp.bfloat16),
            pltpu.VMEM((padded, 2 * width), jnp.bfloat16),
            pltpu.VMEM((2 * SPAN, width), jnp.float32),
            pltpu.VMEM((2 * SPAN, 2 * width), jnp.float32),
            pltpu.VMEM((2, 2 * SPAN, total), COUNTS),
            pltpu.VMEM((2, 2 * SPAN, 2 * width), jnp.float32),
            pltpu.VMEM((blocks, both, SPAN), jnp.bfloat16),
            pltpu.SemaphoreType.DMA((2, 2)),
            pltpu.SemaphoreType.DMA((blocks,)),
        ],
        14.0,
        BIG,
    )(info, count, places, partial, tallies, links, *sources, *rest)


def refit(total, rows):
    extra = total[rows - 16 : rows - 8] + total[rows - 8 : rows]
    high = extra.astype(jnp.bfloat16).astype(jnp.float32)
    return jnp.concatenate([high, extra - high], axis=0)


def pair_kernel(info, mine, theirs, out):
    total = mine[...].astype(jnp.float32) + theirs[...].astype(jnp.float32)
    out[...] = total.astype(jnp.bfloat16)

    @pl.when(info[0] == 1)
    def _():
        rows = total.shape[0]
        out[rows - 16 :, :] = refit(total, rows).astype(jnp.bfloat16)


def pair_sum(info, mine, theirs):
    return call(
        pair_kernel,
        "pair_sum",
        jax.ShapeDtypeStruct(mine.shape, jnp.bfloat16),
        [smem, vmem, vmem],
        vmem,
        [],
        0.6,
        6 << 20,
    )(info, mine, theirs)


def spread_kernel(info, pieces, out):
    total = pieces[0].astype(jnp.float32)
    for k in range(1, pieces.shape[0]):
        total = total + pieces[k].astype(jnp.float32)
    rows = total.shape[0]
    fitted = jnp.concatenate([total[0 : rows - 16], refit(total, rows)], axis=0)
    result = jnp.where(info[1] == 1, fitted, total).astype(jnp.bfloat16)
    for k in range(pieces.shape[0]):
        out[k] = result


def spread_sum(info, pieces):
    return call(
        spread_kernel,
        "spread_sum",
        jax.ShapeDtypeStruct(pieces.shape, jnp.bfloat16),
        [smem, vmem],
        vmem,
        [],
        0.6,
        6 << 20,
    )(info, pieces)


def update_kernel(
    info, fixes, mine, theirs, biases, moment_one, moment_two, *refs
):
    groups = [refs[5 * k : 5 * k + 5] for k in range(3)]
    loss_out = refs[15]
    outs = [refs[16 + 4 * k : 20 + 4 * k] for k in range(3)]
    bias_out, first_out, second_out = refs[28:31]
    packed = refs[31]
    low = jnp.bfloat16
    half = mine.shape[0]
    core = info[0]
    packed[pl.ds(pl.multiple_of(core * half, 16), half), :] = mine[...]
    packed[pl.ds(pl.multiple_of((1 - core) * half, 16), half), :] = theirs[...]
    last = packed.shape[0]
    extra = packed[last - 16 :, :].astype(jnp.float32)
    extra = extra[0:8] + extra[8:16]
    counted = extra[6:7, 1:2]
    inverse = 1.0 / counted
    loss_out[...] = extra[6:7, 0:1] / counted
    scale = 0.5 * inverse * inverse

    row = 0
    for group in range(3):
        master, left, right, left_root, right_root = groups[group]
        new_master, copy, new_left, new_right = outs[group]
        turned = group == 2
        depth, hidden = (master.shape[0], master.shape[2]) if turned else master.shape[1:]
        deep = up(depth, LANES)

        def take(ref, k, middle):
            return ref[:, k, :] if middle else ref[k]

        def put(ref, k, middle, value):
            if middle:
                ref[:, k, :] = value
            else:
                ref[k] = value

        grads = []
        if turned:
            tall = up(depth, 16)
            for k in range(2):
                parts = []
                for column in range(0, hidden, LANES):
                    parts.append(packed[row : row + tall, :])
                    row += tall
                grads.append(grown(jnp.concatenate(parts, axis=1), deep, hidden))
        else:
            parts = []
            for column in range(0, hidden, LANES):
                parts.append(packed[row : row + 2 * depth, :])
                row += 2 * depth
            whole = jnp.concatenate(parts, axis=1)
            grads = [whole[k * depth : (k + 1) * depth] for k in range(2)]

        for k in range(2):
            grad = grads[k]
            for old, new, size, product, middle in (
                (left, new_left, depth, dot_cols(grad, grad), turned),
                (right, new_right, hidden, dot_rows(grad, grad), False),
            ):
                corner = old[0:1, k, 0:1] if middle else old[k, 0:1, 0:1]
                eye = lax.broadcasted_iota(jnp.int32, (size, size), 0) == (
                    lax.broadcasted_iota(jnp.int32, (size, size), 1)
                )
                value = jnp.where(eye, 0.5 * corner, 0.0) + scale * product[0:size, 0:size]
                put(new, k, middle, value)
            root = jnp.concatenate(
                halves(grown(take(left_root, k, turned), deep, deep)), axis=1
            )
            middle_high, middle_rest = halves(dot(root, jnp.concatenate([grad, grad], axis=0)))
            root_high, root_rest = halves(right_root[k])
            way = dot(
                jnp.concatenate([middle_high, middle_high, middle_rest], axis=1),
                jnp.concatenate([root_high, root_rest, root_high], axis=0),
            )[0:depth]
            put(new_master, k, turned, take(master, k, turned) - inverse * way)
        copy[...] = new_master[...].astype(low)

    size = biases.shape[0]
    grad = jnp.concatenate([extra[k : k + 1, :] for k in range(6)], axis=1)[:, 0:size]
    grad = grad / counted

    def line(ref):
        return ref[...].reshape(1, size)

    first = 0.9 * line(moment_one) + 0.1 * grad
    second = 0.95 * line(moment_two) + 0.05 * grad * grad
    old = line(biases)
    fresh = old - 0.1 * (
        (first / fixes[0]) / (jnp.sqrt(second / fixes[1]) + 1e-08) + 0.01 * old
    )
    for ref, value in ((bias_out, fresh), (first_out, first), (second_out, second)):
        ref[...] = value[0]


def run_update(info, fixes, mine, theirs, vectors, groups):
    outs = [jax.ShapeDtypeStruct((1, 1), jnp.float32)]
    flat = []
    for master, left, right, left_root, right_root in groups:
        flat += [master, left, right, left_root, right_root]
        outs += [
            jax.ShapeDtypeStruct(master.shape, jnp.float32),
            jax.ShapeDtypeStruct(master.shape, jnp.bfloat16),
            jax.ShapeDtypeStruct(left_root.shape, jnp.float32),
            jax.ShapeDtypeStruct(right_root.shape, jnp.float32),
        ]
    outs += [jax.ShapeDtypeStruct(vectors[0].shape, jnp.float32)] * 3
    return call(
        update_kernel,
        "update",
        tuple(outs),
        [smem] * 2 + [vmem] * (5 + len(flat)),
        (vmem,) * len(outs),
        [pltpu.VMEM((2 * mine.shape[0], LANES), jnp.bfloat16)],
        4.0,
        16 << 20,
    )(info, fixes, mine, theirs, *vectors, *flat)


def body(
    features,
    requests,
    adjacent_one,
    adjacent_two,
    adjacent_three,
    valid_one,
    valid_two,
    valid_three,
    labels,
    labelled,
    weights_in,
    weights_mid,
    weights_out,
    biases,
    moment_one,
    moment_two,
    step_count,
    left_in,
    left_mid,
    left_out,
    right_in,
    right_mid,
    right_out,
    invleft_in,
    invleft_mid,
    invleft_out,
    invright_in,
    invright_mid,
    invright_out,
    *,
    peers,
):
    width = features.shape[1]
    devices, per = requests.shape
    targets = adjacent_one.shape[0]
    padded = up(targets, 2 * SPAN)
    classes = weights_out.shape[2]
    hidden = weights_in.shape[2]
    core = lax.axis_index("core")
    own = lax.axis_index(PEERS)

    wanted = lax.all_to_all(requests, AXES, split_axis=0, concat_axis=0, tiled=True)
    names, places, near_two, near_three, count = reach(
        adjacent_three, valid_three, labelled, adjacent_two, valid_two, targets, per
    )
    wanted, count = lax.optimization_barrier((wanted.reshape(-1), count))
    early_cut, late_cut = cuts(per)

    def trade(found):
        pulled = lax.all_to_all(
            found.reshape(devices, -1, width), AXES, split_axis=0, concat_axis=0, tiled=True
        )
        return pulled.reshape(-1, width)

    early_source = trade(pick_rows(wanted, features, per, early_cut))
    found = pick_rows(wanted, features, per, late_cut)
    links = link_matrix(count, names, near_two, adjacent_two.shape[1], padded)
    names, places = names.reshape(-1), places.reshape(-1)
    late_tally = tally(
        count, names, adjacent_one, valid_one, padded, devices, per, 1, ()
    )

    core_info = jnp.stack([core, ((core == 1) & (own == peers - 1)).astype(jnp.int32)])
    core_info = core_info.astype(jnp.int32)
    stepped = step_count.astype(jnp.float32)
    fixes = jnp.stack([1.0 - 0.9**stepped, 1.0 - 0.95**stepped])
    found, late_tally, info, fixes = lax.optimization_barrier(
        (found, late_tally, core_info, fixes)
    )
    late_source = trade(found)
    partial = tally(
        count, names, adjacent_one, valid_one, padded, devices, per, 0, (early_source,)
    )

    rows = (2 * width + 2 * weights_mid.shape[1]) * (hidden // LANES)
    rows += up(classes, 16) * (2 * hidden // LANES)
    each = up(-(-(rows + 16) // (2 * peers)), 8)
    half = each * peers
    turned_out = weights_out.transpose(2, 0, 1)
    keep, send = run_step(
        info,
        count,
        places,
        partial,
        late_tally,
        links,
        (early_source, late_source),
        (
            near_two,
            near_three,
            labels,
            labelled,
            weights_in,
            weights_mid,
            turned_out,
            biases,
        ),
        half,
        classes,
        -(-targets // per) * per,
    )
    swap = [(0, 1), (1, 0)]
    theirs = lax.ppermute(send, "core", swap)
    summed = pair_sum(info, keep, theirs).reshape(peers, each, LANES)
    pieces = lax.all_to_all(summed, PEERS, split_axis=0, concat_axis=0, tiled=True)
    shared = spread_sum(info, pieces)
    mine = lax.all_to_all(shared, PEERS, split_axis=0, concat_axis=0, tiled=True)
    mine = mine.reshape(half, LANES)
    theirs = lax.ppermute(mine, "core", swap)

    outs = run_update(
        info,
        fixes,
        mine,
        theirs,
        (biases, moment_one, moment_two),
        (
            (weights_in, left_in, right_in, invleft_in, invright_in),
            (weights_mid, left_mid, right_mid, invleft_mid, invright_mid),
            (
                turned_out,
                right_out.transpose(1, 0, 2),
                left_out,
                invright_out.transpose(1, 0, 2),
                invleft_out,
            ),
        ),
    )
    first, second, third = (outs[1 + 4 * k : 5 + 4 * k] for k in range(3))
    third = (
        third[0].transpose(1, 2, 0),
        third[1].transpose(1, 2, 0),
        third[3],
        third[2].transpose(1, 0, 2),
    )
    return (
        (outs[0].reshape(()),)
        + tuple(group[which] for which in range(4) for group in (first, second, third))
        + tuple(outs[13:16])
    )


def solution(mesh):
    chips, dev = mesh.shape["hst"] // 2, mesh.shape["dev"]
    fine = jax.sharding.Mesh(mesh.devices.reshape(chips, 2, dev), AXES)
    split = P(AXES, None)
    line = P(AXES)
    whole = P()
    mapped = jax.shard_map(
        functools.partial(body, peers=chips * dev),
        mesh=fine,
        in_specs=(split,) * 8 + (line,) * 2 + (whole,) * 19,
        out_specs=(whole,) * 16,
        check_vma=False,
    )

    def run(*args):
        with jax.sharding.use_abstract_mesh(fine.abstract_mesh):
            return mapped(*args)

    return run
```

```python
import functools

import jax
import jax.numpy as jnp
from jax import lax
from jax.experimental import pallas as pl
from jax.experimental.pallas import tpu as pltpu
from jax.sharding import PartitionSpec as P

LANES = 128
SPAN = 256
PARTS = 2
COUNTS = jnp.float8_e4m3fn
BIG = 52 << 20
AXES = ("chip", "core", "dev")
PEERS = ("chip", "dev")

smem = pl.BlockSpec(memory_space=pltpu.SMEM)
vmem = pl.BlockSpec(memory_space=pltpu.VMEM)
anywhere = pl.BlockSpec(memory_space=pltpu.HBM)


def up(value, unit):
    return -(-value // unit) * unit


def call(kernel, name, out_shape, in_specs, out_specs, scratch, cost, room):
    return pl.pallas_call(
        kernel,
        name=name,
        out_shape=out_shape,
        in_specs=in_specs,
        out_specs=out_specs,
        scratch_shapes=scratch,
        compiler_params=pltpu.CompilerParams(vmem_limit_bytes=room),
        cost_estimate=pl.CostEstimate(
            flops=0, transcendentals=0, bytes_accessed=int(cost * 3.6e6)
        ),
    )


def dot(left, right):
    return jnp.dot(left, right, preferred_element_type=jnp.float32)


def dot_rows(left, right):
    return lax.dot_general(
        left, right, (((0,), (0,)), ((), ())), preferred_element_type=jnp.float32
    )


def dot_cols(left, right):
    return lax.dot_general(
        left, right, (((1,), (1,)), ((), ())), preferred_element_type=jnp.float32
    )


def halves(value):
    high = value.astype(jnp.bfloat16)
    return high, (value - high.astype(jnp.float32)).astype(jnp.bfloat16)


def grown(value, rows, columns):
    short = columns - value.shape[1]
    if short:
        value = jnp.concatenate([value, jnp.zeros((value.shape[0], short), value.dtype)], axis=1)
    short = rows - value.shape[0]
    if short:
        value = jnp.concatenate([value, jnp.zeros((short, columns), value.dtype)], axis=0)
    return value


def clipped_counts(valid):
    return jnp.maximum(jnp.sum(valid.astype(jnp.float32), axis=1, keepdims=True), 1.0)


def copy_rows(names, base, size, source, target):
    for u in range(size):
        target[u : u + 1, :] = source[pl.ds(names[base + u], 1), :]


def cuts(per):
    return (0, per // 2), (per // 2, per)


def pick_kernel(wanted, table, out, rows, *, first, last, per):
    part = last - first

    def body(device, carry):
        for u in range(part):
            name = wanted[device * per + (first + u)]
            rows[pl.ds(device * part + u, 1), :] = table[pl.ds(name, 1), :]
        return carry

    lax.fori_loop(0, out.shape[0] // part, body, 0)
    out[...] = rows[...].astype(jnp.bfloat16)


def pick_rows(wanted, table, per, ends):
    first, last = ends
    width = table.shape[1]
    count = wanted.shape[0] // per * (last - first)
    return call(
        functools.partial(pick_kernel, first=first, last=last, per=per),
        "pick_rows",
        jax.ShapeDtypeStruct((count, width), jnp.bfloat16),
        [smem, vmem],
        vmem,
        [pltpu.VMEM((count, width), jnp.float32)],
        4.6,
        20 << 20,
    )(wanted, table)


def stood(flat, unit):
    size = flat.shape[1]
    flat = jnp.concatenate(
        [flat, jnp.full((unit - flat.shape[0], size), -1, jnp.int32)], axis=0
    ).astype(jnp.float32)
    step = min(LANES, size)
    parts = [jnp.transpose(flat[:, k : k + step]) for k in range(0, size, step)]
    return jnp.concatenate(parts, axis=0).astype(jnp.int32)


def reach_kernel(
    adjacent_three,
    valid_three,
    labelled,
    adjacent_two,
    valid_two,
    names,
    places,
    near_two,
    near_three,
    count,
    left,
    right,
    *,
    rows_all,
    per,
):
    fan_three, seeds = adjacent_three.shape
    fan_two, targets = adjacent_two.shape
    low = jnp.bfloat16
    blocks = rows_all // LANES
    deep = names.shape[0]
    line = labelled[...].reshape(1, seeds)
    column = jnp.transpose(jnp.broadcast_to(line.astype(jnp.float32), (8, seeds)))[:, 0:1]
    near = stood(jnp.where(valid_three[...] > 0, adjacent_three[...], -1), near_three.shape[1])
    near_three[...] = near
    here = jnp.where(column > 0.0, near, -1)
    place = lax.broadcasted_iota(jnp.int32, (seeds, targets), 1)
    hit = jnp.zeros((seeds, targets), jnp.float32)
    for j in range(fan_three):
        hit = hit + jnp.where(here[:, j : j + 1] == place, 1.0, 0.0)
    need = jnp.max(hit, axis=0, keepdims=True) + jnp.concatenate(
        [line.astype(jnp.float32), jnp.zeros((1, targets - seeds), jnp.float32)], axis=1
    )

    level = lax.broadcasted_iota(jnp.int32, (deep, targets), 0)
    lane = lax.broadcasted_iota(jnp.int32, (targets, LANES), 1)
    flat = jnp.where(valid_two[...] > 0, adjacent_two[...], -1)
    tall = stood(flat, near_two.shape[1])
    near_two[...] = tall
    flat = jnp.where(need > 0.0, flat, -1)
    for j in range(fan_two):
        left[0:deep, j * targets : (j + 1) * targets] = jnp.where(
            lax.shift_right_arithmetic(flat[j : j + 1, :], 7) == level, 1.0, 0.0
        ).astype(low)
        right[j * targets : (j + 1) * targets, :] = jnp.where(
            (tall[:, j : j + 1] & (LANES - 1)) == lane, 1.0, 0.0
        ).astype(low)
    used = dot(left[0:deep, 0 : fan_two * targets], right[0 : fan_two * targets, :])
    own = [need[:, k : k + LANES] for k in range(0, targets, LANES)]
    own = jnp.concatenate(
        own + [jnp.zeros((deep - len(own), LANES), jnp.float32)], axis=0
    )
    flag = jnp.where(used + own > 0.0, 1.0, 0.0)

    square_row = lax.broadcasted_iota(jnp.int32, (LANES, LANES), 0)
    square_col = lax.broadcasted_iota(jnp.int32, (LANES, LANES), 1)
    full = jnp.concatenate([flag, jnp.zeros((LANES - deep, LANES), jnp.float32)], axis=0)
    flag_low = full.astype(low)
    running = dot(flag_low, jnp.where(square_row <= square_col, 1.0, 0.0).astype(low))
    totals = dot(flag_low, jnp.ones((LANES, LANES), low)).astype(low)
    before = dot(jnp.where(square_row > square_col, 1.0, 0.0).astype(low), totals)
    order = (before + running - full).astype(jnp.int32)
    number = jnp.sum(flag).astype(jnp.int32)
    count[0] = number
    count[1] = 2 * lax.div(number + (2 * SPAN - 1), 2 * SPAN)

    high = jnp.where(full > 0.0, lax.shift_right_arithmetic(order, 7), -1)
    rest = jnp.transpose((order & (LANES - 1)).astype(jnp.float32)).astype(jnp.int32)
    step = lax.broadcasted_iota(jnp.int32, (deep, LANES), 0)
    inner = lax.broadcasted_iota(jnp.int32, (deep, LANES), 1).astype(jnp.float32)
    for b in range(blocks):
        match = jnp.where(high[b : b + 1, :] == step, 1.0, 0.0)
        lanes = slice(b * LANES, (b + 1) * LANES)
        left[0:deep, lanes] = (match * inner).astype(low)
        left[deep : 2 * deep, lanes] = (match * float(b)).astype(low)
        right[lanes, :] = jnp.where(rest[:, b : b + 1] == square_col, 1.0, 0.0).astype(low)
    found = dot(left[:, 0:rows_all], right[0:rows_all, :]).astype(jnp.int32)
    where = step * LANES + lax.broadcasted_iota(jnp.int32, (deep, LANES), 1)
    name = found[deep:] * LANES + found[0:deep]
    names[...] = jnp.where(where < number, name, rows_all)
    name = jnp.minimum(jnp.where(where < number, name, 0), rows_all - 1)
    owners = -(-rows_all // per)
    owner = lax.shift_right_logical(name, per.bit_length() - 1)
    slot = name & (per - 1)
    early, late = (last - first for first, last in cuts(per))
    places[...] = jnp.where(
        slot < early, owner * early + slot, owners * early + owner * late + slot - early
    )


def reach(adjacent_three, valid_three, labelled, adjacent_two, valid_two, rows_all, per):
    targets, fan = adjacent_two.shape
    seeds = labelled.shape[0]
    deep = up(up(rows_all, 2 * SPAN) // LANES, 16)
    area = max(fan * targets, rows_all)
    return call(
        functools.partial(reach_kernel, rows_all=rows_all, per=per),
        "reach",
        (
            jax.ShapeDtypeStruct((deep, LANES), jnp.int32),
            jax.ShapeDtypeStruct((deep, LANES), jnp.int32),
            jax.ShapeDtypeStruct((targets, 16), jnp.int32),
            jax.ShapeDtypeStruct((seeds, 8), jnp.int32),
            jax.ShapeDtypeStruct((2,), jnp.int32),
        ),
        [vmem] * 5,
        (vmem,) * 4 + (smem,),
        [
            pltpu.VMEM((2 * deep, area), jnp.bfloat16),
            pltpu.VMEM((area, LANES), jnp.bfloat16),
        ],
        3.0,
        8 << 20,
    )(adjacent_three.T, valid_three.T, labelled, adjacent_two.T, valid_two.T)


def tally_kernel(count, names, adjacent, valid, *refs, per, which):
    multiply = which == 0
    if multiply:
        source, out, table, rows, spread, marked, buffer, sems, terms, sums = refs
        width = source.shape[1]
        terms[:, 0:width] = source[...]
        terms[:, width:] = jnp.ones((source.shape[0], width), jnp.bfloat16)
    else:
        out, table, rows, spread, marked, buffer, sems = refs
    low = jnp.bfloat16
    fan, targets = adjacent.shape
    unit = spread.shape[0]
    groups = SPAN // unit
    few = 8 if multiply else groups
    used = count[1]
    high_all = buffer.shape[2] // SPAN
    first, last = cuts(per)[which]
    size = last - first

    slot = adjacent[...]
    owner = lax.shift_right_logical(slot, per.bit_length() - 1)
    inner = slot & (per - 1)
    here = (valid[...] > 0) & (inner >= first) & (inner < last)
    slot = jnp.where(here, owner * size + inner - first, -1)
    slot = jnp.concatenate([slot, jnp.full((unit - fan, targets), -1, jnp.int32)], axis=0)
    slot = slot.astype(jnp.float32)
    for b in range(0, targets, LANES):
        table[b : b + LANES, :] = jnp.transpose(slot[:, b : b + LANES]).astype(jnp.int32)
    table[targets:, :] = jnp.full((table.shape[0] - targets, unit), -1, jnp.int32)

    across = lax.broadcasted_iota(jnp.int32, (unit, SPAN), 1)
    down = lax.broadcasted_iota(jnp.int32, (unit, SPAN), 0)
    spread[...] = jnp.where(lax.div(across, unit) == down, 1.0, 0.0).astype(low)
    lane = across.astype(jnp.float32).astype(low)
    one = jnp.ones((unit, SPAN), low)
    zero = jnp.zeros((unit, SPAN), low)

    def copies(block, slot):
        where = pl.ds(pl.multiple_of(block * SPAN, SPAN), SPAN)
        result = sums if multiply else buffer
        return pltpu.make_async_copy(result.at[slot], out.at[where, :], sems.at[slot])

    def body(block, carry):
        slot = lax.rem(block, 2)

        @pl.when(block >= 2)
        def _():
            copies(block - 2, slot).wait()

        copy_rows(names, block * SPAN, SPAN, table, rows)
        high = lax.shift_right_arithmetic(rows[...], 8).astype(jnp.float32).astype(low)
        own = lax.rem(lax.broadcasted_iota(jnp.int32, (SPAN, SPAN), 0), unit) == lax.rem(
            lax.broadcasted_iota(jnp.int32, (SPAN, SPAN), 1), unit
        )
        marked[...] = jnp.where(own, dot(high, spread[...]), -1.0).astype(low)

        def single(g):
            first = pl.multiple_of(g * unit, unit)
            rest = (rows[pl.ds(first, unit), :] & (SPAN - 1)).astype(jnp.float32)
            columns = [
                jnp.where(
                    jnp.broadcast_to(rest[:, j : j + 1], (unit, SPAN)).astype(low) == lane,
                    one,
                    zero,
                )
                for j in range(unit)
            ]
            mark = marked[pl.ds(first, unit), :]
            marks = [
                jnp.where(mark == jnp.full((unit, SPAN), float(q), low), one, zero)
                for q in range(high_all)
            ]
            return dot(jnp.concatenate(marks, axis=0), jnp.concatenate(columns, axis=0))

        def group(step, inner):
            for u in range(0, few, 2):
                pair = [single(step * few + u), single(step * few + u + 1)]
                where = pl.ds(pl.multiple_of((step * few + u) * unit, 2 * unit), 2 * unit)
                for q in range(high_all):
                    tile = jnp.concatenate(
                        [item[q * unit : (q + 1) * unit] for item in pair], axis=0
                    )
                    buffer[slot, where, q * SPAN : (q + 1) * SPAN] = tile.astype(buffer.dtype)
            return inner

        lax.fori_loop(0, groups // few, group, 0)
        if multiply:
            sums[slot] = dot(buffer[slot], terms[...])
        copies(block, slot).start()
        return carry

    lax.fori_loop(0, used, body, 0)

    @pl.when(used >= 2)
    def _():
        copies(used - 2, lax.rem(used - 2, 2)).wait()

    @pl.when(used >= 1)
    def _():
        copies(used - 1, lax.rem(used - 1, 2)).wait()


def tally(count, names, adjacent, valid, padded, devices, per, which, sources):
    targets = adjacent.shape[0]
    unit = 16
    first, last = cuts(per)[which]
    wide = devices * (last - first)
    multiply = which == 0
    width = sources[0].shape[1] if multiply else 0
    scratch = [
        pltpu.VMEM((targets + 8, unit), jnp.int32),
        pltpu.VMEM((SPAN, unit), jnp.int32),
        pltpu.VMEM((unit, SPAN), jnp.bfloat16),
        pltpu.VMEM((SPAN, SPAN), jnp.bfloat16),
        pltpu.VMEM((2, SPAN, wide), jnp.bfloat16 if multiply else COUNTS),
        pltpu.SemaphoreType.DMA((2,)),
    ]
    if multiply:
        out = jax.ShapeDtypeStruct((3 * padded, 2 * width), jnp.float32)
        scratch += [
            pltpu.VMEM((wide, 2 * width), jnp.bfloat16),
            pltpu.VMEM((2, SPAN, 2 * width), jnp.float32),
        ]
    else:
        out = jax.ShapeDtypeStruct((padded, wide), COUNTS)
    return call(
        functools.partial(tally_kernel, per=per, which=which),
        "early_sums" if multiply else "tally",
        out,
        [smem, smem] + [vmem] * (2 + len(sources)),
        anywhere,
        scratch,
        14.0,
        BIG,
    )(count, names, adjacent.T, valid.T, *sources)


def link_kernel(count, names, near, out, buffer, sems, *, fan):
    targets = near.shape[0]
    tile = 32
    blocks = count[1]
    all_blocks = buffer.shape[0] - 2
    across = SPAN // LANES

    def line(block, part):
        return jnp.broadcast_to(names[pl.ds(block * across + part, 1), :], (tile, LANES))

    def save(block):
        return pltpu.make_async_copy(buffer.at[block], out.at[block], sems.at[block])

    def rows(step, carry):
        first = pl.multiple_of(step * tile, tile)
        here = near[pl.ds(first, tile), :]
        spread = [jnp.broadcast_to(here[:, j : j + 1], (tile, LANES)) for j in range(fan)]
        own = first + lax.broadcasted_iota(jnp.int32, (tile, LANES), 0)

        def columns(block, inner):
            for part in range(across):
                name = line(block, part)
                number = jnp.zeros((tile, LANES), jnp.float32)
                for j in range(fan):
                    number = number + jnp.where(spread[j] == name, 1.0, 0.0)
                lanes = pl.ds(part * LANES, LANES)
                buffer[block, pl.ds(first, tile), lanes] = number.astype(jnp.bfloat16)
            return inner

        lax.fori_loop(0, blocks, columns, 0)
        for block in range(2):
            for part in range(across):
                lanes = slice(part * LANES, (part + 1) * LANES)
                buffer[all_blocks + block, pl.ds(first, tile), lanes] = jnp.where(
                    own == line(block, part), 1.0, 0.0
                ).astype(jnp.bfloat16)
        return carry

    lax.fori_loop(0, targets // tile, rows, 0)

    def start(block, carry):
        save(block).start()
        return carry

    def finish(block, carry):
        save(block).wait()
        return carry

    for ends in ((0, blocks), (all_blocks, all_blocks + 2)):
        lax.fori_loop(*ends, start, 0)
    for ends in ((0, blocks), (all_blocks, all_blocks + 2)):
        lax.fori_loop(*ends, finish, 0)


def link_matrix(count, names, near, fan, padded):
    blocks = padded // SPAN
    targets = near.shape[0]
    return call(
        functools.partial(link_kernel, fan=fan),
        "link_matrix",
        jax.ShapeDtypeStruct((4 * blocks, targets, SPAN), jnp.bfloat16),
        [smem, vmem, vmem],
        anywhere,
        [
            pltpu.VMEM((blocks + 2, targets, SPAN), jnp.bfloat16),
            pltpu.SemaphoreType.DMA((blocks + 2,)),
        ],
        5.0,
        BIG,
    )(count, names, near)


def step_kernel(
    info,
    count,
    places,
    partial,
    tallies,
    links,
    *refs,
    classes,
):
    sources = refs[:PARTS]
    step_body(
        info, count, places, partial, tallies, links, sources, *refs[PARTS:],
        classes=classes,
    )


def step_body(
    info,
    count,
    places,
    partial,
    tallies,
    links,
    sources,
    near_two,
    near_three,
    labels,
    labelled,
    weights_in,
    weights_mid,
    weights_out,
    biases_line,
    keep,
    send,
    slopes,
    packed,
    sums,
    weight_sums,
    mid_sums,
    out_sums,
    own_table,
    late_table,
    mixin,
    own_rows,
    joined,
    late,
    early,
    hid,
    down_low,
    link,
    sems,
    link_sems,
    *,
    classes,
):
    targets = links.shape[1]
    hidden = weights_in.shape[2]
    seeds = labels.shape[0]
    biases = biases_line[...].reshape(1, biases_line.shape[0])
    label, marked = [
        jnp.transpose(
            jnp.broadcast_to(item[...].reshape(1, seeds).astype(jnp.float32), (8, seeds))
        )[:, 0:1]
        for item in (labels, labelled)
    ]
    wide = up(classes, LANES)
    core = info[0]
    used = count[1]
    low = jnp.bfloat16
    width = sources[0].shape[1]

    def load(pair, slot):
        rows = pl.ds(pl.multiple_of(pair * 2 * SPAN, 2 * SPAN), 2 * SPAN)
        return (
            pltpu.make_async_copy(tallies.at[rows, :], late.at[slot], sems.at[slot, 0]),
            pltpu.make_async_copy(partial.at[rows, :], early.at[slot], sems.at[slot, 1]),
        )

    def load_link(block):
        return pltpu.make_async_copy(links.at[block], link.at[block], link_sems.at[block])

    @pl.when(used > 0)
    def _():
        for copy in load(0, 0):
            copy.start()

    def start_link(block, carry):
        load_link(block).start()
        return carry

    lax.fori_loop(0, used, start_link, 0)
    own_link = link.shape[0] - 2
    for block in range(2):
        load_link(own_link + block).start()
    late_table[:, 0:width] = sources[-1][...]
    late_table[:, width:] = jnp.ones((late_table.shape[0], width), low)
    filled = 0
    for source in sources:
        held = own_table.shape[0] * source.shape[0] // sum(item.shape[0] for item in sources)
        own_table[filled : filled + held, :] = source[0:held, :].astype(jnp.float32)
        filled += held

    w_in = weights_in[...].astype(low).reshape(2 * weights_in.shape[1], hidden)
    bias_in = biases[:, 0:hidden]
    bias_mid = biases[:, hidden : 2 * hidden]
    bias_out = jnp.concatenate(
        [
            biases[:, 2 * hidden : 2 * hidden + classes],
            jnp.full((1, wide - classes), -1e30, jnp.float32),
        ],
        axis=1,
    )

    sums[...] = jnp.zeros_like(sums)

    def paired(block):
        return jnp.concatenate([link[block], link[block + 1]], axis=1)

    def forward(pair, carry):
        rows = pl.ds(pl.multiple_of(pair * 2 * SPAN, 2 * SPAN), 2 * SPAN)
        slot = lax.rem(pair, 2)
        for copy in load(pair, slot):
            copy.wait()
        load_link(2 * pair).wait()
        load_link(2 * pair + 1).wait()

        @pl.when(2 * pair + 2 < used)
        def _():
            for copy in load(pair + 1, 1 - slot):
                copy.start()

        copy_rows(places, pair * 2 * SPAN, 2 * SPAN, own_table, own_rows)
        joined[...] = dot(late[slot].astype(low), late_table[...]) + early[slot]
        mixin[rows, 0:width] = own_rows[...].astype(low)
        mixin[rows, width:] = (
            joined[:, 0:width] / jnp.maximum(joined[:, width:], 1.0)
        ).astype(low)
        z = dot(mixin[rows, :], w_in) + bias_in
        s = 1.0 / (1.0 + jnp.exp(-z))
        slopes[rows, :] = s * (1.0 + z * (1.0 - s))
        hid[...] = (z * s).astype(low)
        sums[0:targets, :] += dot(paired(2 * pair), hid[...])

        @pl.when(pair == 0)
        def _():
            for block in range(2):
                load_link(own_link + block).wait()
            sums[targets:, :] = dot(paired(own_link), hid[...])

        return carry

    pairs = lax.div(used, 2)
    lax.fori_loop(0, pairs, forward, 0)
    total = sums[...]
    counts_two = clipped_counts(near_two[...] >= 0)
    mixed_one = (total[0:targets] / counts_two).astype(low)
    self_one = total[targets:].astype(low)
    w_mid = weights_mid[...].astype(low)
    both_one = jnp.concatenate([self_one, mixed_one], axis=1)
    z = dot(both_one, w_mid.reshape(2 * hidden, hidden)) + bias_mid
    s = 1.0 / (1.0 + jnp.exp(-z))
    slope_mid = s * (1.0 + z * (1.0 - s))
    hidden_two = (z * s).astype(low)

    here = near_three[...]
    place = lax.broadcasted_iota(jnp.int32, (seeds, targets), 1)
    number = jnp.zeros((seeds, targets), jnp.float32)
    for j in range(here.shape[1]):
        number = number + jnp.where(here[:, j : j + 1] == place, 1.0, 0.0)
    number = number.astype(low)
    counts_three = clipped_counts(here >= 0)
    mixed_two = (dot(number, hidden_two) / counts_three).astype(low)
    self_two = hidden_two[0:seeds]
    w_out = [
        jnp.concatenate(
            [weights_out[:, k, :], jnp.zeros((wide - classes, hidden), jnp.float32)], axis=0
        ).astype(low)
        for k in range(2)
    ]
    both_two = jnp.concatenate([self_two, mixed_two], axis=1)
    logits = dot_cols(both_two, jnp.concatenate(w_out, axis=1)) + bias_out
    top = jnp.max(logits, axis=1, keepdims=True)
    log_total = top + jnp.log(jnp.sum(jnp.exp(logits - top), axis=1, keepdims=True))
    onehot = jnp.where(
        label.astype(jnp.int32) == lax.broadcasted_iota(jnp.int32, (seeds, wide), 1), 1.0, 0.0
    )
    picked = jnp.sum(jnp.where(onehot > 0.0, logits, 0.0), axis=1, keepdims=True)
    loss = jnp.sum(marked * (log_total - picked), axis=0, keepdims=True)
    counted = jnp.sum(marked, axis=0, keepdims=True)
    grad_out = (marked * (jnp.exp(logits - log_total) - onehot)).astype(low)

    out_sums[...] = dot_rows(grad_out, both_two)
    bias_grad_out = jnp.sum(grad_out.astype(jnp.float32), axis=0, keepdims=True)
    to_self = dot(grad_out, w_out[0])
    spread = (dot(grad_out, w_out[1]) / counts_three).astype(low)
    sums[0:targets, :] = dot_rows(number, spread)
    sums[0:seeds, :] += to_self
    grad_mid = (sums[0:targets, :] * slope_mid).astype(low)

    mid_sums[...] = dot_rows(both_one, grad_mid)
    bias_grad_mid = jnp.sum(grad_mid.astype(jnp.float32), axis=0, keepdims=True)
    down = jnp.concatenate(
        [dot_cols(grad_mid, w_mid[1]) / counts_two, dot_cols(grad_mid, w_mid[0])], axis=0
    )
    down_low[...] = down.astype(low)

    weight_sums[...] = jnp.zeros_like(weight_sums)

    def backward(pair, bias):
        rows = pl.ds(pl.multiple_of(pair * 2 * SPAN, 2 * SPAN), 2 * SPAN)
        joined[...] = dot_rows(paired(2 * pair), down_low[0:targets, :])

        @pl.when(pair == 0)
        def _():
            joined[...] += dot_rows(paired(own_link), down_low[targets:, :])

        grad = (joined[...] * slopes[rows, :]).astype(low)
        weight_sums[...] += dot_rows(mixin[rows, :], grad)
        return bias + jnp.sum(grad.astype(jnp.float32), axis=0, keepdims=True)

    bias_grad_in = lax.fori_loop(0, pairs, backward, jnp.zeros((1, hidden), jnp.float32))

    row = 0
    for part in (weight_sums, mid_sums):
        for column in range(0, hidden, LANES):
            packed[row : row + part.shape[0], :] = part[:, column : column + LANES]
            row += part.shape[0]
    tall = up(classes, 16)
    for column in range(0, 2 * hidden, LANES):
        packed[row : row + tall, :] = out_sums[0:tall, column : column + LANES]
        row += tall
    packed[row:, :] = jnp.zeros((packed.shape[0] - row, LANES), jnp.float32)
    lane = lax.broadcasted_iota(jnp.int32, (1, LANES), 1)
    scalars = jnp.where(lane == 0, loss, 0.0) + jnp.where(lane == 1, counted, 0.0)
    extra = [
        item[:, column : column + LANES]
        for item in (bias_grad_in, bias_grad_mid, bias_grad_out)
        for column in range(0, hidden, LANES)
    ] + [scalars, jnp.zeros((1, LANES), jnp.float32)]
    extra = jnp.concatenate(extra, axis=0)
    high = extra.astype(low).astype(jnp.float32)
    packed[packed.shape[0] - 16 :, :] = jnp.concatenate([high, extra - high], axis=0)
    half = keep.shape[0]
    keep[...] = packed[pl.ds(pl.multiple_of(core * half, 16), half), :].astype(low)
    send[...] = packed[pl.ds(pl.multiple_of((1 - core) * half, 16), half), :].astype(low)


def run_step(info, count, places, partial, tallies, links, sources, rest, half, classes, held):
    padded = tallies.shape[0]
    blocks, targets = padded // SPAN, links.shape[1]
    total, width = sources[-1].shape
    hidden = rest[4].shape[2]
    wide = up(classes, LANES)
    return call(
        functools.partial(step_kernel, classes=classes),
        "step",
        (jax.ShapeDtypeStruct((half, LANES), jnp.bfloat16),) * 2,
        [smem] * 3 + [anywhere] * 3 + [vmem] * (PARTS + 8),
        (vmem, vmem),
        [
            pltpu.VMEM((padded, hidden), jnp.float32),
            pltpu.VMEM((2 * half, LANES), jnp.float32),
            pltpu.VMEM((2 * targets, hidden), jnp.float32),
            pltpu.VMEM((2 * width, hidden), jnp.float32),
            pltpu.VMEM((2 * hidden, hidden), jnp.float32),
            pltpu.VMEM((wide, 2 * hidden), jnp.float32),
            pltpu.VMEM((held, width), jnp.float32),
            pltpu.VMEM((total, 2 * width), jnp.bfloat16),
            pltpu.VMEM((padded, 2 * width), jnp.bfloat16),
            pltpu.VMEM((2 * SPAN, width), jnp.float32),
            pltpu.VMEM((2 * SPAN, 2 * width), jnp.float32),
            pltpu.VMEM((2, 2 * SPAN, total), COUNTS),
            pltpu.VMEM((2, 2 * SPAN, 2 * width), jnp.float32),
            pltpu.VMEM((2 * SPAN, hidden), jnp.bfloat16),
            pltpu.VMEM((2 * targets, hidden), jnp.bfloat16),
            pltpu.VMEM((blocks + 2, targets, SPAN), jnp.bfloat16),
            pltpu.SemaphoreType.DMA((2, 2)),
            pltpu.SemaphoreType.DMA((blocks + 2,)),
        ],
        14.0,
        BIG,
    )(info, count, places, partial, tallies, links, *sources, *rest)


def refit(total, rows):
    extra = total[rows - 16 : rows - 8] + total[rows - 8 : rows]
    high = extra.astype(jnp.bfloat16).astype(jnp.float32)
    return jnp.concatenate([high, extra - high], axis=0)


def pair_kernel(info, mine, theirs, out):
    total = mine[...].astype(jnp.float32) + theirs[...].astype(jnp.float32)
    out[...] = total.astype(jnp.bfloat16)

    @pl.when(info[0] == 1)
    def _():
        rows = total.shape[0]
        out[rows - 16 :, :] = refit(total, rows).astype(jnp.bfloat16)


def pair_sum(info, mine, theirs):
    return call(
        pair_kernel,
        "pair_sum",
        jax.ShapeDtypeStruct(mine.shape, jnp.bfloat16),
        [smem, vmem, vmem],
        vmem,
        [],
        0.6,
        6 << 20,
    )(info, mine, theirs)


def spread_kernel(info, pieces, out):
    total = pieces[0].astype(jnp.float32)
    for k in range(1, pieces.shape[0]):
        total = total + pieces[k].astype(jnp.float32)
    rows = total.shape[0]
    fitted = jnp.concatenate([total[0 : rows - 16], refit(total, rows)], axis=0)
    result = jnp.where(info[1] == 1, fitted, total).astype(jnp.bfloat16)
    for k in range(pieces.shape[0]):
        out[k] = result


def spread_sum(info, pieces):
    return call(
        spread_kernel,
        "spread_sum",
        jax.ShapeDtypeStruct(pieces.shape, jnp.bfloat16),
        [smem, vmem],
        vmem,
        [],
        0.6,
        6 << 20,
    )(info, pieces)


def update_kernel(
    info, fixes, mine, theirs, biases, moment_one, moment_two, *refs
):
    groups = [refs[5 * k : 5 * k + 5] for k in range(3)]
    loss_out = refs[15]
    outs = [refs[16 + 4 * k : 20 + 4 * k] for k in range(3)]
    bias_out, first_out, second_out = refs[28:31]
    packed = refs[31]
    low = jnp.bfloat16
    half = mine.shape[0]
    core = info[0]
    packed[pl.ds(pl.multiple_of(core * half, 16), half), :] = mine[...]
    packed[pl.ds(pl.multiple_of((1 - core) * half, 16), half), :] = theirs[...]
    last = packed.shape[0]
    extra = packed[last - 16 :, :].astype(jnp.float32)
    extra = extra[0:8] + extra[8:16]
    counted = extra[6:7, 1:2]
    inverse = 1.0 / counted
    loss_out[...] = extra[6:7, 0:1] / counted
    scale = 0.5 * inverse * inverse

    row = 0
    for group in range(3):
        master, left, right, left_root, right_root = groups[group]
        new_master, copy, new_left, new_right = outs[group]
        turned = group == 2
        depth, hidden = (master.shape[0], master.shape[2]) if turned else master.shape[1:]
        deep = up(depth, LANES)

        def take(ref, k, middle):
            return ref[:, k, :] if middle else ref[k]

        def put(ref, k, middle, value):
            if middle:
                ref[:, k, :] = value
            else:
                ref[k] = value

        grads = []
        if turned:
            tall = up(depth, 16)
            for k in range(2):
                parts = []
                for column in range(0, hidden, LANES):
                    parts.append(packed[row : row + tall, :])
                    row += tall
                grads.append(grown(jnp.concatenate(parts, axis=1), deep, hidden))
        else:
            parts = []
            for column in range(0, hidden, LANES):
                parts.append(packed[row : row + 2 * depth, :])
                row += 2 * depth
            whole = jnp.concatenate(parts, axis=1)
            grads = [whole[k * depth : (k + 1) * depth] for k in range(2)]

        for k in range(2):
            grad = grads[k]
            for old, new, size, product, middle in (
                (left, new_left, depth, dot_cols(grad, grad), turned),
                (right, new_right, hidden, dot_rows(grad, grad), False),
            ):
                corner = old[0:1, k, 0:1] if middle else old[k, 0:1, 0:1]
                eye = lax.broadcasted_iota(jnp.int32, (size, size), 0) == (
                    lax.broadcasted_iota(jnp.int32, (size, size), 1)
                )
                value = jnp.where(eye, 0.5 * corner, 0.0) + scale * product[0:size, 0:size]
                put(new, k, middle, value)
            root = jnp.concatenate(
                halves(grown(take(left_root, k, turned), deep, deep)), axis=1
            )
            middle_high, middle_rest = halves(dot(root, jnp.concatenate([grad, grad], axis=0)))
            root_high, root_rest = halves(right_root[k])
            way = dot(
                jnp.concatenate([middle_high, middle_high, middle_rest], axis=1),
                jnp.concatenate([root_high, root_rest, root_high], axis=0),
            )[0:depth]
            put(new_master, k, turned, take(master, k, turned) - inverse * way)
        copy[...] = new_master[...].astype(low)

    size = biases.shape[0]
    grad = jnp.concatenate([extra[k : k + 1, :] for k in range(6)], axis=1)[:, 0:size]
    grad = grad / counted

    def line(ref):
        return ref[...].reshape(1, size)

    first = 0.9 * line(moment_one) + 0.1 * grad
    second = 0.95 * line(moment_two) + 0.05 * grad * grad
    old = line(biases)
    fresh = old - 0.1 * (
        (first / fixes[0]) / (jnp.sqrt(second / fixes[1]) + 1e-08) + 0.01 * old
    )
    for ref, value in ((bias_out, fresh), (first_out, first), (second_out, second)):
        ref[...] = value[0]


def run_update(info, fixes, mine, theirs, vectors, groups):
    outs = [jax.ShapeDtypeStruct((1, 1), jnp.float32)]
    flat = []
    for master, left, right, left_root, right_root in groups:
        flat += [master, left, right, left_root, right_root]
        outs += [
            jax.ShapeDtypeStruct(master.shape, jnp.float32),
            jax.ShapeDtypeStruct(master.shape, jnp.bfloat16),
            jax.ShapeDtypeStruct(left_root.shape, jnp.float32),
            jax.ShapeDtypeStruct(right_root.shape, jnp.float32),
        ]
    outs += [jax.ShapeDtypeStruct(vectors[0].shape, jnp.float32)] * 3
    return call(
        update_kernel,
        "update",
        tuple(outs),
        [smem] * 2 + [vmem] * (5 + len(flat)),
        (vmem,) * len(outs),
        [pltpu.VMEM((2 * mine.shape[0], LANES), jnp.bfloat16)],
        4.0,
        16 << 20,
    )(info, fixes, mine, theirs, *vectors, *flat)


def body(
    features,
    requests,
    adjacent_one,
    adjacent_two,
    adjacent_three,
    valid_one,
    valid_two,
    valid_three,
    labels,
    labelled,
    weights_in,
    weights_mid,
    weights_out,
    biases,
    moment_one,
    moment_two,
    step_count,
    left_in,
    left_mid,
    left_out,
    right_in,
    right_mid,
    right_out,
    invleft_in,
    invleft_mid,
    invleft_out,
    invright_in,
    invright_mid,
    invright_out,
    *,
    peers,
):
    width = features.shape[1]
    devices, per = requests.shape
    targets = adjacent_one.shape[0]
    padded = up(targets, 2 * SPAN)
    classes = weights_out.shape[2]
    hidden = weights_in.shape[2]
    core = lax.axis_index("core")
    own = lax.axis_index(PEERS)

    wanted = lax.all_to_all(requests, AXES, split_axis=0, concat_axis=0, tiled=True)
    names, places, near_two, near_three, count = reach(
        adjacent_three, valid_three, labelled, adjacent_two, valid_two, targets, per
    )
    wanted, count = lax.optimization_barrier((wanted.reshape(-1), count))
    early_cut, late_cut = cuts(per)

    def trade(found):
        pulled = lax.all_to_all(
            found.reshape(devices, -1, width), AXES, split_axis=0, concat_axis=0, tiled=True
        )
        return pulled.reshape(-1, width)

    early_source = trade(pick_rows(wanted, features, per, early_cut))
    found = pick_rows(wanted, features, per, late_cut)
    links = link_matrix(count, names, near_two, adjacent_two.shape[1], padded)
    names, places = names.reshape(-1), places.reshape(-1)
    late_tally = tally(
        count, names, adjacent_one, valid_one, padded, devices, per, 1, ()
    )

    core_info = jnp.stack([core, ((core == 1) & (own == peers - 1)).astype(jnp.int32)])
    core_info = core_info.astype(jnp.int32)
    stepped = step_count.astype(jnp.float32)
    fixes = jnp.stack([1.0 - 0.9**stepped, 1.0 - 0.95**stepped])
    found, late_tally, links, info, fixes = lax.optimization_barrier(
        (found, late_tally, links, core_info, fixes)
    )
    late_source = trade(found)
    partial = tally(
        count, names, adjacent_one, valid_one, padded, devices, per, 0, (early_source,)
    )

    rows = (2 * width + 2 * weights_mid.shape[1]) * (hidden // LANES)
    rows += up(classes, 16) * (2 * hidden // LANES)
    each = up(-(-(rows + 16) // (2 * peers)), 8)
    half = each * peers
    turned_out = weights_out.transpose(2, 0, 1)
    keep, send = run_step(
        info,
        count,
        places,
        partial,
        late_tally,
        links,
        (early_source, late_source),
        (
            near_two,
            near_three,
            labels,
            labelled,
            weights_in,
            weights_mid,
            turned_out,
            biases,
        ),
        half,
        classes,
        -(-targets // per) * per,
    )
    swap = [(0, 1), (1, 0)]
    theirs = lax.ppermute(send, "core", swap)
    summed = pair_sum(info, keep, theirs).reshape(peers, each, LANES)
    pieces = lax.all_to_all(summed, PEERS, split_axis=0, concat_axis=0, tiled=True)
    shared = spread_sum(info, pieces)
    mine = lax.all_to_all(shared, PEERS, split_axis=0, concat_axis=0, tiled=True)
    mine = mine.reshape(half, LANES)
    theirs = lax.ppermute(mine, "core", swap)

    outs = run_update(
        info,
        fixes,
        mine,
        theirs,
        (biases, moment_one, moment_two),
        (
            (weights_in, left_in, right_in, invleft_in, invright_in),
            (weights_mid, left_mid, right_mid, invleft_mid, invright_mid),
            (
                turned_out,
                right_out.transpose(1, 0, 2),
                left_out,
                invright_out.transpose(1, 0, 2),
                invleft_out,
            ),
        ),
    )
    first, second, third = (outs[1 + 4 * k : 5 + 4 * k] for k in range(3))
    third = (
        third[0].transpose(1, 2, 0),
        third[1].transpose(1, 2, 0),
        third[3],
        third[2].transpose(1, 0, 2),
    )
    return (
        (outs[0].reshape(()),)
        + tuple(group[which] for which in range(4) for group in (first, second, third))
        + tuple(outs[13:16])
    )


def solution(mesh):
    chips, dev = mesh.shape["hst"] // 2, mesh.shape["dev"]
    fine = jax.sharding.Mesh(mesh.devices.reshape(chips, 2, dev), AXES)
    split = P(AXES, None)
    line = P(AXES)
    whole = P()
    mapped = jax.shard_map(
        functools.partial(body, peers=chips * dev),
        mesh=fine,
        in_specs=(split,) * 8 + (line,) * 2 + (whole,) * 19,
        out_specs=(whole,) * 16,
        check_vma=False,
    )

    def run(*args):
        with jax.sharding.use_abstract_mesh(fine.abstract_mesh):
            return mapped(*args)

    return run
```

```python
import functools

import jax
import jax.numpy as jnp
from jax import lax
from jax.experimental import pallas as pl
from jax.experimental.pallas import tpu as pltpu
from jax.sharding import PartitionSpec as P

LANES = 128
SPAN = 256
PARTS = 2
COUNTS = jnp.float8_e4m3fn
BIG = 52 << 20
AXES = ("chip", "core", "dev")
PEERS = ("chip", "dev")

smem = pl.BlockSpec(memory_space=pltpu.SMEM)
vmem = pl.BlockSpec(memory_space=pltpu.VMEM)
anywhere = pl.BlockSpec(memory_space=pltpu.HBM)


def up(value, unit):
    return -(-value // unit) * unit


def call(kernel, name, out_shape, in_specs, out_specs, scratch, cost, room):
    return pl.pallas_call(
        kernel,
        name=name,
        out_shape=out_shape,
        in_specs=in_specs,
        out_specs=out_specs,
        scratch_shapes=scratch,
        compiler_params=pltpu.CompilerParams(vmem_limit_bytes=room),
        cost_estimate=pl.CostEstimate(
            flops=0, transcendentals=0, bytes_accessed=int(cost * 3.6e6)
        ),
    )


def dot(left, right):
    return jnp.dot(left, right, preferred_element_type=jnp.float32)


def dot_rows(left, right):
    return lax.dot_general(
        left, right, (((0,), (0,)), ((), ())), preferred_element_type=jnp.float32
    )


def dot_cols(left, right):
    return lax.dot_general(
        left, right, (((1,), (1,)), ((), ())), preferred_element_type=jnp.float32
    )


def halves(value):
    high = value.astype(jnp.bfloat16)
    return high, (value - high.astype(jnp.float32)).astype(jnp.bfloat16)


def grown(value, rows, columns):
    short = columns - value.shape[1]
    if short:
        value = jnp.concatenate([value, jnp.zeros((value.shape[0], short), value.dtype)], axis=1)
    short = rows - value.shape[0]
    if short:
        value = jnp.concatenate([value, jnp.zeros((short, columns), value.dtype)], axis=0)
    return value


def clipped_counts(valid):
    return jnp.maximum(jnp.sum(valid.astype(jnp.float32), axis=1, keepdims=True), 1.0)


def copy_rows(names, base, size, source, target):
    for u in range(size):
        target[u : u + 1, :] = source[pl.ds(names[base + u], 1), :]


def cuts(per):
    return (0, per // 2), (per // 2, per)


def pick_kernel(wanted, table, out, rows, done, sems, *, first, part, per):
    chunk = rows.shape[0]
    devices = chunk // part

    def save(step):
        where = pl.ds(pl.multiple_of(step * chunk, chunk), chunk)
        return pltpu.make_async_copy(done.at[where, :], out.at[where, :], sems.at[step])

    def body(step, carry):
        for d in range(devices):
            base = (step * devices + d) * per + first
            for u in range(part):
                at = d * part + u
                rows[at : at + 1, :] = table[pl.ds(wanted[base + u], 1), :]
        where = pl.ds(pl.multiple_of(step * chunk, chunk), chunk)
        done[where, :] = rows[...].astype(jnp.bfloat16)
        save(step).start()
        return carry

    lax.fori_loop(0, out.shape[0] // chunk, body, 0)
    for step in range(out.shape[0] // chunk):
        save(step).wait()


def pick_rows(wanted, table, per, ends):
    first, last = ends
    width = table.shape[1]
    count = wanted.shape[0] // per * (last - first)
    chunk = 512
    return call(
        functools.partial(pick_kernel, first=first, part=last - first, per=per),
        "pick_rows",
        jax.ShapeDtypeStruct((count, width), jnp.bfloat16),
        [smem, vmem],
        anywhere,
        [
            pltpu.VMEM((chunk, width), jnp.float32),
            pltpu.VMEM((count, width), jnp.bfloat16),
            pltpu.SemaphoreType.DMA((count // chunk,)),
        ],
        4.6,
        20 << 20,
    )(wanted, table)


def stood(flat, unit):
    size = flat.shape[1]
    flat = jnp.concatenate(
        [flat, jnp.full((unit - flat.shape[0], size), -1, jnp.int32)], axis=0
    ).astype(jnp.float32)
    step = min(LANES, size)
    parts = [jnp.transpose(flat[:, k : k + step]) for k in range(0, size, step)]
    return jnp.concatenate(parts, axis=0).astype(jnp.int32)


def reach_kernel(
    adjacent_three,
    valid_three,
    labelled,
    adjacent_two,
    valid_two,
    names,
    places,
    near_two,
    near_three,
    count,
    left,
    right,
    *,
    rows_all,
    per,
):
    fan_three, seeds = adjacent_three.shape
    fan_two, targets = adjacent_two.shape
    low = jnp.bfloat16
    blocks = rows_all // LANES
    deep = names.shape[0]
    line = labelled[...].reshape(1, seeds)
    column = jnp.transpose(jnp.broadcast_to(line.astype(jnp.float32), (8, seeds)))[:, 0:1]
    near = stood(jnp.where(valid_three[...] > 0, adjacent_three[...], -1), near_three.shape[1])
    near_three[...] = near
    here = jnp.where(column > 0.0, near, -1)
    place = lax.broadcasted_iota(jnp.int32, (seeds, targets), 1)
    hit = jnp.zeros((seeds, targets), jnp.float32)
    for j in range(fan_three):
        hit = hit + jnp.where(here[:, j : j + 1] == place, 1.0, 0.0)
    need = jnp.max(hit, axis=0, keepdims=True) + jnp.concatenate(
        [line.astype(jnp.float32), jnp.zeros((1, targets - seeds), jnp.float32)], axis=1
    )

    level = lax.broadcasted_iota(jnp.int32, (deep, targets), 0)
    lane = lax.broadcasted_iota(jnp.int32, (targets, LANES), 1)
    flat = jnp.where(valid_two[...] > 0, adjacent_two[...], -1)
    tall = stood(flat, near_two.shape[1])
    near_two[...] = tall
    flat = jnp.where(need > 0.0, flat, -1)
    for j in range(fan_two):
        left[0:deep, j * targets : (j + 1) * targets] = jnp.where(
            lax.shift_right_arithmetic(flat[j : j + 1, :], 7) == level, 1.0, 0.0
        ).astype(low)
        right[j * targets : (j + 1) * targets, :] = jnp.where(
            (tall[:, j : j + 1] & (LANES - 1)) == lane, 1.0, 0.0
        ).astype(low)
    used = dot(left[0:deep, 0 : fan_two * targets], right[0 : fan_two * targets, :])
    own = [need[:, k : k + LANES] for k in range(0, targets, LANES)]
    own = jnp.concatenate(
        own + [jnp.zeros((deep - len(own), LANES), jnp.float32)], axis=0
    )
    flag = jnp.where(used + own > 0.0, 1.0, 0.0)

    square_row = lax.broadcasted_iota(jnp.int32, (LANES, LANES), 0)
    square_col = lax.broadcasted_iota(jnp.int32, (LANES, LANES), 1)
    full = jnp.concatenate([flag, jnp.zeros((LANES - deep, LANES), jnp.float32)], axis=0)
    flag_low = full.astype(low)
    running = dot(flag_low, jnp.where(square_row <= square_col, 1.0, 0.0).astype(low))
    totals = dot(flag_low, jnp.ones((LANES, LANES), low)).astype(low)
    before = dot(jnp.where(square_row > square_col, 1.0, 0.0).astype(low), totals)
    order = (before + running - full).astype(jnp.int32)
    number = jnp.sum(flag).astype(jnp.int32)
    count[0] = number
    count[1] = lax.div(number + (SPAN - 1), SPAN)

    high = jnp.where(full > 0.0, lax.shift_right_arithmetic(order, 7), -1)
    rest = jnp.transpose((order & (LANES - 1)).astype(jnp.float32)).astype(jnp.int32)
    step = lax.broadcasted_iota(jnp.int32, (deep, LANES), 0)
    inner = lax.broadcasted_iota(jnp.int32, (deep, LANES), 1).astype(jnp.float32)
    for b in range(blocks):
        match = jnp.where(high[b : b + 1, :] == step, 1.0, 0.0)
        lanes = slice(b * LANES, (b + 1) * LANES)
        left[0:deep, lanes] = (match * inner).astype(low)
        left[deep : 2 * deep, lanes] = (match * float(b)).astype(low)
        right[lanes, :] = jnp.where(rest[:, b : b + 1] == square_col, 1.0, 0.0).astype(low)
    found = dot(left[:, 0:rows_all], right[0:rows_all, :]).astype(jnp.int32)
    where = step * LANES + lax.broadcasted_iota(jnp.int32, (deep, LANES), 1)
    name = found[deep:] * LANES + found[0:deep]
    names[...] = jnp.where(where < number, name, rows_all)
    name = jnp.minimum(jnp.where(where < number, name, 0), rows_all - 1)
    owners = -(-rows_all // per)
    owner = lax.shift_right_logical(name, per.bit_length() - 1)
    slot = name & (per - 1)
    early, late = (last - first for first, last in cuts(per))
    places[...] = jnp.where(
        slot < early, owner * early + slot, owners * early + owner * late + slot - early
    )


def reach(adjacent_three, valid_three, labelled, adjacent_two, valid_two, rows_all, per):
    targets, fan = adjacent_two.shape
    seeds = labelled.shape[0]
    deep = up(up(rows_all, 2 * SPAN) // LANES, 16)
    area = max(fan * targets, rows_all)
    return call(
        functools.partial(reach_kernel, rows_all=rows_all, per=per),
        "reach",
        (
            jax.ShapeDtypeStruct((deep, LANES), jnp.int32),
            jax.ShapeDtypeStruct((deep, LANES), jnp.int32),
            jax.ShapeDtypeStruct((targets, 16), jnp.int32),
            jax.ShapeDtypeStruct((seeds, 8), jnp.int32),
            jax.ShapeDtypeStruct((2,), jnp.int32),
        ),
        [vmem] * 5,
        (vmem,) * 4 + (smem,),
        [
            pltpu.VMEM((2 * deep, area), jnp.bfloat16),
            pltpu.VMEM((area, LANES), jnp.bfloat16),
        ],
        3.0,
        8 << 20,
    )(adjacent_three.T, valid_three.T, labelled, adjacent_two.T, valid_two.T)


def tally_kernel(count, names, adjacent, valid, *refs, per, which):
    multiply = which == 0
    if multiply:
        source, out, table, rows, spread, marked, buffer, sems, terms, sums = refs
        width = source.shape[1]
        terms[:, 0:width] = source[...]
        terms[:, width:] = jnp.ones((source.shape[0], width), jnp.bfloat16)
    else:
        out, table, rows, spread, marked, buffer, sems = refs
    low = jnp.bfloat16
    fan, targets = adjacent.shape
    unit = spread.shape[0]
    groups = SPAN // unit
    few = 8 if multiply else groups
    used = count[1]
    high_all = buffer.shape[2] // SPAN
    first, last = cuts(per)[which]
    size = last - first

    slot = adjacent[...]
    owner = lax.shift_right_logical(slot, per.bit_length() - 1)
    inner = slot & (per - 1)
    here = (valid[...] > 0) & (inner >= first) & (inner < last)
    slot = jnp.where(here, owner * size + inner - first, -1)
    slot = jnp.concatenate([slot, jnp.full((unit - fan, targets), -1, jnp.int32)], axis=0)
    slot = slot.astype(jnp.float32)
    for b in range(0, targets, LANES):
        table[b : b + LANES, :] = jnp.transpose(slot[:, b : b + LANES]).astype(jnp.int32)
    table[targets:, :] = jnp.full((table.shape[0] - targets, unit), -1, jnp.int32)

    across = lax.broadcasted_iota(jnp.int32, (unit, SPAN), 1)
    down = lax.broadcasted_iota(jnp.int32, (unit, SPAN), 0)
    spread[...] = jnp.where(lax.div(across, unit) == down, 1.0, 0.0).astype(low)
    lane = across.astype(jnp.float32).astype(low)
    one = jnp.ones((unit, SPAN), low)
    zero = jnp.zeros((unit, SPAN), low)

    def copies(block, slot):
        where = pl.ds(pl.multiple_of(block * SPAN, SPAN), SPAN)
        result = sums if multiply else buffer
        return pltpu.make_async_copy(result.at[slot], out.at[where, :], sems.at[slot])

    def body(block, carry):
        slot = lax.rem(block, 2)

        @pl.when(block >= 2)
        def _():
            copies(block - 2, slot).wait()

        copy_rows(names, block * SPAN, SPAN, table, rows)
        high = lax.shift_right_arithmetic(rows[...], 8).astype(jnp.float32).astype(low)
        own = lax.rem(lax.broadcasted_iota(jnp.int32, (SPAN, SPAN), 0), unit) == lax.rem(
            lax.broadcasted_iota(jnp.int32, (SPAN, SPAN), 1), unit
        )
        marked[...] = jnp.where(own, dot(high, spread[...]), -1.0).astype(low)

        def single(g):
            first = pl.multiple_of(g * unit, unit)
            rest = (rows[pl.ds(first, unit), :] & (SPAN - 1)).astype(jnp.float32)
            columns = [
                jnp.where(
                    jnp.broadcast_to(rest[:, j : j + 1], (unit, SPAN)).astype(low) == lane,
                    one,
                    zero,
                )
                for j in range(unit)
            ]
            mark = marked[pl.ds(first, unit), :]
            marks = [
                jnp.where(mark == jnp.full((unit, SPAN), float(q), low), one, zero)
                for q in range(high_all)
            ]
            return dot(jnp.concatenate(marks, axis=0), jnp.concatenate(columns, axis=0))

        def group(step, inner):
            for u in range(0, few, 2):
                pair = [single(step * few + u), single(step * few + u + 1)]
                where = pl.ds(pl.multiple_of((step * few + u) * unit, 2 * unit), 2 * unit)
                for q in range(high_all):
                    tile = jnp.concatenate(
                        [item[q * unit : (q + 1) * unit] for item in pair], axis=0
                    )
                    buffer[slot, where, q * SPAN : (q + 1) * SPAN] = tile.astype(buffer.dtype)
            return inner

        lax.fori_loop(0, groups // few, group, 0)
        if multiply:
            sums[slot] = dot(buffer[slot], terms[...])
        copies(block, slot).start()
        return carry

    lax.fori_loop(0, used, body, 0)

    @pl.when(used >= 2)
    def _():
        copies(used - 2, lax.rem(used - 2, 2)).wait()

    @pl.when(used >= 1)
    def _():
        copies(used - 1, lax.rem(used - 1, 2)).wait()


def tally(count, names, adjacent, valid, padded, devices, per, which, sources):
    targets = adjacent.shape[0]
    unit = 16
    first, last = cuts(per)[which]
    wide = devices * (last - first)
    multiply = which == 0
    width = sources[0].shape[1] if multiply else 0
    scratch = [
        pltpu.VMEM((targets + 8, unit), jnp.int32),
        pltpu.VMEM((SPAN, unit), jnp.int32),
        pltpu.VMEM((unit, SPAN), jnp.bfloat16),
        pltpu.VMEM((SPAN, SPAN), jnp.bfloat16),
        pltpu.VMEM((2, SPAN, wide), jnp.bfloat16 if multiply else COUNTS),
        pltpu.SemaphoreType.DMA((2,)),
    ]
    if multiply:
        out = jax.ShapeDtypeStruct((3 * padded, 2 * width), jnp.float32)
        scratch += [
            pltpu.VMEM((wide, 2 * width), jnp.bfloat16),
            pltpu.VMEM((2, SPAN, 2 * width), jnp.float32),
        ]
    else:
        out = jax.ShapeDtypeStruct((padded, wide), COUNTS)
    return call(
        functools.partial(tally_kernel, per=per, which=which),
        "early_sums" if multiply else "tally",
        out,
        [smem, smem] + [vmem] * (2 + len(sources)),
        anywhere,
        scratch,
        14.0,
        BIG,
    )(count, names, adjacent.T, valid.T, *sources)


def link_kernel(count, names, near, out, buffer, sems, *, fan):
    targets = near.shape[0]
    tile = 32
    blocks = count[1]
    all_blocks = buffer.shape[0] - 2
    across = SPAN // LANES

    def line(block, part):
        return jnp.broadcast_to(names[pl.ds(block * across + part, 1), :], (tile, LANES))

    def save(block):
        return pltpu.make_async_copy(buffer.at[block], out.at[block], sems.at[block])

    def rows(step, carry):
        first = pl.multiple_of(step * tile, tile)
        here = near[pl.ds(first, tile), :]
        spread = [jnp.broadcast_to(here[:, j : j + 1], (tile, LANES)) for j in range(fan)]
        own = first + lax.broadcasted_iota(jnp.int32, (tile, LANES), 0)

        def columns(block, inner):
            for part in range(across):
                name = line(block, part)
                number = jnp.zeros((tile, LANES), jnp.float32)
                for j in range(fan):
                    number = number + jnp.where(spread[j] == name, 1.0, 0.0)
                lanes = pl.ds(part * LANES, LANES)
                buffer[block, pl.ds(first, tile), lanes] = number.astype(jnp.bfloat16)
            return inner

        lax.fori_loop(0, blocks, columns, 0)
        for block in range(2):
            for part in range(across):
                lanes = slice(part * LANES, (part + 1) * LANES)
                buffer[all_blocks + block, pl.ds(first, tile), lanes] = jnp.where(
                    own == line(block, part), 1.0, 0.0
                ).astype(jnp.bfloat16)
        return carry

    lax.fori_loop(0, targets // tile, rows, 0)

    def start(block, carry):
        save(block).start()
        return carry

    def finish(block, carry):
        save(block).wait()
        return carry

    for ends in ((0, blocks), (all_blocks, all_blocks + 2)):
        lax.fori_loop(*ends, start, 0)
    for ends in ((0, blocks), (all_blocks, all_blocks + 2)):
        lax.fori_loop(*ends, finish, 0)


def link_matrix(count, names, near, fan, padded):
    blocks = padded // SPAN
    targets = near.shape[0]
    return call(
        functools.partial(link_kernel, fan=fan),
        "link_matrix",
        jax.ShapeDtypeStruct((4 * blocks, targets, SPAN), jnp.bfloat16),
        [smem, vmem, vmem],
        anywhere,
        [
            pltpu.VMEM((blocks + 2, targets, SPAN), jnp.bfloat16),
            pltpu.SemaphoreType.DMA((blocks + 2,)),
        ],
        5.0,
        BIG,
    )(count, names, near)


def step_kernel(
    info,
    count,
    places,
    partial,
    tallies,
    links,
    *refs,
    classes,
):
    sources = refs[:PARTS]
    step_body(
        info, count, places, partial, tallies, links, sources, *refs[PARTS:],
        classes=classes,
    )


def step_body(
    info,
    count,
    places,
    partial,
    tallies,
    links,
    sources,
    near_two,
    near_three,
    labels,
    labelled,
    weights_in,
    weights_mid,
    weights_out,
    biases_line,
    keep,
    send,
    slopes,
    packed,
    sums,
    weight_sums,
    mid_sums,
    out_sums,
    own_table,
    late_table,
    mixin,
    own_rows,
    joined,
    late,
    early,
    hid,
    down_low,
    bias_sums,
    link,
    sems,
    link_sems,
    *,
    classes,
):
    targets = links.shape[1]
    hidden = weights_in.shape[2]
    seeds = labels.shape[0]
    biases = biases_line[...].reshape(1, biases_line.shape[0])
    label, marked = [
        jnp.transpose(
            jnp.broadcast_to(item[...].reshape(1, seeds).astype(jnp.float32), (8, seeds))
        )[:, 0:1]
        for item in (labels, labelled)
    ]
    wide = up(classes, LANES)
    core = info[0]
    used = count[1]
    low = jnp.bfloat16
    width = sources[0].shape[1]

    def load(pair, slot, size):
        rows = pl.ds(pl.multiple_of(pair * 2 * SPAN, 2 * SPAN), size)
        here = pl.ds(0, size)
        return (
            pltpu.make_async_copy(tallies.at[rows, :], late.at[slot, here, :], sems.at[slot, 0]),
            pltpu.make_async_copy(partial.at[rows, :], early.at[slot, here, :], sems.at[slot, 1]),
        )

    def start_load(pair, slot):
        @pl.when(2 * pair + 1 < used)
        def _():
            for copy in load(pair, slot, 2 * SPAN):
                copy.start()

        @pl.when(2 * pair + 1 == used)
        def _():
            for copy in load(pair, slot, SPAN):
                copy.start()

    def load_link(block):
        return pltpu.make_async_copy(links.at[block], link.at[block], link_sems.at[block])

    start_load(0, 0)

    def start_link(block, carry):
        load_link(block).start()
        return carry

    lax.fori_loop(0, used, start_link, 0)
    own_link = link.shape[0] - 2
    for block in range(2):
        load_link(own_link + block).start()
    late_table[:, 0:width] = sources[-1][...]
    late_table[:, width:] = jnp.ones((late_table.shape[0], width), low)
    filled = 0
    for source in sources:
        held = own_table.shape[0] * source.shape[0] // sum(item.shape[0] for item in sources)
        own_table[filled : filled + held, :] = source[0:held, :].astype(jnp.float32)
        filled += held

    w_in = weights_in[...].astype(low).reshape(2 * weights_in.shape[1], hidden)
    bias_in = biases[:, 0:hidden]
    bias_mid = biases[:, hidden : 2 * hidden]
    bias_out = jnp.concatenate(
        [
            biases[:, 2 * hidden : 2 * hidden + classes],
            jnp.full((1, wide - classes), -1e30, jnp.float32),
        ],
        axis=1,
    )

    sums[...] = jnp.zeros_like(sums)

    def paired(block, size):
        if size == SPAN:
            return link[block]
        return jnp.concatenate([link[block], link[block + 1]], axis=1)

    def forward(pair, size):
        base = pair * 2 * SPAN
        rows = pl.ds(pl.multiple_of(base, 2 * SPAN), size)
        slot = lax.rem(pair, 2)
        for copy in load(pair, slot, size):
            copy.wait()
        for step in range(size // SPAN):
            load_link(2 * pair + step).wait()
        start_load(pair + 1, 1 - slot)
        for part in range(0, size, SPAN):
            for u in range(part, part + SPAN):
                own_rows[u : u + 1, :] = own_table[pl.ds(places[base + u], 1), :]
            here = slice(part, part + SPAN)
            joined[here, :] = dot(late[slot, here, :].astype(low), late_table[...]) + (
                early[slot, here, :]
            )
        mixin[rows, 0:width] = own_rows[0:size, :].astype(low)
        mixin[rows, width:] = (
            joined[0:size, 0:width] / jnp.maximum(joined[0:size, width:], 1.0)
        ).astype(low)
        z = dot(mixin[rows, :], w_in) + bias_in
        s = 1.0 / (1.0 + jnp.exp(-z))
        slopes[rows, :] = s * (1.0 + z * (1.0 - s))
        hid[0:size, :] = (z * s).astype(low)
        sums[0:targets, :] += dot(paired(2 * pair, size), hid[0:size, :])

        @pl.when(pair == 0)
        def _():
            for block in range(2):
                load_link(own_link + block).wait()
            sums[targets:, :] = dot(paired(own_link, size), hid[0:size, :])

    pairs = lax.div(used, 2)
    odd = lax.rem(used, 2) == 1

    def forward_pair(pair, carry):
        forward(pair, 2 * SPAN)
        return carry

    lax.fori_loop(0, pairs, forward_pair, 0)

    @pl.when(odd)
    def _():
        forward(pairs, SPAN)

    total = sums[...]
    counts_two = clipped_counts(near_two[...] >= 0)
    mixed_one = (total[0:targets] / counts_two).astype(low)
    self_one = total[targets:].astype(low)
    w_mid = weights_mid[...].astype(low)
    both_one = jnp.concatenate([self_one, mixed_one], axis=1)
    z = dot(both_one, w_mid.reshape(2 * hidden, hidden)) + bias_mid
    s = 1.0 / (1.0 + jnp.exp(-z))
    slope_mid = s * (1.0 + z * (1.0 - s))
    hidden_two = (z * s).astype(low)

    here = near_three[...]
    place = lax.broadcasted_iota(jnp.int32, (seeds, targets), 1)
    number = jnp.zeros((seeds, targets), jnp.float32)
    for j in range(here.shape[1]):
        number = number + jnp.where(here[:, j : j + 1] == place, 1.0, 0.0)
    number = number.astype(low)
    counts_three = clipped_counts(here >= 0)
    mixed_two = (dot(number, hidden_two) / counts_three).astype(low)
    self_two = hidden_two[0:seeds]
    w_out = [
        jnp.concatenate(
            [weights_out[:, k, :], jnp.zeros((wide - classes, hidden), jnp.float32)], axis=0
        ).astype(low)
        for k in range(2)
    ]
    both_two = jnp.concatenate([self_two, mixed_two], axis=1)
    logits = dot_cols(both_two, jnp.concatenate(w_out, axis=1)) + bias_out
    top = jnp.max(logits, axis=1, keepdims=True)
    log_total = top + jnp.log(jnp.sum(jnp.exp(logits - top), axis=1, keepdims=True))
    onehot = jnp.where(
        label.astype(jnp.int32) == lax.broadcasted_iota(jnp.int32, (seeds, wide), 1), 1.0, 0.0
    )
    picked = jnp.sum(jnp.where(onehot > 0.0, logits, 0.0), axis=1, keepdims=True)
    loss = jnp.sum(marked * (log_total - picked), axis=0, keepdims=True)
    counted = jnp.sum(marked, axis=0, keepdims=True)
    grad_out = (marked * (jnp.exp(logits - log_total) - onehot)).astype(low)

    out_sums[...] = dot_rows(grad_out, both_two)
    bias_grad_out = jnp.sum(grad_out.astype(jnp.float32), axis=0, keepdims=True)
    to_self = dot(grad_out, w_out[0])
    spread = (dot(grad_out, w_out[1]) / counts_three).astype(low)
    sums[0:targets, :] = dot_rows(number, spread)
    sums[0:seeds, :] += to_self
    grad_mid = (sums[0:targets, :] * slope_mid).astype(low)

    mid_sums[...] = dot_rows(both_one, grad_mid)
    bias_grad_mid = jnp.sum(grad_mid.astype(jnp.float32), axis=0, keepdims=True)
    down = jnp.concatenate(
        [dot_cols(grad_mid, w_mid[1]) / counts_two, dot_cols(grad_mid, w_mid[0])], axis=0
    )
    down_low[...] = down.astype(low)

    weight_sums[...] = jnp.zeros_like(weight_sums)

    bias_sums[...] = jnp.zeros_like(bias_sums)

    def backward(pair, size):
        rows = pl.ds(pl.multiple_of(pair * 2 * SPAN, 2 * SPAN), size)
        joined[0:size, :] = dot_rows(paired(2 * pair, size), down_low[0:targets, :])

        @pl.when(pair == 0)
        def _():
            joined[0:size, :] += dot_rows(paired(own_link, size), down_low[targets:, :])

        grad = (joined[0:size, :] * slopes[rows, :]).astype(low)
        weight_sums[...] += dot_rows(mixin[rows, :], grad)
        bias_sums[0:1, :] += jnp.sum(grad.astype(jnp.float32), axis=0, keepdims=True)

    def backward_pair(pair, carry):
        backward(pair, 2 * SPAN)
        return carry

    lax.fori_loop(0, pairs, backward_pair, 0)

    @pl.when(odd)
    def _():
        backward(pairs, SPAN)

    bias_grad_in = bias_sums[0:1, :]
    row = 0
    for part in (weight_sums, mid_sums):
        for column in range(0, hidden, LANES):
            packed[row : row + part.shape[0], :] = part[:, column : column + LANES]
            row += part.shape[0]
    tall = up(classes, 16)
    for column in range(0, 2 * hidden, LANES):
        packed[row : row + tall, :] = out_sums[0:tall, column : column + LANES]
        row += tall
    packed[row:, :] = jnp.zeros((packed.shape[0] - row, LANES), jnp.float32)
    lane = lax.broadcasted_iota(jnp.int32, (1, LANES), 1)
    scalars = jnp.where(lane == 0, loss, 0.0) + jnp.where(lane == 1, counted, 0.0)
    extra = [
        item[:, column : column + LANES]
        for item in (bias_grad_in, bias_grad_mid, bias_grad_out)
        for column in range(0, hidden, LANES)
    ] + [scalars, jnp.zeros((1, LANES), jnp.float32)]
    extra = jnp.concatenate(extra, axis=0)
    high = extra.astype(low).astype(jnp.float32)
    packed[packed.shape[0] - 16 :, :] = jnp.concatenate([high, extra - high], axis=0)
    half = keep.shape[0]
    keep[...] = packed[pl.ds(pl.multiple_of(core * half, 16), half), :].astype(low)
    send[...] = packed[pl.ds(pl.multiple_of((1 - core) * half, 16), half), :].astype(low)


def run_step(info, count, places, partial, tallies, links, sources, rest, half, classes, held):
    padded = tallies.shape[0]
    blocks, targets = padded // SPAN, links.shape[1]
    total, width = sources[-1].shape
    hidden = rest[4].shape[2]
    wide = up(classes, LANES)
    return call(
        functools.partial(step_kernel, classes=classes),
        "step",
        (jax.ShapeDtypeStruct((half, LANES), jnp.bfloat16),) * 2,
        [smem] * 3 + [anywhere] * 3 + [vmem] * (PARTS + 8),
        (vmem, vmem),
        [
            pltpu.VMEM((padded, hidden), jnp.float32),
            pltpu.VMEM((2 * half, LANES), jnp.float32),
            pltpu.VMEM((2 * targets, hidden), jnp.float32),
            pltpu.VMEM((2 * width, hidden), jnp.float32),
            pltpu.VMEM((2 * hidden, hidden), jnp.float32),
            pltpu.VMEM((wide, 2 * hidden), jnp.float32),
            pltpu.VMEM((held, width), jnp.float32),
            pltpu.VMEM((total, 2 * width), jnp.bfloat16),
            pltpu.VMEM((padded, 2 * width), jnp.bfloat16),
            pltpu.VMEM((2 * SPAN, width), jnp.float32),
            pltpu.VMEM((2 * SPAN, 2 * width), jnp.float32),
            pltpu.VMEM((2, 2 * SPAN, total), COUNTS),
            pltpu.VMEM((2, 2 * SPAN, 2 * width), jnp.float32),
            pltpu.VMEM((2 * SPAN, hidden), jnp.bfloat16),
            pltpu.VMEM((2 * targets, hidden), jnp.bfloat16),
            pltpu.VMEM((8, hidden), jnp.float32),
            pltpu.VMEM((blocks + 2, targets, SPAN), jnp.bfloat16),
            pltpu.SemaphoreType.DMA((2, 2)),
            pltpu.SemaphoreType.DMA((blocks + 2,)),
        ],
        14.0,
        BIG,
    )(info, count, places, partial, tallies, links, *sources, *rest)


def refit(total, rows):
    extra = total[rows - 16 : rows - 8] + total[rows - 8 : rows]
    high = extra.astype(jnp.bfloat16).astype(jnp.float32)
    return jnp.concatenate([high, extra - high], axis=0)


def pair_kernel(info, mine, theirs, out):
    total = mine[...].astype(jnp.float32) + theirs[...].astype(jnp.float32)
    out[...] = total.astype(jnp.bfloat16)

    @pl.when(info[0] == 1)
    def _():
        rows = total.shape[0]
        out[rows - 16 :, :] = refit(total, rows).astype(jnp.bfloat16)


def pair_sum(info, mine, theirs):
    return call(
        pair_kernel,
        "pair_sum",
        jax.ShapeDtypeStruct(mine.shape, jnp.bfloat16),
        [smem, vmem, vmem],
        vmem,
        [],
        0.6,
        6 << 20,
    )(info, mine, theirs)


def spread_kernel(info, pieces, out):
    total = pieces[0].astype(jnp.float32)
    for k in range(1, pieces.shape[0]):
        total = total + pieces[k].astype(jnp.float32)
    rows = total.shape[0]
    fitted = jnp.concatenate([total[0 : rows - 16], refit(total, rows)], axis=0)
    result = jnp.where(info[1] == 1, fitted, total).astype(jnp.bfloat16)
    for k in range(pieces.shape[0]):
        out[k] = result


def spread_sum(info, pieces):
    return call(
        spread_kernel,
        "spread_sum",
        jax.ShapeDtypeStruct(pieces.shape, jnp.bfloat16),
        [smem, vmem],
        vmem,
        [],
        0.6,
        6 << 20,
    )(info, pieces)


def update_kernel(
    info, fixes, mine, theirs, biases, moment_one, moment_two, *refs
):
    groups = [refs[5 * k : 5 * k + 5] for k in range(3)]
    loss_out = refs[15]
    finals = refs[16:28]
    bias_out, first_out, second_out = refs[28:31]
    packed, sems = refs[31:33]
    held = refs[33:45]
    outs = [held[4 * k : 4 * k + 4] for k in range(3)]
    copies = [
        pltpu.make_async_copy(source, final, sems.at[k])
        for k, (source, final) in enumerate(zip(held, finals))
    ]
    low = jnp.bfloat16
    half = mine.shape[0]
    core = info[0]
    packed[pl.ds(pl.multiple_of(core * half, 16), half), :] = mine[...]
    packed[pl.ds(pl.multiple_of((1 - core) * half, 16), half), :] = theirs[...]
    last = packed.shape[0]
    extra = packed[last - 16 :, :].astype(jnp.float32)
    extra = extra[0:8] + extra[8:16]
    counted = extra[6:7, 1:2]
    inverse = 1.0 / counted
    loss_out[...] = extra[6:7, 0:1] / counted
    scale = 0.5 * inverse * inverse

    starts, row = [], 0
    for group in range(3):
        master = groups[group][0]
        starts.append(row)
        if group == 2:
            row += up(master.shape[0], 16) * 2 * (master.shape[2] // LANES)
        else:
            row += 2 * master.shape[1] * (master.shape[2] // LANES)
    for group in (1, 2, 0):
        row = starts[group]
        master, left, right, left_root, right_root = groups[group]
        new_master, copy, new_left, new_right = outs[group]
        turned = group == 2
        depth, hidden = (master.shape[0], master.shape[2]) if turned else master.shape[1:]
        deep = up(depth, LANES)

        def take(ref, k, middle):
            return ref[:, k, :] if middle else ref[k]

        def put(ref, k, middle, value):
            if middle:
                ref[:, k, :] = value
            else:
                ref[k] = value

        grads = []
        if turned:
            tall = up(depth, 16)
            for k in range(2):
                parts = []
                for column in range(0, hidden, LANES):
                    parts.append(packed[row : row + tall, :])
                    row += tall
                grads.append(grown(jnp.concatenate(parts, axis=1), deep, hidden))
        else:
            parts = []
            for column in range(0, hidden, LANES):
                parts.append(packed[row : row + 2 * depth, :])
                row += 2 * depth
            whole = jnp.concatenate(parts, axis=1)
            grads = [whole[k * depth : (k + 1) * depth] for k in range(2)]

        for k in range(2):
            grad = grads[k]
            for old, new, size, product, middle in (
                (left, new_left, depth, dot_cols(grad, grad), turned),
                (right, new_right, hidden, dot_rows(grad, grad), False),
            ):
                corner = old[0:1, k, 0:1] if middle else old[k, 0:1, 0:1]
                eye = lax.broadcasted_iota(jnp.int32, (size, size), 0) == (
                    lax.broadcasted_iota(jnp.int32, (size, size), 1)
                )
                value = jnp.where(eye, 0.5 * corner, 0.0) + scale * product[0:size, 0:size]
                put(new, k, middle, value)
            root = jnp.concatenate(
                halves(grown(take(left_root, k, turned), deep, deep)), axis=1
            )
            middle_high, middle_rest = halves(dot(root, jnp.concatenate([grad, grad], axis=0)))
            root_high, root_rest = halves(right_root[k])
            way = dot(
                jnp.concatenate([middle_high, middle_high, middle_rest], axis=1),
                jnp.concatenate([root_high, root_rest, root_high], axis=0),
            )[0:depth]
            put(new_master, k, turned, take(master, k, turned) - inverse * way)
        copy[...] = new_master[...].astype(low)
        for which in range(4):
            copies[4 * group + which].start()

    size = biases.shape[0]
    grad = jnp.concatenate([extra[k : k + 1, :] for k in range(6)], axis=1)[:, 0:size]
    grad = grad / counted

    def line(ref):
        return ref[...].reshape(1, size)

    first = 0.9 * line(moment_one) + 0.1 * grad
    second = 0.95 * line(moment_two) + 0.05 * grad * grad
    old = line(biases)
    fresh = old - 0.1 * (
        (first / fixes[0]) / (jnp.sqrt(second / fixes[1]) + 1e-08) + 0.01 * old
    )
    for ref, value in ((bias_out, fresh), (first_out, first), (second_out, second)):
        ref[...] = value[0]
    for copy in copies:
        copy.wait()


def run_update(info, fixes, mine, theirs, vectors, groups):
    outs = [jax.ShapeDtypeStruct((1, 1), jnp.float32)]
    flat = []
    for master, left, right, left_root, right_root in groups:
        flat += [master, left, right, left_root, right_root]
        outs += [
            jax.ShapeDtypeStruct(master.shape, jnp.float32),
            jax.ShapeDtypeStruct(master.shape, jnp.bfloat16),
            jax.ShapeDtypeStruct(left_root.shape, jnp.float32),
            jax.ShapeDtypeStruct(right_root.shape, jnp.float32),
        ]
    outs += [jax.ShapeDtypeStruct(vectors[0].shape, jnp.float32)] * 3
    return call(
        update_kernel,
        "update",
        tuple(outs),
        [smem] * 2 + [vmem] * (5 + len(flat)),
        (vmem,) + (anywhere,) * 12 + (vmem,) * 3,
        [
            pltpu.VMEM((2 * mine.shape[0], LANES), jnp.bfloat16),
            pltpu.SemaphoreType.DMA((12,)),
        ]
        + [pltpu.VMEM(item.shape, item.dtype) for item in outs[1:13]],
        4.0,
        16 << 20,
    )(info, fixes, mine, theirs, *vectors, *flat)


def body(
    features,
    requests,
    adjacent_one,
    adjacent_two,
    adjacent_three,
    valid_one,
    valid_two,
    valid_three,
    labels,
    labelled,
    weights_in,
    weights_mid,
    weights_out,
    biases,
    moment_one,
    moment_two,
    step_count,
    left_in,
    left_mid,
    left_out,
    right_in,
    right_mid,
    right_out,
    invleft_in,
    invleft_mid,
    invleft_out,
    invright_in,
    invright_mid,
    invright_out,
    *,
    peers,
):
    width = features.shape[1]
    devices, per = requests.shape
    targets = adjacent_one.shape[0]
    padded = up(targets, 2 * SPAN)
    classes = weights_out.shape[2]
    hidden = weights_in.shape[2]
    core = lax.axis_index("core")
    own = lax.axis_index(PEERS)

    wanted = lax.all_to_all(requests, AXES, split_axis=0, concat_axis=0, tiled=True)
    names, places, near_two, near_three, count = reach(
        adjacent_three, valid_three, labelled, adjacent_two, valid_two, targets, per
    )
    wanted, count = lax.optimization_barrier((wanted.reshape(-1), count))
    early_cut, late_cut = cuts(per)

    def trade(found):
        pulled = lax.all_to_all(
            found.reshape(devices, -1, width), AXES, split_axis=0, concat_axis=0, tiled=True
        )
        return pulled.reshape(-1, width)

    early_source = trade(pick_rows(wanted, features, per, early_cut))
    found = pick_rows(wanted, features, per, late_cut)
    links = link_matrix(count, names, near_two, adjacent_two.shape[1], padded)
    names, places = names.reshape(-1), places.reshape(-1)
    late_tally = tally(
        count, names, adjacent_one, valid_one, padded, devices, per, 1, ()
    )

    core_info = jnp.stack([core, ((core == 1) & (own == peers - 1)).astype(jnp.int32)])
    core_info = core_info.astype(jnp.int32)
    stepped = step_count.astype(jnp.float32)
    fixes = jnp.stack([1.0 - 0.9**stepped, 1.0 - 0.95**stepped])
    found, late_tally, links, info, fixes = lax.optimization_barrier(
        (found, late_tally, links, core_info, fixes)
    )
    late_source = trade(found)
    partial = tally(
        count, names, adjacent_one, valid_one, padded, devices, per, 0, (early_source,)
    )

    rows = (2 * width + 2 * weights_mid.shape[1]) * (hidden // LANES)
    rows += up(classes, 16) * (2 * hidden // LANES)
    each = up(-(-(rows + 16) // (2 * peers)), 8)
    half = each * peers
    turned_out = weights_out.transpose(2, 0, 1)
    keep, send = run_step(
        info,
        count,
        places,
        partial,
        late_tally,
        links,
        (early_source, late_source),
        (
            near_two,
            near_three,
            labels,
            labelled,
            weights_in,
            weights_mid,
            turned_out,
            biases,
        ),
        half,
        classes,
        -(-targets // per) * per,
    )
    swap = [(0, 1), (1, 0)]
    theirs = lax.ppermute(send, "core", swap)
    summed = pair_sum(info, keep, theirs).reshape(peers, each, LANES)
    pieces = lax.all_to_all(summed, PEERS, split_axis=0, concat_axis=0, tiled=True)
    shared = spread_sum(info, pieces)
    mine = lax.all_to_all(shared, PEERS, split_axis=0, concat_axis=0, tiled=True)
    mine = mine.reshape(half, LANES)
    theirs = lax.ppermute(mine, "core", swap)

    outs = run_update(
        info,
        fixes,
        mine,
        theirs,
        (biases, moment_one, moment_two),
        (
            (weights_in, left_in, right_in, invleft_in, invright_in),
            (weights_mid, left_mid, right_mid, invleft_mid, invright_mid),
            (
                turned_out,
                right_out.transpose(1, 0, 2),
                left_out,
                invright_out.transpose(1, 0, 2),
                invleft_out,
            ),
        ),
    )
    first, second, third = (outs[1 + 4 * k : 5 + 4 * k] for k in range(3))
    third = (
        third[0].transpose(1, 2, 0),
        third[1].transpose(1, 2, 0),
        third[3],
        third[2].transpose(1, 0, 2),
    )
    return (
        (outs[0].reshape(()),)
        + tuple(group[which] for which in range(4) for group in (first, second, third))
        + tuple(outs[13:16])
    )


def solution(mesh):
    chips, dev = mesh.shape["hst"] // 2, mesh.shape["dev"]
    fine = jax.sharding.Mesh(mesh.devices.reshape(chips, 2, dev), AXES)
    split = P(AXES, None)
    line = P(AXES)
    whole = P()
    mapped = jax.shard_map(
        functools.partial(body, peers=chips * dev),
        mesh=fine,
        in_specs=(split,) * 8 + (line,) * 2 + (whole,) * 19,
        out_specs=(whole,) * 16,
        check_vma=False,
    )

    def run(*args):
        with jax.sharding.use_abstract_mesh(fine.abstract_mesh):
            return mapped(*args)

    return run
```

```python
import functools

import jax
import jax.numpy as jnp
from jax import lax
from jax.experimental import pallas as pl
from jax.experimental.pallas import tpu as pltpu
from jax.sharding import PartitionSpec as P

LANES = 128
SPAN = 256
PARTS = 2
COUNTS = jnp.float8_e4m3fn
BIG = 52 << 20
AXES = ("chip", "core", "dev")
PEERS = ("chip", "dev")

smem = pl.BlockSpec(memory_space=pltpu.SMEM)
vmem = pl.BlockSpec(memory_space=pltpu.VMEM)
anywhere = pl.BlockSpec(memory_space=pltpu.HBM)


def up(value, unit):
    return -(-value // unit) * unit


def call(kernel, name, out_shape, in_specs, out_specs, scratch, cost, room):
    return pl.pallas_call(
        kernel,
        name=name,
        out_shape=out_shape,
        in_specs=in_specs,
        out_specs=out_specs,
        scratch_shapes=scratch,
        compiler_params=pltpu.CompilerParams(vmem_limit_bytes=room),
        cost_estimate=pl.CostEstimate(
            flops=0, transcendentals=0, bytes_accessed=int(cost * 3.6e6)
        ),
    )


def dot(left, right):
    return jnp.dot(left, right, preferred_element_type=jnp.float32)


def dot_rows(left, right):
    return lax.dot_general(
        left, right, (((0,), (0,)), ((), ())), preferred_element_type=jnp.float32
    )


def dot_cols(left, right):
    return lax.dot_general(
        left, right, (((1,), (1,)), ((), ())), preferred_element_type=jnp.float32
    )


def halves(value):
    high = value.astype(jnp.bfloat16)
    return high, (value - high.astype(jnp.float32)).astype(jnp.bfloat16)


def grown(value, rows, columns):
    short = columns - value.shape[1]
    if short:
        value = jnp.concatenate([value, jnp.zeros((value.shape[0], short), value.dtype)], axis=1)
    short = rows - value.shape[0]
    if short:
        value = jnp.concatenate([value, jnp.zeros((short, columns), value.dtype)], axis=0)
    return value


def clipped_counts(valid):
    return jnp.maximum(jnp.sum(valid.astype(jnp.float32), axis=1, keepdims=True), 1.0)


def copy_rows(names, base, size, source, target):
    for u in range(size):
        target[u : u + 1, :] = source[pl.ds(names[base + u], 1), :]


def cuts(per):
    return (0, per // 2), (per // 2, per)


def pick_kernel(wanted, table, out, rows, done, sems, *, first, part, per):
    chunk = rows.shape[0]
    devices = chunk // part

    def save(step):
        where = pl.ds(pl.multiple_of(step * chunk, chunk), chunk)
        return pltpu.make_async_copy(done.at[where, :], out.at[where, :], sems.at[step])

    def body(step, carry):
        for d in range(devices):
            base = (step * devices + d) * per + first
            for u in range(part):
                at = d * part + u
                rows[at : at + 1, :] = table[pl.ds(wanted[base + u], 1), :]
        where = pl.ds(pl.multiple_of(step * chunk, chunk), chunk)
        done[where, :] = rows[...].astype(jnp.bfloat16)
        save(step).start()
        return carry

    lax.fori_loop(0, out.shape[0] // chunk, body, 0)
    for step in range(out.shape[0] // chunk):
        save(step).wait()


def pick_rows(wanted, table, per, ends):
    first, last = ends
    width = table.shape[1]
    count = wanted.shape[0] // per * (last - first)
    chunk = 512
    return call(
        functools.partial(pick_kernel, first=first, part=last - first, per=per),
        "pick_rows",
        jax.ShapeDtypeStruct((count, width), jnp.bfloat16),
        [smem, vmem],
        anywhere,
        [
            pltpu.VMEM((chunk, width), jnp.float32),
            pltpu.VMEM((count, width), jnp.bfloat16),
            pltpu.SemaphoreType.DMA((count // chunk,)),
        ],
        4.6,
        20 << 20,
    )(wanted, table)


def stood(flat, unit):
    size = flat.shape[1]
    flat = jnp.concatenate(
        [flat.astype(jnp.float32), jnp.full((unit - flat.shape[0], size), -1.0, jnp.float32)],
        axis=0,
    )
    step = min(LANES, size)
    parts = [jnp.transpose(flat[:, k : k + step]) for k in range(0, size, step)]
    return jnp.concatenate(parts, axis=0).astype(jnp.int32)


def reach_kernel(
    adjacent_three,
    valid_three,
    labelled,
    adjacent_two,
    valid_two,
    names,
    places,
    near_two,
    near_three,
    count,
    left,
    right,
    *,
    rows_all,
    per,
):
    fan_three, seeds = adjacent_three.shape
    fan_two, targets = adjacent_two.shape
    low = jnp.bfloat16
    blocks = rows_all // LANES
    deep = names.shape[0]
    line = labelled[...].reshape(1, seeds)
    column = jnp.transpose(jnp.broadcast_to(line.astype(jnp.float32), (8, seeds)))[:, 0:1]
    near = stood(jnp.where(valid_three[...] > 0, adjacent_three[...], -1), near_three.shape[1])
    near_three[...] = near
    here = jnp.where(column > 0.0, near, -1)
    place = lax.broadcasted_iota(jnp.int32, (seeds, targets), 1)
    hit = jnp.zeros((seeds, targets), jnp.float32)
    for j in range(fan_three):
        hit = hit + jnp.where(here[:, j : j + 1] == place, 1.0, 0.0)
    need = jnp.max(hit, axis=0, keepdims=True) + jnp.concatenate(
        [line.astype(jnp.float32), jnp.zeros((1, targets - seeds), jnp.float32)], axis=1
    )

    level = lax.broadcasted_iota(jnp.int32, (deep, targets), 0)
    lane = lax.broadcasted_iota(jnp.int32, (targets, LANES), 1)
    flat = jnp.where(valid_two[...] > 0, adjacent_two[...], -1)
    tall = stood(flat, near_two.shape[1])
    near_two[...] = tall
    flat = jnp.where(need > 0.0, flat, -1)
    for j in range(fan_two):
        left[0:deep, j * targets : (j + 1) * targets] = jnp.where(
            lax.shift_right_arithmetic(flat[j : j + 1, :], 7) == level, 1.0, 0.0
        ).astype(low)
        right[j * targets : (j + 1) * targets, :] = jnp.where(
            (tall[:, j : j + 1] & (LANES - 1)) == lane, 1.0, 0.0
        ).astype(low)
    used = dot(left[0:deep, 0 : fan_two * targets], right[0 : fan_two * targets, :])
    own = [need[:, k : k + LANES] for k in range(0, targets, LANES)]
    own = jnp.concatenate(
        own + [jnp.zeros((deep - len(own), LANES), jnp.float32)], axis=0
    )
    flag = jnp.where(used + own > 0.0, 1.0, 0.0)

    square_row = lax.broadcasted_iota(jnp.int32, (LANES, LANES), 0)
    square_col = lax.broadcasted_iota(jnp.int32, (LANES, LANES), 1)
    full = jnp.concatenate([flag, jnp.zeros((LANES - deep, LANES), jnp.float32)], axis=0)
    flag_low = full.astype(low)
    running = dot(flag_low, jnp.where(square_row <= square_col, 1.0, 0.0).astype(low))
    totals = dot(flag_low, jnp.ones((LANES, LANES), low)).astype(low)
    before = dot(jnp.where(square_row > square_col, 1.0, 0.0).astype(low), totals)
    order = (before + running - full).astype(jnp.int32)
    number = jnp.sum(flag).astype(jnp.int32)
    count[0] = number
    count[1] = lax.div(number + (SPAN - 1), SPAN)

    high = jnp.where(full > 0.0, lax.shift_right_arithmetic(order, 7), -1)
    rest = jnp.transpose((order & (LANES - 1)).astype(jnp.float32)).astype(jnp.int32)
    step = lax.broadcasted_iota(jnp.int32, (deep, LANES), 0)
    inner = lax.broadcasted_iota(jnp.int32, (deep, LANES), 1).astype(jnp.float32)
    for b in range(blocks):
        match = jnp.where(high[b : b + 1, :] == step, 1.0, 0.0)
        lanes = slice(b * LANES, (b + 1) * LANES)
        left[0:deep, lanes] = (match * inner).astype(low)
        left[deep : 2 * deep, lanes] = (match * float(b)).astype(low)
        right[lanes, :] = jnp.where(rest[:, b : b + 1] == square_col, 1.0, 0.0).astype(low)
    found = dot(left[:, 0:rows_all], right[0:rows_all, :]).astype(jnp.int32)
    where = step * LANES + lax.broadcasted_iota(jnp.int32, (deep, LANES), 1)
    name = found[deep:] * LANES + found[0:deep]
    names[...] = jnp.where(where < number, name, rows_all)
    name = jnp.minimum(jnp.where(where < number, name, 0), rows_all - 1)
    owners = -(-rows_all // per)
    owner = lax.shift_right_logical(name, per.bit_length() - 1)
    slot = name & (per - 1)
    early, late = (last - first for first, last in cuts(per))
    places[...] = jnp.where(
        slot < early, owner * early + slot, owners * early + owner * late + slot - early
    )


def reach(adjacent_three, valid_three, labelled, adjacent_two, valid_two, rows_all, per):
    targets, fan = adjacent_two.shape
    seeds = labelled.shape[0]
    deep = up(up(rows_all, 2 * SPAN) // LANES, 16)
    area = max(fan * targets, rows_all)
    return call(
        functools.partial(reach_kernel, rows_all=rows_all, per=per),
        "reach",
        (
            jax.ShapeDtypeStruct((deep, LANES), jnp.int32),
            jax.ShapeDtypeStruct((deep, LANES), jnp.int32),
            jax.ShapeDtypeStruct((targets, 16), jnp.int32),
            jax.ShapeDtypeStruct((seeds, 8), jnp.int32),
            jax.ShapeDtypeStruct((2,), jnp.int32),
        ),
        [vmem] * 5,
        (vmem,) * 4 + (smem,),
        [
            pltpu.VMEM((2 * deep, area), jnp.bfloat16),
            pltpu.VMEM((area, LANES), jnp.bfloat16),
        ],
        3.0,
        8 << 20,
    )(adjacent_three.T, valid_three.T, labelled, adjacent_two.T, valid_two.T)


def tally_kernel(count, names, adjacent, valid, *refs, per, which):
    multiply = which == 0
    if multiply:
        source, out, table, rows, spread, marked, buffer, sems, terms, sums = refs
        width = source.shape[1]
        terms[:, 0:width] = source[...]
        terms[:, width:] = jnp.ones((source.shape[0], width), jnp.bfloat16)
    else:
        out, table, rows, spread, marked, buffer, sems = refs
    low = jnp.bfloat16
    fan, targets = adjacent.shape
    unit = spread.shape[0]
    groups = SPAN // unit
    few = 8 if multiply else groups
    used = count[1]
    high_all = buffer.shape[2] // SPAN
    first, last = cuts(per)[which]
    size = last - first

    slot = adjacent[...]
    owner = lax.shift_right_logical(slot, per.bit_length() - 1)
    inner = slot & (per - 1)
    here = (valid[...] > 0) & (inner >= first) & (inner < last)
    slot = jnp.where(here, owner * size + inner - first, -1)
    slot = jnp.concatenate(
        [slot.astype(jnp.float32), jnp.full((unit - fan, targets), -1.0, jnp.float32)], axis=0
    )
    for b in range(0, targets, LANES):
        table[b : b + LANES, :] = jnp.transpose(slot[:, b : b + LANES]).astype(jnp.int32)
    table[targets:, :] = jnp.full((table.shape[0] - targets, unit), -1, jnp.int32)

    across = lax.broadcasted_iota(jnp.int32, (unit, SPAN), 1)
    down = lax.broadcasted_iota(jnp.int32, (unit, SPAN), 0)
    spread[...] = jnp.where(lax.div(across, unit) == down, 1.0, 0.0).astype(low)
    lane = across.astype(jnp.float32).astype(low)
    one = jnp.ones((unit, SPAN), low)
    zero = jnp.zeros((unit, SPAN), low)

    def copies(block, slot):
        where = pl.ds(pl.multiple_of(block * SPAN, SPAN), SPAN)
        result = sums if multiply else buffer
        return pltpu.make_async_copy(result.at[slot], out.at[where, :], sems.at[slot])

    def body(block, carry):
        slot = lax.rem(block, 2)

        @pl.when(block >= 2)
        def _():
            copies(block - 2, slot).wait()

        copy_rows(names, block * SPAN, SPAN, table, rows)
        high = lax.shift_right_arithmetic(rows[...], 8).astype(jnp.float32).astype(low)
        own = lax.rem(lax.broadcasted_iota(jnp.int32, (SPAN, SPAN), 0), unit) == lax.rem(
            lax.broadcasted_iota(jnp.int32, (SPAN, SPAN), 1), unit
        )
        marked[...] = jnp.where(own, dot(high, spread[...]), -1.0).astype(low)

        def single(g):
            first = pl.multiple_of(g * unit, unit)
            rest = (rows[pl.ds(first, unit), :] & (SPAN - 1)).astype(jnp.float32)
            columns = [
                jnp.where(
                    jnp.broadcast_to(rest[:, j : j + 1], (unit, SPAN)).astype(low) == lane,
                    one,
                    zero,
                )
                for j in range(unit)
            ]
            mark = marked[pl.ds(first, unit), :]
            marks = [
                jnp.where(mark == jnp.full((unit, SPAN), float(q), low), one, zero)
                for q in range(high_all)
            ]
            return dot(jnp.concatenate(marks, axis=0), jnp.concatenate(columns, axis=0))

        def group(step, inner):
            for u in range(0, few, 2):
                pair = [single(step * few + u), single(step * few + u + 1)]
                where = pl.ds(pl.multiple_of((step * few + u) * unit, 2 * unit), 2 * unit)
                for q in range(high_all):
                    tile = jnp.concatenate(
                        [item[q * unit : (q + 1) * unit] for item in pair], axis=0
                    )
                    buffer[slot, where, q * SPAN : (q + 1) * SPAN] = tile.astype(buffer.dtype)
            return inner

        lax.fori_loop(0, groups // few, group, 0)
        if multiply:
            sums[slot] = dot(buffer[slot], terms[...])
        copies(block, slot).start()
        return carry

    lax.fori_loop(0, used, body, 0)

    @pl.when(used >= 2)
    def _():
        copies(used - 2, lax.rem(used - 2, 2)).wait()

    @pl.when(used >= 1)
    def _():
        copies(used - 1, lax.rem(used - 1, 2)).wait()


def tally(count, names, adjacent, valid, padded, devices, per, which, sources):
    targets = adjacent.shape[0]
    unit = 16
    first, last = cuts(per)[which]
    wide = devices * (last - first)
    multiply = which == 0
    width = sources[0].shape[1] if multiply else 0
    scratch = [
        pltpu.VMEM((targets + 8, unit), jnp.int32),
        pltpu.VMEM((SPAN, unit), jnp.int32),
        pltpu.VMEM((unit, SPAN), jnp.bfloat16),
        pltpu.VMEM((SPAN, SPAN), jnp.bfloat16),
        pltpu.VMEM((2, SPAN, wide), jnp.bfloat16 if multiply else COUNTS),
        pltpu.SemaphoreType.DMA((2,)),
    ]
    if multiply:
        out = jax.ShapeDtypeStruct((3 * padded, 2 * width), jnp.float32)
        scratch += [
            pltpu.VMEM((wide, 2 * width), jnp.bfloat16),
            pltpu.VMEM((2, SPAN, 2 * width), jnp.float32),
        ]
    else:
        out = jax.ShapeDtypeStruct((padded, wide), COUNTS)
    return call(
        functools.partial(tally_kernel, per=per, which=which),
        "early_sums" if multiply else "tally",
        out,
        [smem, smem] + [vmem] * (2 + len(sources)),
        anywhere,
        scratch,
        14.0,
        BIG,
    )(count, names, adjacent.T, valid.T, *sources)


def link_kernel(count, names, near, out, buffer, sems, *, fan):
    targets = near.shape[0]
    tile = 32
    blocks = count[1]
    all_blocks = buffer.shape[0] - 2
    across = SPAN // LANES

    def line(block, part):
        return jnp.broadcast_to(names[pl.ds(block * across + part, 1), :], (tile, LANES))

    def save(block):
        return pltpu.make_async_copy(buffer.at[block], out.at[block], sems.at[block])

    def rows(step, carry):
        first = pl.multiple_of(step * tile, tile)
        here = near[pl.ds(first, tile), :]
        spread = [jnp.broadcast_to(here[:, j : j + 1], (tile, LANES)) for j in range(fan)]
        own = first + lax.broadcasted_iota(jnp.int32, (tile, LANES), 0)

        def columns(block, inner):
            for part in range(across):
                name = line(block, part)
                number = jnp.zeros((tile, LANES), jnp.float32)
                for j in range(fan):
                    number = number + jnp.where(spread[j] == name, 1.0, 0.0)
                lanes = pl.ds(part * LANES, LANES)
                buffer[block, pl.ds(first, tile), lanes] = number.astype(jnp.bfloat16)
            return inner

        lax.fori_loop(0, blocks, columns, 0)
        for block in range(2):
            for part in range(across):
                lanes = slice(part * LANES, (part + 1) * LANES)
                buffer[all_blocks + block, pl.ds(first, tile), lanes] = jnp.where(
                    own == line(block, part), 1.0, 0.0
                ).astype(jnp.bfloat16)
        return carry

    lax.fori_loop(0, targets // tile, rows, 0)

    def start(block, carry):
        save(block).start()
        return carry

    def finish(block, carry):
        save(block).wait()
        return carry

    for ends in ((0, blocks), (all_blocks, all_blocks + 2)):
        lax.fori_loop(*ends, start, 0)
    for ends in ((0, blocks), (all_blocks, all_blocks + 2)):
        lax.fori_loop(*ends, finish, 0)


def link_matrix(count, names, near, fan, padded):
    blocks = padded // SPAN
    targets = near.shape[0]
    return call(
        functools.partial(link_kernel, fan=fan),
        "link_matrix",
        jax.ShapeDtypeStruct((4 * blocks, targets, SPAN), jnp.bfloat16),
        [smem, vmem, vmem],
        anywhere,
        [
            pltpu.VMEM((blocks + 2, targets, SPAN), jnp.bfloat16),
            pltpu.SemaphoreType.DMA((blocks + 2,)),
        ],
        5.0,
        BIG,
    )(count, names, near)


def step_kernel(
    info,
    count,
    places,
    partial,
    tallies,
    links,
    *refs,
    classes,
):
    sources = refs[:PARTS]
    step_body(
        info, count, places, partial, tallies, links, sources, *refs[PARTS:],
        classes=classes,
    )


def step_body(
    info,
    count,
    places,
    partial,
    tallies,
    links,
    sources,
    near_two,
    near_three,
    labels,
    labelled,
    weights_in,
    weights_mid,
    weights_out,
    biases_line,
    keep,
    send,
    slopes,
    packed,
    sums,
    weight_sums,
    mid_sums,
    out_sums,
    own_table,
    late_table,
    mixin,
    own_rows,
    joined,
    late,
    early,
    hid,
    down_low,
    bias_sums,
    link,
    sems,
    link_sems,
    early_rows,
    own_sems,
    *,
    classes,
):
    targets = links.shape[1]
    hidden = weights_in.shape[2]
    seeds = labels.shape[0]
    biases = biases_line[...].reshape(1, biases_line.shape[0])
    label, marked = [
        jnp.transpose(
            jnp.broadcast_to(item[...].reshape(1, seeds).astype(jnp.float32), (8, seeds))
        )[:, 0:1]
        for item in (labels, labelled)
    ]
    wide = up(classes, LANES)
    core = info[0]
    used = count[1]
    low = jnp.bfloat16
    width = sources[0].shape[1]

    def load(pair, slot, size):
        rows = pl.ds(pl.multiple_of(pair * 2 * SPAN, 2 * SPAN), size)
        here = pl.ds(0, size)
        return (
            pltpu.make_async_copy(tallies.at[rows, :], late.at[slot, here, :], sems.at[slot, 0]),
            pltpu.make_async_copy(partial.at[rows, :], early.at[slot, here, :], sems.at[slot, 1]),
        )

    def start_load(pair, slot):
        @pl.when(2 * pair + 1 < used)
        def _():
            for copy in load(pair, slot, 2 * SPAN):
                copy.start()

        @pl.when(2 * pair + 1 == used)
        def _():
            for copy in load(pair, slot, SPAN):
                copy.start()

    def load_link(block):
        return pltpu.make_async_copy(links.at[block], link.at[block], link_sems.at[block])

    held = early_rows.shape[0]
    fetch_early = pltpu.make_async_copy(
        sources[0].at[pl.ds(0, held), :], early_rows, own_sems.at[0]
    )
    fetch_late = pltpu.make_async_copy(
        sources[1], late_table.at[:, pl.ds(0, width)], own_sems.at[1]
    )
    fetch_early.start()
    fetch_late.start()
    start_load(0, 0)

    def start_link(block, carry):
        load_link(block).start()
        return carry

    lax.fori_loop(0, used, start_link, 0)
    own_link = link.shape[0] - 2
    for block in range(2):
        load_link(own_link + block).start()
    late_table[:, width:] = jnp.ones((late_table.shape[0], width), low)
    fetch_early.wait()
    own_table[0:held, :] = early_rows[...].astype(jnp.float32)
    fetch_late.wait()
    own_table[held:, :] = late_table[0 : own_table.shape[0] - held, 0:width].astype(jnp.float32)

    w_in = weights_in[...].astype(low).reshape(2 * weights_in.shape[1], hidden)
    bias_in = biases[:, 0:hidden]
    bias_mid = biases[:, hidden : 2 * hidden]
    bias_out = jnp.concatenate(
        [
            biases[:, 2 * hidden : 2 * hidden + classes],
            jnp.full((1, wide - classes), -1e30, jnp.float32),
        ],
        axis=1,
    )

    sums[...] = jnp.zeros_like(sums)

    def paired(block, size):
        if size == SPAN:
            return link[block]
        return jnp.concatenate([link[block], link[block + 1]], axis=1)

    def forward(pair, size):
        base = pair * 2 * SPAN
        rows = pl.ds(pl.multiple_of(base, 2 * SPAN), size)
        slot = lax.rem(pair, 2)
        for copy in load(pair, slot, size):
            copy.wait()
        for step in range(size // SPAN):
            load_link(2 * pair + step).wait()
        start_load(pair + 1, 1 - slot)
        for part in range(0, size, SPAN):
            for u in range(part, part + SPAN):
                own_rows[u : u + 1, :] = own_table[pl.ds(places[base + u], 1), :]
            here = slice(part, part + SPAN)
            joined[here, :] = dot(late[slot, here, :].astype(low), late_table[...]) + (
                early[slot, here, :]
            )
        mixin[rows, 0:width] = own_rows[0:size, :].astype(low)
        mixin[rows, width:] = (
            joined[0:size, 0:width] / jnp.maximum(joined[0:size, width:], 1.0)
        ).astype(low)
        z = dot(mixin[rows, :], w_in) + bias_in
        s = 1.0 / (1.0 + jnp.exp(-z))
        slopes[rows, :] = s * (1.0 + z * (1.0 - s))
        hid[0:size, :] = (z * s).astype(low)
        sums[0:targets, :] += dot(paired(2 * pair, size), hid[0:size, :])

        @pl.when(pair == 0)
        def _():
            for block in range(2):
                load_link(own_link + block).wait()
            sums[targets:, :] = dot(paired(own_link, size), hid[0:size, :])

    pairs = lax.div(used, 2)
    odd = lax.rem(used, 2) == 1

    def forward_pair(pair, carry):
        forward(pair, 2 * SPAN)
        return carry

    lax.fori_loop(0, pairs, forward_pair, 0)

    @pl.when(odd)
    def _():
        forward(pairs, SPAN)

    total = sums[...]
    counts_two = clipped_counts(near_two[...] >= 0)
    mixed_one = (total[0:targets] / counts_two).astype(low)
    self_one = total[targets:].astype(low)
    w_mid = weights_mid[...].astype(low)
    both_one = jnp.concatenate([self_one, mixed_one], axis=1)
    z = dot(both_one, w_mid.reshape(2 * hidden, hidden)) + bias_mid
    s = 1.0 / (1.0 + jnp.exp(-z))
    slope_mid = s * (1.0 + z * (1.0 - s))
    hidden_two = (z * s).astype(low)

    here = near_three[...]
    place = lax.broadcasted_iota(jnp.int32, (seeds, targets), 1)
    number = jnp.zeros((seeds, targets), jnp.float32)
    for j in range(here.shape[1]):
        number = number + jnp.where(here[:, j : j + 1] == place, 1.0, 0.0)
    number = number.astype(low)
    counts_three = clipped_counts(here >= 0)
    mixed_two = (dot(number, hidden_two) / counts_three).astype(low)
    self_two = hidden_two[0:seeds]
    w_out = [
        jnp.concatenate(
            [weights_out[:, k, :], jnp.zeros((wide - classes, hidden), jnp.float32)], axis=0
        ).astype(low)
        for k in range(2)
    ]
    both_two = jnp.concatenate([self_two, mixed_two], axis=1)
    logits = dot_cols(both_two, jnp.concatenate(w_out, axis=1)) + bias_out
    top = jnp.max(logits, axis=1, keepdims=True)
    log_total = top + jnp.log(jnp.sum(jnp.exp(logits - top), axis=1, keepdims=True))
    onehot = jnp.where(
        label.astype(jnp.int32) == lax.broadcasted_iota(jnp.int32, (seeds, wide), 1), 1.0, 0.0
    )
    picked = jnp.sum(jnp.where(onehot > 0.0, logits, 0.0), axis=1, keepdims=True)
    loss = jnp.sum(marked * (log_total - picked), axis=0, keepdims=True)
    counted = jnp.sum(marked, axis=0, keepdims=True)
    grad_out = (marked * (jnp.exp(logits - log_total) - onehot)).astype(low)

    out_sums[...] = dot_rows(grad_out, both_two)
    bias_grad_out = jnp.sum(grad_out.astype(jnp.float32), axis=0, keepdims=True)
    to_self = dot(grad_out, w_out[0])
    spread = (dot(grad_out, w_out[1]) / counts_three).astype(low)
    sums[0:targets, :] = dot_rows(number, spread)
    sums[0:seeds, :] += to_self
    grad_mid = (sums[0:targets, :] * slope_mid).astype(low)

    mid_sums[...] = dot_rows(both_one, grad_mid)
    bias_grad_mid = jnp.sum(grad_mid.astype(jnp.float32), axis=0, keepdims=True)
    down = jnp.concatenate(
        [dot_cols(grad_mid, w_mid[1]) / counts_two, dot_cols(grad_mid, w_mid[0])], axis=0
    )
    down_low[...] = down.astype(low)

    weight_sums[...] = jnp.zeros_like(weight_sums)

    bias_sums[...] = jnp.zeros_like(bias_sums)

    def backward(pair, size):
        rows = pl.ds(pl.multiple_of(pair * 2 * SPAN, 2 * SPAN), size)
        joined[0:size, :] = dot_rows(paired(2 * pair, size), down_low[0:targets, :])

        @pl.when(pair == 0)
        def _():
            joined[0:size, :] += dot_rows(paired(own_link, size), down_low[targets:, :])

        grad = (joined[0:size, :] * slopes[rows, :]).astype(low)
        weight_sums[...] += dot_rows(mixin[rows, :], grad)
        bias_sums[0:1, :] += jnp.sum(grad.astype(jnp.float32), axis=0, keepdims=True)

    def backward_pair(pair, carry):
        backward(pair, 2 * SPAN)
        return carry

    lax.fori_loop(0, pairs, backward_pair, 0)

    @pl.when(odd)
    def _():
        backward(pairs, SPAN)

    bias_grad_in = bias_sums[0:1, :]
    row = 0
    for part in (weight_sums, mid_sums):
        for column in range(0, hidden, LANES):
            packed[row : row + part.shape[0], :] = part[:, column : column + LANES]
            row += part.shape[0]
    tall = up(classes, 16)
    for column in range(0, 2 * hidden, LANES):
        packed[row : row + tall, :] = out_sums[0:tall, column : column + LANES]
        row += tall
    packed[row:, :] = jnp.zeros((packed.shape[0] - row, LANES), jnp.float32)
    lane = lax.broadcasted_iota(jnp.int32, (1, LANES), 1)
    scalars = jnp.where(lane == 0, loss, 0.0) + jnp.where(lane == 1, counted, 0.0)
    extra = [
        item[:, column : column + LANES]
        for item in (bias_grad_in, bias_grad_mid, bias_grad_out)
        for column in range(0, hidden, LANES)
    ] + [scalars, jnp.zeros((1, LANES), jnp.float32)]
    extra = jnp.concatenate(extra, axis=0)
    high = extra.astype(low).astype(jnp.float32)
    packed[packed.shape[0] - 16 :, :] = jnp.concatenate([high, extra - high], axis=0)
    half = keep.shape[0]
    keep[...] = packed[pl.ds(pl.multiple_of(core * half, 16), half), :].astype(low)
    send[...] = packed[pl.ds(pl.multiple_of((1 - core) * half, 16), half), :].astype(low)


def run_step(info, count, places, partial, tallies, links, sources, rest, half, classes, held):
    padded = tallies.shape[0]
    blocks, targets = padded // SPAN, links.shape[1]
    total, width = sources[-1].shape
    hidden = rest[4].shape[2]
    wide = up(classes, LANES)
    return call(
        functools.partial(step_kernel, classes=classes),
        "step",
        (jax.ShapeDtypeStruct((half, LANES), jnp.bfloat16),) * 2,
        [smem] * 3 + [anywhere] * (3 + PARTS) + [vmem] * 8,
        (vmem, vmem),
        [
            pltpu.VMEM((padded, hidden), jnp.float32),
            pltpu.VMEM((2 * half, LANES), jnp.float32),
            pltpu.VMEM((2 * targets, hidden), jnp.float32),
            pltpu.VMEM((2 * width, hidden), jnp.float32),
            pltpu.VMEM((2 * hidden, hidden), jnp.float32),
            pltpu.VMEM((wide, 2 * hidden), jnp.float32),
            pltpu.VMEM((held, width), jnp.float32),
            pltpu.VMEM((total, 2 * width), jnp.bfloat16),
            pltpu.VMEM((padded, 2 * width), jnp.bfloat16),
            pltpu.VMEM((2 * SPAN, width), jnp.float32),
            pltpu.VMEM((2 * SPAN, 2 * width), jnp.float32),
            pltpu.VMEM((2, 2 * SPAN, total), COUNTS),
            pltpu.VMEM((2, 2 * SPAN, 2 * width), jnp.float32),
            pltpu.VMEM((2 * SPAN, hidden), jnp.bfloat16),
            pltpu.VMEM((2 * targets, hidden), jnp.bfloat16),
            pltpu.VMEM((8, hidden), jnp.float32),
            pltpu.VMEM((blocks + 2, targets, SPAN), jnp.bfloat16),
            pltpu.SemaphoreType.DMA((2, 2)),
            pltpu.SemaphoreType.DMA((blocks + 2,)),
            pltpu.VMEM((held * sources[0].shape[0] // (sources[0].shape[0] + total), width), jnp.bfloat16),
            pltpu.SemaphoreType.DMA((2,)),
        ],
        14.0,
        BIG,
    )(info, count, places, partial, tallies, links, *sources, *rest)


def refit(total, rows):
    extra = total[rows - 16 : rows - 8] + total[rows - 8 : rows]
    high = extra.astype(jnp.bfloat16).astype(jnp.float32)
    return jnp.concatenate([high, extra - high], axis=0)


def pair_kernel(info, mine, theirs, out):
    total = mine[...].astype(jnp.float32) + theirs[...].astype(jnp.float32)
    out[...] = total.astype(jnp.bfloat16)

    @pl.when(info[0] == 1)
    def _():
        rows = total.shape[0]
        out[rows - 16 :, :] = refit(total, rows).astype(jnp.bfloat16)


def pair_sum(info, mine, theirs):
    return call(
        pair_kernel,
        "pair_sum",
        jax.ShapeDtypeStruct(mine.shape, jnp.bfloat16),
        [smem, vmem, vmem],
        vmem,
        [],
        0.6,
        6 << 20,
    )(info, mine, theirs)


def spread_kernel(info, pieces, out):
    total = pieces[0].astype(jnp.float32)
    for k in range(1, pieces.shape[0]):
        total = total + pieces[k].astype(jnp.float32)
    rows = total.shape[0]
    fitted = jnp.concatenate([total[0 : rows - 16], refit(total, rows)], axis=0)
    result = jnp.where(info[1] == 1, fitted, total).astype(jnp.bfloat16)
    for k in range(pieces.shape[0]):
        out[k] = result


def spread_sum(info, pieces):
    return call(
        spread_kernel,
        "spread_sum",
        jax.ShapeDtypeStruct(pieces.shape, jnp.bfloat16),
        [smem, vmem],
        vmem,
        [],
        0.6,
        6 << 20,
    )(info, pieces)


def update_kernel(
    info, fixes, mine, theirs, biases, moment_one, moment_two, *refs
):
    groups = [refs[5 * k : 5 * k + 5] for k in range(3)]
    loss_out = refs[15]
    outs = [refs[16 + 4 * k : 20 + 4 * k] for k in range(3)]
    bias_out, first_out, second_out = refs[28:31]
    packed = refs[31]
    low = jnp.bfloat16
    half = mine.shape[0]
    core = info[0]
    packed[pl.ds(pl.multiple_of(core * half, 16), half), :] = mine[...]
    packed[pl.ds(pl.multiple_of((1 - core) * half, 16), half), :] = theirs[...]
    last = packed.shape[0]
    extra = packed[last - 16 :, :].astype(jnp.float32)
    extra = extra[0:8] + extra[8:16]
    counted = extra[6:7, 1:2]
    inverse = 1.0 / counted
    loss_out[...] = extra[6:7, 0:1] / counted
    scale = 0.5 * inverse * inverse

    row = 0
    for group in range(3):
        master, left, right, left_root, right_root = groups[group]
        new_master, copy, new_left, new_right = outs[group]
        turned = group == 2
        depth, hidden = (master.shape[0], master.shape[2]) if turned else master.shape[1:]
        deep = up(depth, LANES)

        def take(ref, k, middle):
            return ref[:, k, :] if middle else ref[k]

        def put(ref, k, middle, value):
            if middle:
                ref[:, k, :] = value
            else:
                ref[k] = value

        grads = []
        if turned:
            tall = up(depth, 16)
            for k in range(2):
                parts = []
                for column in range(0, hidden, LANES):
                    parts.append(packed[row : row + tall, :])
                    row += tall
                grads.append(grown(jnp.concatenate(parts, axis=1), deep, hidden))
        else:
            parts = []
            for column in range(0, hidden, LANES):
                parts.append(packed[row : row + 2 * depth, :])
                row += 2 * depth
            whole = jnp.concatenate(parts, axis=1)
            grads = [whole[k * depth : (k + 1) * depth] for k in range(2)]

        for k in range(2):
            grad = grads[k]
            for old, new, size, product, middle in (
                (left, new_left, depth, dot_cols(grad, grad), turned),
                (right, new_right, hidden, dot_rows(grad, grad), False),
            ):
                corner = old[0:1, k, 0:1] if middle else old[k, 0:1, 0:1]
                eye = lax.broadcasted_iota(jnp.int32, (size, size), 0) == (
                    lax.broadcasted_iota(jnp.int32, (size, size), 1)
                )
                value = jnp.where(eye, 0.5 * corner, 0.0) + scale * product[0:size, 0:size]
                put(new, k, middle, value)
            root = jnp.concatenate(
                halves(grown(take(left_root, k, turned), deep, deep)), axis=1
            )
            middle_high, middle_rest = halves(dot(root, jnp.concatenate([grad, grad], axis=0)))
            root_high, root_rest = halves(right_root[k])
            way = dot(
                jnp.concatenate([middle_high, middle_high, middle_rest], axis=1),
                jnp.concatenate([root_high, root_rest, root_high], axis=0),
            )[0:depth]
            put(new_master, k, turned, take(master, k, turned) - inverse * way)
        copy[...] = new_master[...].astype(low)

    size = biases.shape[0]
    grad = jnp.concatenate([extra[k : k + 1, :] for k in range(6)], axis=1)[:, 0:size]
    grad = grad / counted

    def line(ref):
        return ref[...].reshape(1, size)

    first = 0.9 * line(moment_one) + 0.1 * grad
    second = 0.95 * line(moment_two) + 0.05 * grad * grad
    old = line(biases)
    fresh = old - 0.1 * (
        (first / fixes[0]) / (jnp.sqrt(second / fixes[1]) + 1e-08) + 0.01 * old
    )
    for ref, value in ((bias_out, fresh), (first_out, first), (second_out, second)):
        ref[...] = value[0]


def run_update(info, fixes, mine, theirs, vectors, groups):
    outs = [jax.ShapeDtypeStruct((1, 1), jnp.float32)]
    flat = []
    for master, left, right, left_root, right_root in groups:
        flat += [master, left, right, left_root, right_root]
        outs += [
            jax.ShapeDtypeStruct(master.shape, jnp.float32),
            jax.ShapeDtypeStruct(master.shape, jnp.bfloat16),
            jax.ShapeDtypeStruct(left_root.shape, jnp.float32),
            jax.ShapeDtypeStruct(right_root.shape, jnp.float32),
        ]
    outs += [jax.ShapeDtypeStruct(vectors[0].shape, jnp.float32)] * 3
    return call(
        update_kernel,
        "update",
        tuple(outs),
        [smem] * 2 + [vmem] * (5 + len(flat)),
        (vmem,) * len(outs),
        [pltpu.VMEM((2 * mine.shape[0], LANES), jnp.bfloat16)],
        4.0,
        16 << 20,
    )(info, fixes, mine, theirs, *vectors, *flat)


def body(
    features,
    requests,
    adjacent_one,
    adjacent_two,
    adjacent_three,
    valid_one,
    valid_two,
    valid_three,
    labels,
    labelled,
    weights_in,
    weights_mid,
    weights_out,
    biases,
    moment_one,
    moment_two,
    step_count,
    left_in,
    left_mid,
    left_out,
    right_in,
    right_mid,
    right_out,
    invleft_in,
    invleft_mid,
    invleft_out,
    invright_in,
    invright_mid,
    invright_out,
    *,
    peers,
):
    width = features.shape[1]
    devices, per = requests.shape
    targets = adjacent_one.shape[0]
    padded = up(targets, 2 * SPAN)
    classes = weights_out.shape[2]
    hidden = weights_in.shape[2]
    core = lax.axis_index("core")
    own = lax.axis_index(PEERS)

    wanted = lax.all_to_all(requests, AXES, split_axis=0, concat_axis=0, tiled=True)
    names, places, near_two, near_three, count = reach(
        adjacent_three, valid_three, labelled, adjacent_two, valid_two, targets, per
    )
    wanted, count = lax.optimization_barrier((wanted.reshape(-1), count))
    early_cut, late_cut = cuts(per)

    def trade(found):
        pulled = lax.all_to_all(
            found.reshape(devices, -1, width), AXES, split_axis=0, concat_axis=0, tiled=True
        )
        return pulled.reshape(-1, width)

    early_source = trade(pick_rows(wanted, features, per, early_cut))
    found = pick_rows(wanted, features, per, late_cut)
    links = link_matrix(count, names, near_two, adjacent_two.shape[1], padded)
    names, places = names.reshape(-1), places.reshape(-1)
    late_tally = tally(
        count, names, adjacent_one, valid_one, padded, devices, per, 1, ()
    )

    core_info = jnp.stack([core, ((core == 1) & (own == peers - 1)).astype(jnp.int32)])
    core_info = core_info.astype(jnp.int32)
    stepped = step_count.astype(jnp.float32)
    fixes = jnp.stack([1.0 - 0.9**stepped, 1.0 - 0.95**stepped])
    found, late_tally, links, info, fixes = lax.optimization_barrier(
        (found, late_tally, links, core_info, fixes)
    )
    late_source = trade(found)
    partial = tally(
        count, names, adjacent_one, valid_one, padded, devices, per, 0, (early_source,)
    )

    rows = (2 * width + 2 * weights_mid.shape[1]) * (hidden // LANES)
    rows += up(classes, 16) * (2 * hidden // LANES)
    each = up(-(-(rows + 16) // (2 * peers)), 8)
    half = each * peers
    turned_out = weights_out.transpose(2, 0, 1)
    keep, send = run_step(
        info,
        count,
        places,
        partial,
        late_tally,
        links,
        (early_source, late_source),
        (
            near_two,
            near_three,
            labels,
            labelled,
            weights_in,
            weights_mid,
            turned_out,
            biases,
        ),
        half,
        classes,
        -(-targets // per) * per,
    )
    swap = [(0, 1), (1, 0)]
    theirs = lax.ppermute(send, "core", swap)
    summed = pair_sum(info, keep, theirs).reshape(peers, each, LANES)
    pieces = lax.all_to_all(summed, PEERS, split_axis=0, concat_axis=0, tiled=True)
    shared = spread_sum(info, pieces)
    mine = lax.all_to_all(shared, PEERS, split_axis=0, concat_axis=0, tiled=True)
    mine = mine.reshape(half, LANES)
    theirs = lax.ppermute(mine, "core", swap)

    outs = run_update(
        info,
        fixes,
        mine,
        theirs,
        (biases, moment_one, moment_two),
        (
            (weights_in, left_in, right_in, invleft_in, invright_in),
            (weights_mid, left_mid, right_mid, invleft_mid, invright_mid),
            (
                turned_out,
                right_out.transpose(1, 0, 2),
                left_out,
                invright_out.transpose(1, 0, 2),
                invleft_out,
            ),
        ),
    )
    first, second, third = (outs[1 + 4 * k : 5 + 4 * k] for k in range(3))
    third = (
        third[0].transpose(1, 2, 0),
        third[1].transpose(1, 2, 0),
        third[3],
        third[2].transpose(1, 0, 2),
    )
    return (
        (outs[0].reshape(()),)
        + tuple(group[which] for which in range(4) for group in (first, second, third))
        + tuple(outs[13:16])
    )


def solution(mesh):
    chips, dev = mesh.shape["hst"] // 2, mesh.shape["dev"]
    fine = jax.sharding.Mesh(mesh.devices.reshape(chips, 2, dev), AXES)
    split = P(AXES, None)
    line = P(AXES)
    whole = P()
    mapped = jax.shard_map(
        functools.partial(body, peers=chips * dev),
        mesh=fine,
        in_specs=(split,) * 8 + (line,) * 2 + (whole,) * 19,
        out_specs=(whole,) * 16,
        check_vma=False,
    )

    def run(*args):
        with jax.sharding.use_abstract_mesh(fine.abstract_mesh):
            return mapped(*args)

    return run
```

```python
import functools

import jax
import jax.numpy as jnp
from jax import lax
from jax.experimental import pallas as pl
from jax.experimental.pallas import tpu as pltpu
from jax.sharding import PartitionSpec as P

LANES = 128
SPAN = 256
PARTS = 2
COUNTS = jnp.float8_e4m3fn
BIG = 52 << 20
AXES = ("chip", "core", "dev")
PEERS = ("chip", "dev")

smem = pl.BlockSpec(memory_space=pltpu.SMEM)
vmem = pl.BlockSpec(memory_space=pltpu.VMEM)
anywhere = pl.BlockSpec(memory_space=pltpu.HBM)


def up(value, unit):
    return -(-value // unit) * unit


def call(kernel, name, out_shape, in_specs, out_specs, scratch, cost, room):
    return pl.pallas_call(
        kernel,
        name=name,
        out_shape=out_shape,
        in_specs=in_specs,
        out_specs=out_specs,
        scratch_shapes=scratch,
        compiler_params=pltpu.CompilerParams(vmem_limit_bytes=room),
        cost_estimate=pl.CostEstimate(
            flops=0, transcendentals=0, bytes_accessed=int(cost * 3.6e6)
        ),
    )


def dot(left, right):
    return jnp.dot(left, right, preferred_element_type=jnp.float32)


def dot_rows(left, right):
    return lax.dot_general(
        left, right, (((0,), (0,)), ((), ())), preferred_element_type=jnp.float32
    )


def dot_cols(left, right):
    return lax.dot_general(
        left, right, (((1,), (1,)), ((), ())), preferred_element_type=jnp.float32
    )


def halves(value):
    high = value.astype(jnp.bfloat16)
    return high, (value - high.astype(jnp.float32)).astype(jnp.bfloat16)


def grown(value, rows, columns):
    short = columns - value.shape[1]
    if short:
        value = jnp.concatenate([value, jnp.zeros((value.shape[0], short), value.dtype)], axis=1)
    short = rows - value.shape[0]
    if short:
        value = jnp.concatenate([value, jnp.zeros((short, columns), value.dtype)], axis=0)
    return value


def clipped_counts(valid):
    return jnp.maximum(jnp.sum(valid.astype(jnp.float32), axis=1, keepdims=True), 1.0)


def copy_rows(names, base, size, source, target):
    for u in range(size):
        target[u : u + 1, :] = source[pl.ds(names[base + u], 1), :]


def cuts(per):
    return (0, per // 2), (per // 2, per)


def pick_kernel(lists, table, out, rows, done, wanted, sems, list_sems, *, first, part, per):
    chunk = rows.shape[0]
    devices = chunk // part
    steps = out.shape[0] // chunk

    def load(step):
        where = pl.ds(pl.multiple_of(step * devices * per, devices * per), devices * per)
        return pltpu.make_async_copy(lists.at[where], wanted.at[where], list_sems.at[step])

    for step in range(steps):
        load(step).start()

    def save(step):
        where = pl.ds(pl.multiple_of(step * chunk, chunk), chunk)
        return pltpu.make_async_copy(done.at[where, :], out.at[where, :], sems.at[step])

    def body(step, carry):
        load(step).wait()
        for d in range(devices):
            base = (step * devices + d) * per + first
            for u in range(part):
                at = d * part + u
                rows[at : at + 1, :] = table[pl.ds(wanted[base + u], 1), :]
        where = pl.ds(pl.multiple_of(step * chunk, chunk), chunk)
        done[where, :] = rows[...].astype(jnp.bfloat16)
        save(step).start()
        return carry

    lax.fori_loop(0, steps, body, 0)
    for step in range(steps):
        save(step).wait()


def pick_rows(wanted, table, per, ends):
    first, last = ends
    width = table.shape[1]
    count = wanted.shape[0] // per * (last - first)
    chunk = 512
    return call(
        functools.partial(pick_kernel, first=first, part=last - first, per=per),
        "pick_rows",
        jax.ShapeDtypeStruct((count, width), jnp.bfloat16),
        [anywhere, vmem],
        anywhere,
        [
            pltpu.VMEM((chunk, width), jnp.float32),
            pltpu.VMEM((count, width), jnp.bfloat16),
            pltpu.SMEM(wanted.shape, jnp.int32),
            pltpu.SemaphoreType.DMA((count // chunk,)),
            pltpu.SemaphoreType.DMA((count // chunk,)),
        ],
        4.6,
        20 << 20,
    )(wanted, table)


def stood(flat, unit):
    size = flat.shape[1]
    flat = jnp.concatenate(
        [flat.astype(jnp.float32), jnp.full((unit - flat.shape[0], size), -1.0, jnp.float32)],
        axis=0,
    )
    step = min(LANES, size)
    parts = [jnp.transpose(flat[:, k : k + step]) for k in range(0, size, step)]
    return jnp.concatenate(parts, axis=0).astype(jnp.int32)


def reach_kernel(
    adjacent_three,
    valid_three,
    labelled,
    adjacent_two,
    valid_two,
    names,
    places,
    near_two,
    near_three,
    count,
    left,
    right,
    *,
    rows_all,
    per,
):
    fan_three, seeds = adjacent_three.shape
    fan_two, targets = adjacent_two.shape
    low = jnp.bfloat16
    blocks = rows_all // LANES
    deep = names.shape[0]
    line = labelled[...].reshape(1, seeds)
    column = jnp.transpose(jnp.broadcast_to(line.astype(jnp.float32), (8, seeds)))[:, 0:1]
    near = stood(jnp.where(valid_three[...] > 0, adjacent_three[...], -1), near_three.shape[1])
    near_three[...] = near
    here = jnp.where(column > 0.0, near, -1)
    place = lax.broadcasted_iota(jnp.int32, (seeds, targets), 1)
    hit = jnp.zeros((seeds, targets), jnp.float32)
    for j in range(fan_three):
        hit = hit + jnp.where(here[:, j : j + 1] == place, 1.0, 0.0)
    need = jnp.max(hit, axis=0, keepdims=True) + jnp.concatenate(
        [line.astype(jnp.float32), jnp.zeros((1, targets - seeds), jnp.float32)], axis=1
    )

    level = lax.broadcasted_iota(jnp.int32, (deep, targets), 0)
    lane = lax.broadcasted_iota(jnp.int32, (targets, LANES), 1)
    flat = jnp.where(valid_two[...] > 0, adjacent_two[...], -1)
    tall = stood(flat, near_two.shape[1])
    near_two[...] = tall
    flat = jnp.where(need > 0.0, flat, -1)
    for j in range(fan_two):
        left[0:deep, j * targets : (j + 1) * targets] = jnp.where(
            lax.shift_right_arithmetic(flat[j : j + 1, :], 7) == level, 1.0, 0.0
        ).astype(low)
        right[j * targets : (j + 1) * targets, :] = jnp.where(
            (tall[:, j : j + 1] & (LANES - 1)) == lane, 1.0, 0.0
        ).astype(low)
    used = dot(left[0:deep, 0 : fan_two * targets], right[0 : fan_two * targets, :])
    own = [need[:, k : k + LANES] for k in range(0, targets, LANES)]
    own = jnp.concatenate(
        own + [jnp.zeros((deep - len(own), LANES), jnp.float32)], axis=0
    )
    flag = jnp.where(used + own > 0.0, 1.0, 0.0)

    square_row = lax.broadcasted_iota(jnp.int32, (LANES, LANES), 0)
    square_col = lax.broadcasted_iota(jnp.int32, (LANES, LANES), 1)
    full = jnp.concatenate([flag, jnp.zeros((LANES - deep, LANES), jnp.float32)], axis=0)
    flag_low = full.astype(low)
    running = dot(flag_low, jnp.where(square_row <= square_col, 1.0, 0.0).astype(low))
    totals = dot(flag_low, jnp.ones((LANES, LANES), low)).astype(low)
    before = dot(jnp.where(square_row > square_col, 1.0, 0.0).astype(low), totals)
    order = (before + running - full).astype(jnp.int32)
    number = jnp.sum(flag).astype(jnp.int32)
    count[0] = number
    count[1] = lax.div(number + (SPAN - 1), SPAN)

    high = jnp.where(full > 0.0, lax.shift_right_arithmetic(order, 7), -1)
    rest = jnp.transpose((order & (LANES - 1)).astype(jnp.float32)).astype(jnp.int32)
    step = lax.broadcasted_iota(jnp.int32, (deep, LANES), 0)
    inner = lax.broadcasted_iota(jnp.int32, (deep, LANES), 1).astype(jnp.float32)
    for b in range(blocks):
        match = jnp.where(high[b : b + 1, :] == step, 1.0, 0.0)
        lanes = slice(b * LANES, (b + 1) * LANES)
        left[0:deep, lanes] = (match * inner).astype(low)
        left[deep : 2 * deep, lanes] = (match * float(b)).astype(low)
        right[lanes, :] = jnp.where(rest[:, b : b + 1] == square_col, 1.0, 0.0).astype(low)
    found = dot(left[:, 0:rows_all], right[0:rows_all, :]).astype(jnp.int32)
    where = step * LANES + lax.broadcasted_iota(jnp.int32, (deep, LANES), 1)
    name = found[deep:] * LANES + found[0:deep]
    names[...] = jnp.where(where < number, name, rows_all)
    name = jnp.minimum(jnp.where(where < number, name, 0), rows_all - 1)
    owners = -(-rows_all // per)
    owner = lax.shift_right_logical(name, per.bit_length() - 1)
    slot = name & (per - 1)
    early, late = (last - first for first, last in cuts(per))
    places[...] = jnp.where(
        slot < early, owner * early + slot, owners * early + owner * late + slot - early
    )


def reach(adjacent_three, valid_three, labelled, adjacent_two, valid_two, rows_all, per):
    targets, fan = adjacent_two.shape
    seeds = labelled.shape[0]
    deep = up(up(rows_all, 2 * SPAN) // LANES, 16)
    area = max(fan * targets, rows_all)
    return call(
        functools.partial(reach_kernel, rows_all=rows_all, per=per),
        "reach",
        (
            jax.ShapeDtypeStruct((deep, LANES), jnp.int32),
            jax.ShapeDtypeStruct((deep, LANES), jnp.int32),
            jax.ShapeDtypeStruct((targets, 16), jnp.int32),
            jax.ShapeDtypeStruct((seeds, 8), jnp.int32),
            jax.ShapeDtypeStruct((2,), jnp.int32),
        ),
        [vmem] * 5,
        (vmem,) * 4 + (smem,),
        [
            pltpu.VMEM((2 * deep, area), jnp.bfloat16),
            pltpu.VMEM((area, LANES), jnp.bfloat16),
        ],
        3.0,
        8 << 20,
    )(adjacent_three.T, valid_three.T, labelled, adjacent_two.T, valid_two.T)


def tally_kernel(count, names, adjacent, valid, *refs, per, which):
    multiply = which == 0
    if multiply:
        source, out, table, rows, spread, marked, buffer, sems, terms, sums = refs
        width = source.shape[1]
        terms[:, 0:width] = source[...]
        terms[:, width:] = jnp.ones((source.shape[0], width), jnp.bfloat16)
    else:
        out, table, rows, spread, marked, buffer, sems = refs
    low = jnp.bfloat16
    fan, targets = adjacent.shape
    unit = spread.shape[0]
    groups = SPAN // unit
    few = 8 if multiply else groups
    used = count[1]
    high_all = buffer.shape[2] // SPAN
    first, last = cuts(per)[which]
    size = last - first

    slot = adjacent[...]
    owner = lax.shift_right_logical(slot, per.bit_length() - 1)
    inner = slot & (per - 1)
    here = (valid[...] > 0) & (inner >= first) & (inner < last)
    slot = jnp.where(here, owner * size + inner - first, -1)
    slot = jnp.concatenate(
        [slot.astype(jnp.float32), jnp.full((unit - fan, targets), -1.0, jnp.float32)], axis=0
    )
    for b in range(0, targets, LANES):
        table[b : b + LANES, :] = jnp.transpose(slot[:, b : b + LANES]).astype(jnp.int32)
    table[targets:, :] = jnp.full((table.shape[0] - targets, unit), -1, jnp.int32)

    across = lax.broadcasted_iota(jnp.int32, (unit, SPAN), 1)
    down = lax.broadcasted_iota(jnp.int32, (unit, SPAN), 0)
    spread[...] = jnp.where(lax.div(across, unit) == down, 1.0, 0.0).astype(low)
    lane = across.astype(jnp.float32).astype(low)
    one = jnp.ones((unit, SPAN), low)
    zero = jnp.zeros((unit, SPAN), low)

    def copies(block, slot):
        where = pl.ds(pl.multiple_of(block * SPAN, SPAN), SPAN)
        result = sums if multiply else buffer
        return pltpu.make_async_copy(result.at[slot], out.at[where, :], sems.at[slot])

    def body(block, carry):
        slot = lax.rem(block, 2)

        @pl.when(block >= 2)
        def _():
            copies(block - 2, slot).wait()

        copy_rows(names, block * SPAN, SPAN, table, rows)
        high = lax.shift_right_arithmetic(rows[...], 8).astype(jnp.float32).astype(low)
        own = lax.rem(lax.broadcasted_iota(jnp.int32, (SPAN, SPAN), 0), unit) == lax.rem(
            lax.broadcasted_iota(jnp.int32, (SPAN, SPAN), 1), unit
        )
        marked[...] = jnp.where(own, dot(high, spread[...]), -1.0).astype(low)

        def single(g):
            first = pl.multiple_of(g * unit, unit)
            rest = (rows[pl.ds(first, unit), :] & (SPAN - 1)).astype(jnp.float32)
            columns = [
                jnp.where(
                    jnp.broadcast_to(rest[:, j : j + 1], (unit, SPAN)).astype(low) == lane,
                    one,
                    zero,
                )
                for j in range(unit)
            ]
            mark = marked[pl.ds(first, unit), :]
            marks = [
                jnp.where(mark == jnp.full((unit, SPAN), float(q), low), one, zero)
                for q in range(high_all)
            ]
            return dot(jnp.concatenate(marks, axis=0), jnp.concatenate(columns, axis=0))

        def group(step, inner):
            for u in range(0, few, 2):
                pair = [single(step * few + u), single(step * few + u + 1)]
                where = pl.ds(pl.multiple_of((step * few + u) * unit, 2 * unit), 2 * unit)
                for q in range(high_all):
                    tile = jnp.concatenate(
                        [item[q * unit : (q + 1) * unit] for item in pair], axis=0
                    )
                    buffer[slot, where, q * SPAN : (q + 1) * SPAN] = tile.astype(buffer.dtype)
            return inner

        lax.fori_loop(0, groups // few, group, 0)
        if multiply:
            sums[slot] = dot(buffer[slot], terms[...])
        copies(block, slot).start()
        return carry

    lax.fori_loop(0, used, body, 0)

    @pl.when(used >= 2)
    def _():
        copies(used - 2, lax.rem(used - 2, 2)).wait()

    @pl.when(used >= 1)
    def _():
        copies(used - 1, lax.rem(used - 1, 2)).wait()


def tally(count, names, adjacent, valid, padded, devices, per, which, sources):
    targets = adjacent.shape[0]
    unit = 16
    first, last = cuts(per)[which]
    wide = devices * (last - first)
    multiply = which == 0
    width = sources[0].shape[1] if multiply else 0
    scratch = [
        pltpu.VMEM((targets + 8, unit), jnp.int32),
        pltpu.VMEM((SPAN, unit), jnp.int32),
        pltpu.VMEM((unit, SPAN), jnp.bfloat16),
        pltpu.VMEM((SPAN, SPAN), jnp.bfloat16),
        pltpu.VMEM((2, SPAN, wide), jnp.bfloat16 if multiply else COUNTS),
        pltpu.SemaphoreType.DMA((2,)),
    ]
    if multiply:
        out = jax.ShapeDtypeStruct((3 * padded, 2 * width), jnp.float32)
        scratch += [
            pltpu.VMEM((wide, 2 * width), jnp.bfloat16),
            pltpu.VMEM((2, SPAN, 2 * width), jnp.float32),
        ]
    else:
        out = jax.ShapeDtypeStruct((padded, wide), COUNTS)
    return call(
        functools.partial(tally_kernel, per=per, which=which),
        "early_sums" if multiply else "tally",
        out,
        [smem, smem] + [vmem] * (2 + len(sources)),
        anywhere,
        scratch,
        14.0,
        BIG,
    )(count, names, adjacent.T, valid.T, *sources)


def link_kernel(count, names, near, out, buffer, sems, *, fan):
    targets = near.shape[0]
    tile = 32
    blocks = count[1]
    all_blocks = buffer.shape[0] - 2
    across = SPAN // LANES

    def line(block, part):
        return jnp.broadcast_to(names[pl.ds(block * across + part, 1), :], (tile, LANES))

    def save(block):
        return pltpu.make_async_copy(buffer.at[block], out.at[block], sems.at[block])

    def rows(step, carry):
        first = pl.multiple_of(step * tile, tile)
        here = near[pl.ds(first, tile), :]
        spread = [jnp.broadcast_to(here[:, j : j + 1], (tile, LANES)) for j in range(fan)]
        own = first + lax.broadcasted_iota(jnp.int32, (tile, LANES), 0)

        def columns(block, inner):
            for part in range(across):
                name = line(block, part)
                number = jnp.zeros((tile, LANES), jnp.float32)
                for j in range(fan):
                    number = number + jnp.where(spread[j] == name, 1.0, 0.0)
                lanes = pl.ds(part * LANES, LANES)
                buffer[block, pl.ds(first, tile), lanes] = number.astype(jnp.bfloat16)
            return inner

        lax.fori_loop(0, blocks, columns, 0)
        for block in range(2):
            for part in range(across):
                lanes = slice(part * LANES, (part + 1) * LANES)
                buffer[all_blocks + block, pl.ds(first, tile), lanes] = jnp.where(
                    own == line(block, part), 1.0, 0.0
                ).astype(jnp.bfloat16)
        return carry

    lax.fori_loop(0, targets // tile, rows, 0)

    def start(block, carry):
        save(block).start()
        return carry

    def finish(block, carry):
        save(block).wait()
        return carry

    for ends in ((0, blocks), (all_blocks, all_blocks + 2)):
        lax.fori_loop(*ends, start, 0)
    for ends in ((0, blocks), (all_blocks, all_blocks + 2)):
        lax.fori_loop(*ends, finish, 0)


def link_matrix(count, names, near, fan, padded):
    blocks = padded // SPAN
    targets = near.shape[0]
    return call(
        functools.partial(link_kernel, fan=fan),
        "link_matrix",
        jax.ShapeDtypeStruct((4 * blocks, targets, SPAN), jnp.bfloat16),
        [smem, vmem, vmem],
        anywhere,
        [
            pltpu.VMEM((blocks + 2, targets, SPAN), jnp.bfloat16),
            pltpu.SemaphoreType.DMA((blocks + 2,)),
        ],
        5.0,
        BIG,
    )(count, names, near)


def step_kernel(
    info,
    count,
    places,
    partial,
    tallies,
    links,
    *refs,
    classes,
):
    sources = refs[:PARTS]
    step_body(
        info, count, places, partial, tallies, links, sources, *refs[PARTS:],
        classes=classes,
    )


def step_body(
    info,
    count,
    places,
    partial,
    tallies,
    links,
    sources,
    near_two,
    near_three,
    labels,
    labelled,
    weights_in,
    weights_mid,
    weights_out,
    biases_line,
    keep,
    send,
    slopes,
    packed,
    sums,
    weight_sums,
    mid_sums,
    out_sums,
    own_table,
    late_table,
    mixin,
    own_rows,
    joined,
    late,
    early,
    hid,
    down_low,
    bias_sums,
    link,
    sems,
    link_sems,
    early_rows,
    spots,
    own_sems,
    *,
    classes,
):
    targets = links.shape[1]
    hidden = weights_in.shape[2]
    seeds = labels.shape[0]
    biases = biases_line[...].reshape(1, biases_line.shape[0])
    label, marked = [
        jnp.transpose(
            jnp.broadcast_to(item[...].reshape(1, seeds).astype(jnp.float32), (8, seeds))
        )[:, 0:1]
        for item in (labels, labelled)
    ]
    wide = up(classes, LANES)
    core = info[0]
    used = count[1]
    low = jnp.bfloat16
    width = sources[0].shape[1]

    def load(pair, slot, size):
        rows = pl.ds(pl.multiple_of(pair * 2 * SPAN, 2 * SPAN), size)
        here = pl.ds(0, size)
        return (
            pltpu.make_async_copy(tallies.at[rows, :], late.at[slot, here, :], sems.at[slot, 0]),
            pltpu.make_async_copy(partial.at[rows, :], early.at[slot, here, :], sems.at[slot, 1]),
        )

    def start_load(pair, slot):
        @pl.when(2 * pair + 1 < used)
        def _():
            for copy in load(pair, slot, 2 * SPAN):
                copy.start()

        @pl.when(2 * pair + 1 == used)
        def _():
            for copy in load(pair, slot, SPAN):
                copy.start()

    def load_link(block):
        return pltpu.make_async_copy(links.at[block], link.at[block], link_sems.at[block])

    held = early_rows.shape[0]
    fetch_early = pltpu.make_async_copy(
        sources[0].at[pl.ds(0, held), :], early_rows, own_sems.at[0]
    )
    fetch_late = pltpu.make_async_copy(
        sources[1], late_table.at[:, pl.ds(0, width)], own_sems.at[1]
    )
    fetch_places = pltpu.make_async_copy(places, spots, own_sems.at[2])
    fetch_early.start()
    fetch_places.start()
    fetch_late.start()
    start_load(0, 0)

    def start_link(block, carry):
        load_link(block).start()
        return carry

    lax.fori_loop(0, used, start_link, 0)
    own_link = link.shape[0] - 2
    for block in range(2):
        load_link(own_link + block).start()
    late_table[:, width:] = jnp.ones((late_table.shape[0], width), low)
    fetch_places.wait()
    fetch_early.wait()
    own_table[0:held, :] = early_rows[...].astype(jnp.float32)
    fetch_late.wait()
    own_table[held:, :] = late_table[0 : own_table.shape[0] - held, 0:width].astype(jnp.float32)

    w_in = weights_in[...].astype(low).reshape(2 * weights_in.shape[1], hidden)
    bias_in = biases[:, 0:hidden]
    bias_mid = biases[:, hidden : 2 * hidden]
    bias_out = jnp.concatenate(
        [
            biases[:, 2 * hidden : 2 * hidden + classes],
            jnp.full((1, wide - classes), -1e30, jnp.float32),
        ],
        axis=1,
    )

    sums[...] = jnp.zeros_like(sums)

    def paired(block, size):
        if size == SPAN:
            return link[block]
        return jnp.concatenate([link[block], link[block + 1]], axis=1)

    def forward(pair, size):
        base = pair * 2 * SPAN
        rows = pl.ds(pl.multiple_of(base, 2 * SPAN), size)
        slot = lax.rem(pair, 2)
        for copy in load(pair, slot, size):
            copy.wait()
        for step in range(size // SPAN):
            load_link(2 * pair + step).wait()
        start_load(pair + 1, 1 - slot)
        for part in range(0, size, SPAN):
            for u in range(part, part + SPAN):
                own_rows[u : u + 1, :] = own_table[pl.ds(spots[base + u], 1), :]
            here = slice(part, part + SPAN)
            joined[here, :] = dot(late[slot, here, :].astype(low), late_table[...]) + (
                early[slot, here, :]
            )
        mixin[rows, 0:width] = own_rows[0:size, :].astype(low)
        mixin[rows, width:] = (
            joined[0:size, 0:width] / jnp.maximum(joined[0:size, width:], 1.0)
        ).astype(low)
        z = dot(mixin[rows, :], w_in) + bias_in
        s = 1.0 / (1.0 + jnp.exp(-z))
        slopes[rows, :] = s * (1.0 + z * (1.0 - s))
        hid[0:size, :] = (z * s).astype(low)
        sums[0:targets, :] += dot(paired(2 * pair, size), hid[0:size, :])

        @pl.when(pair == 0)
        def _():
            for block in range(2):
                load_link(own_link + block).wait()
            sums[targets:, :] = dot(paired(own_link, size), hid[0:size, :])

    pairs = lax.div(used, 2)
    odd = lax.rem(used, 2) == 1

    def forward_pair(pair, carry):
        forward(pair, 2 * SPAN)
        return carry

    lax.fori_loop(0, pairs, forward_pair, 0)

    @pl.when(odd)
    def _():
        forward(pairs, SPAN)

    total = sums[...]
    counts_two = clipped_counts(near_two[...] >= 0)
    mixed_one = (total[0:targets] / counts_two).astype(low)
    self_one = total[targets:].astype(low)
    w_mid = weights_mid[...].astype(low)
    both_one = jnp.concatenate([self_one, mixed_one], axis=1)
    z = dot(both_one, w_mid.reshape(2 * hidden, hidden)) + bias_mid
    s = 1.0 / (1.0 + jnp.exp(-z))
    slope_mid = s * (1.0 + z * (1.0 - s))
    hidden_two = (z * s).astype(low)

    here = near_three[...]
    place = lax.broadcasted_iota(jnp.int32, (seeds, targets), 1)
    number = jnp.zeros((seeds, targets), jnp.float32)
    for j in range(here.shape[1]):
        number = number + jnp.where(here[:, j : j + 1] == place, 1.0, 0.0)
    number = number.astype(low)
    counts_three = clipped_counts(here >= 0)
    mixed_two = (dot(number, hidden_two) / counts_three).astype(low)
    self_two = hidden_two[0:seeds]
    w_out = [
        jnp.concatenate(
            [weights_out[:, k, :], jnp.zeros((wide - classes, hidden), jnp.float32)], axis=0
        ).astype(low)
        for k in range(2)
    ]
    both_two = jnp.concatenate([self_two, mixed_two], axis=1)
    logits = dot_cols(both_two, jnp.concatenate(w_out, axis=1)) + bias_out
    top = jnp.max(logits, axis=1, keepdims=True)
    log_total = top + jnp.log(jnp.sum(jnp.exp(logits - top), axis=1, keepdims=True))
    onehot = jnp.where(
        label.astype(jnp.int32) == lax.broadcasted_iota(jnp.int32, (seeds, wide), 1), 1.0, 0.0
    )
    picked = jnp.sum(jnp.where(onehot > 0.0, logits, 0.0), axis=1, keepdims=True)
    loss = jnp.sum(marked * (log_total - picked), axis=0, keepdims=True)
    counted = jnp.sum(marked, axis=0, keepdims=True)
    grad_out = (marked * (jnp.exp(logits - log_total) - onehot)).astype(low)

    out_sums[...] = dot_rows(grad_out, both_two)
    bias_grad_out = jnp.sum(grad_out.astype(jnp.float32), axis=0, keepdims=True)
    to_self = dot(grad_out, w_out[0])
    spread = (dot(grad_out, w_out[1]) / counts_three).astype(low)
    sums[0:targets, :] = dot_rows(number, spread)
    sums[0:seeds, :] += to_self
    grad_mid = (sums[0:targets, :] * slope_mid).astype(low)

    mid_sums[...] = dot_rows(both_one, grad_mid)
    bias_grad_mid = jnp.sum(grad_mid.astype(jnp.float32), axis=0, keepdims=True)
    down = jnp.concatenate(
        [dot_cols(grad_mid, w_mid[1]) / counts_two, dot_cols(grad_mid, w_mid[0])], axis=0
    )
    down_low[...] = down.astype(low)

    weight_sums[...] = jnp.zeros_like(weight_sums)

    bias_sums[...] = jnp.zeros_like(bias_sums)

    def backward(pair, size):
        rows = pl.ds(pl.multiple_of(pair * 2 * SPAN, 2 * SPAN), size)
        joined[0:size, :] = dot_rows(paired(2 * pair, size), down_low[0:targets, :])

        @pl.when(pair == 0)
        def _():
            joined[0:size, :] += dot_rows(paired(own_link, size), down_low[targets:, :])

        grad = (joined[0:size, :] * slopes[rows, :]).astype(low)
        weight_sums[...] += dot_rows(mixin[rows, :], grad)
        bias_sums[0:1, :] += jnp.sum(grad.astype(jnp.float32), axis=0, keepdims=True)

    def backward_pair(pair, carry):
        backward(pair, 2 * SPAN)
        return carry

    lax.fori_loop(0, pairs, backward_pair, 0)

    @pl.when(odd)
    def _():
        backward(pairs, SPAN)

    bias_grad_in = bias_sums[0:1, :]
    row = 0
    for part in (weight_sums, mid_sums):
        for column in range(0, hidden, LANES):
            packed[row : row + part.shape[0], :] = part[:, column : column + LANES]
            row += part.shape[0]
    tall = up(classes, 16)
    for column in range(0, 2 * hidden, LANES):
        packed[row : row + tall, :] = out_sums[0:tall, column : column + LANES]
        row += tall
    packed[row:, :] = jnp.zeros((packed.shape[0] - row, LANES), jnp.float32)
    lane = lax.broadcasted_iota(jnp.int32, (1, LANES), 1)
    scalars = jnp.where(lane == 0, loss, 0.0) + jnp.where(lane == 1, counted, 0.0)
    extra = [
        item[:, column : column + LANES]
        for item in (bias_grad_in, bias_grad_mid, bias_grad_out)
        for column in range(0, hidden, LANES)
    ] + [scalars, jnp.zeros((1, LANES), jnp.float32)]
    extra = jnp.concatenate(extra, axis=0)
    high = extra.astype(low).astype(jnp.float32)
    packed[packed.shape[0] - 16 :, :] = jnp.concatenate([high, extra - high], axis=0)
    half = keep.shape[0]
    keep[...] = packed[pl.ds(pl.multiple_of(core * half, 16), half), :].astype(low)
    send[...] = packed[pl.ds(pl.multiple_of((1 - core) * half, 16), half), :].astype(low)


def run_step(info, count, places, partial, tallies, links, sources, rest, half, classes, held):
    padded = tallies.shape[0]
    blocks, targets = padded // SPAN, links.shape[1]
    total, width = sources[-1].shape
    hidden = rest[4].shape[2]
    wide = up(classes, LANES)
    return call(
        functools.partial(step_kernel, classes=classes),
        "step",
        (jax.ShapeDtypeStruct((half, LANES), jnp.bfloat16),) * 2,
        [smem] * 2 + [anywhere] * (4 + PARTS) + [vmem] * 8,
        (vmem, vmem),
        [
            pltpu.VMEM((padded, hidden), jnp.float32),
            pltpu.VMEM((2 * half, LANES), jnp.float32),
            pltpu.VMEM((2 * targets, hidden), jnp.float32),
            pltpu.VMEM((2 * width, hidden), jnp.float32),
            pltpu.VMEM((2 * hidden, hidden), jnp.float32),
            pltpu.VMEM((wide, 2 * hidden), jnp.float32),
            pltpu.VMEM((held, width), jnp.float32),
            pltpu.VMEM((total, 2 * width), jnp.bfloat16),
            pltpu.VMEM((padded, 2 * width), jnp.bfloat16),
            pltpu.VMEM((2 * SPAN, width), jnp.float32),
            pltpu.VMEM((2 * SPAN, 2 * width), jnp.float32),
            pltpu.VMEM((2, 2 * SPAN, total), COUNTS),
            pltpu.VMEM((2, 2 * SPAN, 2 * width), jnp.float32),
            pltpu.VMEM((2 * SPAN, hidden), jnp.bfloat16),
            pltpu.VMEM((2 * targets, hidden), jnp.bfloat16),
            pltpu.VMEM((8, hidden), jnp.float32),
            pltpu.VMEM((blocks + 2, targets, SPAN), jnp.bfloat16),
            pltpu.SemaphoreType.DMA((2, 2)),
            pltpu.SemaphoreType.DMA((blocks + 2,)),
            pltpu.VMEM((held * sources[0].shape[0] // (sources[0].shape[0] + total), width), jnp.bfloat16),
            pltpu.SMEM(places.shape, jnp.int32),
            pltpu.SemaphoreType.DMA((3,)),
        ],
        14.0,
        BIG,
    )(info, count, places, partial, tallies, links, *sources, *rest)


def refit(total, rows):
    extra = total[rows - 16 : rows - 8] + total[rows - 8 : rows]
    high = extra.astype(jnp.bfloat16).astype(jnp.float32)
    return jnp.concatenate([high, extra - high], axis=0)


def pair_kernel(info, mine, theirs, out):
    total = mine[...].astype(jnp.float32) + theirs[...].astype(jnp.float32)
    out[...] = total.astype(jnp.bfloat16)

    @pl.when(info[0] == 1)
    def _():
        rows = total.shape[0]
        out[rows - 16 :, :] = refit(total, rows).astype(jnp.bfloat16)


def pair_sum(info, mine, theirs):
    return call(
        pair_kernel,
        "pair_sum",
        jax.ShapeDtypeStruct(mine.shape, jnp.bfloat16),
        [smem, vmem, vmem],
        vmem,
        [],
        0.6,
        6 << 20,
    )(info, mine, theirs)


def spread_kernel(info, pieces, out):
    total = pieces[0].astype(jnp.float32)
    for k in range(1, pieces.shape[0]):
        total = total + pieces[k].astype(jnp.float32)
    rows = total.shape[0]
    fitted = jnp.concatenate([total[0 : rows - 16], refit(total, rows)], axis=0)
    result = jnp.where(info[1] == 1, fitted, total).astype(jnp.bfloat16)
    for k in range(pieces.shape[0]):
        out[k] = result


def spread_sum(info, pieces):
    return call(
        spread_kernel,
        "spread_sum",
        jax.ShapeDtypeStruct(pieces.shape, jnp.bfloat16),
        [smem, vmem],
        vmem,
        [],
        0.6,
        6 << 20,
    )(info, pieces)


def update_kernel(
    info, fixes, mine, theirs, biases, moment_one, moment_two, *refs
):
    groups = [refs[5 * k : 5 * k + 5] for k in range(3)]
    loss_out = refs[15]
    outs = [refs[16 + 4 * k : 20 + 4 * k] for k in range(3)]
    bias_out, first_out, second_out = refs[28:31]
    packed = refs[31]
    low = jnp.bfloat16
    half = mine.shape[0]
    core = info[0]
    packed[pl.ds(pl.multiple_of(core * half, 16), half), :] = mine[...]
    packed[pl.ds(pl.multiple_of((1 - core) * half, 16), half), :] = theirs[...]
    last = packed.shape[0]
    extra = packed[last - 16 :, :].astype(jnp.float32)
    extra = extra[0:8] + extra[8:16]
    counted = extra[6:7, 1:2]
    inverse = 1.0 / counted
    loss_out[...] = extra[6:7, 0:1] / counted
    scale = 0.5 * inverse * inverse

    row = 0
    for group in range(3):
        master, left, right, left_root, right_root = groups[group]
        new_master, copy, new_left, new_right = outs[group]
        turned = group == 2
        depth, hidden = (master.shape[0], master.shape[2]) if turned else master.shape[1:]
        deep = up(depth, LANES)

        def take(ref, k, middle):
            return ref[:, k, :] if middle else ref[k]

        def put(ref, k, middle, value):
            if middle:
                ref[:, k, :] = value
            else:
                ref[k] = value

        grads = []
        if turned:
            tall = up(depth, 16)
            for k in range(2):
                parts = []
                for column in range(0, hidden, LANES):
                    parts.append(packed[row : row + tall, :])
                    row += tall
                grads.append(grown(jnp.concatenate(parts, axis=1), deep, hidden))
        else:
            parts = []
            for column in range(0, hidden, LANES):
                parts.append(packed[row : row + 2 * depth, :])
                row += 2 * depth
            whole = jnp.concatenate(parts, axis=1)
            grads = [whole[k * depth : (k + 1) * depth] for k in range(2)]

        for k in range(2):
            grad = grads[k]
            for old, new, size, product, middle in (
                (left, new_left, depth, dot_cols(grad, grad), turned),
                (right, new_right, hidden, dot_rows(grad, grad), False),
            ):
                corner = old[0:1, k, 0:1] if middle else old[k, 0:1, 0:1]
                eye = lax.broadcasted_iota(jnp.int32, (size, size), 0) == (
                    lax.broadcasted_iota(jnp.int32, (size, size), 1)
                )
                value = jnp.where(eye, 0.5 * corner, 0.0) + scale * product[0:size, 0:size]
                put(new, k, middle, value)
            root = jnp.concatenate(
                halves(grown(take(left_root, k, turned), deep, deep)), axis=1
            )
            middle_high, middle_rest = halves(dot(root, jnp.concatenate([grad, grad], axis=0)))
            root_high, root_rest = halves(right_root[k])
            way = dot(
                jnp.concatenate([middle_high, middle_high, middle_rest], axis=1),
                jnp.concatenate([root_high, root_rest, root_high], axis=0),
            )[0:depth]
            put(new_master, k, turned, take(master, k, turned) - inverse * way)
        copy[...] = new_master[...].astype(low)

    size = biases.shape[0]
    grad = jnp.concatenate([extra[k : k + 1, :] for k in range(6)], axis=1)[:, 0:size]
    grad = grad / counted

    def line(ref):
        return ref[...].reshape(1, size)

    first = 0.9 * line(moment_one) + 0.1 * grad
    second = 0.95 * line(moment_two) + 0.05 * grad * grad
    old = line(biases)
    fresh = old - 0.1 * (
        (first / fixes[0]) / (jnp.sqrt(second / fixes[1]) + 1e-08) + 0.01 * old
    )
    for ref, value in ((bias_out, fresh), (first_out, first), (second_out, second)):
        ref[...] = value[0]


def run_update(info, fixes, mine, theirs, vectors, groups):
    outs = [jax.ShapeDtypeStruct((1, 1), jnp.float32)]
    flat = []
    for master, left, right, left_root, right_root in groups:
        flat += [master, left, right, left_root, right_root]
        outs += [
            jax.ShapeDtypeStruct(master.shape, jnp.float32),
            jax.ShapeDtypeStruct(master.shape, jnp.bfloat16),
            jax.ShapeDtypeStruct(left_root.shape, jnp.float32),
            jax.ShapeDtypeStruct(right_root.shape, jnp.float32),
        ]
    outs += [jax.ShapeDtypeStruct(vectors[0].shape, jnp.float32)] * 3
    return call(
        update_kernel,
        "update",
        tuple(outs),
        [smem] * 2 + [vmem] * (5 + len(flat)),
        (vmem,) * len(outs),
        [pltpu.VMEM((2 * mine.shape[0], LANES), jnp.bfloat16)],
        4.0,
        16 << 20,
    )(info, fixes, mine, theirs, *vectors, *flat)


def body(
    features,
    requests,
    adjacent_one,
    adjacent_two,
    adjacent_three,
    valid_one,
    valid_two,
    valid_three,
    labels,
    labelled,
    weights_in,
    weights_mid,
    weights_out,
    biases,
    moment_one,
    moment_two,
    step_count,
    left_in,
    left_mid,
    left_out,
    right_in,
    right_mid,
    right_out,
    invleft_in,
    invleft_mid,
    invleft_out,
    invright_in,
    invright_mid,
    invright_out,
    *,
    peers,
):
    width = features.shape[1]
    devices, per = requests.shape
    targets = adjacent_one.shape[0]
    padded = up(targets, 2 * SPAN)
    classes = weights_out.shape[2]
    hidden = weights_in.shape[2]
    core = lax.axis_index("core")
    own = lax.axis_index(PEERS)

    wanted = lax.all_to_all(requests, AXES, split_axis=0, concat_axis=0, tiled=True)
    names, places, near_two, near_three, count = reach(
        adjacent_three, valid_three, labelled, adjacent_two, valid_two, targets, per
    )
    wanted, count = lax.optimization_barrier((wanted.reshape(-1), count))
    early_cut, late_cut = cuts(per)

    def trade(found):
        pulled = lax.all_to_all(
            found.reshape(devices, -1, width), AXES, split_axis=0, concat_axis=0, tiled=True
        )
        return pulled.reshape(-1, width)

    early_source = trade(pick_rows(wanted, features, per, early_cut))
    found = pick_rows(wanted, features, per, late_cut)
    links = link_matrix(count, names, near_two, adjacent_two.shape[1], padded)
    names, places = names.reshape(-1), places.reshape(-1)
    late_tally = tally(
        count, names, adjacent_one, valid_one, padded, devices, per, 1, ()
    )

    core_info = jnp.stack([core, ((core == 1) & (own == peers - 1)).astype(jnp.int32)])
    core_info = core_info.astype(jnp.int32)
    stepped = step_count.astype(jnp.float32)
    fixes = jnp.stack([1.0 - 0.9**stepped, 1.0 - 0.95**stepped])
    found, late_tally, links, info, fixes = lax.optimization_barrier(
        (found, late_tally, links, core_info, fixes)
    )
    late_source = trade(found)
    partial = tally(
        count, names, adjacent_one, valid_one, padded, devices, per, 0, (early_source,)
    )

    rows = (2 * width + 2 * weights_mid.shape[1]) * (hidden // LANES)
    rows += up(classes, 16) * (2 * hidden // LANES)
    each = up(-(-(rows + 16) // (2 * peers)), 8)
    half = each * peers
    turned_out = weights_out.transpose(2, 0, 1)
    keep, send = run_step(
        info,
        count,
        places,
        partial,
        late_tally,
        links,
        (early_source, late_source),
        (
            near_two,
            near_three,
            labels,
            labelled,
            weights_in,
            weights_mid,
            turned_out,
            biases,
        ),
        half,
        classes,
        -(-targets // per) * per,
    )
    swap = [(0, 1), (1, 0)]
    theirs = lax.ppermute(send, "core", swap)
    summed = pair_sum(info, keep, theirs).reshape(peers, each, LANES)
    pieces = lax.all_to_all(summed, PEERS, split_axis=0, concat_axis=0, tiled=True)
    shared = spread_sum(info, pieces)
    mine = lax.all_to_all(shared, PEERS, split_axis=0, concat_axis=0, tiled=True)
    mine = mine.reshape(half, LANES)
    theirs = lax.ppermute(mine, "core", swap)

    outs = run_update(
        info,
        fixes,
        mine,
        theirs,
        (biases, moment_one, moment_two),
        (
            (weights_in, left_in, right_in, invleft_in, invright_in),
            (weights_mid, left_mid, right_mid, invleft_mid, invright_mid),
            (
                turned_out,
                right_out.transpose(1, 0, 2),
                left_out,
                invright_out.transpose(1, 0, 2),
                invleft_out,
            ),
        ),
    )
    first, second, third = (outs[1 + 4 * k : 5 + 4 * k] for k in range(3))
    third = (
        third[0].transpose(1, 2, 0),
        third[1].transpose(1, 2, 0),
        third[3],
        third[2].transpose(1, 0, 2),
    )
    return (
        (outs[0].reshape(()),)
        + tuple(group[which] for which in range(4) for group in (first, second, third))
        + tuple(outs[13:16])
    )


def solution(mesh):
    chips, dev = mesh.shape["hst"] // 2, mesh.shape["dev"]
    fine = jax.sharding.Mesh(mesh.devices.reshape(chips, 2, dev), AXES)
    split = P(AXES, None)
    line = P(AXES)
    whole = P()
    mapped = jax.shard_map(
        functools.partial(body, peers=chips * dev),
        mesh=fine,
        in_specs=(split,) * 8 + (line,) * 2 + (whole,) * 19,
        out_specs=(whole,) * 16,
        check_vma=False,
    )

    def run(*args):
        with jax.sharding.use_abstract_mesh(fine.abstract_mesh):
            return mapped(*args)

    return run
```

```python
import functools

import jax
import jax.numpy as jnp
from jax import lax
from jax.experimental import pallas as pl
from jax.experimental.pallas import tpu as pltpu
from jax.sharding import PartitionSpec as P

LANES = 128
SPAN = 256
PARTS = 2
COUNTS = jnp.float8_e4m3fn
BIG = 52 << 20
ALL = (64 << 20) - (64 << 10)
AXES = ("chip", "core", "dev")
PEERS = ("chip", "dev")

smem = pl.BlockSpec(memory_space=pltpu.SMEM)
vmem = pl.BlockSpec(memory_space=pltpu.VMEM)
anywhere = pl.BlockSpec(memory_space=pltpu.HBM)


def up(value, unit):
    return -(-value // unit) * unit


def call(kernel, name, out_shape, in_specs, out_specs, scratch, cost, room):
    return pl.pallas_call(
        kernel,
        name=name,
        out_shape=out_shape,
        in_specs=in_specs,
        out_specs=out_specs,
        scratch_shapes=scratch,
        compiler_params=pltpu.CompilerParams(vmem_limit_bytes=room),
        cost_estimate=pl.CostEstimate(
            flops=0, transcendentals=0, bytes_accessed=int(cost * 3.6e6)
        ),
    )


def dot(left, right):
    return jnp.dot(left, right, preferred_element_type=jnp.float32)


def dot_rows(left, right):
    return lax.dot_general(
        left, right, (((0,), (0,)), ((), ())), preferred_element_type=jnp.float32
    )


def dot_cols(left, right):
    return lax.dot_general(
        left, right, (((1,), (1,)), ((), ())), preferred_element_type=jnp.float32
    )


def halves(value):
    high = value.astype(jnp.bfloat16)
    return high, (value - high.astype(jnp.float32)).astype(jnp.bfloat16)


def grown(value, rows, columns):
    short = columns - value.shape[1]
    if short:
        value = jnp.concatenate([value, jnp.zeros((value.shape[0], short), value.dtype)], axis=1)
    short = rows - value.shape[0]
    if short:
        value = jnp.concatenate([value, jnp.zeros((short, columns), value.dtype)], axis=0)
    return value


def clipped_counts(valid):
    return jnp.maximum(jnp.sum(valid.astype(jnp.float32), axis=1, keepdims=True), 1.0)


def copy_rows(names, base, size, source, target):
    for u in range(size):
        target[u : u + 1, :] = source[pl.ds(names[base + u], 1), :]


def cuts(per):
    return (0, per // 2), (per // 2, per)


def list_kernel(requests, out, sem):
    copy = pltpu.make_async_copy(requests, out.at[:, 0, :], sem)
    copy.start()
    copy.wait()


def as_lists(requests):
    devices, per = requests.shape
    return call(
        list_kernel,
        "as_lists",
        jax.ShapeDtypeStruct((devices, 1, per), jnp.int32),
        [anywhere],
        anywhere,
        [pltpu.SemaphoreType.DMA(())],
        0.6,
        ALL,
    )(requests)


def pick_kernel(
    lists, source, out, rows, done, wanted, sems, list_sems, table, table_sem, *, first, part, per
):
    fill = pltpu.make_async_copy(source, table, table_sem)
    fill.start()
    chunk = rows.shape[0]
    devices = chunk // part
    steps = out.shape[0] // chunk

    def load(step):
        where = pl.ds(pl.multiple_of(step * devices * per, devices * per), devices * per)
        return pltpu.make_async_copy(lists.at[where], wanted.at[where], list_sems.at[step])

    for step in range(steps):
        load(step).start()
    fill.wait()

    def save(step):
        where = pl.ds(pl.multiple_of(step * chunk, chunk), chunk)
        return pltpu.make_async_copy(done.at[where, :], out.at[where, :], sems.at[step])

    def body(step, carry):
        load(step).wait()
        for d in range(devices):
            base = (step * devices + d) * per + first
            for u in range(part):
                at = d * part + u
                rows[at : at + 1, :] = table[pl.ds(wanted[base + u], 1), :]
        where = pl.ds(pl.multiple_of(step * chunk, chunk), chunk)
        done[where, :] = rows[...].astype(jnp.bfloat16)
        save(step).start()
        return carry

    lax.fori_loop(0, steps, body, 0)
    for step in range(steps):
        save(step).wait()


def pick_rows(wanted, table, per, ends):
    first, last = ends
    width = table.shape[1]
    count = wanted.shape[0] // per * (last - first)
    chunk = 512
    return call(
        functools.partial(pick_kernel, first=first, part=last - first, per=per),
        "pick_rows",
        jax.ShapeDtypeStruct((count, width), jnp.bfloat16),
        [anywhere, anywhere],
        anywhere,
        [
            pltpu.VMEM((chunk, width), jnp.float32),
            pltpu.VMEM((count, width), jnp.bfloat16),
            pltpu.SMEM(wanted.shape, jnp.int32),
            pltpu.SemaphoreType.DMA((count // chunk,)),
            pltpu.SemaphoreType.DMA((count // chunk,)),
            pltpu.VMEM(table.shape, jnp.float32),
            pltpu.SemaphoreType.DMA(()),
        ],
        8.0,
        ALL,
    )(wanted, table)


def stood(flat, unit):
    size = flat.shape[1]
    flat = jnp.concatenate(
        [flat.astype(jnp.float32), jnp.full((unit - flat.shape[0], size), -1.0, jnp.float32)],
        axis=0,
    )
    step = min(LANES, size)
    parts = [jnp.transpose(flat[:, k : k + step]) for k in range(0, size, step)]
    return jnp.concatenate(parts, axis=0).astype(jnp.int32)


def reach_kernel(
    adjacent_three,
    valid_three,
    labelled,
    adjacent_two,
    valid_two,
    names,
    places,
    near_two,
    near_three,
    count,
    left,
    right,
    *,
    rows_all,
    per,
):
    fan_three, seeds = adjacent_three.shape
    fan_two, targets = adjacent_two.shape
    low = jnp.bfloat16
    blocks = rows_all // LANES
    deep = names.shape[0]
    line = labelled[...].reshape(1, seeds)
    column = jnp.transpose(jnp.broadcast_to(line.astype(jnp.float32), (8, seeds)))[:, 0:1]
    near = stood(jnp.where(valid_three[...] > 0, adjacent_three[...], -1), near_three.shape[1])
    near_three[...] = near
    here = jnp.where(column > 0.0, near, -1)
    place = lax.broadcasted_iota(jnp.int32, (seeds, targets), 1)
    hit = jnp.zeros((seeds, targets), jnp.float32)
    for j in range(fan_three):
        hit = hit + jnp.where(here[:, j : j + 1] == place, 1.0, 0.0)
    need = jnp.max(hit, axis=0, keepdims=True) + jnp.concatenate(
        [line.astype(jnp.float32), jnp.zeros((1, targets - seeds), jnp.float32)], axis=1
    )

    level = lax.broadcasted_iota(jnp.int32, (deep, targets), 0)
    lane = lax.broadcasted_iota(jnp.int32, (targets, LANES), 1)
    flat = jnp.where(valid_two[...] > 0, adjacent_two[...], -1)
    tall = stood(flat, near_two.shape[1])
    near_two[...] = tall
    flat = jnp.where(need > 0.0, flat, -1)
    for j in range(fan_two):
        left[0:deep, j * targets : (j + 1) * targets] = jnp.where(
            lax.shift_right_arithmetic(flat[j : j + 1, :], 7) == level, 1.0, 0.0
        ).astype(low)
        right[j * targets : (j + 1) * targets, :] = jnp.where(
            (tall[:, j : j + 1] & (LANES - 1)) == lane, 1.0, 0.0
        ).astype(low)
    used = dot(left[0:deep, 0 : fan_two * targets], right[0 : fan_two * targets, :])
    own = [need[:, k : k + LANES] for k in range(0, targets, LANES)]
    own = jnp.concatenate(
        own + [jnp.zeros((deep - len(own), LANES), jnp.float32)], axis=0
    )
    flag = jnp.where(used + own > 0.0, 1.0, 0.0)

    square_row = lax.broadcasted_iota(jnp.int32, (LANES, LANES), 0)
    square_col = lax.broadcasted_iota(jnp.int32, (LANES, LANES), 1)
    full = jnp.concatenate([flag, jnp.zeros((LANES - deep, LANES), jnp.float32)], axis=0)
    flag_low = full.astype(low)
    running = dot(flag_low, jnp.where(square_row <= square_col, 1.0, 0.0).astype(low))
    totals = dot(flag_low, jnp.ones((LANES, LANES), low)).astype(low)
    before = dot(jnp.where(square_row > square_col, 1.0, 0.0).astype(low), totals)
    order = (before + running - full).astype(jnp.int32)
    number = jnp.sum(flag).astype(jnp.int32)
    count[0] = number
    count[1] = lax.div(number + (SPAN - 1), SPAN)

    high = jnp.where(full > 0.0, lax.shift_right_arithmetic(order, 7), -1)
    rest = jnp.transpose((order & (LANES - 1)).astype(jnp.float32)).astype(jnp.int32)
    step = lax.broadcasted_iota(jnp.int32, (deep, LANES), 0)
    inner = lax.broadcasted_iota(jnp.int32, (deep, LANES), 1).astype(jnp.float32)
    for b in range(blocks):
        match = jnp.where(high[b : b + 1, :] == step, 1.0, 0.0)
        lanes = slice(b * LANES, (b + 1) * LANES)
        left[0:deep, lanes] = (match * inner).astype(low)
        left[deep : 2 * deep, lanes] = (match * float(b)).astype(low)
        right[lanes, :] = jnp.where(rest[:, b : b + 1] == square_col, 1.0, 0.0).astype(low)
    found = dot(left[:, 0:rows_all], right[0:rows_all, :]).astype(jnp.int32)
    where = step * LANES + lax.broadcasted_iota(jnp.int32, (deep, LANES), 1)
    name = found[deep:] * LANES + found[0:deep]
    names[...] = jnp.where(where < number, name, rows_all)
    name = jnp.minimum(jnp.where(where < number, name, 0), rows_all - 1)
    owners = -(-rows_all // per)
    owner = lax.shift_right_logical(name, per.bit_length() - 1)
    slot = name & (per - 1)
    early, late = (last - first for first, last in cuts(per))
    places[...] = jnp.where(
        slot < early, owner * early + slot, owners * early + owner * late + slot - early
    )


def reach(adjacent_three, valid_three, labelled, adjacent_two, valid_two, rows_all, per):
    targets, fan = adjacent_two.shape
    seeds = labelled.shape[0]
    deep = up(up(rows_all, 2 * SPAN) // LANES, 16)
    area = max(fan * targets, rows_all)
    return call(
        functools.partial(reach_kernel, rows_all=rows_all, per=per),
        "reach",
        (
            jax.ShapeDtypeStruct((deep, LANES), jnp.int32),
            jax.ShapeDtypeStruct((deep, LANES), jnp.int32),
            jax.ShapeDtypeStruct((targets, 16), jnp.int32),
            jax.ShapeDtypeStruct((seeds, 8), jnp.int32),
            jax.ShapeDtypeStruct((2,), jnp.int32),
        ),
        [vmem] * 5,
        (vmem,) * 4 + (smem,),
        [
            pltpu.VMEM((2 * deep, area), jnp.bfloat16),
            pltpu.VMEM((area, LANES), jnp.bfloat16),
        ],
        3.0,
        ALL,
    )(adjacent_three.T, valid_three.T, labelled, adjacent_two.T, valid_two.T)


def tally_kernel(count, names, adjacent, valid, *refs, per, which):
    multiply = which == 0
    if multiply:
        source, out, table, rows, spread, marked, buffer, sems, terms, sums = refs
        width = source.shape[1]
        terms[:, 0:width] = source[...]
        terms[:, width:] = jnp.ones((source.shape[0], width), jnp.bfloat16)
    else:
        out, table, rows, spread, marked, buffer, sems = refs
    low = jnp.bfloat16
    fan, targets = adjacent.shape
    unit = spread.shape[0]
    groups = SPAN // unit
    few = 8 if multiply else groups
    used = count[1]
    high_all = buffer.shape[2] // SPAN
    first, last = cuts(per)[which]
    size = last - first

    slot = adjacent[...]
    owner = lax.shift_right_logical(slot, per.bit_length() - 1)
    inner = slot & (per - 1)
    here = (valid[...] > 0) & (inner >= first) & (inner < last)
    slot = jnp.where(here, owner * size + inner - first, -1)
    slot = jnp.concatenate(
        [slot.astype(jnp.float32), jnp.full((unit - fan, targets), -1.0, jnp.float32)], axis=0
    )
    for b in range(0, targets, LANES):
        table[b : b + LANES, :] = jnp.transpose(slot[:, b : b + LANES]).astype(jnp.int32)
    table[targets:, :] = jnp.full((table.shape[0] - targets, unit), -1, jnp.int32)

    across = lax.broadcasted_iota(jnp.int32, (unit, SPAN), 1)
    down = lax.broadcasted_iota(jnp.int32, (unit, SPAN), 0)
    spread[...] = jnp.where(lax.div(across, unit) == down, 1.0, 0.0).astype(low)
    lane = across.astype(jnp.float32).astype(low)
    one = jnp.ones((unit, SPAN), low)
    zero = jnp.zeros((unit, SPAN), low)

    def copies(block, slot):
        where = pl.ds(pl.multiple_of(block * SPAN, SPAN), SPAN)
        result = sums if multiply else buffer
        return pltpu.make_async_copy(result.at[slot], out.at[where, :], sems.at[slot])

    def body(block, carry):
        slot = lax.rem(block, 2)

        @pl.when(block >= 2)
        def _():
            copies(block - 2, slot).wait()

        copy_rows(names, block * SPAN, SPAN, table, rows)
        high = lax.shift_right_arithmetic(rows[...], 8).astype(jnp.float32).astype(low)
        own = lax.rem(lax.broadcasted_iota(jnp.int32, (SPAN, SPAN), 0), unit) == lax.rem(
            lax.broadcasted_iota(jnp.int32, (SPAN, SPAN), 1), unit
        )
        marked[...] = jnp.where(own, dot(high, spread[...]), -1.0).astype(low)

        def single(g):
            first = pl.multiple_of(g * unit, unit)
            rest = (rows[pl.ds(first, unit), :] & (SPAN - 1)).astype(jnp.float32)
            columns = [
                jnp.where(
                    jnp.broadcast_to(rest[:, j : j + 1], (unit, SPAN)).astype(low) == lane,
                    one,
                    zero,
                )
                for j in range(unit)
            ]
            mark = marked[pl.ds(first, unit), :]
            marks = [
                jnp.where(mark == jnp.full((unit, SPAN), float(q), low), one, zero)
                for q in range(high_all)
            ]
            return dot(jnp.concatenate(marks, axis=0), jnp.concatenate(columns, axis=0))

        def group(step, inner):
            for u in range(0, few, 2):
                pair = [single(step * few + u), single(step * few + u + 1)]
                where = pl.ds(pl.multiple_of((step * few + u) * unit, 2 * unit), 2 * unit)
                for q in range(high_all):
                    tile = jnp.concatenate(
                        [item[q * unit : (q + 1) * unit] for item in pair], axis=0
                    )
                    buffer[slot, where, q * SPAN : (q + 1) * SPAN] = tile.astype(buffer.dtype)
            return inner

        lax.fori_loop(0, groups // few, group, 0)
        if multiply:
            sums[slot] = dot(buffer[slot], terms[...])
        copies(block, slot).start()
        return carry

    lax.fori_loop(0, used, body, 0)

    @pl.when(used >= 2)
    def _():
        copies(used - 2, lax.rem(used - 2, 2)).wait()

    @pl.when(used >= 1)
    def _():
        copies(used - 1, lax.rem(used - 1, 2)).wait()


def tally(count, names, adjacent, valid, padded, devices, per, which, sources):
    targets = adjacent.shape[0]
    unit = 16
    first, last = cuts(per)[which]
    wide = devices * (last - first)
    multiply = which == 0
    width = sources[0].shape[1] if multiply else 0
    scratch = [
        pltpu.VMEM((targets + 8, unit), jnp.int32),
        pltpu.VMEM((SPAN, unit), jnp.int32),
        pltpu.VMEM((unit, SPAN), jnp.bfloat16),
        pltpu.VMEM((SPAN, SPAN), jnp.bfloat16),
        pltpu.VMEM((2, SPAN, wide), jnp.bfloat16 if multiply else COUNTS),
        pltpu.SemaphoreType.DMA((2,)),
    ]
    if multiply:
        out = jax.ShapeDtypeStruct((3 * padded, 2 * width), jnp.float32)
        scratch += [
            pltpu.VMEM((wide, 2 * width), jnp.bfloat16),
            pltpu.VMEM((2, SPAN, 2 * width), jnp.float32),
        ]
    else:
        out = jax.ShapeDtypeStruct((padded, wide), COUNTS)
    return call(
        functools.partial(tally_kernel, per=per, which=which),
        "early_sums" if multiply else "tally",
        out,
        [smem, smem] + [vmem] * (2 + len(sources)),
        anywhere,
        scratch,
        14.0,
        BIG,
    )(count, names, adjacent.T, valid.T, *sources)


def link_kernel(count, names, near, out, buffer, sems, *, fan):
    targets = near.shape[0]
    tile = 32
    blocks = count[1]
    all_blocks = buffer.shape[0] - 2
    across = SPAN // LANES

    def line(block, part):
        return jnp.broadcast_to(names[pl.ds(block * across + part, 1), :], (tile, LANES))

    def save(block):
        return pltpu.make_async_copy(buffer.at[block], out.at[block], sems.at[block])

    def rows(step, carry):
        first = pl.multiple_of(step * tile, tile)
        here = near[pl.ds(first, tile), :]
        spread = [jnp.broadcast_to(here[:, j : j + 1], (tile, LANES)) for j in range(fan)]
        own = first + lax.broadcasted_iota(jnp.int32, (tile, LANES), 0)

        def columns(block, inner):
            for part in range(across):
                name = line(block, part)
                number = jnp.zeros((tile, LANES), jnp.float32)
                for j in range(fan):
                    number = number + jnp.where(spread[j] == name, 1.0, 0.0)
                lanes = pl.ds(part * LANES, LANES)
                buffer[block, pl.ds(first, tile), lanes] = number.astype(jnp.bfloat16)
            return inner

        lax.fori_loop(0, blocks, columns, 0)
        for block in range(2):
            for part in range(across):
                lanes = slice(part * LANES, (part + 1) * LANES)
                buffer[all_blocks + block, pl.ds(first, tile), lanes] = jnp.where(
                    own == line(block, part), 1.0, 0.0
                ).astype(jnp.bfloat16)
        return carry

    lax.fori_loop(0, targets // tile, rows, 0)

    def start(block, carry):
        save(block).start()
        return carry

    def finish(block, carry):
        save(block).wait()
        return carry

    for ends in ((0, blocks), (all_blocks, all_blocks + 2)):
        lax.fori_loop(*ends, start, 0)
    for ends in ((0, blocks), (all_blocks, all_blocks + 2)):
        lax.fori_loop(*ends, finish, 0)


def link_matrix(count, names, near, fan, padded):
    blocks = padded // SPAN
    targets = near.shape[0]
    return call(
        functools.partial(link_kernel, fan=fan),
        "link_matrix",
        jax.ShapeDtypeStruct((4 * blocks, targets, SPAN), jnp.bfloat16),
        [smem, vmem, vmem],
        anywhere,
        [
            pltpu.VMEM((blocks + 2, targets, SPAN), jnp.bfloat16),
            pltpu.SemaphoreType.DMA((blocks + 2,)),
        ],
        5.0,
        BIG,
    )(count, names, near)


def step_kernel(
    info,
    count,
    places,
    partial,
    tallies,
    links,
    *refs,
    classes,
):
    sources = refs[:PARTS]
    step_body(
        info, count, places, partial, tallies, links, sources, *refs[PARTS:],
        classes=classes,
    )


def step_body(
    info,
    count,
    places,
    partial,
    tallies,
    links,
    sources,
    near_two,
    near_three,
    labels,
    labelled,
    weights_in,
    weights_mid,
    weights_out,
    biases_line,
    keep,
    send,
    slopes,
    packed,
    sums,
    weight_sums,
    mid_sums,
    out_sums,
    own_table,
    late_table,
    mixin,
    own_rows,
    joined,
    late,
    early,
    hid,
    down_low,
    bias_sums,
    link,
    sems,
    link_sems,
    early_rows,
    spots,
    own_sems,
    *,
    classes,
):
    targets = links.shape[1]
    hidden = weights_in.shape[2]
    seeds = labels.shape[0]
    biases = biases_line[...].reshape(1, biases_line.shape[0])
    label, marked = [
        jnp.transpose(
            jnp.broadcast_to(item[...].reshape(1, seeds).astype(jnp.float32), (8, seeds))
        )[:, 0:1]
        for item in (labels, labelled)
    ]
    wide = up(classes, LANES)
    core = info[0]
    used = count[1]
    low = jnp.bfloat16
    width = sources[0].shape[1]

    def load(pair, slot, size):
        rows = pl.ds(pl.multiple_of(pair * 2 * SPAN, 2 * SPAN), size)
        here = pl.ds(0, size)
        return (
            pltpu.make_async_copy(tallies.at[rows, :], late.at[slot, here, :], sems.at[slot, 0]),
            pltpu.make_async_copy(partial.at[rows, :], early.at[slot, here, :], sems.at[slot, 1]),
        )

    def start_load(pair, slot):
        @pl.when(2 * pair + 1 < used)
        def _():
            for copy in load(pair, slot, 2 * SPAN):
                copy.start()

        @pl.when(2 * pair + 1 == used)
        def _():
            for copy in load(pair, slot, SPAN):
                copy.start()

    def load_link(block):
        return pltpu.make_async_copy(links.at[block], link.at[block], link_sems.at[block])

    held = early_rows.shape[0]
    fetch_early = pltpu.make_async_copy(
        sources[0].at[pl.ds(0, held), :], early_rows, own_sems.at[0]
    )
    fetch_late = pltpu.make_async_copy(
        sources[1], late_table.at[:, pl.ds(0, width)], own_sems.at[1]
    )
    fetch_places = pltpu.make_async_copy(places, spots, own_sems.at[2])
    fetch_early.start()
    fetch_places.start()
    fetch_late.start()
    start_load(0, 0)

    def start_link(block, carry):
        load_link(block).start()
        return carry

    lax.fori_loop(0, used, start_link, 0)
    own_link = link.shape[0] - 2
    for block in range(2):
        load_link(own_link + block).start()
    late_table[:, width:] = jnp.ones((late_table.shape[0], width), low)
    fetch_places.wait()
    fetch_early.wait()
    own_table[0:held, :] = early_rows[...].astype(jnp.float32)
    fetch_late.wait()
    own_table[held:, :] = late_table[0 : own_table.shape[0] - held, 0:width].astype(jnp.float32)

    w_in = weights_in[...].astype(low).reshape(2 * weights_in.shape[1], hidden)
    bias_in = biases[:, 0:hidden]
    bias_mid = biases[:, hidden : 2 * hidden]
    bias_out = jnp.concatenate(
        [
            biases[:, 2 * hidden : 2 * hidden + classes],
            jnp.full((1, wide - classes), -1e30, jnp.float32),
        ],
        axis=1,
    )

    sums[...] = jnp.zeros_like(sums)

    def paired(block, size):
        if size == SPAN:
            return link[block]
        return jnp.concatenate([link[block], link[block + 1]], axis=1)

    def forward(pair, size):
        base = pair * 2 * SPAN
        rows = pl.ds(pl.multiple_of(base, 2 * SPAN), size)
        slot = lax.rem(pair, 2)
        for copy in load(pair, slot, size):
            copy.wait()
        for step in range(size // SPAN):
            load_link(2 * pair + step).wait()
        start_load(pair + 1, 1 - slot)
        for part in range(0, size, SPAN):
            for u in range(part, part + SPAN):
                own_rows[u : u + 1, :] = own_table[pl.ds(spots[base + u], 1), :]
            here = slice(part, part + SPAN)
            joined[here, :] = dot(late[slot, here, :].astype(low), late_table[...]) + (
                early[slot, here, :]
            )
        mixin[rows, 0:width] = own_rows[0:size, :].astype(low)
        mixin[rows, width:] = (
            joined[0:size, 0:width] / jnp.maximum(joined[0:size, width:], 1.0)
        ).astype(low)
        z = dot(mixin[rows, :], w_in) + bias_in
        s = 1.0 / (1.0 + jnp.exp(-z))
        slopes[rows, :] = s * (1.0 + z * (1.0 - s))
        hid[0:size, :] = (z * s).astype(low)
        sums[0:targets, :] += dot(paired(2 * pair, size), hid[0:size, :])

        @pl.when(pair == 0)
        def _():
            for block in range(2):
                load_link(own_link + block).wait()
            sums[targets:, :] = dot(paired(own_link, size), hid[0:size, :])

    pairs = lax.div(used, 2)
    odd = lax.rem(used, 2) == 1

    def forward_pair(pair, carry):
        forward(pair, 2 * SPAN)
        return carry

    lax.fori_loop(0, pairs, forward_pair, 0)

    @pl.when(odd)
    def _():
        forward(pairs, SPAN)

    total = sums[...]
    counts_two = clipped_counts(near_two[...] >= 0)
    mixed_one = (total[0:targets] / counts_two).astype(low)
    self_one = total[targets:].astype(low)
    w_mid = weights_mid[...].astype(low)
    both_one = jnp.concatenate([self_one, mixed_one], axis=1)
    z = dot(both_one, w_mid.reshape(2 * hidden, hidden)) + bias_mid
    s = 1.0 / (1.0 + jnp.exp(-z))
    slope_mid = s * (1.0 + z * (1.0 - s))
    hidden_two = (z * s).astype(low)

    here = near_three[...]
    place = lax.broadcasted_iota(jnp.int32, (seeds, targets), 1)
    number = jnp.zeros((seeds, targets), jnp.float32)
    for j in range(here.shape[1]):
        number = number + jnp.where(here[:, j : j + 1] == place, 1.0, 0.0)
    number = number.astype(low)
    counts_three = clipped_counts(here >= 0)
    mixed_two = (dot(number, hidden_two) / counts_three).astype(low)
    self_two = hidden_two[0:seeds]
    w_out = [
        jnp.concatenate(
            [weights_out[:, k, :], jnp.zeros((wide - classes, hidden), jnp.float32)], axis=0
        ).astype(low)
        for k in range(2)
    ]
    both_two = jnp.concatenate([self_two, mixed_two], axis=1)
    logits = dot_cols(both_two, jnp.concatenate(w_out, axis=1)) + bias_out
    top = jnp.max(logits, axis=1, keepdims=True)
    log_total = top + jnp.log(jnp.sum(jnp.exp(logits - top), axis=1, keepdims=True))
    onehot = jnp.where(
        label.astype(jnp.int32) == lax.broadcasted_iota(jnp.int32, (seeds, wide), 1), 1.0, 0.0
    )
    picked = jnp.sum(jnp.where(onehot > 0.0, logits, 0.0), axis=1, keepdims=True)
    loss = jnp.sum(marked * (log_total - picked), axis=0, keepdims=True)
    counted = jnp.sum(marked, axis=0, keepdims=True)
    grad_out = (marked * (jnp.exp(logits - log_total) - onehot)).astype(low)

    out_sums[...] = dot_rows(grad_out, both_two)
    bias_grad_out = jnp.sum(grad_out.astype(jnp.float32), axis=0, keepdims=True)
    to_self = dot(grad_out, w_out[0])
    spread = (dot(grad_out, w_out[1]) / counts_three).astype(low)
    sums[0:targets, :] = dot_rows(number, spread)
    sums[0:seeds, :] += to_self
    grad_mid = (sums[0:targets, :] * slope_mid).astype(low)

    mid_sums[...] = dot_rows(both_one, grad_mid)
    bias_grad_mid = jnp.sum(grad_mid.astype(jnp.float32), axis=0, keepdims=True)
    down = jnp.concatenate(
        [dot_cols(grad_mid, w_mid[1]) / counts_two, dot_cols(grad_mid, w_mid[0])], axis=0
    )
    down_low[...] = down.astype(low)

    weight_sums[...] = jnp.zeros_like(weight_sums)

    bias_sums[...] = jnp.zeros_like(bias_sums)

    def backward(pair, size):
        rows = pl.ds(pl.multiple_of(pair * 2 * SPAN, 2 * SPAN), size)
        joined[0:size, :] = dot_rows(paired(2 * pair, size), down_low[0:targets, :])

        @pl.when(pair == 0)
        def _():
            joined[0:size, :] += dot_rows(paired(own_link, size), down_low[targets:, :])

        grad = (joined[0:size, :] * slopes[rows, :]).astype(low)
        weight_sums[...] += dot_rows(mixin[rows, :], grad)
        bias_sums[0:1, :] += jnp.sum(grad.astype(jnp.float32), axis=0, keepdims=True)

    def backward_pair(pair, carry):
        backward(pair, 2 * SPAN)
        return carry

    lax.fori_loop(0, pairs, backward_pair, 0)

    @pl.when(odd)
    def _():
        backward(pairs, SPAN)

    bias_grad_in = bias_sums[0:1, :]
    row = 0
    for part in (weight_sums, mid_sums):
        for column in range(0, hidden, LANES):
            packed[row : row + part.shape[0], :] = part[:, column : column + LANES]
            row += part.shape[0]
    tall = up(classes, 16)
    for column in range(0, 2 * hidden, LANES):
        packed[row : row + tall, :] = out_sums[0:tall, column : column + LANES]
        row += tall
    packed[row:, :] = jnp.zeros((packed.shape[0] - row, LANES), jnp.float32)
    lane = lax.broadcasted_iota(jnp.int32, (1, LANES), 1)
    scalars = jnp.where(lane == 0, loss, 0.0) + jnp.where(lane == 1, counted, 0.0)
    extra = [
        item[:, column : column + LANES]
        for item in (bias_grad_in, bias_grad_mid, bias_grad_out)
        for column in range(0, hidden, LANES)
    ] + [scalars, jnp.zeros((1, LANES), jnp.float32)]
    extra = jnp.concatenate(extra, axis=0)
    high = extra.astype(low).astype(jnp.float32)
    packed[packed.shape[0] - 16 :, :] = jnp.concatenate([high, extra - high], axis=0)
    half = keep.shape[0]
    keep[...] = packed[pl.ds(pl.multiple_of(core * half, 16), half), :].astype(low)
    send[...] = packed[pl.ds(pl.multiple_of((1 - core) * half, 16), half), :].astype(low)


def run_step(info, count, places, partial, tallies, links, sources, rest, half, classes, held):
    padded = tallies.shape[0]
    blocks, targets = padded // SPAN, links.shape[1]
    total, width = sources[-1].shape
    hidden = rest[4].shape[2]
    wide = up(classes, LANES)
    return call(
        functools.partial(step_kernel, classes=classes),
        "step",
        (jax.ShapeDtypeStruct((half, LANES), jnp.bfloat16),) * 2,
        [smem] * 2 + [anywhere] * (4 + PARTS) + [vmem] * 8,
        (vmem, vmem),
        [
            pltpu.VMEM((padded, hidden), jnp.float32),
            pltpu.VMEM((2 * half, LANES), jnp.float32),
            pltpu.VMEM((2 * targets, hidden), jnp.float32),
            pltpu.VMEM((2 * width, hidden), jnp.float32),
            pltpu.VMEM((2 * hidden, hidden), jnp.float32),
            pltpu.VMEM((wide, 2 * hidden), jnp.float32),
            pltpu.VMEM((held, width), jnp.float32),
            pltpu.VMEM((total, 2 * width), jnp.bfloat16),
            pltpu.VMEM((padded, 2 * width), jnp.bfloat16),
            pltpu.VMEM((2 * SPAN, width), jnp.float32),
            pltpu.VMEM((2 * SPAN, 2 * width), jnp.float32),
            pltpu.VMEM((2, 2 * SPAN, total), COUNTS),
            pltpu.VMEM((2, 2 * SPAN, 2 * width), jnp.float32),
            pltpu.VMEM((2 * SPAN, hidden), jnp.bfloat16),
            pltpu.VMEM((2 * targets, hidden), jnp.bfloat16),
            pltpu.VMEM((8, hidden), jnp.float32),
            pltpu.VMEM((blocks + 2, targets, SPAN), jnp.bfloat16),
            pltpu.SemaphoreType.DMA((2, 2)),
            pltpu.SemaphoreType.DMA((blocks + 2,)),
            pltpu.VMEM((held * sources[0].shape[0] // (sources[0].shape[0] + total), width), jnp.bfloat16),
            pltpu.SMEM(places.shape, jnp.int32),
            pltpu.SemaphoreType.DMA((3,)),
        ],
        14.0,
        BIG,
    )(info, count, places, partial, tallies, links, *sources, *rest)


def refit(total, rows):
    extra = total[rows - 16 : rows - 8] + total[rows - 8 : rows]
    high = extra.astype(jnp.bfloat16).astype(jnp.float32)
    return jnp.concatenate([high, extra - high], axis=0)


def pair_kernel(info, mine, theirs, out):
    total = mine[...].astype(jnp.float32) + theirs[...].astype(jnp.float32)
    out[...] = total.astype(jnp.bfloat16)

    @pl.when(info[0] == 1)
    def _():
        rows = total.shape[0]
        out[rows - 16 :, :] = refit(total, rows).astype(jnp.bfloat16)


def pair_sum(info, mine, theirs):
    return call(
        pair_kernel,
        "pair_sum",
        jax.ShapeDtypeStruct(mine.shape, jnp.bfloat16),
        [smem, vmem, vmem],
        vmem,
        [],
        0.6,
        6 << 20,
    )(info, mine, theirs)


def spread_kernel(info, pieces, out):
    total = pieces[0].astype(jnp.float32)
    for k in range(1, pieces.shape[0]):
        total = total + pieces[k].astype(jnp.float32)
    rows = total.shape[0]
    fitted = jnp.concatenate([total[0 : rows - 16], refit(total, rows)], axis=0)
    result = jnp.where(info[1] == 1, fitted, total).astype(jnp.bfloat16)
    for k in range(pieces.shape[0]):
        out[k] = result


def spread_sum(info, pieces):
    return call(
        spread_kernel,
        "spread_sum",
        jax.ShapeDtypeStruct(pieces.shape, jnp.bfloat16),
        [smem, vmem],
        vmem,
        [],
        0.6,
        6 << 20,
    )(info, pieces)


def update_kernel(
    info, fixes, mine, theirs, biases, moment_one, moment_two, *refs
):
    groups = [refs[5 * k : 5 * k + 5] for k in range(3)]
    loss_out = refs[15]
    outs = [refs[16 + 4 * k : 20 + 4 * k] for k in range(3)]
    bias_out, first_out, second_out = refs[28:31]
    packed = refs[31]
    low = jnp.bfloat16
    half = mine.shape[0]
    core = info[0]
    packed[pl.ds(pl.multiple_of(core * half, 16), half), :] = mine[...]
    packed[pl.ds(pl.multiple_of((1 - core) * half, 16), half), :] = theirs[...]
    last = packed.shape[0]
    extra = packed[last - 16 :, :].astype(jnp.float32)
    extra = extra[0:8] + extra[8:16]
    counted = extra[6:7, 1:2]
    inverse = 1.0 / counted
    loss_out[...] = extra[6:7, 0:1] / counted
    scale = 0.5 * inverse * inverse

    row = 0
    for group in range(3):
        master, left, right, left_root, right_root = groups[group]
        new_master, copy, new_left, new_right = outs[group]
        turned = group == 2
        depth, hidden = (master.shape[0], master.shape[2]) if turned else master.shape[1:]
        deep = up(depth, LANES)

        def take(ref, k, middle):
            return ref[:, k, :] if middle else ref[k]

        def put(ref, k, middle, value):
            if middle:
                ref[:, k, :] = value
            else:
                ref[k] = value

        grads = []
        if turned:
            tall = up(depth, 16)
            for k in range(2):
                parts = []
                for column in range(0, hidden, LANES):
                    parts.append(packed[row : row + tall, :])
                    row += tall
                grads.append(grown(jnp.concatenate(parts, axis=1), deep, hidden))
        else:
            parts = []
            for column in range(0, hidden, LANES):
                parts.append(packed[row : row + 2 * depth, :])
                row += 2 * depth
            whole = jnp.concatenate(parts, axis=1)
            grads = [whole[k * depth : (k + 1) * depth] for k in range(2)]

        for k in range(2):
            grad = grads[k]
            for old, new, size, product, middle in (
                (left, new_left, depth, dot_cols(grad, grad), turned),
                (right, new_right, hidden, dot_rows(grad, grad), False),
            ):
                corner = old[0:1, k, 0:1] if middle else old[k, 0:1, 0:1]
                eye = lax.broadcasted_iota(jnp.int32, (size, size), 0) == (
                    lax.broadcasted_iota(jnp.int32, (size, size), 1)
                )
                value = jnp.where(eye, 0.5 * corner, 0.0) + scale * product[0:size, 0:size]
                put(new, k, middle, value)
            root = jnp.concatenate(
                halves(grown(take(left_root, k, turned), deep, deep)), axis=1
            )
            middle_high, middle_rest = halves(dot(root, jnp.concatenate([grad, grad], axis=0)))
            root_high, root_rest = halves(right_root[k])
            way = dot(
                jnp.concatenate([middle_high, middle_high, middle_rest], axis=1),
                jnp.concatenate([root_high, root_rest, root_high], axis=0),
            )[0:depth]
            put(new_master, k, turned, take(master, k, turned) - inverse * way)
        copy[...] = new_master[...].astype(low)

    size = biases.shape[0]
    grad = jnp.concatenate([extra[k : k + 1, :] for k in range(6)], axis=1)[:, 0:size]
    grad = grad / counted

    def line(ref):
        return ref[...].reshape(1, size)

    first = 0.9 * line(moment_one) + 0.1 * grad
    second = 0.95 * line(moment_two) + 0.05 * grad * grad
    old = line(biases)
    fresh = old - 0.1 * (
        (first / fixes[0]) / (jnp.sqrt(second / fixes[1]) + 1e-08) + 0.01 * old
    )
    for ref, value in ((bias_out, fresh), (first_out, first), (second_out, second)):
        ref[...] = value[0]


def run_update(info, fixes, mine, theirs, vectors, groups):
    outs = [jax.ShapeDtypeStruct((1, 1), jnp.float32)]
    flat = []
    for master, left, right, left_root, right_root in groups:
        flat += [master, left, right, left_root, right_root]
        outs += [
            jax.ShapeDtypeStruct(master.shape, jnp.float32),
            jax.ShapeDtypeStruct(master.shape, jnp.bfloat16),
            jax.ShapeDtypeStruct(left_root.shape, jnp.float32),
            jax.ShapeDtypeStruct(right_root.shape, jnp.float32),
        ]
    outs += [jax.ShapeDtypeStruct(vectors[0].shape, jnp.float32)] * 3
    return call(
        update_kernel,
        "update",
        tuple(outs),
        [smem] * 2 + [vmem] * (5 + len(flat)),
        (vmem,) * len(outs),
        [pltpu.VMEM((2 * mine.shape[0], LANES), jnp.bfloat16)],
        4.0,
        16 << 20,
    )(info, fixes, mine, theirs, *vectors, *flat)


def body(
    features,
    requests,
    adjacent_one,
    adjacent_two,
    adjacent_three,
    valid_one,
    valid_two,
    valid_three,
    labels,
    labelled,
    weights_in,
    weights_mid,
    weights_out,
    biases,
    moment_one,
    moment_two,
    step_count,
    left_in,
    left_mid,
    left_out,
    right_in,
    right_mid,
    right_out,
    invleft_in,
    invleft_mid,
    invleft_out,
    invright_in,
    invright_mid,
    invright_out,
    *,
    peers,
):
    width = features.shape[1]
    devices, per = requests.shape
    targets = adjacent_one.shape[0]
    padded = up(targets, 2 * SPAN)
    classes = weights_out.shape[2]
    hidden = weights_in.shape[2]
    core = lax.axis_index("core")
    own = lax.axis_index(PEERS)

    wanted = lax.all_to_all(as_lists(requests), AXES, split_axis=0, concat_axis=0, tiled=True)
    names, places, near_two, near_three, count = reach(
        adjacent_three, valid_three, labelled, adjacent_two, valid_two, targets, per
    )
    wanted, count = lax.optimization_barrier((wanted.reshape(-1), count))
    early_cut, late_cut = cuts(per)

    def trade(found):
        pulled = lax.all_to_all(
            found.reshape(devices, -1, width), AXES, split_axis=0, concat_axis=0, tiled=True
        )
        return pulled.reshape(-1, width)

    early_source = trade(pick_rows(wanted, features, per, early_cut))
    found = pick_rows(wanted, features, per, late_cut)
    links = link_matrix(count, names, near_two, adjacent_two.shape[1], padded)
    names, places = names.reshape(-1), places.reshape(-1)
    late_tally = tally(
        count, names, adjacent_one, valid_one, padded, devices, per, 1, ()
    )

    core_info = jnp.stack([core, ((core == 1) & (own == peers - 1)).astype(jnp.int32)])
    core_info = core_info.astype(jnp.int32)
    stepped = step_count.astype(jnp.float32)
    fixes = jnp.stack([1.0 - 0.9**stepped, 1.0 - 0.95**stepped])
    found, late_tally, links, info, fixes = lax.optimization_barrier(
        (found, late_tally, links, core_info, fixes)
    )
    late_source = trade(found)
    partial = tally(
        count, names, adjacent_one, valid_one, padded, devices, per, 0, (early_source,)
    )

    rows = (2 * width + 2 * weights_mid.shape[1]) * (hidden // LANES)
    rows += up(classes, 16) * (2 * hidden // LANES)
    each = up(-(-(rows + 16) // (2 * peers)), 8)
    half = each * peers
    turned_out = weights_out.transpose(2, 0, 1)
    keep, send = run_step(
        info,
        count,
        places,
        partial,
        late_tally,
        links,
        (early_source, late_source),
        (
            near_two,
            near_three,
            labels,
            labelled,
            weights_in,
            weights_mid,
            turned_out,
            biases,
        ),
        half,
        classes,
        -(-targets // per) * per,
    )
    swap = [(0, 1), (1, 0)]
    theirs = lax.ppermute(send, "core", swap)
    summed = pair_sum(info, keep, theirs).reshape(peers, each, LANES)
    pieces = lax.all_to_all(summed, PEERS, split_axis=0, concat_axis=0, tiled=True)
    shared = spread_sum(info, pieces)
    mine = lax.all_to_all(shared, PEERS, split_axis=0, concat_axis=0, tiled=True)
    mine = mine.reshape(half, LANES)
    theirs = lax.ppermute(mine, "core", swap)

    outs = run_update(
        info,
        fixes,
        mine,
        theirs,
        (biases, moment_one, moment_two),
        (
            (weights_in, left_in, right_in, invleft_in, invright_in),
            (weights_mid, left_mid, right_mid, invleft_mid, invright_mid),
            (
                turned_out,
                right_out.transpose(1, 0, 2),
                left_out,
                invright_out.transpose(1, 0, 2),
                invleft_out,
            ),
        ),
    )
    first, second, third = (outs[1 + 4 * k : 5 + 4 * k] for k in range(3))
    third = (
        third[0].transpose(1, 2, 0),
        third[1].transpose(1, 2, 0),
        third[3],
        third[2].transpose(1, 0, 2),
    )
    return (
        (outs[0].reshape(()),)
        + tuple(group[which] for which in range(4) for group in (first, second, third))
        + tuple(outs[13:16])
    )


def solution(mesh):
    chips, dev = mesh.shape["hst"] // 2, mesh.shape["dev"]
    fine = jax.sharding.Mesh(mesh.devices.reshape(chips, 2, dev), AXES)
    split = P(AXES, None)
    line = P(AXES)
    whole = P()
    mapped = jax.shard_map(
        functools.partial(body, peers=chips * dev),
        mesh=fine,
        in_specs=(split,) * 8 + (line,) * 2 + (whole,) * 19,
        out_specs=(whole,) * 16,
        check_vma=False,
    )

    def run(*args):
        with jax.sharding.use_abstract_mesh(fine.abstract_mesh):
            return mapped(*args)

    return run
```

```python
import functools

import jax
import jax.numpy as jnp
from jax import lax
from jax.experimental import pallas as pl
from jax.experimental.pallas import tpu as pltpu
from jax.sharding import PartitionSpec as P

LANES = 128
SPAN = 256
PARTS = 2
COUNTS = jnp.float8_e4m3fn
BIG = 52 << 20
MOST = 57 << 20
AXES = ("chip", "core", "dev")
PEERS = ("chip", "dev")

smem = pl.BlockSpec(memory_space=pltpu.SMEM)
vmem = pl.BlockSpec(memory_space=pltpu.VMEM)
anywhere = pl.BlockSpec(memory_space=pltpu.HBM)


def up(value, unit):
    return -(-value // unit) * unit


def call(kernel, name, out_shape, in_specs, out_specs, scratch, cost, room):
    return pl.pallas_call(
        kernel,
        name=name,
        out_shape=out_shape,
        in_specs=in_specs,
        out_specs=out_specs,
        scratch_shapes=scratch,
        compiler_params=pltpu.CompilerParams(vmem_limit_bytes=room),
        cost_estimate=pl.CostEstimate(
            flops=0, transcendentals=0, bytes_accessed=int(cost * 3.6e6)
        ),
    )


def dot(left, right):
    return jnp.dot(left, right, preferred_element_type=jnp.float32)


def dot_rows(left, right):
    return lax.dot_general(
        left, right, (((0,), (0,)), ((), ())), preferred_element_type=jnp.float32
    )


def dot_cols(left, right):
    return lax.dot_general(
        left, right, (((1,), (1,)), ((), ())), preferred_element_type=jnp.float32
    )


def halves(value):
    high = value.astype(jnp.bfloat16)
    return high, (value - high.astype(jnp.float32)).astype(jnp.bfloat16)


def grown(value, rows, columns):
    short = columns - value.shape[1]
    if short:
        value = jnp.concatenate([value, jnp.zeros((value.shape[0], short), value.dtype)], axis=1)
    short = rows - value.shape[0]
    if short:
        value = jnp.concatenate([value, jnp.zeros((short, columns), value.dtype)], axis=0)
    return value


def clipped_counts(valid):
    return jnp.maximum(jnp.sum(valid.astype(jnp.float32), axis=1, keepdims=True), 1.0)


def copy_rows(names, base, size, source, target):
    for u in range(size):
        target[u : u + 1, :] = source[pl.ds(names[base + u], 1), :]


def cuts(per):
    return (0, per // 2), (per // 2, per)


def pick_kernel(
    lists, source, out, rows, done, wanted, sems, list_sems, table, table_sem, *, first, part, per
):
    fill = pltpu.make_async_copy(source, table, table_sem)
    fill.start()
    chunk = rows.shape[0]
    devices = chunk // part
    steps = out.shape[0] // chunk

    def load(step):
        where = pl.ds(pl.multiple_of(step * devices * per, devices * per), devices * per)
        return pltpu.make_async_copy(lists.at[where], wanted.at[where], list_sems.at[step])

    for step in range(steps):
        load(step).start()
    fill.wait()

    def save(step):
        where = pl.ds(pl.multiple_of(step * chunk, chunk), chunk)
        return pltpu.make_async_copy(done.at[where, :], out.at[where, :], sems.at[step])

    def body(step, carry):
        load(step).wait()
        for d in range(devices):
            base = (step * devices + d) * per + first
            for u in range(part):
                at = d * part + u
                rows[at : at + 1, :] = table[pl.ds(wanted[base + u], 1), :]
        where = pl.ds(pl.multiple_of(step * chunk, chunk), chunk)
        done[where, :] = rows[...].astype(jnp.bfloat16)
        save(step).start()
        return carry

    lax.fori_loop(0, steps, body, 0)
    for step in range(steps):
        save(step).wait()


def pick_rows(wanted, table, per, ends):
    first, last = ends
    width = table.shape[1]
    count = wanted.shape[0] // per * (last - first)
    chunk = 512
    return call(
        functools.partial(pick_kernel, first=first, part=last - first, per=per),
        "pick_rows",
        jax.ShapeDtypeStruct((count, width), jnp.bfloat16),
        [anywhere, anywhere],
        anywhere,
        [
            pltpu.VMEM((chunk, width), jnp.float32),
            pltpu.VMEM((count, width), jnp.bfloat16),
            pltpu.SMEM(wanted.shape, jnp.int32),
            pltpu.SemaphoreType.DMA((count // chunk,)),
            pltpu.SemaphoreType.DMA((count // chunk,)),
            pltpu.VMEM(table.shape, jnp.float32),
            pltpu.SemaphoreType.DMA(()),
        ],
        8.0,
        MOST,
    )(wanted, table)


def stood(flat, unit):
    size = flat.shape[1]
    flat = jnp.concatenate(
        [flat.astype(jnp.float32), jnp.full((unit - flat.shape[0], size), -1.0, jnp.float32)],
        axis=0,
    )
    step = min(LANES, size)
    parts = [jnp.transpose(flat[:, k : k + step]) for k in range(0, size, step)]
    return jnp.concatenate(parts, axis=0).astype(jnp.int32)


def reach_kernel(
    adjacent_three,
    valid_three,
    labelled,
    adjacent_two,
    valid_two,
    names,
    places,
    near_two,
    near_three,
    count,
    left,
    right,
    *,
    rows_all,
    per,
):
    fan_three, seeds = adjacent_three.shape
    fan_two, targets = adjacent_two.shape
    low = jnp.bfloat16
    blocks = rows_all // LANES
    deep = names.shape[0]
    line = labelled[...].reshape(1, seeds)
    column = jnp.transpose(jnp.broadcast_to(line.astype(jnp.float32), (8, seeds)))[:, 0:1]
    near = stood(jnp.where(valid_three[...] > 0, adjacent_three[...], -1), near_three.shape[1])
    near_three[...] = near
    here = jnp.where(column > 0.0, near, -1)
    place = lax.broadcasted_iota(jnp.int32, (seeds, targets), 1)
    hit = jnp.zeros((seeds, targets), jnp.float32)
    for j in range(fan_three):
        hit = hit + jnp.where(here[:, j : j + 1] == place, 1.0, 0.0)
    need = jnp.max(hit, axis=0, keepdims=True) + jnp.concatenate(
        [line.astype(jnp.float32), jnp.zeros((1, targets - seeds), jnp.float32)], axis=1
    )

    level = lax.broadcasted_iota(jnp.int32, (deep, targets), 0)
    lane = lax.broadcasted_iota(jnp.int32, (targets, LANES), 1)
    flat = jnp.where(valid_two[...] > 0, adjacent_two[...], -1)
    tall = stood(flat, near_two.shape[1])
    near_two[...] = tall
    flat = jnp.where(need > 0.0, flat, -1)
    for j in range(fan_two):
        left[0:deep, j * targets : (j + 1) * targets] = jnp.where(
            lax.shift_right_arithmetic(flat[j : j + 1, :], 7) == level, 1.0, 0.0
        ).astype(low)
        right[j * targets : (j + 1) * targets, :] = jnp.where(
            (tall[:, j : j + 1] & (LANES - 1)) == lane, 1.0, 0.0
        ).astype(low)
    used = dot(left[0:deep, 0 : fan_two * targets], right[0 : fan_two * targets, :])
    own = [need[:, k : k + LANES] for k in range(0, targets, LANES)]
    own = jnp.concatenate(
        own + [jnp.zeros((deep - len(own), LANES), jnp.float32)], axis=0
    )
    flag = jnp.where(used + own > 0.0, 1.0, 0.0)

    square_row = lax.broadcasted_iota(jnp.int32, (LANES, LANES), 0)
    square_col = lax.broadcasted_iota(jnp.int32, (LANES, LANES), 1)
    full = jnp.concatenate([flag, jnp.zeros((LANES - deep, LANES), jnp.float32)], axis=0)
    flag_low = full.astype(low)
    running = dot(flag_low, jnp.where(square_row <= square_col, 1.0, 0.0).astype(low))
    totals = dot(flag_low, jnp.ones((LANES, LANES), low)).astype(low)
    before = dot(jnp.where(square_row > square_col, 1.0, 0.0).astype(low), totals)
    order = (before + running - full).astype(jnp.int32)
    number = jnp.sum(flag).astype(jnp.int32)
    count[0] = number
    count[1] = lax.div(number + (SPAN - 1), SPAN)

    high = jnp.where(full > 0.0, lax.shift_right_arithmetic(order, 7), -1)
    rest = jnp.transpose((order & (LANES - 1)).astype(jnp.float32)).astype(jnp.int32)
    step = lax.broadcasted_iota(jnp.int32, (deep, LANES), 0)
    inner = lax.broadcasted_iota(jnp.int32, (deep, LANES), 1).astype(jnp.float32)
    for b in range(blocks):
        match = jnp.where(high[b : b + 1, :] == step, 1.0, 0.0)
        lanes = slice(b * LANES, (b + 1) * LANES)
        left[0:deep, lanes] = (match * inner).astype(low)
        left[deep : 2 * deep, lanes] = (match * float(b)).astype(low)
        right[lanes, :] = jnp.where(rest[:, b : b + 1] == square_col, 1.0, 0.0).astype(low)
    found = dot(left[:, 0:rows_all], right[0:rows_all, :]).astype(jnp.int32)
    where = step * LANES + lax.broadcasted_iota(jnp.int32, (deep, LANES), 1)
    name = found[deep:] * LANES + found[0:deep]
    names[...] = jnp.where(where < number, name, rows_all)
    name = jnp.minimum(jnp.where(where < number, name, 0), rows_all - 1)
    owners = -(-rows_all // per)
    owner = lax.shift_right_logical(name, per.bit_length() - 1)
    slot = name & (per - 1)
    early, late = (last - first for first, last in cuts(per))
    places[...] = jnp.where(
        slot < early, owner * early + slot, owners * early + owner * late + slot - early
    )


def reach(adjacent_three, valid_three, labelled, adjacent_two, valid_two, rows_all, per):
    targets, fan = adjacent_two.shape
    seeds = labelled.shape[0]
    deep = up(up(rows_all, 2 * SPAN) // LANES, 16)
    area = max(fan * targets, rows_all)
    return call(
        functools.partial(reach_kernel, rows_all=rows_all, per=per),
        "reach",
        (
            jax.ShapeDtypeStruct((deep, LANES), jnp.int32),
            jax.ShapeDtypeStruct((deep, LANES), jnp.int32),
            jax.ShapeDtypeStruct((targets, 16), jnp.int32),
            jax.ShapeDtypeStruct((seeds, 8), jnp.int32),
            jax.ShapeDtypeStruct((2,), jnp.int32),
        ),
        [vmem] * 5,
        (vmem,) * 4 + (smem,),
        [
            pltpu.VMEM((2 * deep, area), jnp.bfloat16),
            pltpu.VMEM((area, LANES), jnp.bfloat16),
        ],
        3.0,
        8 << 20,
    )(adjacent_three.T, valid_three.T, labelled, adjacent_two.T, valid_two.T)


def tally_kernel(count, names, adjacent, valid, *refs, per, which):
    multiply = which == 0
    if multiply:
        source, out, table, rows, spread, marked, buffer, sems, terms, sums = refs
        width = source.shape[1]
        terms[:, 0:width] = source[...]
        terms[:, width:] = jnp.ones((source.shape[0], width), jnp.bfloat16)
    else:
        out, table, rows, spread, marked, buffer, sems = refs
    low = jnp.bfloat16
    fan, targets = adjacent.shape
    unit = spread.shape[0]
    groups = SPAN // unit
    few = 8 if multiply else groups
    used = count[1]
    high_all = buffer.shape[2] // SPAN
    first, last = cuts(per)[which]
    size = last - first

    slot = adjacent[...]
    owner = lax.shift_right_logical(slot, per.bit_length() - 1)
    inner = slot & (per - 1)
    here = (valid[...] > 0) & (inner >= first) & (inner < last)
    slot = jnp.where(here, owner * size + inner - first, -1)
    slot = jnp.concatenate(
        [slot.astype(jnp.float32), jnp.full((unit - fan, targets), -1.0, jnp.float32)], axis=0
    )
    for b in range(0, targets, LANES):
        table[b : b + LANES, :] = jnp.transpose(slot[:, b : b + LANES]).astype(jnp.int32)
    table[targets:, :] = jnp.full((table.shape[0] - targets, unit), -1, jnp.int32)

    across = lax.broadcasted_iota(jnp.int32, (unit, SPAN), 1)
    down = lax.broadcasted_iota(jnp.int32, (unit, SPAN), 0)
    spread[...] = jnp.where(lax.div(across, unit) == down, 1.0, 0.0).astype(low)
    lane = across.astype(jnp.float32).astype(low)
    one = jnp.ones((unit, SPAN), low)
    zero = jnp.zeros((unit, SPAN), low)

    def copies(block, slot):
        where = pl.ds(pl.multiple_of(block * SPAN, SPAN), SPAN)
        result = sums if multiply else buffer
        return pltpu.make_async_copy(result.at[slot], out.at[where, :], sems.at[slot])

    def body(block, carry):
        slot = lax.rem(block, 2)

        @pl.when(block >= 2)
        def _():
            copies(block - 2, slot).wait()

        copy_rows(names, block * SPAN, SPAN, table, rows)
        high = lax.shift_right_arithmetic(rows[...], 8).astype(jnp.float32).astype(low)
        own = lax.rem(lax.broadcasted_iota(jnp.int32, (SPAN, SPAN), 0), unit) == lax.rem(
            lax.broadcasted_iota(jnp.int32, (SPAN, SPAN), 1), unit
        )
        marked[...] = jnp.where(own, dot(high, spread[...]), -1.0).astype(low)

        def single(g):
            first = pl.multiple_of(g * unit, unit)
            rest = (rows[pl.ds(first, unit), :] & (SPAN - 1)).astype(jnp.float32)
            columns = [
                jnp.where(
                    jnp.broadcast_to(rest[:, j : j + 1], (unit, SPAN)).astype(low) == lane,
                    one,
                    zero,
                )
                for j in range(unit)
            ]
            mark = marked[pl.ds(first, unit), :]
            marks = [
                jnp.where(mark == jnp.full((unit, SPAN), float(q), low), one, zero)
                for q in range(high_all)
            ]
            return dot(jnp.concatenate(marks, axis=0), jnp.concatenate(columns, axis=0))

        def group(step, inner):
            for u in range(0, few, 2):
                pair = [single(step * few + u), single(step * few + u + 1)]
                where = pl.ds(pl.multiple_of((step * few + u) * unit, 2 * unit), 2 * unit)
                for q in range(high_all):
                    tile = jnp.concatenate(
                        [item[q * unit : (q + 1) * unit] for item in pair], axis=0
                    )
                    buffer[slot, where, q * SPAN : (q + 1) * SPAN] = tile.astype(buffer.dtype)
            return inner

        lax.fori_loop(0, groups // few, group, 0)
        if multiply:
            sums[slot] = dot(buffer[slot], terms[...])
        copies(block, slot).start()
        return carry

    lax.fori_loop(0, used, body, 0)

    @pl.when(used >= 2)
    def _():
        copies(used - 2, lax.rem(used - 2, 2)).wait()

    @pl.when(used >= 1)
    def _():
        copies(used - 1, lax.rem(used - 1, 2)).wait()


def tally(count, names, adjacent, valid, padded, devices, per, which, sources):
    targets = adjacent.shape[0]
    unit = 16
    first, last = cuts(per)[which]
    wide = devices * (last - first)
    multiply = which == 0
    width = sources[0].shape[1] if multiply else 0
    scratch = [
        pltpu.VMEM((targets + 8, unit), jnp.int32),
        pltpu.VMEM((SPAN, unit), jnp.int32),
        pltpu.VMEM((unit, SPAN), jnp.bfloat16),
        pltpu.VMEM((SPAN, SPAN), jnp.bfloat16),
        pltpu.VMEM((2, SPAN, wide), jnp.bfloat16 if multiply else COUNTS),
        pltpu.SemaphoreType.DMA((2,)),
    ]
    if multiply:
        out = jax.ShapeDtypeStruct((3 * padded, 2 * width), jnp.float32)
        scratch += [
            pltpu.VMEM((wide, 2 * width), jnp.bfloat16),
            pltpu.VMEM((2, SPAN, 2 * width), jnp.float32),
        ]
    else:
        out = jax.ShapeDtypeStruct((padded, wide), COUNTS)
    return call(
        functools.partial(tally_kernel, per=per, which=which),
        "early_sums" if multiply else "tally",
        out,
        [smem, smem] + [vmem] * (2 + len(sources)),
        anywhere,
        scratch,
        14.0,
        BIG,
    )(count, names, adjacent.T, valid.T, *sources)


def link_kernel(count, names, near, out, buffer, sems, *, fan):
    targets = near.shape[0]
    tile = 32
    blocks = count[1]
    all_blocks = buffer.shape[0] - 2
    across = SPAN // LANES

    def line(block, part):
        return jnp.broadcast_to(names[pl.ds(block * across + part, 1), :], (tile, LANES))

    def save(block):
        return pltpu.make_async_copy(buffer.at[block], out.at[block], sems.at[block])

    def rows(step, carry):
        first = pl.multiple_of(step * tile, tile)
        here = near[pl.ds(first, tile), :]
        spread = [jnp.broadcast_to(here[:, j : j + 1], (tile, LANES)) for j in range(fan)]
        own = first + lax.broadcasted_iota(jnp.int32, (tile, LANES), 0)

        def columns(block, inner):
            for part in range(across):
                name = line(block, part)
                number = jnp.zeros((tile, LANES), jnp.float32)
                for j in range(fan):
                    number = number + jnp.where(spread[j] == name, 1.0, 0.0)
                lanes = pl.ds(part * LANES, LANES)
                buffer[block, pl.ds(first, tile), lanes] = number.astype(jnp.bfloat16)
            return inner

        lax.fori_loop(0, blocks, columns, 0)
        for block in range(2):
            for part in range(across):
                lanes = slice(part * LANES, (part + 1) * LANES)
                buffer[all_blocks + block, pl.ds(first, tile), lanes] = jnp.where(
                    own == line(block, part), 1.0, 0.0
                ).astype(jnp.bfloat16)
        return carry

    lax.fori_loop(0, targets // tile, rows, 0)

    def start(block, carry):
        save(block).start()
        return carry

    def finish(block, carry):
        save(block).wait()
        return carry

    for ends in ((0, blocks), (all_blocks, all_blocks + 2)):
        lax.fori_loop(*ends, start, 0)
    for ends in ((0, blocks), (all_blocks, all_blocks + 2)):
        lax.fori_loop(*ends, finish, 0)


def link_matrix(count, names, near, fan, padded):
    blocks = padded // SPAN
    targets = near.shape[0]
    return call(
        functools.partial(link_kernel, fan=fan),
        "link_matrix",
        jax.ShapeDtypeStruct((4 * blocks, targets, SPAN), jnp.bfloat16),
        [smem, vmem, vmem],
        anywhere,
        [
            pltpu.VMEM((blocks + 2, targets, SPAN), jnp.bfloat16),
            pltpu.SemaphoreType.DMA((blocks + 2,)),
        ],
        5.0,
        BIG,
    )(count, names, near)


def step_kernel(
    info,
    count,
    places,
    partial,
    tallies,
    links,
    *refs,
    classes,
):
    sources = refs[:PARTS]
    step_body(
        info, count, places, partial, tallies, links, sources, *refs[PARTS:],
        classes=classes,
    )


def step_body(
    info,
    count,
    places,
    partial,
    tallies,
    links,
    sources,
    near_two,
    near_three,
    labels,
    labelled,
    weights_in,
    weights_mid,
    weights_out,
    biases_line,
    keep,
    send,
    slopes,
    packed,
    sums,
    weight_sums,
    mid_sums,
    out_sums,
    own_table,
    late_table,
    mixin,
    own_rows,
    joined,
    late,
    early,
    hid,
    down_low,
    bias_sums,
    link,
    sems,
    link_sems,
    early_rows,
    spots,
    own_sems,
    *,
    classes,
):
    targets = links.shape[1]
    hidden = weights_in.shape[2]
    seeds = labels.shape[0]
    biases = biases_line[...].reshape(1, biases_line.shape[0])
    label, marked = [
        jnp.transpose(
            jnp.broadcast_to(item[...].reshape(1, seeds).astype(jnp.float32), (8, seeds))
        )[:, 0:1]
        for item in (labels, labelled)
    ]
    wide = up(classes, LANES)
    core = info[0]
    used = count[1]
    low = jnp.bfloat16
    width = sources[0].shape[1]

    def load(pair, slot, size):
        rows = pl.ds(pl.multiple_of(pair * 2 * SPAN, 2 * SPAN), size)
        here = pl.ds(0, size)
        return (
            pltpu.make_async_copy(tallies.at[rows, :], late.at[slot, here, :], sems.at[slot, 0]),
            pltpu.make_async_copy(partial.at[rows, :], early.at[slot, here, :], sems.at[slot, 1]),
        )

    def start_load(pair, slot):
        @pl.when(2 * pair + 1 < used)
        def _():
            for copy in load(pair, slot, 2 * SPAN):
                copy.start()

        @pl.when(2 * pair + 1 == used)
        def _():
            for copy in load(pair, slot, SPAN):
                copy.start()

    def load_link(block):
        return pltpu.make_async_copy(links.at[block], link.at[block], link_sems.at[block])

    held = early_rows.shape[0]
    fetch_early = pltpu.make_async_copy(
        sources[0].at[pl.ds(0, held), :], early_rows, own_sems.at[0]
    )
    fetch_late = pltpu.make_async_copy(
        sources[1], late_table.at[:, pl.ds(0, width)], own_sems.at[1]
    )
    fetch_places = pltpu.make_async_copy(places, spots, own_sems.at[2])
    fetch_early.start()
    fetch_places.start()
    fetch_late.start()
    start_load(0, 0)

    def start_link(block, carry):
        load_link(block).start()
        return carry

    lax.fori_loop(0, used, start_link, 0)
    own_link = link.shape[0] - 2
    for block in range(2):
        load_link(own_link + block).start()
    late_table[:, width:] = jnp.ones((late_table.shape[0], width), low)
    fetch_places.wait()
    fetch_early.wait()
    own_table[0:held, :] = early_rows[...].astype(jnp.float32)
    fetch_late.wait()
    own_table[held:, :] = late_table[0 : own_table.shape[0] - held, 0:width].astype(jnp.float32)

    w_in = weights_in[...].astype(low).reshape(2 * weights_in.shape[1], hidden)
    bias_in = biases[:, 0:hidden]
    bias_mid = biases[:, hidden : 2 * hidden]
    bias_out = jnp.concatenate(
        [
            biases[:, 2 * hidden : 2 * hidden + classes],
            jnp.full((1, wide - classes), -1e30, jnp.float32),
        ],
        axis=1,
    )

    sums[...] = jnp.zeros_like(sums)

    def paired(block, size):
        if size == SPAN:
            return link[block]
        return jnp.concatenate([link[block], link[block + 1]], axis=1)

    def forward(pair, size):
        base = pair * 2 * SPAN
        rows = pl.ds(pl.multiple_of(base, 2 * SPAN), size)
        slot = lax.rem(pair, 2)
        for copy in load(pair, slot, size):
            copy.wait()
        for step in range(size // SPAN):
            load_link(2 * pair + step).wait()
        start_load(pair + 1, 1 - slot)
        for part in range(0, size, SPAN):
            for u in range(part, part + SPAN):
                own_rows[u : u + 1, :] = own_table[pl.ds(spots[base + u], 1), :]
            here = slice(part, part + SPAN)
            joined[here, :] = dot(late[slot, here, :].astype(low), late_table[...]) + (
                early[slot, here, :]
            )
        mixin[rows, 0:width] = own_rows[0:size, :].astype(low)
        mixin[rows, width:] = (
            joined[0:size, 0:width] / jnp.maximum(joined[0:size, width:], 1.0)
        ).astype(low)
        z = dot(mixin[rows, :], w_in) + bias_in
        s = 1.0 / (1.0 + jnp.exp(-z))
        slopes[rows, :] = s * (1.0 + z * (1.0 - s))
        hid[0:size, :] = (z * s).astype(low)
        sums[0:targets, :] += dot(paired(2 * pair, size), hid[0:size, :])

        @pl.when(pair == 0)
        def _():
            for block in range(2):
                load_link(own_link + block).wait()
            sums[targets:, :] = dot(paired(own_link, size), hid[0:size, :])

    pairs = lax.div(used, 2)
    odd = lax.rem(used, 2) == 1

    def forward_pair(pair, carry):
        forward(pair, 2 * SPAN)
        return carry

    lax.fori_loop(0, pairs, forward_pair, 0)

    @pl.when(odd)
    def _():
        forward(pairs, SPAN)

    total = sums[...]
    counts_two = clipped_counts(near_two[...] >= 0)
    mixed_one = (total[0:targets] / counts_two).astype(low)
    self_one = total[targets:].astype(low)
    w_mid = weights_mid[...].astype(low)
    both_one = jnp.concatenate([self_one, mixed_one], axis=1)
    z = dot(both_one, w_mid.reshape(2 * hidden, hidden)) + bias_mid
    s = 1.0 / (1.0 + jnp.exp(-z))
    slope_mid = s * (1.0 + z * (1.0 - s))
    hidden_two = (z * s).astype(low)

    here = near_three[...]
    place = lax.broadcasted_iota(jnp.int32, (seeds, targets), 1)
    number = jnp.zeros((seeds, targets), jnp.float32)
    for j in range(here.shape[1]):
        number = number + jnp.where(here[:, j : j + 1] == place, 1.0, 0.0)
    number = number.astype(low)
    counts_three = clipped_counts(here >= 0)
    mixed_two = (dot(number, hidden_two) / counts_three).astype(low)
    self_two = hidden_two[0:seeds]
    w_out = [
        jnp.concatenate(
            [weights_out[:, k, :], jnp.zeros((wide - classes, hidden), jnp.float32)], axis=0
        ).astype(low)
        for k in range(2)
    ]
    both_two = jnp.concatenate([self_two, mixed_two], axis=1)
    logits = dot_cols(both_two, jnp.concatenate(w_out, axis=1)) + bias_out
    top = jnp.max(logits, axis=1, keepdims=True)
    log_total = top + jnp.log(jnp.sum(jnp.exp(logits - top), axis=1, keepdims=True))
    onehot = jnp.where(
        label.astype(jnp.int32) == lax.broadcasted_iota(jnp.int32, (seeds, wide), 1), 1.0, 0.0
    )
    picked = jnp.sum(jnp.where(onehot > 0.0, logits, 0.0), axis=1, keepdims=True)
    loss = jnp.sum(marked * (log_total - picked), axis=0, keepdims=True)
    counted = jnp.sum(marked, axis=0, keepdims=True)
    grad_out = (marked * (jnp.exp(logits - log_total) - onehot)).astype(low)

    out_sums[...] = dot_rows(grad_out, both_two)
    bias_grad_out = jnp.sum(grad_out.astype(jnp.float32), axis=0, keepdims=True)
    to_self = dot(grad_out, w_out[0])
    spread = (dot(grad_out, w_out[1]) / counts_three).astype(low)
    sums[0:targets, :] = dot_rows(number, spread)
    sums[0:seeds, :] += to_self
    grad_mid = (sums[0:targets, :] * slope_mid).astype(low)

    mid_sums[...] = dot_rows(both_one, grad_mid)
    bias_grad_mid = jnp.sum(grad_mid.astype(jnp.float32), axis=0, keepdims=True)
    down = jnp.concatenate(
        [dot_cols(grad_mid, w_mid[1]) / counts_two, dot_cols(grad_mid, w_mid[0])], axis=0
    )
    down_low[...] = down.astype(low)

    weight_sums[...] = jnp.zeros_like(weight_sums)

    bias_sums[...] = jnp.zeros_like(bias_sums)

    def backward(pair, size):
        rows = pl.ds(pl.multiple_of(pair * 2 * SPAN, 2 * SPAN), size)
        joined[0:size, :] = dot_rows(paired(2 * pair, size), down_low[0:targets, :])

        @pl.when(pair == 0)
        def _():
            joined[0:size, :] += dot_rows(paired(own_link, size), down_low[targets:, :])

        grad = (joined[0:size, :] * slopes[rows, :]).astype(low)
        weight_sums[...] += dot_rows(mixin[rows, :], grad)
        bias_sums[0:1, :] += jnp.sum(grad.astype(jnp.float32), axis=0, keepdims=True)

    def backward_pair(pair, carry):
        backward(pair, 2 * SPAN)
        return carry

    lax.fori_loop(0, pairs, backward_pair, 0)

    @pl.when(odd)
    def _():
        backward(pairs, SPAN)

    bias_grad_in = bias_sums[0:1, :]
    row = 0
    for part in (weight_sums, mid_sums):
        for column in range(0, hidden, LANES):
            packed[row : row + part.shape[0], :] = part[:, column : column + LANES]
            row += part.shape[0]
    tall = up(classes, 16)
    for column in range(0, 2 * hidden, LANES):
        packed[row : row + tall, :] = out_sums[0:tall, column : column + LANES]
        row += tall
    packed[row:, :] = jnp.zeros((packed.shape[0] - row, LANES), jnp.float32)
    lane = lax.broadcasted_iota(jnp.int32, (1, LANES), 1)
    scalars = jnp.where(lane == 0, loss, 0.0) + jnp.where(lane == 1, counted, 0.0)
    extra = [
        item[:, column : column + LANES]
        for item in (bias_grad_in, bias_grad_mid, bias_grad_out)
        for column in range(0, hidden, LANES)
    ] + [scalars, jnp.zeros((1, LANES), jnp.float32)]
    extra = jnp.concatenate(extra, axis=0)
    high = extra.astype(low).astype(jnp.float32)
    packed[packed.shape[0] - 16 :, :] = jnp.concatenate([high, extra - high], axis=0)
    half = keep.shape[0]
    keep[...] = packed[pl.ds(pl.multiple_of(core * half, 16), half), :].astype(low)
    send[...] = packed[pl.ds(pl.multiple_of((1 - core) * half, 16), half), :].astype(low)


def run_step(info, count, places, partial, tallies, links, sources, rest, half, classes, held):
    padded = tallies.shape[0]
    blocks, targets = padded // SPAN, links.shape[1]
    total, width = sources[-1].shape
    hidden = rest[4].shape[2]
    wide = up(classes, LANES)
    return call(
        functools.partial(step_kernel, classes=classes),
        "step",
        (jax.ShapeDtypeStruct((half, LANES), jnp.bfloat16),) * 2,
        [smem] * 2 + [anywhere] * (4 + PARTS) + [vmem] * 8,
        (vmem, vmem),
        [
            pltpu.VMEM((padded, hidden), jnp.float32),
            pltpu.VMEM((2 * half, LANES), jnp.float32),
            pltpu.VMEM((2 * targets, hidden), jnp.float32),
            pltpu.VMEM((2 * width, hidden), jnp.float32),
            pltpu.VMEM((2 * hidden, hidden), jnp.float32),
            pltpu.VMEM((wide, 2 * hidden), jnp.float32),
            pltpu.VMEM((held, width), jnp.float32),
            pltpu.VMEM((total, 2 * width), jnp.bfloat16),
            pltpu.VMEM((padded, 2 * width), jnp.bfloat16),
            pltpu.VMEM((2 * SPAN, width), jnp.float32),
            pltpu.VMEM((2 * SPAN, 2 * width), jnp.float32),
            pltpu.VMEM((2, 2 * SPAN, total), COUNTS),
            pltpu.VMEM((2, 2 * SPAN, 2 * width), jnp.float32),
            pltpu.VMEM((2 * SPAN, hidden), jnp.bfloat16),
            pltpu.VMEM((2 * targets, hidden), jnp.bfloat16),
            pltpu.VMEM((8, hidden), jnp.float32),
            pltpu.VMEM((blocks + 2, targets, SPAN), jnp.bfloat16),
            pltpu.SemaphoreType.DMA((2, 2)),
            pltpu.SemaphoreType.DMA((blocks + 2,)),
            pltpu.VMEM((held * sources[0].shape[0] // (sources[0].shape[0] + total), width), jnp.bfloat16),
            pltpu.SMEM(places.shape, jnp.int32),
            pltpu.SemaphoreType.DMA((3,)),
        ],
        14.0,
        BIG,
    )(info, count, places, partial, tallies, links, *sources, *rest)


def refit(total, rows):
    extra = total[rows - 16 : rows - 8] + total[rows - 8 : rows]
    high = extra.astype(jnp.bfloat16).astype(jnp.float32)
    return jnp.concatenate([high, extra - high], axis=0)


def pair_kernel(info, mine, theirs, out):
    total = mine[...].astype(jnp.float32) + theirs[...].astype(jnp.float32)
    out[...] = total.astype(jnp.bfloat16)

    @pl.when(info[0] == 1)
    def _():
        rows = total.shape[0]
        out[rows - 16 :, :] = refit(total, rows).astype(jnp.bfloat16)


def pair_sum(info, mine, theirs):
    return call(
        pair_kernel,
        "pair_sum",
        jax.ShapeDtypeStruct(mine.shape, jnp.bfloat16),
        [smem, vmem, vmem],
        vmem,
        [],
        0.6,
        6 << 20,
    )(info, mine, theirs)


def spread_kernel(info, pieces, out):
    total = pieces[0].astype(jnp.float32)
    for k in range(1, pieces.shape[0]):
        total = total + pieces[k].astype(jnp.float32)
    rows = total.shape[0]
    fitted = jnp.concatenate([total[0 : rows - 16], refit(total, rows)], axis=0)
    result = jnp.where(info[1] == 1, fitted, total).astype(jnp.bfloat16)
    for k in range(pieces.shape[0]):
        out[k] = result


def spread_sum(info, pieces):
    return call(
        spread_kernel,
        "spread_sum",
        jax.ShapeDtypeStruct(pieces.shape, jnp.bfloat16),
        [smem, vmem],
        vmem,
        [],
        0.6,
        6 << 20,
    )(info, pieces)


def update_kernel(
    info, fixes, mine, theirs, biases, moment_one, moment_two, *refs
):
    groups = [refs[5 * k : 5 * k + 5] for k in range(3)]
    loss_out = refs[15]
    outs = [refs[16 + 4 * k : 20 + 4 * k] for k in range(3)]
    bias_out, first_out, second_out = refs[28:31]
    packed = refs[31]
    low = jnp.bfloat16
    half = mine.shape[0]
    core = info[0]
    packed[pl.ds(pl.multiple_of(core * half, 16), half), :] = mine[...]
    packed[pl.ds(pl.multiple_of((1 - core) * half, 16), half), :] = theirs[...]
    last = packed.shape[0]
    extra = packed[last - 16 :, :].astype(jnp.float32)
    extra = extra[0:8] + extra[8:16]
    counted = extra[6:7, 1:2]
    inverse = 1.0 / counted
    loss_out[...] = extra[6:7, 0:1] / counted
    scale = 0.5 * inverse * inverse

    row = 0
    for group in range(3):
        master, left, right, left_root, right_root = groups[group]
        new_master, copy, new_left, new_right = outs[group]
        turned = group == 2
        depth, hidden = (master.shape[0], master.shape[2]) if turned else master.shape[1:]
        deep = up(depth, LANES)

        def take(ref, k, middle):
            return ref[:, k, :] if middle else ref[k]

        def put(ref, k, middle, value):
            if middle:
                ref[:, k, :] = value
            else:
                ref[k] = value

        grads = []
        if turned:
            tall = up(depth, 16)
            for k in range(2):
                parts = []
                for column in range(0, hidden, LANES):
                    parts.append(packed[row : row + tall, :])
                    row += tall
                grads.append(grown(jnp.concatenate(parts, axis=1), deep, hidden))
        else:
            parts = []
            for column in range(0, hidden, LANES):
                parts.append(packed[row : row + 2 * depth, :])
                row += 2 * depth
            whole = jnp.concatenate(parts, axis=1)
            grads = [whole[k * depth : (k + 1) * depth] for k in range(2)]

        for k in range(2):
            grad = grads[k]
            for old, new, size, product, middle in (
                (left, new_left, depth, dot_cols(grad, grad), turned),
                (right, new_right, hidden, dot_rows(grad, grad), False),
            ):
                corner = old[0:1, k, 0:1] if middle else old[k, 0:1, 0:1]
                eye = lax.broadcasted_iota(jnp.int32, (size, size), 0) == (
                    lax.broadcasted_iota(jnp.int32, (size, size), 1)
                )
                value = jnp.where(eye, 0.5 * corner, 0.0) + scale * product[0:size, 0:size]
                put(new, k, middle, value)
            root = jnp.concatenate(
                halves(grown(take(left_root, k, turned), deep, deep)), axis=1
            )
            middle_high, middle_rest = halves(dot(root, jnp.concatenate([grad, grad], axis=0)))
            root_high, root_rest = halves(right_root[k])
            way = dot(
                jnp.concatenate([middle_high, middle_high, middle_rest], axis=1),
                jnp.concatenate([root_high, root_rest, root_high], axis=0),
            )[0:depth]
            put(new_master, k, turned, take(master, k, turned) - inverse * way)
        copy[...] = new_master[...].astype(low)

    size = biases.shape[0]
    grad = jnp.concatenate([extra[k : k + 1, :] for k in range(6)], axis=1)[:, 0:size]
    grad = grad / counted

    def line(ref):
        return ref[...].reshape(1, size)

    first = 0.9 * line(moment_one) + 0.1 * grad
    second = 0.95 * line(moment_two) + 0.05 * grad * grad
    old = line(biases)
    fresh = old - 0.1 * (
        (first / fixes[0]) / (jnp.sqrt(second / fixes[1]) + 1e-08) + 0.01 * old
    )
    for ref, value in ((bias_out, fresh), (first_out, first), (second_out, second)):
        ref[...] = value[0]


def run_update(info, fixes, mine, theirs, vectors, groups):
    outs = [jax.ShapeDtypeStruct((1, 1), jnp.float32)]
    flat = []
    for master, left, right, left_root, right_root in groups:
        flat += [master, left, right, left_root, right_root]
        outs += [
            jax.ShapeDtypeStruct(master.shape, jnp.float32),
            jax.ShapeDtypeStruct(master.shape, jnp.bfloat16),
            jax.ShapeDtypeStruct(left_root.shape, jnp.float32),
            jax.ShapeDtypeStruct(right_root.shape, jnp.float32),
        ]
    outs += [jax.ShapeDtypeStruct(vectors[0].shape, jnp.float32)] * 3
    return call(
        update_kernel,
        "update",
        tuple(outs),
        [smem] * 2 + [vmem] * (5 + len(flat)),
        (vmem,) * len(outs),
        [pltpu.VMEM((2 * mine.shape[0], LANES), jnp.bfloat16)],
        4.0,
        16 << 20,
    )(info, fixes, mine, theirs, *vectors, *flat)


def body(
    features,
    requests,
    adjacent_one,
    adjacent_two,
    adjacent_three,
    valid_one,
    valid_two,
    valid_three,
    labels,
    labelled,
    weights_in,
    weights_mid,
    weights_out,
    biases,
    moment_one,
    moment_two,
    step_count,
    left_in,
    left_mid,
    left_out,
    right_in,
    right_mid,
    right_out,
    invleft_in,
    invleft_mid,
    invleft_out,
    invright_in,
    invright_mid,
    invright_out,
    *,
    peers,
):
    width = features.shape[1]
    devices, per = requests.shape
    targets = adjacent_one.shape[0]
    padded = up(targets, 2 * SPAN)
    classes = weights_out.shape[2]
    hidden = weights_in.shape[2]
    core = lax.axis_index("core")
    own = lax.axis_index(PEERS)

    wanted = lax.all_to_all(requests, AXES, split_axis=0, concat_axis=0, tiled=True)
    names, places, near_two, near_three, count = reach(
        adjacent_three, valid_three, labelled, adjacent_two, valid_two, targets, per
    )
    wanted, count = lax.optimization_barrier((wanted.reshape(-1), count))
    early_cut, late_cut = cuts(per)

    def trade(found):
        pulled = lax.all_to_all(
            found.reshape(devices, -1, width), AXES, split_axis=0, concat_axis=0, tiled=True
        )
        return pulled.reshape(-1, width)

    early_source = trade(pick_rows(wanted, features, per, early_cut))
    found = pick_rows(wanted, features, per, late_cut)
    links = link_matrix(count, names, near_two, adjacent_two.shape[1], padded)
    names, places = names.reshape(-1), places.reshape(-1)
    late_tally = tally(
        count, names, adjacent_one, valid_one, padded, devices, per, 1, ()
    )

    core_info = jnp.stack([core, ((core == 1) & (own == peers - 1)).astype(jnp.int32)])
    core_info = core_info.astype(jnp.int32)
    stepped = step_count.astype(jnp.float32)
    fixes = jnp.stack([1.0 - 0.9**stepped, 1.0 - 0.95**stepped])
    found, late_tally, links, info, fixes = lax.optimization_barrier(
        (found, late_tally, links, core_info, fixes)
    )
    late_source = trade(found)
    partial = tally(
        count, names, adjacent_one, valid_one, padded, devices, per, 0, (early_source,)
    )

    rows = (2 * width + 2 * weights_mid.shape[1]) * (hidden // LANES)
    rows += up(classes, 16) * (2 * hidden // LANES)
    each = up(-(-(rows + 16) // (2 * peers)), 8)
    half = each * peers
    turned_out = weights_out.transpose(2, 0, 1)
    keep, send = run_step(
        info,
        count,
        places,
        partial,
        late_tally,
        links,
        (early_source, late_source),
        (
            near_two,
            near_three,
            labels,
            labelled,
            weights_in,
            weights_mid,
            turned_out,
            biases,
        ),
        half,
        classes,
        -(-targets // per) * per,
    )
    swap = [(0, 1), (1, 0)]
    theirs = lax.ppermute(send, "core", swap)
    summed = pair_sum(info, keep, theirs).reshape(peers, each, LANES)
    pieces = lax.all_to_all(summed, PEERS, split_axis=0, concat_axis=0, tiled=True)
    shared = spread_sum(info, pieces)
    mine = lax.all_to_all(shared, PEERS, split_axis=0, concat_axis=0, tiled=True)
    mine = mine.reshape(half, LANES)
    theirs = lax.ppermute(mine, "core", swap)

    outs = run_update(
        info,
        fixes,
        mine,
        theirs,
        (biases, moment_one, moment_two),
        (
            (weights_in, left_in, right_in, invleft_in, invright_in),
            (weights_mid, left_mid, right_mid, invleft_mid, invright_mid),
            (
                turned_out,
                right_out.transpose(1, 0, 2),
                left_out,
                invright_out.transpose(1, 0, 2),
                invleft_out,
            ),
        ),
    )
    first, second, third = (outs[1 + 4 * k : 5 + 4 * k] for k in range(3))
    third = (
        third[0].transpose(1, 2, 0),
        third[1].transpose(1, 2, 0),
        third[3],
        third[2].transpose(1, 0, 2),
    )
    return (
        (outs[0].reshape(()),)
        + tuple(group[which] for which in range(4) for group in (first, second, third))
        + tuple(outs[13:16])
    )


def solution(mesh):
    chips, dev = mesh.shape["hst"] // 2, mesh.shape["dev"]
    fine = jax.sharding.Mesh(mesh.devices.reshape(chips, 2, dev), AXES)
    split = P(AXES, None)
    line = P(AXES)
    whole = P()
    mapped = jax.shard_map(
        functools.partial(body, peers=chips * dev),
        mesh=fine,
        in_specs=(split,) * 8 + (line,) * 2 + (whole,) * 19,
        out_specs=(whole,) * 16,
        check_vma=False,
    )

    def run(*args):
        with jax.sharding.use_abstract_mesh(fine.abstract_mesh):
            return mapped(*args)

    return run
```
